32 devices in a mesh: seq: 8 (over y, x, core), batch: 4 (over z).
Axes of the slice: x: 2, y: 2, z: 4, core: 2. Of those that a mesh axis runs over, the one named last changes fastest.
Arguments:
- inputs: bfloat16 [4, 1024, 1024], P('batch', 'seq'), may hold values from -6 to 6
- first_gain: float32 [1024], replicated, may hold values from 0.5 to 1.5
- first_shift: float32 [1024], replicated, may hold values from -3 to 3
- decay_rate: float32 [1024, 32], replicated, may hold values from 0.00024414062 to 0.05
- rotation: float32 [1024, 32], replicated, may hold values from 0 to 0.5
- out_real: float32 [1024, 32], replicated, may hold values from -0.15625 to 0.15625
- out_imag: float32 [1024, 32], replicated, may hold values from -0.15625 to 0.15625
- skip_gain: float32 [1024], replicated, may hold values from -4 to 4
- glu_weight: bfloat16 [1024, 2048], replicated, may hold values from -0.1875 to 0.1875
- glu_bias: float32 [2048], replicated, may hold values from -3 to 3
- second_gain: float32 [1024], replicated, may hold values from 0.5 to 1.5
- second_shift: float32 [1024], replicated, may hold values from -3 to 3
- up_weight: bfloat16 [1024, 4096], replicated, may hold values from -0.1875 to 0.1875
- up_bias: float32 [4096], replicated, may hold values from -3 to 3
- down_weight: bfloat16 [4096, 1024], replicated, may hold values from -0.09375 to 0.09375
- down_bias: float32 [1024], replicated, may hold values from -3 to 3
- prior_state: float32 [4, 2, 32, 1024], P('batch'), may hold values from -67.88225 to 67.88225
- cotangent: bfloat16 [4, 1024, 1024], P('batch', 'seq'), may hold values from -6 to 6
Outputs:
- outputs: bfloat16 [4, 1024, 1024], P('batch', 'seq')
- input_grad: bfloat16 [4, 1024, 1024], P('batch', 'seq')
- state_grad: float32 [4, 2, 32, 1024], P('batch')
- first_gain_grad: float32 [1024], P(('seq', 'batch'))
- first_shift_grad: float32 [1024], P(('seq', 'batch'))
- decay_rate_grad: float32 [1024, 32], P(('seq', 'batch'))
- rotation_grad: float32 [1024, 32], P(('seq', 'batch'))
- out_real_grad: float32 [1024, 32], P(('seq', 'batch'))
- out_imag_grad: float32 [1024, 32], P(('seq', 'batch'))
- skip_gain_grad: float32 [1024], P(('seq', 'batch'))
- glu_weight_grad: float32 [1024, 2048], P(('seq', 'batch'))
- glu_bias_grad: float32 [2048], P(('seq', 'batch'))
- second_gain_grad: float32 [1024], P(('seq', 'batch'))
- second_shift_grad: float32 [1024], P(('seq', 'batch'))
- up_weight_grad: float32 [1024, 4096], P(('seq', 'batch'))
- up_bias_grad: float32 [4096], P(('seq', 'batch'))
- down_weight_grad: float32 [4096, 1024], P(('seq', 'batch'))
- down_bias_grad: float32 [1024], P(('seq', 'batch'))
The draws below stay inside these ranges and needn't reach their ends.
All inputs are finite; a program needn't handle non-finite values.
Results may differ from the reference program's by a relative error of at most 0.0058.
Values sent between devices are 32-bit elements; how exact they have to be, the bound alone decides.
A program may use at most 256 MiB of HBM per device.

```python
import math
import jax
import jax.numpy as jnp
from jax import lax

H = 1024
FF = 4096
MODES = 32
KLEN = 128
TOK_DEV = 128
SEQLEN = 1024
SEGS = 4
N_SEQ = 8


def steps_of(own_key, dims, shards, low, high):
    loudness, own = 1.0, jax.random.fold_in(own_key, 6)
    for dim, shards_of in shards:
        heights = jnp.exp(jax.random.uniform(jax.random.fold_in(own, dim), (shards_of,), jnp.float32, low / len(shards), high / len(shards)))
        loudness = loudness * jnp.repeat(heights, dims[dim] // shards_of).reshape([-1 if axis == dim else 1 for axis in range(len(dims))])
    return loudness


def scatter_about(key, dims, scale, reach, split=(), kind=jnp.bfloat16):
    entries = jax.random.normal(key, dims, jnp.float32) * scale
    if len(split) > 0:
        entries = steps_of(key, dims, split, -0.22, 0.18) * entries
    return jnp.clip(entries, min=-reach, max=reach).astype(kind)


def setup_inputs(seed: int = 0) -> dict:
    splits = jax.random.split(jax.random.key(seed), 19)
    return {
        "inputs": scatter_about(splits[0], (SEGS, SEQLEN, H), 1.0, 6.0, ((0, 4), (1, 8))),
        "first_gain": jnp.clip(1.0 + 0.1 * jax.random.normal(splits[1], (H,), jnp.float32), 0.5, 1.5),
        "first_shift": scatter_about(splits[2], (H,), 0.3, 3.0, (), jnp.float32),
        "decay_rate": jnp.clip(jnp.exp(jax.random.uniform(splits[3], (H, MODES), jnp.float32, math.log(0.00024414062), math.log(0.05))), 0.00024414062, 0.05),
        "rotation": jnp.clip(jax.random.uniform(splits[4], (H, MODES), jnp.float32, 0.0, 0.5), 0.0, 0.5),
        "out_real": scatter_about(splits[5], (H, MODES), ((2 * KLEN * MODES) ** -0.5), 0.15625, (), jnp.float32),
        "out_imag": scatter_about(splits[6], (H, MODES), ((2 * KLEN * MODES) ** -0.5), 0.15625, (), jnp.float32),
        "skip_gain": scatter_about(splits[7], (H,), 1.0, 4.0, (), jnp.float32),
        "glu_weight": scatter_about(splits[8], (H, 2 * H), H ** -0.5, 0.1875),
        "glu_bias": scatter_about(splits[9], (2 * H,), 0.3, 3.0, (), jnp.float32),
        "second_gain": jnp.clip(1.0 + 0.1 * jax.random.normal(splits[10], (H,), jnp.float32), 0.5, 1.5),
        "second_shift": scatter_about(splits[11], (H,), 0.3, 3.0, (), jnp.float32),
        "up_weight": scatter_about(splits[12], (H, FF), H ** -0.5, 0.1875),
        "up_bias": scatter_about(splits[13], (FF,), 0.3, 3.0, (), jnp.float32),
        "down_weight": scatter_about(splits[14], (FF, H), FF ** -0.5, 0.09375),
        "down_bias": scatter_about(splits[15], (H,), 0.3, 3.0, (), jnp.float32),
        "prior_state": scatter_about(splits[16], (SEGS, 2, MODES, H), (KLEN ** 0.5), 67.88225, ((0, 4),), jnp.float32),
        "cotangent": scatter_about(splits[17], (SEGS, SEQLEN, H), 1.0, 6.0, ((0, 4), (1, 8))),
    }


@jax.custom_vjp
def low(v):
    return lax.optimization_barrier(v.astype(jnp.bfloat16)).astype(jnp.float32)

@jax.custom_vjp
def low_back(v):
    return v

def low_keep(v):
    return (low(v), None)

def low_pass(kept, grad):
    return (grad,)

def back_keep(v):
    return (v, None)

def back_low(kept, grad):
    return (low(grad),)
low.defvjp(low_keep, low_pass)
low_back.defvjp(back_keep, back_low)
EPSILON = 1e-05
HIGHEST = lax.Precision.HIGHEST

def norm_rows(values, gain, shift):
    center = values - lax.optimization_barrier(jnp.mean(values, axis=-1, keepdims=True))
    spread = lax.optimization_barrier(jnp.mean(center * center, axis=-1, keepdims=True))
    return center * lax.rsqrt(spread + EPSILON) * gain + shift

def mode_terms(rate_modes, freq_modes, elapsed):
    moment = elapsed[None, :, None]
    damping = jnp.exp(-rate_modes[:, None, :] * moment)
    return (damping * jnp.cos(freq_modes[:, None, :] * moment), damping * jnp.sin(freq_modes[:, None, :] * moment))

def state_block(offset, rate_modes, freq_modes, drive_real, drive_imag):
    elapsed = (offset + jnp.arange(TOK_DEV) + 1).astype(jnp.float32)
    power_real, power_imag = mode_terms(rate_modes, freq_modes, elapsed)
    return lax.optimization_barrier(jnp.sum(power_real * drive_real[:, None, :] - power_imag * drive_imag[:, None, :], axis=0))

def segment_forward(params, source, prior_seg):
    first_gain, first_shift, decay_rate, rotation, out_real, out_imag, skip_gain, glu_weight, glu_bias, second_gain, second_shift, up_weight, up_bias, down_weight, down_bias = params
    rate_modes = decay_rate.T
    freq_modes = rotation.T
    real_modes = out_real.T
    imag_modes = out_imag.T
    normed = norm_rows(source, first_gain, first_shift)
    lag_power_real, lag_power_imag = mode_terms(rate_modes, freq_modes, jnp.arange(KLEN).astype(jnp.float32))
    kernel = lax.optimization_barrier(jnp.sum(real_modes[:, None, :] * lag_power_real - imag_modes[:, None, :] * lag_power_imag, axis=0))
    fft_length = SEQLEN + KLEN
    spectrum = jnp.fft.rfft(normed, n=fft_length, axis=0) * jnp.fft.rfft(kernel, n=fft_length, axis=0)
    convolved = jnp.fft.irfft(spectrum, n=fft_length, axis=0)[:SEQLEN]
    drive_real = real_modes * prior_seg[0] - imag_modes * prior_seg[1]
    drive_imag = real_modes * prior_seg[1] + imag_modes * prior_seg[0]
    block_fn = jax.checkpoint(state_block)
    offsets = jnp.arange(N_SEQ) * TOK_DEV
    response = lax.map(lambda offset: block_fn(offset, rate_modes, freq_modes, drive_real, drive_imag), offsets)
    response = response.reshape(SEQLEN, -1)
    activated = jax.nn.gelu(convolved + skip_gain * normed + response, approximate=False)
    glu_pre = low_back(jnp.dot(low(activated), glu_weight, precision=HIGHEST)) + glu_bias
    split_at = glu_pre.shape[-1] // 2
    merged = source + glu_pre[:, :split_at] * jax.nn.sigmoid(glu_pre[:, split_at:])
    second = norm_rows(merged, second_gain, second_shift)
    hidden = jax.nn.gelu(low_back(jnp.dot(low(second), up_weight, precision=HIGHEST)) + up_bias, approximate=False)
    return merged + low_back(jnp.dot(low(hidden), down_weight, precision=HIGHEST)) + down_bias

def reference(inputs, first_gain, first_shift, decay_rate, rotation, out_real, out_imag, skip_gain, glu_weight, glu_bias, second_gain, second_shift, up_weight, up_bias, down_weight, down_bias, prior_state, cotangent):
    params = tuple((member.astype(jnp.float32) for member in (first_gain, first_shift, decay_rate, rotation, out_real, out_imag, skip_gain, glu_weight, glu_bias, second_gain, second_shift, up_weight, up_bias, down_weight, down_bias)))
    zero_grads = tuple((jnp.zeros_like(member) for member in params))

    def one_segment(totals, item):
        seg_source, seg_prior, seg_cot = item
        result, pullback = jax.vjp(segment_forward, params, seg_source, seg_prior)
        grad_params, grad_source, grad_prior = pullback(seg_cot)
        totals = tuple((left + right for left, right in zip(totals, grad_params)))
        return (totals, (result, grad_source, grad_prior))
    totals, (results, grad_inputs, grad_priors) = lax.scan(one_segment, zero_grads, (inputs.astype(jnp.float32), prior_state.astype(jnp.float32), cotangent.astype(jnp.float32)))
    return (results.astype(jnp.bfloat16), grad_inputs.astype(jnp.bfloat16), grad_priors, totals[0], totals[1], totals[2], totals[3], totals[4], totals[5], totals[6], totals[7], totals[8], totals[9], totals[10], totals[11], totals[12], totals[13], totals[14])
```

```python
import functools
import math

import jax
import jax.numpy as jnp
import numpy as np
from jax import lax
from jax.experimental import pallas as pl
from jax.experimental.pallas import tpu as pltpu
from jax.sharding import PartitionSpec as P

KLEN = 128
LT = 128
MESH = pl.DeviceIdType.MESH
F32, BF16 = jnp.float32, jnp.bfloat16


EPSILON = 1e-05
HIGHEST = lax.Precision.HIGHEST


def from_behind(value, axis, by):
    peers = lax.axis_size(axis)
    pairs = [(i, i + by) for i in range(peers) if 0 <= i + by < peers]
    return lax.ppermute(value, axis, pairs)


def norm_rows(values, gain, shift):
    center = values - jnp.mean(values, axis=-1, keepdims=True)
    spread = jnp.mean(center * center, axis=-1, keepdims=True)
    return center * lax.rsqrt(spread + EPSILON) * gain + shift


def mode_terms(rate_modes, freq_modes, elapsed):
    moment = elapsed[None, :, None]
    damping = jnp.exp(-rate_modes[:, None, :] * moment)
    return (
        damping * jnp.cos(freq_modes[:, None, :] * moment),
        damping * jnp.sin(freq_modes[:, None, :] * moment),
    )


def glu_gate(glu_pre):
    split_at = glu_pre.shape[-1] // 2
    return glu_pre[:, :split_at] * jax.nn.sigmoid(glu_pre[:, split_at:])


def gelu_exact(values):
    return jax.nn.gelu(values, approximate=False)


def shards(
    inputs,
    first_gain,
    first_shift,
    decay_rate,
    rotation,
    out_real,
    out_imag,
    skip_gain,
    glu_weight,
    glu_bias,
    second_gain,
    second_shift,
    up_weight,
    up_bias,
    down_weight,
    down_bias,
    prior_state,
    cotangent,
):
    seg_count, tok_count, feature = inputs.shape
    row_count = seg_count * tok_count
    window = tok_count + KLEN
    half = window // 2 + 1
    offset = lax.axis_index("seq") * tok_count
    freq_index = jnp.arange(half, dtype=jnp.int32)
    time_index = jnp.arange(window, dtype=jnp.int32)
    phase = (freq_index[:, None] * time_index[None, :] % window).astype(jnp.float32) * (
        2.0 * math.pi / window
    )
    cos_half = jnp.cos(phase)
    sin_half = jnp.sin(phase)
    forward_table = jnp.concatenate([cos_half, -sin_half], axis=0)
    weights = jnp.where((freq_index == 0) | (2 * freq_index == window), 1.0, 2.0).astype(
        jnp.float32
    )
    inverse_table = (
        jnp.concatenate(
            [(weights[:, None] * cos_half).T, -(weights[:, None] * sin_half).T], axis=1
        )[KLEN:]
        / window
    )
    local_steps = jnp.arange(tok_count).astype(jnp.float32)
    advance_steps = (offset + 1).astype(jnp.float32)

    def mixing(
        normed, halo_rows, rate_modes, freq_modes, real_modes, imag_modes, skip_local, prior_local
    ):
        table_real, table_imag = mode_terms(rate_modes, freq_modes, local_steps)
        kernel = jnp.einsum("mkh,mh->kh", table_real, real_modes, precision=HIGHEST) - jnp.einsum(
            "mkh,mh->kh", table_imag, imag_modes, precision=HIGHEST
        )
        extended = jnp.concatenate([halo_rows, normed], axis=1)
        spectrum = jnp.einsum("ft,sth->sfh", forward_table, extended, precision=HIGHEST)
        kern_spec = jnp.dot(forward_table[:, :KLEN], kernel, precision=HIGHEST)
        spec_real, spec_imag = (spectrum[:, :half], spectrum[:, half:])
        kern_real, kern_imag = (kern_spec[:half], kern_spec[half:])
        product = jnp.concatenate(
            [
                spec_real * kern_real - spec_imag * kern_imag,
                spec_real * kern_imag + spec_imag * kern_real,
            ],
            axis=1,
        )
        convolved = jnp.einsum("tf,sfh->sth", inverse_table, product, precision=HIGHEST)
        damping = jnp.exp(-rate_modes * advance_steps)
        adv_real = damping * jnp.cos(freq_modes * advance_steps)
        adv_imag = damping * jnp.sin(freq_modes * advance_steps)
        coef_real = real_modes * adv_real - imag_modes * adv_imag
        coef_imag = real_modes * adv_imag + imag_modes * adv_real
        drive_real = coef_real * prior_local[:, 0] - coef_imag * prior_local[:, 1]
        drive_imag = coef_real * prior_local[:, 1] + coef_imag * prior_local[:, 0]
        response = jnp.einsum(
            "mth,smh->sth", table_real, drive_real, precision=HIGHEST
        ) - jnp.einsum("mth,smh->sth", table_imag, drive_imag, precision=HIGHEST)
        return gelu_exact(convolved + skip_local * normed + response)

    source = inputs.astype(jnp.float32)
    normed, first_pull = jax.vjp(norm_rows, source, first_gain, first_shift)
    halo_rows = from_behind(normed, "seq", 1)
    activated, mix_pull = jax.vjp(
        mixing,
        normed,
        halo_rows,
        decay_rate.T,
        rotation.T,
        out_real.T,
        out_imag.T,
        skip_gain,
        prior_state,
    )
    activated_low = activated.reshape(row_count, feature).astype(jnp.bfloat16)
    glu_pre = jnp.dot(activated_low, glu_weight, preferred_element_type=jnp.float32) + glu_bias
    branch, glu_pull = jax.vjp(glu_gate, glu_pre)
    merged = source.reshape(row_count, feature) + branch
    second, second_pull = jax.vjp(norm_rows, merged, second_gain, second_shift)
    second_low = second.astype(jnp.bfloat16)
    up_pre = jnp.dot(second_low, up_weight, preferred_element_type=jnp.float32) + up_bias
    hidden, hidden_pull = jax.vjp(gelu_exact, up_pre)
    hidden_low = hidden.astype(jnp.bfloat16)
    result = (
        merged + jnp.dot(hidden_low, down_weight, preferred_element_type=jnp.float32) + down_bias
    )
    outputs = result.astype(jnp.bfloat16).reshape(seg_count, tok_count, feature)
    grad_out = cotangent.astype(jnp.float32).reshape(row_count, feature)
    down_bias_grad = jnp.sum(grad_out, axis=0)
    grad_low = grad_out.astype(jnp.bfloat16)
    down_grad = jnp.einsum("rf,rh->fh", hidden_low, grad_low, preferred_element_type=jnp.float32)
    grad_hidden = jnp.einsum("rh,fh->rf", grad_low, down_weight, preferred_element_type=jnp.float32)
    (grad_up,) = hidden_pull(grad_hidden)
    up_bias_grad = jnp.sum(grad_up, axis=0)
    up_low = grad_up.astype(jnp.bfloat16)
    up_grad = jnp.einsum("rh,rf->hf", second_low, up_low, preferred_element_type=jnp.float32)
    grad_second = jnp.einsum("rf,hf->rh", up_low, up_weight, preferred_element_type=jnp.float32)
    grad_merged, second_gain_grad, second_shift_grad = second_pull(grad_second)
    grad_merged = grad_merged + grad_out
    (grad_glu,) = glu_pull(grad_merged)
    glu_bias_grad = jnp.sum(grad_glu, axis=0)
    glu_low = grad_glu.astype(jnp.bfloat16)
    glu_grad = jnp.einsum("rh,rg->hg", activated_low, glu_low, preferred_element_type=jnp.float32)
    grad_activated = jnp.einsum(
        "rg,hg->rh", glu_low, glu_weight, preferred_element_type=jnp.float32
    )
    grad_normed, grad_halo, rate_grad, freq_grad, real_grad, imag_grad, skip_grad, prior_grad = (
        mix_pull(grad_activated.reshape(seg_count, tok_count, feature))
    )
    grad_tail = from_behind(grad_halo, "seq", -1)
    grad_normed = jnp.concatenate(
        [grad_normed[:, : tok_count - KLEN], grad_normed + grad_tail], axis=1
    )
    grad_source, first_gain_grad, first_shift_grad = first_pull(grad_normed)
    input_grad = (grad_source + grad_merged.reshape(seg_count, tok_count, feature)).astype(
        jnp.bfloat16
    )
    state_grad = lax.psum(prior_grad, "seq")
    rate_back = rate_grad.T
    freq_back = freq_grad.T
    real_back = real_grad.T
    imag_back = imag_grad.T
    summed = (
        lax.psum_scatter(first_gain_grad, ("seq", "batch"), scatter_dimension=0, tiled=True),
        lax.psum_scatter(first_shift_grad, ("seq", "batch"), scatter_dimension=0, tiled=True),
        lax.psum_scatter(rate_back, ("seq", "batch"), scatter_dimension=0, tiled=True),
        lax.psum_scatter(freq_back, ("seq", "batch"), scatter_dimension=0, tiled=True),
        lax.psum_scatter(real_back, ("seq", "batch"), scatter_dimension=0, tiled=True),
        lax.psum_scatter(imag_back, ("seq", "batch"), scatter_dimension=0, tiled=True),
        lax.psum_scatter(skip_grad, ("seq", "batch"), scatter_dimension=0, tiled=True),
        lax.psum_scatter(glu_grad, ("seq", "batch"), scatter_dimension=0, tiled=True),
        lax.psum_scatter(glu_bias_grad, ("seq", "batch"), scatter_dimension=0, tiled=True),
        lax.psum_scatter(second_gain_grad, ("seq", "batch"), scatter_dimension=0, tiled=True),
        lax.psum_scatter(second_shift_grad, ("seq", "batch"), scatter_dimension=0, tiled=True),
        lax.psum_scatter(up_grad, ("seq", "batch"), scatter_dimension=0, tiled=True),
        lax.psum_scatter(up_bias_grad, ("seq", "batch"), scatter_dimension=0, tiled=True),
        lax.psum_scatter(down_grad, ("seq", "batch"), scatter_dimension=0, tiled=True),
        lax.psum_scatter(down_bias_grad, ("seq", "batch"), scatter_dimension=0, tiled=True),
    )
    return (
        outputs,
        input_grad,
        state_grad,
        summed[0],
        summed[1],
        summed[2],
        summed[3],
        summed[4],
        summed[5],
        summed[6],
        summed[7],
        summed[8],
        summed[9],
        summed[10],
        summed[11],
        summed[12],
        summed[13],
        summed[14],
    )


def plane():
    s = lax.axis_index("seq")
    i = lax.rem(s, 8)
    base = s - i
    c, x, y = lax.rem(i, 2), lax.rem(i // 2, 2), i // 4
    ic, ix, iy = i + 1 - 2 * c, i + 2 - 4 * x, i + 4 - 8 * y
    idg = iy + 2 - 4 * x
    return dict(s=s, i=i, base=base, c=c, x=x, y=y, ic=ic, ix=ix, iy=iy, idg=idg)

def sib_of(p, j):
    return j + 1 - 2 * p["c"]

def remote(src, dst, ss, rs, dev):
    return pltpu.make_async_remote_copy(src_ref=src, dst_ref=dst, send_sem=ss, recv_sem=rs,
                                        device_id=dev, device_id_type=MESH)

def greet(devs):
    bar = pltpu.get_barrier_semaphore()
    for d in devs:
        pl.semaphore_signal(bar, inc=1, device_id=d, device_id_type=MESH)
    pl.semaphore_wait(bar, len(devs))

def ag8_kernel(T, *refs):
    ins, outs = refs[:T], refs[T:2*T]
    land, ssem, rsem = refs[2*T:]
    p = plane()
    seq = lambda j: {"seq": p["base"] + j}
    X, Y, S = seq(p["ix"]), seq(p["iy"]), seq(p["ic"])
    greet([X, Y, S])
    R = ins[0].shape[0]; H = R // 2
    half = lambda ref, t, j, h: ref.at[t, j, pl.ds(h * H, H)]
    def cp(t, k, j, h, dev, src=None):
        return remote(half(land, t, j, h) if src is None else src, half(land, t, j, h), ssem.at[t, k], rsem.at[t, k], dev)
    sends = []
    for t in range(T):
        own = lambda h: ins[t].at[pl.ds(h * H, H)]
        for k, h, d in ((0, 0, X), (2, 1, Y), (1, 1, X), (3, 0, Y), (6, 0, S), (7, 1, S)):
            c = cp(t, k, p["i"], h, d, own(h)); c.start(); sends.append(c)
    def arr(t, k, j, h):
        cp(t, k, j, h, S).wait_recv()
    def fwd(t, k, j, h, d):
        c = cp(t, k, j, h, d); c.start(); sends.append(c)
    for t in range(T):
        ix, iy, idg = p["ix"], p["iy"], p["idg"]
        outs[t][pl.ds(pl.multiple_of(p["i"] * R, R), R), :] = ins[t][...].astype(BF16)
        arr(t, 0, ix, 0); fwd(t, 4, ix, 0, Y); fwd(t, 8, ix, 0, S)
        arr(t, 2, iy, 1); fwd(t, 5, iy, 1, X); fwd(t, 11, iy, 1, S)
        arr(t, 1, ix, 1); fwd(t, 9, ix, 1, S)
        arr(t, 3, iy, 0); fwd(t, 10, iy, 0, S)
    for t in range(T):
        arr(t, 4, idg, 0); fwd(t, 12, idg, 0, S)
        arr(t, 5, idg, 1); fwd(t, 13, idg, 1, S)
    for t in range(T):
        for k, j in ((6, p["ic"]), (8, sib_of(p, ix)), (10, sib_of(p, iy)), (12, sib_of(p, idg))):
            arr(t, k, j, 0); arr(t, k + 1, j, 1)
        for j in (ix, iy, idg, p["ic"], sib_of(p, ix), sib_of(p, iy), sib_of(p, idg)):
            outs[t][pl.ds(pl.multiple_of(j * R, R), R), :] = land[t, j].astype(BF16)
    for c in sends:
        c.wait_send()

def ag8(*arrs, cid=0):
    T = len(arrs)
    R, D = arrs[0].shape
    return pl.pallas_call(
        functools.partial(ag8_kernel, T),
        out_shape=[jax.ShapeDtypeStruct((8 * R, D), BF16)] * T,
        in_specs=[pl.BlockSpec(memory_space=pltpu.VMEM)] * T,
        out_specs=[pl.BlockSpec(memory_space=pltpu.VMEM)] * T,
        scratch_shapes=[pltpu.VMEM((T, 8, R, D), F32), pltpu.SemaphoreType.DMA((T, 14)), pltpu.SemaphoreType.DMA((T, 14))],
        compiler_params=pltpu.CompilerParams(collective_id=cid, has_side_effects=True, vmem_limit_bytes=60 << 20),
        name="ag8",
    )(*arrs)

def rsz_kernel(N, Z, nch, *refs):
    ins, outs = refs[:N], refs[N:2*N]
    ups, dns = refs[2*N:3*N], refs[3*N:4*N]
    su, ru, sd, rd = refs[4*N:]
    z = lax.axis_index("batch")
    UP, DN = {"batch": lax.rem(z + 1, Z)}, {"batch": lax.rem(z + Z - 1, Z)}
    greet([UP, DN])
    def chunk(ref, t, n, ch):
        r = ref.shape[1] // nch[n]
        return ref.at[t, pl.ds(ch * r, r)]
    def cpu(n, t, ch, src):
        return remote(src, chunk(ups[n], t, n, ch), su.at[n, t, ch], ru.at[n, t, ch], UP)
    def cpd(n, t, ch, src):
        return remote(src, chunk(dns[n], t, n, ch), sd.at[n, t, ch], rd.at[n, t, ch], DN)
    order = [(n, ch) for n in range(N) for ch in range(nch[n])]
    for k in range(1, Z):
        for n, ch in order:
            tu, td = Z - k, k - 1
            @pl.when(z == 0)
            def _():
                cpu(n, tu, ch, chunk(ins[n], tu, n, ch)).start()
            @pl.when(z == Z - 1)
            def _():
                cpd(n, td, ch, chunk(ins[n], td, n, ch)).start()
    for k in range(1, Z):
        for n, ch in order:
            tu, td = Z - k, k - 1
            @pl.when((z > 0) & (z < tu))
            def _():
                cpu(n, tu, ch, chunk(ups[n], tu, n, ch)).wait_recv()
                b = chunk(ups[n], tu, n, ch)
                b[...] = b[...] + chunk(ins[n], tu, n, ch)[...]
                cpu(n, tu, ch, b).start()
            @pl.when((z < Z - 1) & (z > td))
            def _():
                cpd(n, td, ch, chunk(dns[n], td, n, ch)).wait_recv()
                b = chunk(dns[n], td, n, ch)
                b[...] = b[...] + chunk(ins[n], td, n, ch)[...]
                cpd(n, td, ch, b).start()
            for t in range(Z):
                pass
    for n, ch in order:
        r = ins[n].shape[1] // nch[n]
        for t in range(Z):
            @pl.when(z == t)
            def _():
                v = chunk(ins[n], t, n, ch)[...]
                if t > 0:
                    cpu(n, t, ch, chunk(ups[n], t, n, ch)).wait_recv()
                    v = v + chunk(ups[n], t, n, ch)[...]
                if t < Z - 1:
                    cpd(n, t, ch, chunk(dns[n], t, n, ch)).wait_recv()
                    v = v + chunk(dns[n], t, n, ch)[...]
                outs[n][pl.ds(ch * r, r)] = v
    for n, ch in order:
        for t in range(Z):
            @pl.when(z < t)
            def _():
                cpu(n, t, ch, chunk(ups[n], t, n, ch)).wait_send()
            @pl.when(z > t)
            def _():
                cpd(n, t, ch, chunk(dns[n], t, n, ch)).wait_send()

def rsz(*arrs, nch, Z, cid=1):
    N = len(arrs); M = max(nch)
    return pl.pallas_call(
        functools.partial(rsz_kernel, N, Z, nch),
        out_shape=[jax.ShapeDtypeStruct(a.shape[1:], F32) for a in arrs],
        in_specs=[pl.BlockSpec(memory_space=pltpu.VMEM)] * N,
        out_specs=[pl.BlockSpec(memory_space=pltpu.VMEM)] * N,
        scratch_shapes=[pltpu.VMEM(a.shape, F32) for a in arrs] * 2 + [pltpu.SemaphoreType.DMA((N, Z, M))] * 4,
        compiler_params=pltpu.CompilerParams(collective_id=cid, has_side_effects=True, vmem_limit_bytes=60 << 20),
        name="rsz",
    )(*arrs)

def peers(p):
    return [lax.rem(p["i"] + k, 8) for k in range(1, 8)]

def a2a8_kernel(N, *refs):
    ins, outs = refs[:N], refs[N:2*N]
    ss, rs, ls = refs[2*N:]
    p = plane()
    ps = peers(p)
    greet([{"seq": p["base"] + j} for j in ps])
    sends = []
    for n in range(N):
        l = pltpu.make_async_copy(ins[n].at[p["i"]], outs[n].at[p["i"]], ls.at[n]); l.start()
        for k, j in enumerate(ps):
            c = remote(ins[n].at[j], outs[n].at[p["i"]], ss.at[n, k], rs.at[n, k], {"seq": p["base"] + j})
            c.start(); sends.append(c)
        l.wait()
    for n in range(N):
        for k in range(7):
            src = lax.rem(p["i"] + 7 - k, 8)
            remote(ins[n].at[src], outs[n].at[src], ss.at[n, k], rs.at[n, k], {"seq": p["base"] + src}).wait_recv()
    for c in sends: c.wait_send()

def a2a8(*arrs, cid):
    N = len(arrs)
    v = pl.BlockSpec(memory_space=pltpu.VMEM)
    return pl.pallas_call(functools.partial(a2a8_kernel, N),
        out_shape=[jax.ShapeDtypeStruct(a.shape, F32) for a in arrs], in_specs=[v]*N, out_specs=[v]*N,
        scratch_shapes=[pltpu.SemaphoreType.DMA((N, 7))]*2 + [pltpu.SemaphoreType.DMA((N,))],
        compiler_params=pltpu.CompilerParams(collective_id=cid, has_side_effects=True), name="a2a8")(*arrs)

def small_kernel(Z, NV, NS, x_ref, v_ref, o_ref, st_ref, land, mine, zland, stall, ss, rs, zs, zr, bs, br):
    p = plane(); z = lax.axis_index("batch")
    ps = peers(p)
    zp = [lax.rem(z + k, Z) for k in range(1, Z)]
    greet([{"seq": p["base"] + j} for j in ps] + [{"batch": q} for q in zp])
    sends = []
    for k, j in enumerate(ps):
        c = remote(x_ref.at[j], land.at[p["i"]], ss.at[k], rs.at[k], {"seq": p["base"] + j})
        c.start(); sends.append(c)
    tot = x_ref[p["i"]]
    for k in range(7):
        src = lax.rem(p["i"] + 7 - k, 8)
        remote(x_ref.at[src], land.at[src], ss.at[k], rs.at[k], {"seq": p["base"] + src}).wait_recv()
        tot = tot + land[src]
    mine[0:NV + NS] = tot
    mine[NV + NS:] = v_ref[...]
    stall[p["i"]] = tot[NV:NV + NS]
    for k, j in enumerate(ps):
        c = remote(mine.at[pl.ds(NV, NS)], stall.at[p["i"]], bs.at[k], br.at[k], {"seq": p["base"] + j})
        c.start(); sends.append(c)
    for k, q in enumerate(zp):
        c = remote(mine, zland.at[z], zs.at[k], zr.at[k], {"batch": q})
        c.start(); sends.append(c)
    acc = mine[...]
    for k in range(Z - 1):
        src = lax.rem(z + Z - 1 - k, Z)
        remote(mine, zland.at[src], zs.at[k], zr.at[k], {"batch": src}).wait_recv()
        acc = acc + zland[src]
    o_ref[...] = acc
    for k in range(7):
        src = lax.rem(p["i"] + 7 - k, 8)
        remote(mine.at[pl.ds(NV, NS)], stall.at[src], bs.at[k], br.at[k], {"seq": p["base"] + src}).wait_recv()
    for c in sends: c.wait_send()
    st_ref[...] = stall[...]

def small(x, v, NV, NS, Z, cid):
    NT = NV + NS + v.shape[0]
    vm = pl.BlockSpec(memory_space=pltpu.VMEM)
    D = pltpu.SemaphoreType.DMA
    return pl.pallas_call(functools.partial(small_kernel, Z, NV, NS),
        out_shape=[jax.ShapeDtypeStruct((NT, 128), F32), jax.ShapeDtypeStruct((8, NS, 128), F32)], in_specs=[vm]*2, out_specs=[vm]*2,
        scratch_shapes=[pltpu.VMEM(x.shape, F32), pltpu.VMEM((NT, 128), F32), pltpu.VMEM((Z, NT, 128), F32), pltpu.VMEM((8, NS, 128), F32),
                        D((7,)), D((7,)), D((Z-1,)), D((Z-1,)), D((7,)), D((7,))],
        compiler_params=pltpu.CompilerParams(collective_id=cid, has_side_effects=True), name="small")(x, v)


def cmul(ar, ai, br, bi):
    return ar * br - ai * bi, ar * bi + ai * br

def lam_of(rate, freq):
    damp = jnp.exp(-rate)
    q = freq * freq
    cosv = 1.0 + q * (-1.0/2 + q * (1.0/24 + q * (-1.0/720 + q * (1.0/40320 + q * (-1.0/3628800)))))
    sinv = freq * (1.0 + q * (-1.0/6 + q * (1.0/120 + q * (-1.0/5040 + q * (1.0/362880)))))
    return damp * cosv, damp * sinv

def power_rows(lr, li, qr, qi, A):
    l2 = cmul(lr, li, lr, li); l4 = cmul(*l2, *l2); l8 = cmul(*l4, *l4)
    cur = (jnp.ones_like(lr), jnp.zeros_like(lr))
    for a in range(A):
        qr[a] = cur[0]; qi[a] = cur[1]
        cur = cmul(*cur, *l8)
    return l2, l4, cur

def offset_power(top, s, nbits):
    res = (jnp.ones_like(top[0]), jnp.zeros_like(top[0]))
    sq = top
    for bit in range(nbits):
        on = lax.rem(lax.div(s, 1 << bit), 2) == 1
        nxt = cmul(*res, *sq)
        res = (jnp.where(on, nxt[0], res[0]), jnp.where(on, nxt[1], res[1]))
        if bit + 1 < nbits: sq = cmul(*sq, *sq)
    return res

def e8_tile(tab, m, b):
    row = lambda k: jnp.broadcast_to(tab[k, pl.ds(m, 1), :], b.shape)
    one, zero = jnp.ones(b.shape, F32), jnp.zeros(b.shape, F32)
    o1, o2, o4 = (b % 2) == 1, ((b // 2) % 2) == 1, b >= 4
    r = jnp.where(o1, row(0), one), jnp.where(o1, row(1), zero)
    r = cmul(*r, jnp.where(o2, row(2), one), jnp.where(o2, row(3), zero))
    return cmul(*r, jnp.where(o4, row(4), one), jnp.where(o4, row(5), zero))

def fwd_kernel(nbits, rate, freq, cre, cim, prior, kern, resp, qr, qi, tab, co):
    M = rate.shape[0]; A = kern.shape[0] // 8
    s = lax.axis_index("seq")
    b = lax.broadcasted_iota(jnp.int32, (8, LT), 0)
    @pl.loop(0, rate.shape[1] // LT)
    def _(lt):
        cols = pl.ds(pl.multiple_of(lt * LT, LT), LT)
        lr, li = lam_of(rate[:, cols], freq[:, cols])
        l2, l4, top = power_rows(lr, li, qr, qi, A)
        for k, v in enumerate((lr, li, *l2, *l4)): tab[k] = v
        off = cmul(*offset_power(top, s, nbits), lr, li)
        c = cre[:, cols], cim[:, cols]
        d = cmul(*cmul(*c, *off), prior[0, 0, :, cols], prior[0, 1, :, cols])
        for a in range(A):
            q = qr[a], qi[a]
            ca = cmul(*c, *q); da = cmul(*d, *q)
            co[0, a], co[1, a], co[2, a], co[3, a] = ca[0], ca[1], da[0], da[1]
        def step(m, accs):
            er, ei = e8_tile(tab, m, b)
            out = []
            for a in range(A):
                row = lambda k: co[k, a, pl.ds(m, 1), :]
                out.append(accs[2*a] + (er * row(0) - ei * row(1)))
                out.append(accs[2*a+1] + (er * row(2) - ei * row(3)))
            return tuple(out)
        accs = lax.fori_loop(0, M, step, tuple(jnp.zeros((8, LT), F32) for _ in range(2 * A)))
        for a in range(A):
            kern[pl.ds(8*a, 8), cols] = accs[2*a]
            resp[pl.ds(8*a, 8), cols] = accs[2*a+1]

def modes_fwd(rate, freq, cre, cim, prior, nbits):
    M, H = rate.shape; A = 16
    v = pl.BlockSpec(memory_space=pltpu.VMEM)
    return pl.pallas_call(functools.partial(fwd_kernel, nbits),
        out_shape=[jax.ShapeDtypeStruct((8*A, H), F32)] * 2, in_specs=[v]*5, out_specs=[v]*2,
        scratch_shapes=[pltpu.VMEM((A, M, LT), F32)]*2 + [pltpu.VMEM((6, M, LT), F32), pltpu.VMEM((4, A, M, LT), F32)],
        name="modes_fwd")(rate, freq, cre, cim, prior)

def bwd_kernel(nbits, TOK, rate, freq, cre, cim, prior, kg, gz, out, state, qr, qi, acc):
    M = rate.shape[0]; A = kg.shape[0] // 8
    s = lax.axis_index("seq")
    adv = (s * TOK + 1).astype(F32)
    @pl.loop(0, rate.shape[1] // LT)
    def _(lt):
        cols = pl.ds(pl.multiple_of(lt * LT, LT), LT)
        lr, li = lam_of(rate[:, cols], freq[:, cols])
        l2, l4, top = power_rows(lr, li, qr, qi, A)
        def step(m, carry):
            for j, g in enumerate((kg, gz)):
                z = jnp.zeros((8, LT), F32)
                sr, si, tr, ti = z, z, z, z
                for a in range(A - 1, -1, -1):
                    ga = g[pl.ds(8*a, 8), cols]
                    sr = sr + ga * qr[a, pl.ds(m, 1), :]
                    si = si + ga * qi[a, pl.ds(m, 1), :]
                    if a > 0:
                        tr = tr + sr; ti = ti + si
                rows = pl.ds(pl.multiple_of(m * 8, 8), 8)
                for q, v in enumerate((sr, si, tr, ti)): acc[4*j+q, rows, :] = v
            return carry
        lax.fori_loop(0, M, step, 0)
        pw = (jnp.ones_like(lr), jnp.zeros_like(lr))
        tot = []
        zero = jnp.zeros_like(lr)
        ar, ai, br, bi = [zero]*2, [zero]*2, [zero]*2, [zero]*2
        for b in range(8):
            for j in range(2):
                ld = lambda q: acc[4*j+q, pl.ds(b, M, stride=8), :]
                S = ld(0), ld(1)
                U = 8.0 * ld(2), 8.0 * ld(3)
                if b: U = U[0] + float(b) * S[0], U[1] + float(b) * S[1]
                p = cmul(*pw, *S); ar[j] = ar[j] + p[0]; ai[j] = ai[j] + p[1]
                p = cmul(*pw, *U); br[j] = br[j] + p[0]; bi[j] = bi[j] + p[1]
            pw = cmul(*pw, lr, li)
        off = cmul(*offset_power(top, s, nbits), lr, li)
        c = cre[:, cols], cim[:, cols]
        ps = cmul(*off, prior[0, 0, :, cols], prior[0, 1, :, cols])
        u = cmul(*ps, ar[1], ai[1])
        u = u[0] + ar[0], u[1] + ai[0]
        v = cmul(*ps, br[1] + adv * ar[1], bi[1] + adv * ai[1])
        v = cmul(*c, v[0] + br[0], v[1] + bi[0])
        w = cmul(*cmul(*c, *off), ar[1], ai[1])
        out[0, :, cols] = -v[0]; out[1, :, cols] = -v[1]; out[2, :, cols] = u[0]; out[3, :, cols] = -u[1]
        state[0, :, cols] = w[0]; state[1, :, cols] = -w[1]

def modes_bwd(rate, freq, cre, cim, prior, kg, gz, nbits):
    M, H = rate.shape; A = 16
    v = pl.BlockSpec(memory_space=pltpu.VMEM)
    return pl.pallas_call(functools.partial(bwd_kernel, nbits, gz.shape[0]),
        out_shape=[jax.ShapeDtypeStruct((4, M, H), F32), jax.ShapeDtypeStruct((2, M, H), F32)], in_specs=[v]*7, out_specs=[v]*2,
        scratch_shapes=[pltpu.VMEM((A, M, LT), F32)]*2 + [pltpu.VMEM((8, 8*M, LT), F32)],
        name="modes_bwd")(rate, freq, cre, cim, prior, kg, gz)


def fast_shards(Z, n_seq, inputs, first_gain, first_shift, decay_rate, rotation, out_real, out_imag, skip_gain, glu_weight,
                glu_bias, second_gain, second_shift, up_weight, up_bias, down_weight, down_bias, prior_state, cotangent):
    T, D = inputs.shape[1:]
    FF = up_weight.shape[1]
    nbits = max(1, (n_seq - 1).bit_length())
    s = lax.axis_index("seq")
    window = T + KLEN
    half = window // 2 + 1
    fi = np.arange(half)[:, None]; ti = np.arange(window)[None, :]
    ph = (fi * ti % window) * (2.0 * np.pi / window)
    fwd_tab = jnp.asarray(np.concatenate([np.cos(ph), -np.sin(ph)], 0), F32)
    wt = np.where((fi == 0) | (2 * fi == window), 1.0, 2.0) / window
    inv_tab = jnp.asarray(np.concatenate([(wt * np.cos(ph)).T, -(wt * np.sin(ph)).T], 1)[KLEN:], F32)
    hi = functools.partial(jnp.einsum, precision=HIGHEST)
    source = inputs[0].astype(F32)
    def stats(v):
        center = v - jnp.mean(v, axis=-1, keepdims=True)
        inv = lax.rsqrt(jnp.mean(center * center, axis=-1, keepdims=True) + EPSILON)
        return center * inv, inv
    xhat, xinv = stats(source)
    normed = xhat * first_gain + first_shift
    halo_src = from_behind(source, "seq", 1)
    halo = jnp.where(s == 0, 0.0, stats(halo_src)[0] * first_gain + first_shift)
    rate, freq, cre, cim = decay_rate.T, rotation.T, out_real.T, out_imag.T
    kern, resp = modes_fwd(rate, freq, cre, cim, prior_state, nbits)
    ext = jnp.concatenate([halo, normed], 0)
    X = hi("ft,th->fh", fwd_tab, ext)
    K = hi("ft,th->fh", fwd_tab[:, :KLEN], kern)
    Xr, Xi, Kr, Ki = X[:half], X[half:], K[:half], K[half:]
    conv = hi("tf,fh->th", inv_tab, jnp.concatenate([Xr * Kr - Xi * Ki, Xr * Ki + Xi * Kr], 0))
    pre = conv + skip_gain * normed + resp
    act, act_pull = jax.vjp(gelu_exact, pre)
    act_low = act.astype(BF16)
    dot = functools.partial(lax.dot_general, preferred_element_type=F32)
    mm = lambda a, b: dot(a, b, (((1,), (0,)), ((), ())))
    mt = lambda a, b: dot(a, b, (((1,), (1,)), ((), ())))
    tm = lambda a, b: dot(a, b, (((0,), (0,)), ((), ())))
    glu_pre = mm(act_low, glu_weight) + glu_bias
    value, sg = glu_pre[:, :D], jax.nn.sigmoid(glu_pre[:, D:])
    merged = source + value * sg
    mhat, minv = stats(merged)
    second_low = (mhat * second_gain + second_shift).astype(BF16)
    up_pre = mm(second_low, up_weight) + up_bias
    hidden, hidden_pull = jax.vjp(gelu_exact, up_pre)
    outputs = (merged + mm(hidden.astype(BF16), down_weight) + down_bias).astype(BF16)
    cot = cotangent[0]
    grad_out = cot.astype(F32)
    (grad_up,) = hidden_pull(mt(cot, down_weight))
    grad_second = mt(grad_up.astype(BF16), up_weight)
    def ln_back(g, gain, hat, inv):
        gg = g * gain
        return inv * (gg - jnp.mean(gg, -1, keepdims=True) - hat * jnp.mean(gg * hat, -1, keepdims=True))
    grad_merged = grad_out + ln_back(grad_second, second_gain, mhat, minv)
    grad_value, grad_gate = grad_merged * sg, grad_merged * value * sg * (1 - sg)
    glu_low = jnp.concatenate([grad_value, grad_gate], 1).astype(BF16)
    (gz,) = act_pull(mt(glu_low, glu_weight))
    cot_all, second_all, act_all = ag8(grad_out, second_low.astype(F32), act_low.astype(F32), cid=0)
    gm_blocks = grad_merged.reshape(T, 8, D // 8).transpose(1, 0, 2)
    (gm_all,) = a2a8(gm_blocks, cid=1)
    gm_all = gm_all.reshape(8 * T, D // 8)
    i = lax.rem(s, 8)
    FS, GS = FF // 8, D // 8
    fcol = lambda w, ax: lax.dynamic_slice_in_dim(w, i * FS, FS, ax)
    up_pre_s = mm(second_all, fcol(up_weight, 1)) + fcol(up_bias, 0)
    hidden_s, hidden_pull_s = jax.vjp(gelu_exact, up_pre_s)
    (grad_up_s,) = hidden_pull_s(mt(cot_all, fcol(down_weight, 0)))
    down_g = tm(hidden_s.astype(BF16), cot_all).reshape(Z, FS // Z, D)
    up_g = tm(second_all, grad_up_s.astype(BF16)).reshape(8, Z, D // 8 // Z, FS).transpose(1, 0, 2, 3).reshape(Z, D // Z, FS)
    up_bias_s = jnp.sum(grad_up_s, 0)
    gcol = lambda w: jnp.concatenate([lax.dynamic_slice_in_dim(w, i * GS, GS, -1 if w.ndim > 1 else 0),
                                      lax.dynamic_slice_in_dim(w, D + i * GS, GS, -1 if w.ndim > 1 else 0)], -1)
    gp = mm(act_all, gcol(glu_weight)) + gcol(glu_bias)
    v_s, sg_s = gp[:, :GS], jax.nn.sigmoid(gp[:, GS:])
    gg_s = jnp.concatenate([gm_all * sg_s, gm_all * v_s * sg_s * (1 - sg_s)], 1)
    glu_g = tm(act_all, gg_s.astype(BF16)).reshape(8, Z, D // 8 // Z, 2 * GS).transpose(1, 0, 2, 3).reshape(Z, D // Z, 2 * GS)
    down_o, up_o, glu_o = rsz(down_g, up_g, glu_g, nch=(2, 2, 1), Z=Z, cid=2)
    up_x, glu_x = a2a8(up_o.reshape(8, D // 8 // Z, FS), glu_o.reshape(8, D // 8 // Z, 2 * GS), cid=3)
    up_final = up_x.transpose(1, 0, 2).reshape(-1, FF)
    glu_final = glu_x.reshape(8, -1, 2, GS).transpose(1, 2, 0, 3).reshape(-1, 2 * D)
    gp_ = hi("tf,th->fh", inv_tab, gz)
    gr, gi = gp_[:half], gp_[half:]
    kg = hi("ft,fh->th", fwd_tab[:, :KLEN], jnp.concatenate([gr * Xr + gi * Xi, gi * Xr - gr * Xi], 0))
    gext = hi("ft,fh->th", fwd_tab, jnp.concatenate([gr * Kr + gi * Ki, gi * Kr - gr * Ki], 0))
    modes_g, state_g = modes_bwd(rate, freq, cre, cim, prior_state, kg, gz, nbits)
    tail = from_behind(gext[:KLEN], "seq", -1)
    grad_normed = gext[KLEN:] + tail + skip_gain * gz
    input_grad = (grad_merged + ln_back(grad_normed, first_gain, xhat, xinv)).astype(BF16)
    vec = jnp.stack([jnp.sum(grad_normed * xhat, 0), jnp.sum(grad_normed, 0), jnp.sum(gz * normed, 0),
                     jnp.sum(grad_second * mhat, 0), jnp.sum(grad_second, 0), jnp.sum(grad_out, 0)])
    glu_vec = jnp.concatenate([jnp.sum(grad_value, 0), jnp.sum(grad_gate, 0)]).reshape(8, 2, 128)
    M = rate.shape[0]
    NV, NS = 4 * M + 8, 2 * M
    lanes = lambda v: v.reshape(-1, 8, D // 8).transpose(1, 0, 2)
    packed = jnp.concatenate([lanes(modes_g), lanes(vec), glu_vec, lanes(state_g)], 1)
    tv = jnp.concatenate([up_bias_s.reshape(-1, 128), jnp.zeros((4, 128), F32)], 0)
    tot, st = small(packed, tv, NV, NS, Z, cid=4)
    state_grad = st.transpose(1, 0, 2).reshape(1, 2, M, D)
    b = lax.axis_index("batch")
    W = D // 8 // Z
    mine = lax.dynamic_slice_in_dim(tot[:NV], b * W, W, 1)
    mg = [mine[k * M:(k + 1) * M].T for k in range(4)]
    vg = [mine[4 * M + k] for k in range(6)]
    ub = lax.dynamic_slice_in_dim(tot[NV + NS:NV + NS + FS // 128].reshape(FS), b * (FS // Z), FS // Z, 0)
    gb = lax.dynamic_slice_in_dim(tot[4 * M + 6:NV].reshape(2 * D // 8), b * (2 * W), 2 * W, 0)
    return (outputs[None], input_grad[None], state_grad, vg[0], vg[1], mg[0], mg[1], mg[2], mg[3], vg[2], glu_final, gb,
            vg[3], vg[4], up_final, ub, down_o, vg[5])


def solution(mesh):
    in_specs = (
        P("batch", "seq", None),
        P(),
        P(),
        P(),
        P(),
        P(),
        P(),
        P(),
        P(),
        P(),
        P(),
        P(),
        P(),
        P(),
        P(),
        P(),
        P("batch", None, None, None),
        P("batch", "seq", None),
    )
    out_specs = (
        P("batch", "seq", None),
        P("batch", "seq", None),
        P("batch", None, None, None),
        P(("seq", "batch")),
        P(("seq", "batch")),
        P(("seq", "batch"), None),
        P(("seq", "batch"), None),
        P(("seq", "batch"), None),
        P(("seq", "batch"), None),
        P(("seq", "batch")),
        P(("seq", "batch"), None),
        P(("seq", "batch")),
        P(("seq", "batch")),
        P(("seq", "batch")),
        P(("seq", "batch"), None),
        P(("seq", "batch")),
        P(("seq", "batch"), None),
        P(("seq", "batch")),
    )
    body = shards
    if mesh.shape["seq"] == 8:
        body = functools.partial(fast_shards, mesh.shape["batch"], mesh.shape["seq"])
    return jax.shard_map(body, mesh=mesh, in_specs=in_specs, out_specs=out_specs, check_vma=False)
```

```python
import functools
import math

import jax
import jax.numpy as jnp
import numpy as np
from jax import lax
from jax.experimental import pallas as pl
from jax.experimental.pallas import tpu as pltpu
from jax.sharding import PartitionSpec as P

KLEN = 128
LT = 128
MESH = pl.DeviceIdType.MESH
F32, BF16 = jnp.float32, jnp.bfloat16


EPSILON = 1e-05
HIGHEST = lax.Precision.HIGHEST


def from_behind(value, axis, by):
    peers = lax.axis_size(axis)
    pairs = [(i, i + by) for i in range(peers) if 0 <= i + by < peers]
    return lax.ppermute(value, axis, pairs)


def norm_rows(values, gain, shift):
    center = values - jnp.mean(values, axis=-1, keepdims=True)
    spread = jnp.mean(center * center, axis=-1, keepdims=True)
    return center * lax.rsqrt(spread + EPSILON) * gain + shift


def mode_terms(rate_modes, freq_modes, elapsed):
    moment = elapsed[None, :, None]
    damping = jnp.exp(-rate_modes[:, None, :] * moment)
    return (
        damping * jnp.cos(freq_modes[:, None, :] * moment),
        damping * jnp.sin(freq_modes[:, None, :] * moment),
    )


def glu_gate(glu_pre):
    split_at = glu_pre.shape[-1] // 2
    return glu_pre[:, :split_at] * jax.nn.sigmoid(glu_pre[:, split_at:])


def gelu_exact(values):
    return jax.nn.gelu(values, approximate=False)


def shards(
    inputs,
    first_gain,
    first_shift,
    decay_rate,
    rotation,
    out_real,
    out_imag,
    skip_gain,
    glu_weight,
    glu_bias,
    second_gain,
    second_shift,
    up_weight,
    up_bias,
    down_weight,
    down_bias,
    prior_state,
    cotangent,
):
    seg_count, tok_count, feature = inputs.shape
    row_count = seg_count * tok_count
    window = tok_count + KLEN
    half = window // 2 + 1
    offset = lax.axis_index("seq") * tok_count
    freq_index = jnp.arange(half, dtype=jnp.int32)
    time_index = jnp.arange(window, dtype=jnp.int32)
    phase = (freq_index[:, None] * time_index[None, :] % window).astype(jnp.float32) * (
        2.0 * math.pi / window
    )
    cos_half = jnp.cos(phase)
    sin_half = jnp.sin(phase)
    forward_table = jnp.concatenate([cos_half, -sin_half], axis=0)
    weights = jnp.where((freq_index == 0) | (2 * freq_index == window), 1.0, 2.0).astype(
        jnp.float32
    )
    inverse_table = (
        jnp.concatenate(
            [(weights[:, None] * cos_half).T, -(weights[:, None] * sin_half).T], axis=1
        )[KLEN:]
        / window
    )
    local_steps = jnp.arange(tok_count).astype(jnp.float32)
    advance_steps = (offset + 1).astype(jnp.float32)

    def mixing(
        normed, halo_rows, rate_modes, freq_modes, real_modes, imag_modes, skip_local, prior_local
    ):
        table_real, table_imag = mode_terms(rate_modes, freq_modes, local_steps)
        kernel = jnp.einsum("mkh,mh->kh", table_real, real_modes, precision=HIGHEST) - jnp.einsum(
            "mkh,mh->kh", table_imag, imag_modes, precision=HIGHEST
        )
        extended = jnp.concatenate([halo_rows, normed], axis=1)
        spectrum = jnp.einsum("ft,sth->sfh", forward_table, extended, precision=HIGHEST)
        kern_spec = jnp.dot(forward_table[:, :KLEN], kernel, precision=HIGHEST)
        spec_real, spec_imag = (spectrum[:, :half], spectrum[:, half:])
        kern_real, kern_imag = (kern_spec[:half], kern_spec[half:])
        product = jnp.concatenate(
            [
                spec_real * kern_real - spec_imag * kern_imag,
                spec_real * kern_imag + spec_imag * kern_real,
            ],
            axis=1,
        )
        convolved = jnp.einsum("tf,sfh->sth", inverse_table, product, precision=HIGHEST)
        damping = jnp.exp(-rate_modes * advance_steps)
        adv_real = damping * jnp.cos(freq_modes * advance_steps)
        adv_imag = damping * jnp.sin(freq_modes * advance_steps)
        coef_real = real_modes * adv_real - imag_modes * adv_imag
        coef_imag = real_modes * adv_imag + imag_modes * adv_real
        drive_real = coef_real * prior_local[:, 0] - coef_imag * prior_local[:, 1]
        drive_imag = coef_real * prior_local[:, 1] + coef_imag * prior_local[:, 0]
        response = jnp.einsum(
            "mth,smh->sth", table_real, drive_real, precision=HIGHEST
        ) - jnp.einsum("mth,smh->sth", table_imag, drive_imag, precision=HIGHEST)
        return gelu_exact(convolved + skip_local * normed + response)

    source = inputs.astype(jnp.float32)
    normed, first_pull = jax.vjp(norm_rows, source, first_gain, first_shift)
    halo_rows = from_behind(normed, "seq", 1)
    activated, mix_pull = jax.vjp(
        mixing,
        normed,
        halo_rows,
        decay_rate.T,
        rotation.T,
        out_real.T,
        out_imag.T,
        skip_gain,
        prior_state,
    )
    activated_low = activated.reshape(row_count, feature).astype(jnp.bfloat16)
    glu_pre = jnp.dot(activated_low, glu_weight, preferred_element_type=jnp.float32) + glu_bias
    branch, glu_pull = jax.vjp(glu_gate, glu_pre)
    merged = source.reshape(row_count, feature) + branch
    second, second_pull = jax.vjp(norm_rows, merged, second_gain, second_shift)
    second_low = second.astype(jnp.bfloat16)
    up_pre = jnp.dot(second_low, up_weight, preferred_element_type=jnp.float32) + up_bias
    hidden, hidden_pull = jax.vjp(gelu_exact, up_pre)
    hidden_low = hidden.astype(jnp.bfloat16)
    result = (
        merged + jnp.dot(hidden_low, down_weight, preferred_element_type=jnp.float32) + down_bias
    )
    outputs = result.astype(jnp.bfloat16).reshape(seg_count, tok_count, feature)
    grad_out = cotangent.astype(jnp.float32).reshape(row_count, feature)
    down_bias_grad = jnp.sum(grad_out, axis=0)
    grad_low = grad_out.astype(jnp.bfloat16)
    down_grad = jnp.einsum("rf,rh->fh", hidden_low, grad_low, preferred_element_type=jnp.float32)
    grad_hidden = jnp.einsum("rh,fh->rf", grad_low, down_weight, preferred_element_type=jnp.float32)
    (grad_up,) = hidden_pull(grad_hidden)
    up_bias_grad = jnp.sum(grad_up, axis=0)
    up_low = grad_up.astype(jnp.bfloat16)
    up_grad = jnp.einsum("rh,rf->hf", second_low, up_low, preferred_element_type=jnp.float32)
    grad_second = jnp.einsum("rf,hf->rh", up_low, up_weight, preferred_element_type=jnp.float32)
    grad_merged, second_gain_grad, second_shift_grad = second_pull(grad_second)
    grad_merged = grad_merged + grad_out
    (grad_glu,) = glu_pull(grad_merged)
    glu_bias_grad = jnp.sum(grad_glu, axis=0)
    glu_low = grad_glu.astype(jnp.bfloat16)
    glu_grad = jnp.einsum("rh,rg->hg", activated_low, glu_low, preferred_element_type=jnp.float32)
    grad_activated = jnp.einsum(
        "rg,hg->rh", glu_low, glu_weight, preferred_element_type=jnp.float32
    )
    grad_normed, grad_halo, rate_grad, freq_grad, real_grad, imag_grad, skip_grad, prior_grad = (
        mix_pull(grad_activated.reshape(seg_count, tok_count, feature))
    )
    grad_tail = from_behind(grad_halo, "seq", -1)
    grad_normed = jnp.concatenate(
        [grad_normed[:, : tok_count - KLEN], grad_normed + grad_tail], axis=1
    )
    grad_source, first_gain_grad, first_shift_grad = first_pull(grad_normed)
    input_grad = (grad_source + grad_merged.reshape(seg_count, tok_count, feature)).astype(
        jnp.bfloat16
    )
    state_grad = lax.psum(prior_grad, "seq")
    rate_back = rate_grad.T
    freq_back = freq_grad.T
    real_back = real_grad.T
    imag_back = imag_grad.T
    summed = (
        lax.psum_scatter(first_gain_grad, ("seq", "batch"), scatter_dimension=0, tiled=True),
        lax.psum_scatter(first_shift_grad, ("seq", "batch"), scatter_dimension=0, tiled=True),
        lax.psum_scatter(rate_back, ("seq", "batch"), scatter_dimension=0, tiled=True),
        lax.psum_scatter(freq_back, ("seq", "batch"), scatter_dimension=0, tiled=True),
        lax.psum_scatter(real_back, ("seq", "batch"), scatter_dimension=0, tiled=True),
        lax.psum_scatter(imag_back, ("seq", "batch"), scatter_dimension=0, tiled=True),
        lax.psum_scatter(skip_grad, ("seq", "batch"), scatter_dimension=0, tiled=True),
        lax.psum_scatter(glu_grad, ("seq", "batch"), scatter_dimension=0, tiled=True),
        lax.psum_scatter(glu_bias_grad, ("seq", "batch"), scatter_dimension=0, tiled=True),
        lax.psum_scatter(second_gain_grad, ("seq", "batch"), scatter_dimension=0, tiled=True),
        lax.psum_scatter(second_shift_grad, ("seq", "batch"), scatter_dimension=0, tiled=True),
        lax.psum_scatter(up_grad, ("seq", "batch"), scatter_dimension=0, tiled=True),
        lax.psum_scatter(up_bias_grad, ("seq", "batch"), scatter_dimension=0, tiled=True),
        lax.psum_scatter(down_grad, ("seq", "batch"), scatter_dimension=0, tiled=True),
        lax.psum_scatter(down_bias_grad, ("seq", "batch"), scatter_dimension=0, tiled=True),
    )
    return (
        outputs,
        input_grad,
        state_grad,
        summed[0],
        summed[1],
        summed[2],
        summed[3],
        summed[4],
        summed[5],
        summed[6],
        summed[7],
        summed[8],
        summed[9],
        summed[10],
        summed[11],
        summed[12],
        summed[13],
        summed[14],
    )


def plane():
    s = lax.axis_index("seq")
    i = lax.rem(s, 8)
    base = s - i
    c, x, y = lax.rem(i, 2), lax.rem(i // 2, 2), i // 4
    ic, ix, iy = i + 1 - 2 * c, i + 2 - 4 * x, i + 4 - 8 * y
    idg = iy + 2 - 4 * x
    return dict(s=s, i=i, base=base, c=c, x=x, y=y, ic=ic, ix=ix, iy=iy, idg=idg)

def sib_of(p, j):
    return j + 1 - 2 * p["c"]

def remote(src, dst, ss, rs, dev):
    return pltpu.make_async_remote_copy(src_ref=src, dst_ref=dst, send_sem=ss, recv_sem=rs,
                                        device_id=dev, device_id_type=MESH)

def greet(devs):
    bar = pltpu.get_barrier_semaphore()
    for d in devs:
        pl.semaphore_signal(bar, inc=1, device_id=d, device_id_type=MESH)
    pl.semaphore_wait(bar, len(devs))

def ag8_kernel(T, *refs):
    ins, outs = refs[:T], refs[T:2*T]
    land, ssem, rsem = refs[2*T:]
    p = plane()
    seq = lambda j: {"seq": p["base"] + j}
    X, Y, S = seq(p["ix"]), seq(p["iy"]), seq(p["ic"])
    greet([X, Y, S])
    R = ins[0].shape[0]; H = R // 2
    half = lambda ref, t, j, h: ref.at[t, j, pl.ds(h * H, H)]
    def cp(t, k, j, h, dev, src=None):
        return remote(half(land, t, j, h) if src is None else src, half(land, t, j, h), ssem.at[t, k], rsem.at[t, k], dev)
    sends = []
    for t in range(T):
        own = lambda h: ins[t].at[pl.ds(h * H, H)]
        for k, h, d in ((0, 0, X), (2, 1, Y), (1, 1, X), (3, 0, Y), (6, 0, S), (7, 1, S)):
            c = cp(t, k, p["i"], h, d, own(h)); c.start(); sends.append(c)
    def arr(t, k, j, h):
        cp(t, k, j, h, S).wait_recv()
    def fwd(t, k, j, h, d):
        c = cp(t, k, j, h, d); c.start(); sends.append(c)
    for t in range(T):
        ix, iy, idg = p["ix"], p["iy"], p["idg"]
        outs[t][pl.ds(pl.multiple_of(p["i"] * R, R), R), :] = ins[t][...].astype(BF16)
        arr(t, 0, ix, 0); fwd(t, 4, ix, 0, Y); fwd(t, 8, ix, 0, S)
        arr(t, 2, iy, 1); fwd(t, 5, iy, 1, X); fwd(t, 11, iy, 1, S)
        arr(t, 1, ix, 1); fwd(t, 9, ix, 1, S)
        arr(t, 3, iy, 0); fwd(t, 10, iy, 0, S)
    for t in range(T):
        arr(t, 4, idg, 0); fwd(t, 12, idg, 0, S)
        arr(t, 5, idg, 1); fwd(t, 13, idg, 1, S)
    for t in range(T):
        for k, j in ((6, p["ic"]), (8, sib_of(p, ix)), (10, sib_of(p, iy)), (12, sib_of(p, idg))):
            arr(t, k, j, 0); arr(t, k + 1, j, 1)
        for j in (ix, iy, idg, p["ic"], sib_of(p, ix), sib_of(p, iy), sib_of(p, idg)):
            outs[t][pl.ds(pl.multiple_of(j * R, R), R), :] = land[t, j].astype(BF16)
    for c in sends:
        c.wait_send()

def ag8(*arrs, cid=0):
    T = len(arrs)
    R, D = arrs[0].shape
    return pl.pallas_call(
        functools.partial(ag8_kernel, T),
        out_shape=[jax.ShapeDtypeStruct((8 * R, D), BF16)] * T,
        in_specs=[pl.BlockSpec(memory_space=pltpu.VMEM)] * T,
        out_specs=[pl.BlockSpec(memory_space=pltpu.VMEM)] * T,
        scratch_shapes=[pltpu.VMEM((T, 8, R, D), F32), pltpu.SemaphoreType.DMA((T, 14)), pltpu.SemaphoreType.DMA((T, 14))],
        compiler_params=pltpu.CompilerParams(collective_id=cid, has_side_effects=True, vmem_limit_bytes=60 << 20),
        name="ag8",
    )(*arrs)

def rsz_kernel(N, Z, nch, *refs):
    ins, outs = refs[:N], refs[N:2*N]
    ups, dns = refs[2*N:3*N], refs[3*N:4*N]
    su, ru, sd, rd = refs[4*N:]
    z = lax.axis_index("batch")
    UP, DN = {"batch": lax.rem(z + 1, Z)}, {"batch": lax.rem(z + Z - 1, Z)}
    greet([UP, DN])
    def chunk(ref, t, n, ch):
        r = ref.shape[1] // nch[n]
        return ref.at[t, pl.ds(ch * r, r)]
    def cpu(n, t, ch, src):
        return remote(src, chunk(ups[n], t, n, ch), su.at[n, t, ch], ru.at[n, t, ch], UP)
    def cpd(n, t, ch, src):
        return remote(src, chunk(dns[n], t, n, ch), sd.at[n, t, ch], rd.at[n, t, ch], DN)
    order = [(n, ch) for n in range(N) for ch in range(nch[n])]
    for k in range(1, Z):
        for n, ch in order:
            tu, td = Z - k, k - 1
            @pl.when(z == 0)
            def _():
                cpu(n, tu, ch, chunk(ins[n], tu, n, ch)).start()
            @pl.when(z == Z - 1)
            def _():
                cpd(n, td, ch, chunk(ins[n], td, n, ch)).start()
    for k in range(1, Z):
        for n, ch in order:
            tu, td = Z - k, k - 1
            @pl.when((z > 0) & (z < tu))
            def _():
                cpu(n, tu, ch, chunk(ups[n], tu, n, ch)).wait_recv()
                b = chunk(ups[n], tu, n, ch)
                b[...] = b[...] + chunk(ins[n], tu, n, ch)[...]
                cpu(n, tu, ch, b).start()
            @pl.when((z < Z - 1) & (z > td))
            def _():
                cpd(n, td, ch, chunk(dns[n], td, n, ch)).wait_recv()
                b = chunk(dns[n], td, n, ch)
                b[...] = b[...] + chunk(ins[n], td, n, ch)[...]
                cpd(n, td, ch, b).start()
            for t in range(Z):
                pass
    for n, ch in order:
        r = ins[n].shape[1] // nch[n]
        for t in range(Z):
            @pl.when(z == t)
            def _():
                v = chunk(ins[n], t, n, ch)[...]
                if t > 0:
                    cpu(n, t, ch, chunk(ups[n], t, n, ch)).wait_recv()
                    v = v + chunk(ups[n], t, n, ch)[...]
                if t < Z - 1:
                    cpd(n, t, ch, chunk(dns[n], t, n, ch)).wait_recv()
                    v = v + chunk(dns[n], t, n, ch)[...]
                outs[n][pl.ds(ch * r, r)] = v
    for n, ch in order:
        for t in range(Z):
            @pl.when(z < t)
            def _():
                cpu(n, t, ch, chunk(ups[n], t, n, ch)).wait_send()
            @pl.when(z > t)
            def _():
                cpd(n, t, ch, chunk(dns[n], t, n, ch)).wait_send()

def rsz(*arrs, nch, Z, cid=1):
    N = len(arrs); M = max(nch)
    return pl.pallas_call(
        functools.partial(rsz_kernel, N, Z, nch),
        out_shape=[jax.ShapeDtypeStruct(a.shape[1:], F32) for a in arrs],
        in_specs=[pl.BlockSpec(memory_space=pltpu.VMEM)] * N,
        out_specs=[pl.BlockSpec(memory_space=pltpu.VMEM)] * N,
        scratch_shapes=[pltpu.VMEM(a.shape, F32) for a in arrs] * 2 + [pltpu.SemaphoreType.DMA((N, Z, M))] * 4,
        compiler_params=pltpu.CompilerParams(collective_id=cid, has_side_effects=True, vmem_limit_bytes=60 << 20),
        name="rsz",
    )(*arrs)

def peers(p):
    return [lax.rem(p["i"] + k, 8) for k in range(1, 8)]

def a2a8_kernel(N, *refs):
    ins, outs = refs[:N], refs[N:2*N]
    ss, rs, ls = refs[2*N:]
    p = plane()
    ps = peers(p)
    greet([{"seq": p["base"] + j} for j in ps])
    sends = []
    for n in range(N):
        l = pltpu.make_async_copy(ins[n].at[p["i"]], outs[n].at[p["i"]], ls.at[n]); l.start()
        for k, j in enumerate(ps):
            c = remote(ins[n].at[j], outs[n].at[p["i"]], ss.at[n, k], rs.at[n, k], {"seq": p["base"] + j})
            c.start(); sends.append(c)
        l.wait()
    for n in range(N):
        for k in range(7):
            src = lax.rem(p["i"] + 7 - k, 8)
            remote(ins[n].at[src], outs[n].at[src], ss.at[n, k], rs.at[n, k], {"seq": p["base"] + src}).wait_recv()
    for c in sends: c.wait_send()

def a2a8(*arrs, cid):
    N = len(arrs)
    v = pl.BlockSpec(memory_space=pltpu.VMEM)
    return pl.pallas_call(functools.partial(a2a8_kernel, N),
        out_shape=[jax.ShapeDtypeStruct(a.shape, F32) for a in arrs], in_specs=[v]*N, out_specs=[v]*N,
        scratch_shapes=[pltpu.SemaphoreType.DMA((N, 7))]*2 + [pltpu.SemaphoreType.DMA((N,))],
        compiler_params=pltpu.CompilerParams(collective_id=cid, has_side_effects=True), name="a2a8")(*arrs)

def small_kernel(Z, NV, NS, x_ref, v_ref, o_ref, st_ref, land, mine, zland, stall, ss, rs, zs, zr, bs, br):
    p = plane(); z = lax.axis_index("batch")
    ps = peers(p)
    zp = [lax.rem(z + k, Z) for k in range(1, Z)]
    greet([{"seq": p["base"] + j} for j in ps] + [{"batch": q} for q in zp])
    sends = []
    for k, j in enumerate(ps):
        c = remote(x_ref.at[j], land.at[p["i"]], ss.at[k], rs.at[k], {"seq": p["base"] + j})
        c.start(); sends.append(c)
    tot = x_ref[p["i"]]
    for k in range(7):
        src = lax.rem(p["i"] + 7 - k, 8)
        remote(x_ref.at[src], land.at[src], ss.at[k], rs.at[k], {"seq": p["base"] + src}).wait_recv()
        tot = tot + land[src]
    mine[0:NV + NS] = tot
    mine[NV + NS:] = v_ref[...]
    stall[p["i"]] = tot[NV:NV + NS]
    for k, j in enumerate(ps):
        c = remote(mine.at[pl.ds(NV, NS)], stall.at[p["i"]], bs.at[k], br.at[k], {"seq": p["base"] + j})
        c.start(); sends.append(c)
    for k, q in enumerate(zp):
        c = remote(mine, zland.at[z], zs.at[k], zr.at[k], {"batch": q})
        c.start(); sends.append(c)
    acc = mine[...]
    for k in range(Z - 1):
        src = lax.rem(z + Z - 1 - k, Z)
        remote(mine, zland.at[src], zs.at[k], zr.at[k], {"batch": src}).wait_recv()
        acc = acc + zland[src]
    o_ref[...] = acc
    for k in range(7):
        src = lax.rem(p["i"] + 7 - k, 8)
        remote(mine.at[pl.ds(NV, NS)], stall.at[src], bs.at[k], br.at[k], {"seq": p["base"] + src}).wait_recv()
    for c in sends: c.wait_send()
    st_ref[...] = stall[...]

def small(x, v, NV, NS, Z, cid):
    NT = NV + NS + v.shape[0]
    vm = pl.BlockSpec(memory_space=pltpu.VMEM)
    D = pltpu.SemaphoreType.DMA
    return pl.pallas_call(functools.partial(small_kernel, Z, NV, NS),
        out_shape=[jax.ShapeDtypeStruct((NT, 128), F32), jax.ShapeDtypeStruct((8, NS, 128), F32)], in_specs=[vm]*2, out_specs=[vm]*2,
        scratch_shapes=[pltpu.VMEM(x.shape, F32), pltpu.VMEM((NT, 128), F32), pltpu.VMEM((Z, NT, 128), F32), pltpu.VMEM((8, NS, 128), F32),
                        D((7,)), D((7,)), D((Z-1,)), D((Z-1,)), D((7,)), D((7,))],
        compiler_params=pltpu.CompilerParams(collective_id=cid, has_side_effects=True), name="small")(x, v)


def cmul(ar, ai, br, bi):
    return ar * br - ai * bi, ar * bi + ai * br

def lam_of(rate, freq):
    damp = jnp.exp(-rate)
    q = freq * freq
    cosv = 1.0 + q * (-1.0/2 + q * (1.0/24 + q * (-1.0/720 + q * (1.0/40320 + q * (-1.0/3628800)))))
    sinv = freq * (1.0 + q * (-1.0/6 + q * (1.0/120 + q * (-1.0/5040 + q * (1.0/362880)))))
    return damp * cosv, damp * sinv

def power_rows(lr, li, qr, qi, A):
    l2 = cmul(lr, li, lr, li); l4 = cmul(*l2, *l2); l8 = cmul(*l4, *l4)
    cur = (jnp.ones_like(lr), jnp.zeros_like(lr))
    for a in range(A):
        qr[a] = cur[0]; qi[a] = cur[1]
        cur = cmul(*cur, *l8)
    return l2, l4, cur

def offset_power(top, s, nbits):
    res = (jnp.ones_like(top[0]), jnp.zeros_like(top[0]))
    sq = top
    for bit in range(nbits):
        on = lax.rem(lax.div(s, 1 << bit), 2) == 1
        nxt = cmul(*res, *sq)
        res = (jnp.where(on, nxt[0], res[0]), jnp.where(on, nxt[1], res[1]))
        if bit + 1 < nbits: sq = cmul(*sq, *sq)
    return res

def e8_tile(tab, m, b):
    row = lambda k: jnp.broadcast_to(tab[k, pl.ds(m, 1), :], b.shape)
    one, zero = jnp.ones(b.shape, F32), jnp.zeros(b.shape, F32)
    o1, o2, o4 = (b % 2) == 1, ((b // 2) % 2) == 1, b >= 4
    r = jnp.where(o1, row(0), one), jnp.where(o1, row(1), zero)
    r = cmul(*r, jnp.where(o2, row(2), one), jnp.where(o2, row(3), zero))
    return cmul(*r, jnp.where(o4, row(4), one), jnp.where(o4, row(5), zero))

def fwd_tiles(nbits, lo, hi, rate, freq, cre, cim, prior, kern, resp, qr, qi, tab, co):
    M = rate.shape[0]; A = kern.shape[0] // 8
    s = lax.axis_index("seq")
    b = lax.broadcasted_iota(jnp.int32, (8, LT), 0)
    @pl.loop(lo, hi)
    def _(lt):
        cols = pl.ds(pl.multiple_of(lt * LT, LT), LT)
        lr, li = lam_of(rate[:, cols], freq[:, cols])
        l2, l4, top = power_rows(lr, li, qr, qi, A)
        for k, v in enumerate((lr, li, *l2, *l4)): tab[k] = v
        off = cmul(*offset_power(top, s, nbits), lr, li)
        c = cre[:, cols], cim[:, cols]
        d = cmul(*cmul(*c, *off), prior[0, 0, :, cols], prior[0, 1, :, cols])
        for a in range(A):
            q = qr[a], qi[a]
            ca = cmul(*c, *q); da = cmul(*d, *q)
            co[0, a], co[1, a], co[2, a], co[3, a] = ca[0], ca[1], da[0], da[1]
        def step(m, accs):
            er, ei = e8_tile(tab, m, b)
            out = []
            for a in range(A):
                row = lambda k: co[k, a, pl.ds(m, 1), :]
                out.append(accs[2*a] + (er * row(0) - ei * row(1)))
                out.append(accs[2*a+1] + (er * row(2) - ei * row(3)))
            return tuple(out)
        accs = lax.fori_loop(0, M, step, tuple(jnp.zeros((8, LT), F32) for _ in range(2 * A)))
        for a in range(A):
            kern[pl.ds(8*a, 8), cols] = accs[2*a]
            resp[pl.ds(8*a, 8), cols] = accs[2*a+1]

class Gather:
    def __init__(self, p, own, land, ssem, rsem):
        self.p, self.own, self.land, self.ss, self.rs = p, own, land, ssem, rsem
        self.H = own.shape[0] // 2
        seq = lambda j: {"seq": p["base"] + j}
        self.X, self.Y, self.S = seq(p["ix"]), seq(p["iy"]), seq(p["ic"])

    def cp(self, k, j, h, dev, src=None):
        blk = self.land.at[j, pl.ds(h * self.H, self.H)]
        return remote(blk if src is None else src, blk, self.ss.at[k], self.rs.at[k], dev)

    def plan(self):
        i, ix, iy, idg = self.p["i"], self.p["ix"], self.p["iy"], self.p["idg"]
        return [(0, i, 0, self.X), (2, i, 1, self.Y), (1, i, 1, self.X), (3, i, 0, self.Y), (6, i, 0, self.S), (7, i, 1, self.S),
                (4, ix, 0, self.Y), (8, ix, 0, self.S), (5, iy, 1, self.X), (11, iy, 1, self.S), (9, ix, 1, self.S),
                (10, iy, 0, self.S), (12, idg, 0, self.S), (13, idg, 1, self.S)]

    def _send(self, k, own=False):
        k, j, h, dev = next(e for e in self.plan() if e[0] == k)
        self.cp(k, j, h, dev, self.own.at[pl.ds(h * self.H, self.H)] if own else None).start()

    def _got(self, k, j, h):
        self.cp(k, j, h, self.S).wait_recv()

    def start(self):
        for k in (0, 2, 1, 3, 6, 7):
            self._send(k, True)

    def relay1(self):
        p = self.p
        self._got(0, p["ix"], 0); self._send(4); self._send(8)
        self._got(2, p["iy"], 1); self._send(5); self._send(11)

    def relay2(self):
        p = self.p
        self._got(1, p["ix"], 1); self._send(9)
        self._got(3, p["iy"], 0); self._send(10)

    def relay3(self):
        p = self.p
        self._got(4, p["idg"], 0); self._send(12)
        self._got(5, p["idg"], 1); self._send(13)

    def finish(self):
        p = self.p
        for k, j in ((6, p["ic"]), (8, sib_of(p, p["ix"])), (10, sib_of(p, p["iy"])), (12, sib_of(p, p["idg"]))):
            self._got(k, j, 0); self._got(k + 1, j, 1)

    def others(self):
        p = self.p
        return (p["ix"], p["iy"], p["idg"], p["ic"], sib_of(p, p["ix"]), sib_of(p, p["iy"]), sib_of(p, p["idg"]))

    def drain(self):
        for k, j, h, dev in self.plan():
            self.cp(k, j, h, dev).wait_send()


def ka_kernel(nbits, rate, freq, cre, cim, prior, cot, kern, resp, cot_all, qr, qi, tab, co, own, land, ssem, rsem):
    p = plane()
    R = cot.shape[0]
    own[...] = cot[...].astype(F32)
    g = Gather(p, own, land, ssem, rsem)
    greet([g.X, g.Y, g.S])
    g.start()
    half = rate.shape[1] // LT // 2
    fwd_tiles(nbits, 0, half, rate, freq, cre, cim, prior, kern, resp, qr, qi, tab, co)
    g.relay1()
    g.relay2()
    fwd_tiles(nbits, half, 2 * half, rate, freq, cre, cim, prior, kern, resp, qr, qi, tab, co)
    g.relay3()
    cot_all[pl.ds(pl.multiple_of(p["i"] * R, R), R), :] = cot[...]
    g.finish()
    for j in g.others():
        cot_all[pl.ds(pl.multiple_of(j * R, R), R), :] = land[j].astype(BF16)
    g.drain()


def ka(rate, freq, cre, cim, prior, cot, nbits, cid):
    M, H = rate.shape
    A = 16
    R = cot.shape[0]
    v = pl.BlockSpec(memory_space=pltpu.VMEM)
    D = pltpu.SemaphoreType.DMA
    return pl.pallas_call(
        functools.partial(ka_kernel, nbits),
        out_shape=[jax.ShapeDtypeStruct((8 * A, H), F32)] * 2 + [jax.ShapeDtypeStruct((8 * R, H), BF16)],
        in_specs=[v] * 6, out_specs=[v] * 3,
        scratch_shapes=[pltpu.VMEM((A, M, LT), F32)] * 2 + [pltpu.VMEM((6, M, LT), F32), pltpu.VMEM((4, A, M, LT), F32),
                        pltpu.VMEM((R, H), F32), pltpu.VMEM((8, R, H), F32), D((14,)), D((14,))],
        compiler_params=pltpu.CompilerParams(collective_id=cid, has_side_effects=True, vmem_limit_bytes=60 << 20),
        name="ka")(rate, freq, cre, cim, prior, cot)


def bwd_kernel(nbits, TOK, rate, freq, cre, cim, prior, kg, gz, out, state, qr, qi, acc):
    M = rate.shape[0]; A = kg.shape[0] // 8
    s = lax.axis_index("seq")
    adv = (s * TOK + 1).astype(F32)
    @pl.loop(0, rate.shape[1] // LT)
    def _(lt):
        cols = pl.ds(pl.multiple_of(lt * LT, LT), LT)
        lr, li = lam_of(rate[:, cols], freq[:, cols])
        l2, l4, top = power_rows(lr, li, qr, qi, A)
        def step(m, carry):
            for j, g in enumerate((kg, gz)):
                z = jnp.zeros((8, LT), F32)
                sr, si, tr, ti = z, z, z, z
                for a in range(A - 1, -1, -1):
                    ga = g[pl.ds(8*a, 8), cols]
                    sr = sr + ga * qr[a, pl.ds(m, 1), :]
                    si = si + ga * qi[a, pl.ds(m, 1), :]
                    if a > 0:
                        tr = tr + sr; ti = ti + si
                rows = pl.ds(pl.multiple_of(m * 8, 8), 8)
                for q, v in enumerate((sr, si, tr, ti)): acc[4*j+q, rows, :] = v
            return carry
        lax.fori_loop(0, M, step, 0)
        pw = (jnp.ones_like(lr), jnp.zeros_like(lr))
        tot = []
        zero = jnp.zeros_like(lr)
        ar, ai, br, bi = [zero]*2, [zero]*2, [zero]*2, [zero]*2
        for b in range(8):
            for j in range(2):
                ld = lambda q: acc[4*j+q, pl.ds(b, M, stride=8), :]
                S = ld(0), ld(1)
                U = 8.0 * ld(2), 8.0 * ld(3)
                if b: U = U[0] + float(b) * S[0], U[1] + float(b) * S[1]
                p = cmul(*pw, *S); ar[j] = ar[j] + p[0]; ai[j] = ai[j] + p[1]
                p = cmul(*pw, *U); br[j] = br[j] + p[0]; bi[j] = bi[j] + p[1]
            pw = cmul(*pw, lr, li)
        off = cmul(*offset_power(top, s, nbits), lr, li)
        c = cre[:, cols], cim[:, cols]
        ps = cmul(*off, prior[0, 0, :, cols], prior[0, 1, :, cols])
        u = cmul(*ps, ar[1], ai[1])
        u = u[0] + ar[0], u[1] + ai[0]
        v = cmul(*ps, br[1] + adv * ar[1], bi[1] + adv * ai[1])
        v = cmul(*c, v[0] + br[0], v[1] + bi[0])
        w = cmul(*cmul(*c, *off), ar[1], ai[1])
        out[0, :, cols] = -v[0]; out[1, :, cols] = -v[1]; out[2, :, cols] = u[0]; out[3, :, cols] = -u[1]
        state[0, :, cols] = w[0]; state[1, :, cols] = -w[1]

def modes_bwd(rate, freq, cre, cim, prior, kg, gz, nbits):
    M, H = rate.shape; A = 16
    v = pl.BlockSpec(memory_space=pltpu.VMEM)
    return pl.pallas_call(functools.partial(bwd_kernel, nbits, gz.shape[0]),
        out_shape=[jax.ShapeDtypeStruct((4, M, H), F32), jax.ShapeDtypeStruct((2, M, H), F32)], in_specs=[v]*7, out_specs=[v]*2,
        scratch_shapes=[pltpu.VMEM((A, M, LT), F32)]*2 + [pltpu.VMEM((8, 8*M, LT), F32)],
        name="modes_bwd")(rate, freq, cre, cim, prior, kg, gz)


def fast_shards(Z, n_seq, inputs, first_gain, first_shift, decay_rate, rotation, out_real, out_imag, skip_gain, glu_weight,
                glu_bias, second_gain, second_shift, up_weight, up_bias, down_weight, down_bias, prior_state, cotangent):
    T, D = inputs.shape[1:]
    FF = up_weight.shape[1]
    nbits = max(1, (n_seq - 1).bit_length())
    s = lax.axis_index("seq")
    window = T + KLEN
    half = window // 2 + 1
    fi = np.arange(half)[:, None]; ti = np.arange(window)[None, :]
    ph = (fi * ti % window) * (2.0 * np.pi / window)
    fwd_tab = jnp.asarray(np.concatenate([np.cos(ph), -np.sin(ph)], 0), F32)
    wt = np.where((fi == 0) | (2 * fi == window), 1.0, 2.0) / window
    inv_tab = jnp.asarray(np.concatenate([(wt * np.cos(ph)).T, -(wt * np.sin(ph)).T], 1)[KLEN:], F32)
    hi = functools.partial(jnp.einsum, precision=HIGHEST)
    source = inputs[0].astype(F32)
    def stats(v):
        center = v - jnp.mean(v, axis=-1, keepdims=True)
        inv = lax.rsqrt(jnp.mean(center * center, axis=-1, keepdims=True) + EPSILON)
        return center * inv, inv
    xhat, xinv = stats(source)
    normed = xhat * first_gain + first_shift
    halo_src = from_behind(source, "seq", 1)
    halo = jnp.where(s == 0, 0.0, stats(halo_src)[0] * first_gain + first_shift)
    rate, freq, cre, cim = decay_rate.T, rotation.T, out_real.T, out_imag.T
    cot = cotangent[0]
    kern, resp, cot_all = ka(rate, freq, cre, cim, prior_state, cot, nbits, 5)
    ext = jnp.concatenate([halo, normed], 0)
    X = hi("ft,th->fh", fwd_tab, ext)
    K = hi("ft,th->fh", fwd_tab[:, :KLEN], kern)
    Xr, Xi, Kr, Ki = X[:half], X[half:], K[:half], K[half:]
    conv = hi("tf,fh->th", inv_tab, jnp.concatenate([Xr * Kr - Xi * Ki, Xr * Ki + Xi * Kr], 0))
    pre = conv + skip_gain * normed + resp
    act, act_pull = jax.vjp(gelu_exact, pre)
    act_low = act.astype(BF16)
    dot = functools.partial(lax.dot_general, preferred_element_type=F32)
    mm = lambda a, b: dot(a, b, (((1,), (0,)), ((), ())))
    mt = lambda a, b: dot(a, b, (((1,), (1,)), ((), ())))
    tm = lambda a, b: dot(a, b, (((0,), (0,)), ((), ())))
    glu_pre = mm(act_low, glu_weight) + glu_bias
    value, sg = glu_pre[:, :D], jax.nn.sigmoid(glu_pre[:, D:])
    merged = source + value * sg
    mhat, minv = stats(merged)
    second_low = (mhat * second_gain + second_shift).astype(BF16)
    up_pre = mm(second_low, up_weight) + up_bias
    hidden, hidden_pull = jax.vjp(gelu_exact, up_pre)
    outputs = (merged + mm(hidden.astype(BF16), down_weight) + down_bias).astype(BF16)
    grad_out = cot.astype(F32)
    (grad_up,) = hidden_pull(mt(cot, down_weight))
    grad_second = mt(grad_up.astype(BF16), up_weight)
    def ln_back(g, gain, hat, inv):
        gg = g * gain
        return inv * (gg - jnp.mean(gg, -1, keepdims=True) - hat * jnp.mean(gg * hat, -1, keepdims=True))
    grad_merged = grad_out + ln_back(grad_second, second_gain, mhat, minv)
    grad_value, grad_gate = grad_merged * sg, grad_merged * value * sg * (1 - sg)
    glu_low = jnp.concatenate([grad_value, grad_gate], 1).astype(BF16)
    (gz,) = act_pull(mt(glu_low, glu_weight))
    second_all, act_all = ag8(second_low.astype(F32), act_low.astype(F32), cid=0)
    gm_blocks = grad_merged.reshape(T, 8, D // 8).transpose(1, 0, 2)
    (gm_all,) = a2a8(gm_blocks, cid=1)
    gm_all = gm_all.reshape(8 * T, D // 8)
    i = lax.rem(s, 8)
    FS, GS = FF // 8, D // 8
    fcol = lambda w, ax: lax.dynamic_slice_in_dim(w, i * FS, FS, ax)
    up_pre_s = mm(second_all, fcol(up_weight, 1)) + fcol(up_bias, 0)
    hidden_s, hidden_pull_s = jax.vjp(gelu_exact, up_pre_s)
    (grad_up_s,) = hidden_pull_s(mt(cot_all, fcol(down_weight, 0)))
    down_g = tm(hidden_s.astype(BF16), cot_all).reshape(Z, FS // Z, D)
    up_g = tm(second_all, grad_up_s.astype(BF16)).reshape(8, Z, D // 8 // Z, FS).transpose(1, 0, 2, 3).reshape(Z, D // Z, FS)
    up_bias_s = jnp.sum(grad_up_s, 0)
    gcol = lambda w: jnp.concatenate([lax.dynamic_slice_in_dim(w, i * GS, GS, -1 if w.ndim > 1 else 0),
                                      lax.dynamic_slice_in_dim(w, D + i * GS, GS, -1 if w.ndim > 1 else 0)], -1)
    gp = mm(act_all, gcol(glu_weight)) + gcol(glu_bias)
    v_s, sg_s = gp[:, :GS], jax.nn.sigmoid(gp[:, GS:])
    gg_s = jnp.concatenate([gm_all * sg_s, gm_all * v_s * sg_s * (1 - sg_s)], 1)
    glu_g = tm(act_all, gg_s.astype(BF16)).reshape(8, Z, D // 8 // Z, 2 * GS).transpose(1, 0, 2, 3).reshape(Z, D // Z, 2 * GS)
    down_o, up_o, glu_o = rsz(down_g, up_g, glu_g, nch=(2, 2, 1), Z=Z, cid=2)
    up_x, glu_x = a2a8(up_o.reshape(8, D // 8 // Z, FS), glu_o.reshape(8, D // 8 // Z, 2 * GS), cid=3)
    up_final = up_x.transpose(1, 0, 2).reshape(-1, FF)
    glu_final = glu_x.reshape(8, -1, 2, GS).transpose(1, 2, 0, 3).reshape(-1, 2 * D)
    gp_ = hi("tf,th->fh", inv_tab, gz)
    gr, gi = gp_[:half], gp_[half:]
    kg = hi("ft,fh->th", fwd_tab[:, :KLEN], jnp.concatenate([gr * Xr + gi * Xi, gi * Xr - gr * Xi], 0))
    gext = hi("ft,fh->th", fwd_tab, jnp.concatenate([gr * Kr + gi * Ki, gi * Kr - gr * Ki], 0))
    modes_g, state_g = modes_bwd(rate, freq, cre, cim, prior_state, kg, gz, nbits)
    tail = from_behind(gext[:KLEN], "seq", -1)
    grad_normed = gext[KLEN:] + tail + skip_gain * gz
    input_grad = (grad_merged + ln_back(grad_normed, first_gain, xhat, xinv)).astype(BF16)
    vec = jnp.stack([jnp.sum(grad_normed * xhat, 0), jnp.sum(grad_normed, 0), jnp.sum(gz * normed, 0),
                     jnp.sum(grad_second * mhat, 0), jnp.sum(grad_second, 0), jnp.sum(grad_out, 0)])
    glu_vec = jnp.concatenate([jnp.sum(grad_value, 0), jnp.sum(grad_gate, 0)]).reshape(8, 2, 128)
    M = rate.shape[0]
    NV, NS = 4 * M + 8, 2 * M
    lanes = lambda v: v.reshape(-1, 8, D // 8).transpose(1, 0, 2)
    packed = jnp.concatenate([lanes(modes_g), lanes(vec), glu_vec, lanes(state_g)], 1)
    tv = jnp.concatenate([up_bias_s.reshape(-1, 128), jnp.zeros((4, 128), F32)], 0)
    tot, st = small(packed, tv, NV, NS, Z, cid=4)
    state_grad = st.transpose(1, 0, 2).reshape(1, 2, M, D)
    b = lax.axis_index("batch")
    W = D // 8 // Z
    mine = lax.dynamic_slice_in_dim(tot[:NV], b * W, W, 1)
    mg = [mine[k * M:(k + 1) * M].T for k in range(4)]
    vg = [mine[4 * M + k] for k in range(6)]
    ub = lax.dynamic_slice_in_dim(tot[NV + NS:NV + NS + FS // 128].reshape(FS), b * (FS // Z), FS // Z, 0)
    gb = lax.dynamic_slice_in_dim(tot[4 * M + 6:NV].reshape(2 * D // 8), b * (2 * W), 2 * W, 0)
    return (outputs[None], input_grad[None], state_grad, vg[0], vg[1], mg[0], mg[1], mg[2], mg[3], vg[2], glu_final, gb,
            vg[3], vg[4], up_final, ub, down_o, vg[5])


def solution(mesh):
    in_specs = (
        P("batch", "seq", None),
        P(),
        P(),
        P(),
        P(),
        P(),
        P(),
        P(),
        P(),
        P(),
        P(),
        P(),
        P(),
        P(),
        P(),
        P(),
        P("batch", None, None, None),
        P("batch", "seq", None),
    )
    out_specs = (
        P("batch", "seq", None),
        P("batch", "seq", None),
        P("batch", None, None, None),
        P(("seq", "batch")),
        P(("seq", "batch")),
        P(("seq", "batch"), None),
        P(("seq", "batch"), None),
        P(("seq", "batch"), None),
        P(("seq", "batch"), None),
        P(("seq", "batch")),
        P(("seq", "batch"), None),
        P(("seq", "batch")),
        P(("seq", "batch")),
        P(("seq", "batch")),
        P(("seq", "batch"), None),
        P(("seq", "batch")),
        P(("seq", "batch"), None),
        P(("seq", "batch")),
    )
    body = shards
    if mesh.shape["seq"] == 8:
        body = functools.partial(fast_shards, mesh.shape["batch"], mesh.shape["seq"])
    return jax.shard_map(body, mesh=mesh, in_specs=in_specs, out_specs=out_specs, check_vma=False)
```

```python
import functools
import math

import jax
import jax.numpy as jnp
import ml_dtypes
import numpy as np
from jax import lax
from jax.experimental import pallas as pl
from jax.experimental.pallas import tpu as pltpu
from jax.sharding import PartitionSpec as P

KLEN = 128
LT = 128
MESH = pl.DeviceIdType.MESH
F32, BF16 = jnp.float32, jnp.bfloat16


EPSILON = 1e-05
HIGHEST = lax.Precision.HIGHEST


def from_behind(value, axis, by):
    peers = lax.axis_size(axis)
    pairs = [(i, i + by) for i in range(peers) if 0 <= i + by < peers]
    return lax.ppermute(value, axis, pairs)


def norm_rows(values, gain, shift):
    center = values - jnp.mean(values, axis=-1, keepdims=True)
    spread = jnp.mean(center * center, axis=-1, keepdims=True)
    return center * lax.rsqrt(spread + EPSILON) * gain + shift


def mode_terms(rate_modes, freq_modes, elapsed):
    moment = elapsed[None, :, None]
    damping = jnp.exp(-rate_modes[:, None, :] * moment)
    return (
        damping * jnp.cos(freq_modes[:, None, :] * moment),
        damping * jnp.sin(freq_modes[:, None, :] * moment),
    )


def glu_gate(glu_pre):
    split_at = glu_pre.shape[-1] // 2
    return glu_pre[:, :split_at] * jax.nn.sigmoid(glu_pre[:, split_at:])


def gelu_exact(values):
    return jax.nn.gelu(values, approximate=False)


def shards(
    inputs,
    first_gain,
    first_shift,
    decay_rate,
    rotation,
    out_real,
    out_imag,
    skip_gain,
    glu_weight,
    glu_bias,
    second_gain,
    second_shift,
    up_weight,
    up_bias,
    down_weight,
    down_bias,
    prior_state,
    cotangent,
):
    seg_count, tok_count, feature = inputs.shape
    row_count = seg_count * tok_count
    window = tok_count + KLEN
    half = window // 2 + 1
    offset = lax.axis_index("seq") * tok_count
    freq_index = jnp.arange(half, dtype=jnp.int32)
    time_index = jnp.arange(window, dtype=jnp.int32)
    phase = (freq_index[:, None] * time_index[None, :] % window).astype(jnp.float32) * (
        2.0 * math.pi / window
    )
    cos_half = jnp.cos(phase)
    sin_half = jnp.sin(phase)
    forward_table = jnp.concatenate([cos_half, -sin_half], axis=0)
    weights = jnp.where((freq_index == 0) | (2 * freq_index == window), 1.0, 2.0).astype(
        jnp.float32
    )
    inverse_table = (
        jnp.concatenate(
            [(weights[:, None] * cos_half).T, -(weights[:, None] * sin_half).T], axis=1
        )[KLEN:]
        / window
    )
    local_steps = jnp.arange(tok_count).astype(jnp.float32)
    advance_steps = (offset + 1).astype(jnp.float32)

    def mixing(
        normed, halo_rows, rate_modes, freq_modes, real_modes, imag_modes, skip_local, prior_local
    ):
        table_real, table_imag = mode_terms(rate_modes, freq_modes, local_steps)
        kernel = jnp.einsum("mkh,mh->kh", table_real, real_modes, precision=HIGHEST) - jnp.einsum(
            "mkh,mh->kh", table_imag, imag_modes, precision=HIGHEST
        )
        extended = jnp.concatenate([halo_rows, normed], axis=1)
        spectrum = jnp.einsum("ft,sth->sfh", forward_table, extended, precision=HIGHEST)
        kern_spec = jnp.dot(forward_table[:, :KLEN], kernel, precision=HIGHEST)
        spec_real, spec_imag = (spectrum[:, :half], spectrum[:, half:])
        kern_real, kern_imag = (kern_spec[:half], kern_spec[half:])
        product = jnp.concatenate(
            [
                spec_real * kern_real - spec_imag * kern_imag,
                spec_real * kern_imag + spec_imag * kern_real,
            ],
            axis=1,
        )
        convolved = jnp.einsum("tf,sfh->sth", inverse_table, product, precision=HIGHEST)
        damping = jnp.exp(-rate_modes * advance_steps)
        adv_real = damping * jnp.cos(freq_modes * advance_steps)
        adv_imag = damping * jnp.sin(freq_modes * advance_steps)
        coef_real = real_modes * adv_real - imag_modes * adv_imag
        coef_imag = real_modes * adv_imag + imag_modes * adv_real
        drive_real = coef_real * prior_local[:, 0] - coef_imag * prior_local[:, 1]
        drive_imag = coef_real * prior_local[:, 1] + coef_imag * prior_local[:, 0]
        response = jnp.einsum(
            "mth,smh->sth", table_real, drive_real, precision=HIGHEST
        ) - jnp.einsum("mth,smh->sth", table_imag, drive_imag, precision=HIGHEST)
        return gelu_exact(convolved + skip_local * normed + response)

    source = inputs.astype(jnp.float32)
    normed, first_pull = jax.vjp(norm_rows, source, first_gain, first_shift)
    halo_rows = from_behind(normed, "seq", 1)
    activated, mix_pull = jax.vjp(
        mixing,
        normed,
        halo_rows,
        decay_rate.T,
        rotation.T,
        out_real.T,
        out_imag.T,
        skip_gain,
        prior_state,
    )
    activated_low = activated.reshape(row_count, feature).astype(jnp.bfloat16)
    glu_pre = jnp.dot(activated_low, glu_weight, preferred_element_type=jnp.float32) + glu_bias
    branch, glu_pull = jax.vjp(glu_gate, glu_pre)
    merged = source.reshape(row_count, feature) + branch
    second, second_pull = jax.vjp(norm_rows, merged, second_gain, second_shift)
    second_low = second.astype(jnp.bfloat16)
    up_pre = jnp.dot(second_low, up_weight, preferred_element_type=jnp.float32) + up_bias
    hidden, hidden_pull = jax.vjp(gelu_exact, up_pre)
    hidden_low = hidden.astype(jnp.bfloat16)
    result = (
        merged + jnp.dot(hidden_low, down_weight, preferred_element_type=jnp.float32) + down_bias
    )
    outputs = result.astype(jnp.bfloat16).reshape(seg_count, tok_count, feature)
    grad_out = cotangent.astype(jnp.float32).reshape(row_count, feature)
    down_bias_grad = jnp.sum(grad_out, axis=0)
    grad_low = grad_out.astype(jnp.bfloat16)
    down_grad = jnp.einsum("rf,rh->fh", hidden_low, grad_low, preferred_element_type=jnp.float32)
    grad_hidden = jnp.einsum("rh,fh->rf", grad_low, down_weight, preferred_element_type=jnp.float32)
    (grad_up,) = hidden_pull(grad_hidden)
    up_bias_grad = jnp.sum(grad_up, axis=0)
    up_low = grad_up.astype(jnp.bfloat16)
    up_grad = jnp.einsum("rh,rf->hf", second_low, up_low, preferred_element_type=jnp.float32)
    grad_second = jnp.einsum("rf,hf->rh", up_low, up_weight, preferred_element_type=jnp.float32)
    grad_merged, second_gain_grad, second_shift_grad = second_pull(grad_second)
    grad_merged = grad_merged + grad_out
    (grad_glu,) = glu_pull(grad_merged)
    glu_bias_grad = jnp.sum(grad_glu, axis=0)
    glu_low = grad_glu.astype(jnp.bfloat16)
    glu_grad = jnp.einsum("rh,rg->hg", activated_low, glu_low, preferred_element_type=jnp.float32)
    grad_activated = jnp.einsum(
        "rg,hg->rh", glu_low, glu_weight, preferred_element_type=jnp.float32
    )
    grad_normed, grad_halo, rate_grad, freq_grad, real_grad, imag_grad, skip_grad, prior_grad = (
        mix_pull(grad_activated.reshape(seg_count, tok_count, feature))
    )
    grad_tail = from_behind(grad_halo, "seq", -1)
    grad_normed = jnp.concatenate(
        [grad_normed[:, : tok_count - KLEN], grad_normed + grad_tail], axis=1
    )
    grad_source, first_gain_grad, first_shift_grad = first_pull(grad_normed)
    input_grad = (grad_source + grad_merged.reshape(seg_count, tok_count, feature)).astype(
        jnp.bfloat16
    )
    state_grad = lax.psum(prior_grad, "seq")
    rate_back = rate_grad.T
    freq_back = freq_grad.T
    real_back = real_grad.T
    imag_back = imag_grad.T
    summed = (
        lax.psum_scatter(first_gain_grad, ("seq", "batch"), scatter_dimension=0, tiled=True),
        lax.psum_scatter(first_shift_grad, ("seq", "batch"), scatter_dimension=0, tiled=True),
        lax.psum_scatter(rate_back, ("seq", "batch"), scatter_dimension=0, tiled=True),
        lax.psum_scatter(freq_back, ("seq", "batch"), scatter_dimension=0, tiled=True),
        lax.psum_scatter(real_back, ("seq", "batch"), scatter_dimension=0, tiled=True),
        lax.psum_scatter(imag_back, ("seq", "batch"), scatter_dimension=0, tiled=True),
        lax.psum_scatter(skip_grad, ("seq", "batch"), scatter_dimension=0, tiled=True),
        lax.psum_scatter(glu_grad, ("seq", "batch"), scatter_dimension=0, tiled=True),
        lax.psum_scatter(glu_bias_grad, ("seq", "batch"), scatter_dimension=0, tiled=True),
        lax.psum_scatter(second_gain_grad, ("seq", "batch"), scatter_dimension=0, tiled=True),
        lax.psum_scatter(second_shift_grad, ("seq", "batch"), scatter_dimension=0, tiled=True),
        lax.psum_scatter(up_grad, ("seq", "batch"), scatter_dimension=0, tiled=True),
        lax.psum_scatter(up_bias_grad, ("seq", "batch"), scatter_dimension=0, tiled=True),
        lax.psum_scatter(down_grad, ("seq", "batch"), scatter_dimension=0, tiled=True),
        lax.psum_scatter(down_bias_grad, ("seq", "batch"), scatter_dimension=0, tiled=True),
    )
    return (
        outputs,
        input_grad,
        state_grad,
        summed[0],
        summed[1],
        summed[2],
        summed[3],
        summed[4],
        summed[5],
        summed[6],
        summed[7],
        summed[8],
        summed[9],
        summed[10],
        summed[11],
        summed[12],
        summed[13],
        summed[14],
    )


def plane():
    s = lax.axis_index("seq")
    i = lax.rem(s, 8)
    base = s - i
    c, x, y = lax.rem(i, 2), lax.rem(i // 2, 2), i // 4
    ic, ix, iy = i + 1 - 2 * c, i + 2 - 4 * x, i + 4 - 8 * y
    idg = iy + 2 - 4 * x
    return dict(s=s, i=i, base=base, c=c, x=x, y=y, ic=ic, ix=ix, iy=iy, idg=idg)

def sib_of(p, j):
    return j + 1 - 2 * p["c"]

def remote(src, dst, ss, rs, dev):
    return pltpu.make_async_remote_copy(src_ref=src, dst_ref=dst, send_sem=ss, recv_sem=rs,
                                        device_id=dev, device_id_type=MESH)

def greet(devs):
    bar = pltpu.get_barrier_semaphore()
    for d in devs:
        pl.semaphore_signal(bar, inc=1, device_id=d, device_id_type=MESH)
    pl.semaphore_wait(bar, len(devs))

def peers(p):
    return [lax.rem(p["i"] + k, 8) for k in range(1, 8)]

class Gather:
    def __init__(self, p, own, land, ssem, rsem):
        self.p, self.own, self.land, self.ss, self.rs = p, own, land, ssem, rsem
        self.H = own.shape[0] // 2
        seq = lambda j: {"seq": p["base"] + j}
        self.X, self.Y, self.S = seq(p["ix"]), seq(p["iy"]), seq(p["ic"])

    def cp(self, k, j, h, dev, src=None):
        blk = self.land.at[j, pl.ds(h * self.H, self.H)]
        return remote(blk if src is None else src, blk, self.ss.at[k], self.rs.at[k], dev)

    def plan(self):
        i, ix, iy, idg = self.p["i"], self.p["ix"], self.p["iy"], self.p["idg"]
        return [(0, i, 0, self.X), (2, i, 1, self.Y), (1, i, 1, self.X), (3, i, 0, self.Y), (6, i, 0, self.S), (7, i, 1, self.S),
                (4, ix, 0, self.Y), (8, ix, 0, self.S), (5, iy, 1, self.X), (11, iy, 1, self.S), (9, ix, 1, self.S),
                (10, iy, 0, self.S), (12, idg, 0, self.S), (13, idg, 1, self.S)]

    def _send(self, k, own=False):
        k, j, h, dev = next(e for e in self.plan() if e[0] == k)
        self.cp(k, j, h, dev, self.own.at[pl.ds(h * self.H, self.H)] if own else None).start()

    def _got(self, k, j, h):
        self.cp(k, j, h, self.S).wait_recv()

    def start(self):
        for k in (0, 2, 1, 3, 6, 7):
            self._send(k, True)

    def relay1(self):
        p = self.p
        self._got(0, p["ix"], 0); self._send(4); self._send(8)
        self._got(2, p["iy"], 1); self._send(5); self._send(11)

    def relay2(self):
        p = self.p
        self._got(1, p["ix"], 1); self._send(9)
        self._got(3, p["iy"], 0); self._send(10)

    def relay3(self):
        p = self.p
        self._got(4, p["idg"], 0); self._send(12)
        self._got(5, p["idg"], 1); self._send(13)

    def finish(self):
        p = self.p
        for k, j in ((6, p["ic"]), (8, sib_of(p, p["ix"])), (10, sib_of(p, p["iy"])), (12, sib_of(p, p["idg"]))):
            self._got(k, j, 0); self._got(k + 1, j, 1)

    def others(self):
        p = self.p
        return (p["ix"], p["iy"], p["idg"], p["ic"], sib_of(p, p["ix"]), sib_of(p, p["iy"]), sib_of(p, p["idg"]))

    def drain(self):
        for k, j, h, dev in self.plan():
            self.cp(k, j, h, dev).wait_send()


def cmul(ar, ai, br, bi):
    return ar * br - ai * bi, ar * bi + ai * br

def lam_of(rate, freq):
    damp = jnp.exp(-rate)
    q = freq * freq
    cosv = 1.0 + q * (-1.0/2 + q * (1.0/24 + q * (-1.0/720 + q * (1.0/40320 + q * (-1.0/3628800)))))
    sinv = freq * (1.0 + q * (-1.0/6 + q * (1.0/120 + q * (-1.0/5040 + q * (1.0/362880)))))
    return damp * cosv, damp * sinv

def power_rows(lr, li, qr, qi, A):
    l2 = cmul(lr, li, lr, li); l4 = cmul(*l2, *l2); l8 = cmul(*l4, *l4)
    cur = (jnp.ones_like(lr), jnp.zeros_like(lr))
    for a in range(A):
        qr[a] = cur[0]; qi[a] = cur[1]
        cur = cmul(*cur, *l8)
    return l2, l4, cur

def offset_power(top, s, nbits):
    res = (jnp.ones_like(top[0]), jnp.zeros_like(top[0]))
    sq = top
    for bit in range(nbits):
        on = lax.rem(lax.div(s, 1 << bit), 2) == 1
        nxt = cmul(*res, *sq)
        res = (jnp.where(on, nxt[0], res[0]), jnp.where(on, nxt[1], res[1]))
        if bit + 1 < nbits: sq = cmul(*sq, *sq)
    return res

def e8_tile(tab, m, b):
    row = lambda k: jnp.broadcast_to(tab[k, pl.ds(m, 1), :], b.shape)
    one, zero = jnp.ones(b.shape, F32), jnp.zeros(b.shape, F32)
    o1, o2, o4 = (b % 2) == 1, ((b // 2) % 2) == 1, b >= 4
    r = jnp.where(o1, row(0), one), jnp.where(o1, row(1), zero)
    r = cmul(*r, jnp.where(o2, row(2), one), jnp.where(o2, row(3), zero))
    return cmul(*r, jnp.where(o4, row(4), one), jnp.where(o4, row(5), zero))

def fwd_tiles(nbits, lo, hi, rate, freq, cre, cim, prior, kern, resp, qr, qi, tab, co):
    M = rate.shape[0]
    A = kern.shape[0] // 8
    s = lax.axis_index("seq")
    b = lax.broadcasted_iota(jnp.int32, (8, LT), 0)
    @pl.loop(lo, hi)
    def _(lt):
        cols = pl.ds(pl.multiple_of(lt * LT, LT), LT)
        lr, li = lam_of(rate[:, cols], freq[:, cols])
        l2, l4, top = power_rows(lr, li, qr, qi, A)
        for k, v in enumerate((lr, li, *l2, *l4)): tab[k] = v
        off = cmul(*offset_power(top, s, nbits), lr, li)
        c = cre[:, cols], cim[:, cols]
        d = cmul(*cmul(*c, *off), prior[0, 0, :, cols], prior[0, 1, :, cols])
        for a in range(A):
            q = qr[a], qi[a]
            for k, v in enumerate((*cmul(*c, *q), *cmul(*d, *q))): co[pl.ds((k * A + a) * M, M), :] = v
        def step(m, accs):
            er, ei = e8_tile(tab, m, b)
            out = []
            for a in range(A):
                row = lambda k: co[pl.ds((k * A + a) * M + m, 1), :]
                out.append(accs[2 * a] + (er * row(0) - ei * row(1)))
                out.append(accs[2 * a + 1] + (er * row(2) - ei * row(3)))
            return tuple(out)
        accs = lax.fori_loop(0, M, step, tuple(jnp.zeros((8, LT), F32) for _ in range(2 * A)))
        for a in range(A):
            kern[pl.ds(8 * a, 8), cols] = accs[2 * a]
            resp[pl.ds(8 * a, 8), cols] = accs[2 * a + 1]


def bwd_tiles(lo, hi, srow, nbits, TOK, rate, freq, cre, cim, prior, kg, gz, out, qr, qi, acc):
    M = rate.shape[0]
    A = kg.shape[0] // 8
    s = lax.axis_index("seq")
    adv = (s * TOK + 1).astype(F32)
    @pl.loop(lo, hi)
    def _(lt):
        cols = pl.ds(pl.multiple_of(lt * LT, LT), LT)
        lr, li = lam_of(rate[:, cols], freq[:, cols])
        l2, l4, top = power_rows(lr, li, qr, qi, A)
        def step(m, carry):
            for j, g in enumerate((kg, gz)):
                z = jnp.zeros((8, LT), F32)
                sr, si, tr, ti = z, z, z, z
                for a in range(A - 1, -1, -1):
                    ga = g[pl.ds(8 * a, 8), cols]
                    sr = sr + ga * qr[a, pl.ds(m, 1), :]
                    si = si + ga * qi[a, pl.ds(m, 1), :]
                    if a > 0:
                        tr = tr + sr
                        ti = ti + si
                for q, v in enumerate((sr, si, tr, ti)):
                    acc[pl.ds(pl.multiple_of(((4 * j + q) * M + m) * 8, 8), 8), :] = v
            return carry
        lax.fori_loop(0, M, step, 0)
        pw = (jnp.ones_like(lr), jnp.zeros_like(lr))
        zero = jnp.zeros_like(lr)
        ar, ai, br, bi = [zero] * 2, [zero] * 2, [zero] * 2, [zero] * 2
        for b in range(8):
            for j in range(2):
                ld = lambda q: acc[pl.ds((4 * j + q) * M * 8 + b, M, stride=8), :]
                S = ld(0), ld(1)
                U = 8.0 * ld(2), 8.0 * ld(3)
                if b: U = U[0] + float(b) * S[0], U[1] + float(b) * S[1]
                w = cmul(*pw, *S)
                ar[j], ai[j] = ar[j] + w[0], ai[j] + w[1]
                w = cmul(*pw, *U)
                br[j], bi[j] = br[j] + w[0], bi[j] + w[1]
            pw = cmul(*pw, lr, li)
        off = cmul(*offset_power(top, s, nbits), lr, li)
        c = cre[:, cols], cim[:, cols]
        ps = cmul(*off, prior[0, 0, :, cols], prior[0, 1, :, cols])
        u = cmul(*ps, ar[1], ai[1])
        v = cmul(*ps, br[1] + adv * ar[1], bi[1] + adv * ai[1])
        v = cmul(*c, v[0] + br[0], v[1] + bi[0])
        w = cmul(*cmul(*c, *off), ar[1], ai[1])
        for k, val in enumerate((-v[0], -v[1], u[0] + ar[0], -(u[1] + ai[0]))): out[k * M:(k + 1) * M, cols] = val
        for k, val in enumerate((w[0], -w[1])): out[srow + k * M:srow + (k + 1) * M, cols] = val


class Bag:
    pass


def dot(a, b, ca=1, cb=0):
    return lax.dot_general(a, b, (((ca,), (cb,)), ((), ())), preferred_element_type=F32)


def split_low(v):
    high = v.astype(BF16)
    return high, (v - high.astype(F32)).astype(BF16)


def table_dot(tab, v, rows=slice(None), cols=slice(None)):
    high, low = split_low(v)
    th, tl = tab[0, rows, cols], tab[1, rows, cols]
    return dot(th, high) + dot(th, low) + dot(tl, high)


def gelu_both(u):
    cdf = 0.5 + 0.5 * lax.erf(u * (0.5 ** 0.5))
    return u * cdf, cdf + u * (jnp.exp(-0.5 * u * u) * ((2.0 * math.pi) ** -0.5))


def tiles(n, step):
    def run(body, init=None):
        if init is None:
            @pl.loop(0, n // step)
            def _(k):
                body(pl.ds(pl.multiple_of(k * step, step), step))
            return None
        return lax.fori_loop(0, n // step, lambda k, c: body(pl.ds(pl.multiple_of(k * step, step), step), c), init)
    return run


def sub(off, q):
    return pl.ds(pl.multiple_of(off + q.start, q.size), q.size)


def row_mean(v):
    return jnp.sum(v, axis=-1, keepdims=True) * (1.0 / v.shape[-1])


def norm_hat(v):
    center = v - row_mean(v)
    inv = lax.rsqrt(row_mean(center * center) + EPSILON)
    return center * inv, inv


def norm_back(gg, hat, inv):
    return inv * (gg - row_mean(gg) - hat * row_mean(gg * hat))


def fold(v):
    return jnp.sum(v, axis=0, keepdims=True)


LC = 256
ROWS = 8
VEC = ("first_gain", "first_shift", "skip_gain", "second_gain", "second_shift", "down_bias", "value_bias", "gate_bias")


def layer_kernel(cfg, names, *refs):
    r = Bag()
    r.__dict__.update(zip(names, refs))
    Z, NSEQ, nbits, T, D, FF, M = cfg
    FT = FF // 8
    HB = D // 8 // Z
    p = plane()
    s, i = p["s"], p["i"]
    z = lax.axis_index("batch")
    vec = {k: (lambda q: (lambda c=slice(None): r.vecs[q:q + 1, c]))(q) for q, k in enumerate(VEC)}
    iblk = pl.ds(pl.multiple_of(i * T, T), T)

    lane = lambda off, n: pl.ds(pl.multiple_of(off, 128), n)
    local = lambda src, dst, sem: pltpu.make_async_copy(src, dst, sem)
    gw_copy = local(r.glu_w, r.gw, r.lsem.at[0])
    gw_copy.start()
    def tile_copy(t, slot):
        return (local(r.up_w.at[:, lane(t * FT, FT)], r.wu.at[slot], r.tsem.at[0, slot]),
                local(r.down_w.at[pl.ds(pl.multiple_of(t * FT, FT), FT)], r.wd.at[slot], r.tsem.at[1, slot]))
    for t in range(2):
        for c in tile_copy(t, t): c.start()
    wgs_copy = [local(r.glu_w.at[:, lane(q * D + i * 128, 128)], r.wgs.at[:, pl.ds(q * 128, 128)], r.lsem.at[1 + q]) for q in range(2)]
    for c in wgs_copy: c.start()

    @tiles(T, 16)
    def _(q):
        r.xs[q, :] = r.x[q, :].astype(F32)
        r.own_cot[q, :] = r.cot[q, :].astype(F32)
    ps = peers(p)
    zu, zd = {"batch": lax.rem(z + 1, Z)}, {"batch": lax.rem(z + Z - 1, Z)}
    zp = [lax.rem(z + k, Z) for k in range(1, Z)]
    greet([{"seq": p["base"] + j} for j in ps] + [{"batch": q} for q in zp])
    nxt, prv = {"seq": lax.rem(s + 1, NSEQ)}, {"seq": lax.rem(s + NSEQ - 1, NSEQ)}
    halo_copy = remote(r.xs, r.halo, r.hsem.at[0], r.hsem.at[1], nxt)
    pl.when(s < NSEQ - 1)(lambda: halo_copy.start())
    gc = Gather(p, r.own_cot, r.land_cot, r.gss.at[0], r.gsr.at[0])
    gs = Gather(p, r.own_sec, r.land_sec, r.gss.at[1], r.gsr.at[1])
    ga = Gather(p, r.own_act, r.land_act, r.gss.at[2], r.gsr.at[2])
    gc.start()

    mode_args = (r.rate, r.freq, r.cre, r.cim, r.prior)
    fwd_tiles(nbits, 0, D // LT, *mode_args, r.kern, r.resp, r.qr, r.qi, r.tab, r.big)
    gc.relay1()
    gc.relay2()

    @tiles(T, ROWS)
    def _(q):
        hat, inv = norm_hat(r.xs[q, :])
        r.xhat[q, :] = hat
        r.xinv[q, :] = jnp.broadcast_to(inv, (ROWS, 128))
        r.ext[sub(T, q), :] = hat * vec["first_gain"]() + vec["first_shift"]()
    @pl.when(s > 0)
    def _():
        halo_copy.wait_recv()
    @pl.when(s == 0)
    def _():
        r.halo[...] = jnp.zeros_like(r.halo)
    keep = jnp.where(s == 0, 0.0, 1.0)
    @tiles(T, ROWS)
    def _(q):
        hat, _ = norm_hat(r.halo[q, :])
        r.ext[q, :] = (hat * vec["first_gain"]() + vec["first_shift"]()) * keep

    inner = lax.broadcasted_iota(jnp.int32, (KLEN, LC), 0) > 0
    @tiles(D, LC)
    def _(c):
        X = table_dot(r.ftab, r.ext[:, c])
        K = table_dot(r.ftab, r.kern[:, c], cols=slice(0, KLEN))
        r.X[:, c] = X
        r.K[:, c] = K
        P_, Q_, KP, KQ = X[:KLEN], X[KLEN:], K[:KLEN], K[KLEN:]
        qq = Q_ * KQ
        po = P_ * KP - jnp.where(inner, qq, 0.0)
        qo = jnp.where(inner, P_ * KQ + Q_ * KP, qq)
        y = table_dot(r.itab, jnp.concatenate([po, qo], 0))
        r.pre[:, c] = y + vec["skip_gain"](c) * r.ext[T:, c] + r.resp[:, c]
    @tiles(T, 16)
    def _(q):
        a = gelu_both(r.pre[q, :])[0].astype(BF16)
        r.own_act[q, :] = a.astype(F32)
        r.act_all[sub(i * T, q), :] = a
    gc.relay3()

    gw_copy.wait()
    act = r.act_all[iblk, :]
    @tiles(D, LC)
    def _(c):
        r.val[:, c] = dot(act, r.gw[:, c])
        r.sg[:, c] = dot(act, r.gw[:, lane(D + c.start, LC)])
    @tiles(T, ROWS)
    def _(q):
        v = r.val[q, :] + vec["value_bias"]()
        g = jax.nn.sigmoid(r.sg[q, :] + vec["gate_bias"]())
        r.val[q, :] = v
        r.sg[q, :] = g
        m = r.xs[q, :] + v * g
        r.merged[q, :] = m
        hat, inv = norm_hat(m)
        r.mhat[q, :] = hat
        r.minv[q, :] = jnp.broadcast_to(inv, (ROWS, 128))
        r.own_sec[q, :] = (hat * vec["second_gain"]() + vec["second_shift"]()).astype(BF16).astype(F32)
    @tiles(T, 16)
    def _(q):
        r.sec_all[sub(i * T, q), :] = r.own_sec[q, :].astype(BF16)
    gs.start()

    r.oacc[...] = jnp.zeros_like(r.oacc)
    r.sacc[...] = jnp.zeros_like(r.sacc)
    sec = r.sec_all[iblk, :]
    @pl.loop(0, 8)
    def _(t):
        slot = lax.rem(t, 2)
        for c in tile_copy(t, slot): c.wait()
        r.u[pl.ds(0, T)] = dot(sec, r.wu[slot])
        r.gh[pl.ds(0, T)] = dot(r.cot[...], r.wd[slot], 1, 1)
        @tiles(T, 16)
        def _(q):
            hid, slope = gelu_both(r.u[q, :] + r.upb[pl.ds(t, 1), :])
            r.hid[q, :] = hid.astype(BF16)
            r.gul[q, :] = (r.gh[q, :] * slope).astype(BF16)
        r.oacc[...] += dot(r.hid[pl.ds(0, T), :], r.wd[slot])
        r.sacc[...] += dot(r.gul[pl.ds(0, T), :], r.wu[slot], 1, 1)
        @pl.when(t < 6)
        def _():
            for c in tile_copy(t + 2, slot): c.start()
    for c in tile_copy(i, 0): c.start()

    zero = jnp.zeros((ROWS, D), F32)
    def rows_a(q, carry):
        r.oacc[q, :] = r.merged[q, :] + r.oacc[q, :] + vec["down_bias"]()
        g, hat, c = r.sacc[q, :], r.mhat[q, :], r.own_cot[q, :]
        gm = c + norm_back(g * vec["second_gain"](), hat, r.minv[q, 0:1])
        r.gm[q, :] = gm
        return carry[0] + g * hat, carry[1] + g, carry[2] + c
    sums = tiles(T, ROWS)(rows_a, (zero,) * 3)
    for k, v in zip((3, 4, 5), sums): r.ssrc[4 * M + k:4 * M + k + 1, :] = fold(v)
    gs.relay1()
    gs.relay2()
    ga.start()
    gm_sends = []
    for k, j in enumerate(ps):
        c = remote(r.gm.at[:, lane(j * 128, 128)], r.gm_all.at[i], r.ms.at[k], r.mr.at[k], {"seq": p["base"] + j})
        c.start()
        gm_sends.append(c)
    r.gm_all[i] = r.gm[:, lane(i * 128, 128)]
    @tiles(T, 16)
    def _(q):
        r.out[q, :] = r.oacc[q, :].astype(BF16)
    def rows_b(q, carry):
        gm, g = r.gm[q, :], r.sg[q, :]
        gv, gg = gm * g, gm * r.val[q, :] * g * (1.0 - g)
        r.glow[q, pl.ds(0, D)] = gv.astype(BF16)
        r.glow[q, pl.ds(D, D)] = gg.astype(BF16)
        return carry[0] + jnp.sum(gv.reshape(2, ROWS, D), 0), carry[1] + jnp.sum(gg.reshape(2, ROWS, D), 0)
    gb = tiles(T, 16)(rows_b, (zero,) * 2)
    gb = [fold(v) for v in gb]
    for j in range(8):
        for q in range(2):
            off = (j % 4) * 256 + q * 128
            r.ssrc[4 * M + 6 + q:4 * M + 7 + q, j * 128:(j + 1) * 128] = gb[j // 4][:, off:off + 128]
    glow = r.glow[...]
    @tiles(D, LC)
    def _(c):
        r.gz[:, c] = dot(glow, r.gw[c, :], 1, 1)
    @tiles(T, ROWS)
    def _(q):
        r.gz[q, :] = r.gz[q, :] * gelu_both(r.pre[q, :])[1]

    def settle(g, whole):
        g.finish()
        for j in g.others():
            @tiles(T, 16)
            def _(q):
                whole[sub(j * T, q), :] = g.land[j, q, :].astype(BF16)
    @tiles(T, 16)
    def _(q):
        r.cot_all[sub(i * T, q), :] = r.cot[q, :]
    settle(gc, r.cot_all)
    gc.drain()
    pl.when(z < Z - 1)(lambda: pl.semaphore_signal(r.free.at[0], inc=1, device_id=zu, device_id_type=MESH))
    pl.when(z > 0)(lambda: pl.semaphore_signal(r.free.at[1], inc=1, device_id=zd, device_id_type=MESH))
    gs.relay3()
    settle(gs, r.sec_all)

    for c in tile_copy(i, 0): c.wait()
    def slice_rows(q, carry):
        r.u[...] = dot(r.sec_all[q, :], r.wu[0])
        r.gh[...] = dot(r.cot_all[q, :], r.wd[0], 1, 1)
        def inner_rows(k, acc):
            hid, slope = gelu_both(r.u[k, :] + r.upb[pl.ds(i, 1), :])
            gu = r.gh[k, :] * slope
            rows = pl.ds(pl.multiple_of(q.start + k.start, 16), 16)
            r.hid[rows, :] = hid.astype(BF16)
            r.gul[rows, :] = gu.astype(BF16)
            return acc + jnp.sum(gu.reshape(2, 8, FT), 0)
        return tiles(256, 16)(inner_rows, carry)
    ub = fold(tiles(8 * T, 256)(slice_rows, jnp.zeros((8, FT), F32)))

    own = (r.upg, r.glg, r.dng)
    LU = (lambda t: r.lup.at[0, t - 1], lambda t: r.lgl.at[0, t - 1], lambda t: r.land_cot.at[t - 1])
    LD = (lambda t: r.lup.at[1, t], lambda t: r.lgl.at[1, t], lambda t: r.land_cot.at[Z - 1 + t])
    def cu(n, t, src=None):
        return remote(LU[n](t) if src is None else src, LU[n](t), r.zs.at[n, 0, t - 1], r.zr.at[n, 0, t - 1], zu)
    def cd(n, t, src=None):
        return remote(LD[n](t) if src is None else src, LD[n](t), r.zs.at[n, 1, t], r.zr.at[n, 1, t], zd)
    def z_start(n):
        @pl.when(z == 0)
        def _():
            for t in range(Z - 1, 0, -1): cu(n, t, own[n].at[t]).start()
        @pl.when(z == Z - 1)
        def _():
            for t in range(Z - 1): cd(n, t, own[n].at[t]).start()
    def add_into(dst, srcs):
        @tiles(dst.shape[0], 16)
        def _(q):
            v = srcs[0][q, :]
            for e in srcs[1:]: v = v + e[q, :]
            dst[q, :] = v
    def z_slot(n, slot):
        for zz in range(1, Z - 1):
            @pl.when(z == zz)
            def _():
                for t in range(Z - 1, zz, -1):
                    if (Z - 1 - t) + zz == slot:
                        c = cu(n, t)
                        c.wait_recv()
                        add_into(LU[n](t), (LU[n](t), own[n].at[t]))
                        c.start()
                for t in range(zz):
                    if t + (Z - 1 - zz) == slot:
                        c = cd(n, t)
                        c.wait_recv()
                        add_into(LD[n](t), (LD[n](t), own[n].at[t]))
                        c.start()
    def z_final(n, dst):
        for zz in range(Z):
            @pl.when(z == zz)
            def _():
                srcs = [own[n].at[zz]]
                if zz > 0:
                    cu(n, zz).wait_recv()
                    srcs.append(LU[n](zz))
                if zz < Z - 1:
                    cd(n, zz).wait_recv()
                    srcs.append(LD[n](zz))
                add_into(dst, srcs)
    def z_drain(n):
        for zz in range(Z):
            @pl.when(z == zz)
            def _():
                for t in range(zz + 1, Z): cu(n, t).wait_send()
                for t in range(zz): cd(n, t).wait_send()

    @tiles(D, 256)
    def _(c):
        g = dot(r.sec_all[:, c], r.gul[...], 0, 0)
        for q in range(256 // HB):
            j = c.start // 128 + q // Z
            r.upg[q % Z, pl.ds(pl.multiple_of(j * HB, HB), HB), :] = g[q * HB:(q + 1) * HB]
    z_start(0)
    for fc in range(FT // 256):
        for nh in range(D // 512):
            g = dot(r.hid[:, fc * 256:(fc + 1) * 256], r.cot_all[:, nh * 512:(nh + 1) * 512], 0, 0)
            n = 256 * Z // FT
            for q in range(n):
                r.dng[fc * n + q, :, nh * 512:(nh + 1) * 512] = g[q * (FT // Z):(q + 1) * (FT // Z)]

    ga.relay1()
    ga.relay2()
    @tiles(D, LC)
    def _(c):
        G = table_dot(r.jtab, r.gz[:, c])
        gp, gq = G[:KLEN], G[KLEN:]
        def pair(ref):
            a, b = ref[pl.ds(0, KLEN), c], ref[pl.ds(KLEN, KLEN), c]
            bq = gq * b
            return jnp.concatenate([gp * a + jnp.where(inner, bq, 0.0), jnp.where(inner, gq * a - gp * b, bq)], 0)
        r.kern[:, c] = table_dot(r.gtab, pair(r.X), rows=slice(0, KLEN))
        r.ext[:, c] = table_dot(r.gtab, pair(r.K))
    tail_copy = remote(r.ext.at[pl.ds(0, T)], r.tail, r.hsem.at[2], r.hsem.at[3], prv)
    pl.when(s > 0)(lambda: tail_copy.start())

    ga.relay3()
    settle(ga, r.act_all)
    for k in range(7):
        src = lax.rem(i + 7 - k, 8)
        remote(r.gm_all.at[src], r.gm_all.at[src], r.ms.at[k], r.mr.at[k], nxt).wait_recv()
    for c in wgs_copy: c.wait()
    gbias = jnp.concatenate([r.vecs[6:7, lane(i * 128, 128)], r.vecs[7:8, lane(i * 128, 128)]], 1)
    @tiles(8 * T, 256)
    def _(q):
        r.u[:, pl.ds(0, 256)] = dot(r.act_all[q, :], r.wgs[...]) + gbias
        for h in range(256 // T):
            blk = q.start // T + h
            @tiles(T, 16)
            def _(k):
                row = pl.ds(pl.multiple_of(h * T + k.start, 16), 16)
                v, g = r.u[row, pl.ds(0, 128)], jax.nn.sigmoid(r.u[row, pl.ds(128, 128)])
                gm = r.gm_all[blk, k, :]
                rows = pl.ds(pl.multiple_of(q.start + h * T + k.start, 16), 16)
                r.ggl[rows, :] = jnp.concatenate([gm * g, gm * v * g * (1.0 - g)], 1).astype(BF16)
    @tiles(D, 256)
    def _(c):
        g = dot(r.act_all[:, c], r.ggl[...], 0, 0)
        for q in range(256 // HB):
            j = c.start // 128 + q // Z
            r.glg[q % Z, pl.ds(pl.multiple_of(j * HB, HB), HB), :] = g[q * HB:(q + 1) * HB]
    z_start(1)
    pl.when(z > 0)(lambda: pl.semaphore_wait(r.free.at[0], 1))
    pl.when(z < Z - 1)(lambda: pl.semaphore_wait(r.free.at[1], 1))
    z_start(2)

    z_slot(0, 1)
    bwd_args = (nbits, T, *mode_args, r.kern, r.gz, r.ssrc, r.qr, r.qi, r.big)
    bwd_tiles(0, 4, 4 * M + 8, *bwd_args)
    z_slot(0, 2)
    bwd_tiles(4, D // LT, 4 * M + 8, *bwd_args)
    pl.when(s < NSEQ - 1)(lambda: tail_copy.wait_recv())
    @pl.when(s == NSEQ - 1)
    def _():
        r.tail[...] = jnp.zeros_like(r.tail)
    def rows_c(q, carry):
        hat, gz = r.xhat[q, :], r.gz[q, :]
        gn = r.ext[sub(T, q), :] + r.tail[q, :] + vec["skip_gain"]() * gz
        r.oacc[q, :] = r.gm[q, :] + norm_back(gn * vec["first_gain"](), hat, r.xinv[q, 0:1])
        return carry[0] + gn * hat, carry[1] + gn, carry[2] + gz * hat, carry[3] + gz
    sums = [fold(v) for v in tiles(T, ROWS)(rows_c, (zero,) * 4)]
    sums = (sums[0], sums[1], sums[2] * vec["first_gain"]() + sums[3] * vec["first_shift"]())
    for k, v in enumerate(sums): r.ssrc[4 * M + k:4 * M + k + 1, :] = v
    @tiles(T, 16)
    def _(q):
        r.ig[q, :] = r.oacc[q, :].astype(BF16)

    NR, NS = 4 * M + 8 + 2 * M, 2 * M
    sends = []
    def push(src, dst, a, b, dev):
        c = remote(src, dst, a, b, dev)
        c.start()
        sends.append(c)
    for k, j in enumerate(ps):
        push(r.ssrc.at[:, lane(j * 128, 128)], r.sland.at[i], r.sa.at[0, k], r.sa.at[1, k], {"seq": p["base"] + j})
    z_final(0, r.upf)
    for k, j in enumerate(ps):
        push(r.upf.at[pl.ds(pl.multiple_of(j * HB, HB), HB)], r.up_out.at[:, lane(i * FT, FT)], r.ua.at[0, k], r.ua.at[1, k],
             {"seq": p["base"] + j})
    r.up_out[:, lane(i * FT, FT)] = r.upf[pl.ds(pl.multiple_of(i * HB, HB), HB), :]
    z_slot(1, 1)
    tot = r.ssrc[:, lane(i * 128, 128)]
    for k in range(7):
        src = lax.rem(i + 7 - k, 8)
        remote(r.sland.at[src], r.sland.at[src], r.sa.at[0, k], r.sa.at[1, k], nxt).wait_recv()
        tot = tot + r.sland[src]
    r.mine[0:NR, :] = tot
    for q in range(FT // 128): r.mine[NR + q:NR + q + 1, :] = ub[:, q * 128:(q + 1) * 128]
    r.mine[NR + FT // 128:, :] = jnp.zeros((r.mine.shape[0] - NR - FT // 128, 128), F32)
    r.st[i] = tot[NR - NS:NR]
    for k, j in enumerate(ps):
        push(r.mine.at[pl.ds(NR - NS, NS)], r.st.at[i], r.sb.at[0, k], r.sb.at[1, k], {"seq": p["base"] + j})
    for k, q in enumerate(zp):
        push(r.mine, r.zland.at[z], r.sz.at[0, k], r.sz.at[1, k], {"batch": q})
    z_slot(1, 2)
    z_final(1, r.glf)
    for k, j in enumerate(ps):
        for q in range(2):
            push(r.glf.at[pl.ds(pl.multiple_of(j * HB, HB), HB), pl.ds(q * 128, 128)], r.glu_out.at[:, lane(q * D + i * 128, 128)],
                 r.ga.at[0, q, k], r.ga.at[1, q, k], {"seq": p["base"] + j})
    for q in range(2):
        r.glu_out[:, lane(q * D + i * 128, 128)] = r.glf[pl.ds(pl.multiple_of(i * HB, HB), HB), pl.ds(q * 128, 128)]
    z_slot(2, 1)
    acc = r.mine[...]
    for k in range(Z - 1):
        src = lax.rem(z + Z - 1 - k, Z)
        remote(r.mine, r.zland.at[src], r.sz.at[0, k], r.sz.at[1, k], zu).wait_recv()
        acc = acc + r.zland[src]
    r.tot[...] = acc
    z_slot(2, 2)
    for k in range(7):
        src = lax.rem(i + 7 - k, 8)
        blk = r.up_out.at[:, lane(src * FT, FT)]
        remote(blk, blk, r.ua.at[0, k], r.ua.at[1, k], nxt).wait_recv()
        remote(r.st.at[src], r.st.at[src], r.sb.at[0, k], r.sb.at[1, k], nxt).wait_recv()
        for q in range(2):
            blk = r.glu_out.at[:, lane(q * D + src * 128, 128)]
            remote(blk, blk, r.ga.at[0, q, k], r.ga.at[1, q, k], nxt).wait_recv()
    z_final(2, r.down_o)

    pl.when(s < NSEQ - 1)(lambda: halo_copy.wait_send())
    pl.when(s > 0)(lambda: tail_copy.wait_send())
    for c in gm_sends + sends: c.wait_send()
    gs.drain()
    ga.drain()
    for n in range(3): z_drain(n)


def layer(cfg, tabs, vecs, upb, rate, freq, cre, cim, prior, x, cot, glu_w, up_w, down_w, cid):
    Z, NSEQ, nbits, T, D, FF, M = cfg
    FT, HB = FF // 8, D // 8 // Z
    NR = 4 * M + 8 + 2 * M
    NT = -(-(NR + FT // 128) // 8) * 8
    vm, hbm = pl.BlockSpec(memory_space=pltpu.VMEM), pl.BlockSpec(memory_space=pl.ANY)
    S = lambda shape, dt=F32: jax.ShapeDtypeStruct(shape, dt)
    ins = dict(ftab=vm, itab=vm, jtab=vm, gtab=vm, vecs=vm, upb=vm, rate=vm, freq=vm, cre=vm, cim=vm, prior=vm, x=vm, cot=vm,
               glu_w=hbm, up_w=hbm, down_w=hbm)
    outs = dict(out=S((T, D), BF16), ig=S((T, D), BF16), st=S((8, 2 * M, 128)), tot=S((NT, 128)), down_o=S((FT // Z, D)),
                up_out=S((HB, FF)), glu_out=S((HB, 2 * D)))
    V, DS = pltpu.VMEM, lambda *n: pltpu.SemaphoreType.DMA(n)
    row = lambda: V((T, D), F32)
    scr = dict(
        xs=row(), own_cot=row(), own_sec=row(), own_act=row(), halo=row(), tail=row(), xhat=row(), pre=row(), val=row(), sg=row(),
        merged=row(), mhat=row(), gm=row(), gz=row(), oacc=row(), sacc=row(), resp=row(), kern=row(),
        xinv=V((T, 128), F32), minv=V((T, 128), F32), ext=V((2 * T, D), F32), X=V((2 * KLEN, D), F32), K=V((2 * KLEN, D), F32),
        land_cot=V((8, T, D), F32), land_sec=V((8, T, D), F32), land_act=V((8, T, D), F32),
        cot_all=V((8 * T, D), BF16), sec_all=V((8 * T, D), BF16), act_all=V((8 * T, D), BF16),
        gw=V((D, 2 * D), BF16), wu=V((2, D, FT), BF16), wd=V((2, FT, D), BF16), wgs=V((D, 256), BF16),
        u=V((256, FT), F32), gh=V((256, FT), F32), hid=V((8 * T, FT), BF16), gul=V((8 * T, FT), BF16),
        glow=V((T, 2 * D), BF16), gm_all=V((8, T, 128), F32), ggl=V((8 * T, 256), BF16),
        upg=V((Z, D // Z, FT), F32), glg=V((Z, D // Z, 256), F32), dng=V((Z, FT // Z, D), F32),
        lup=V((2, Z - 1, D // Z, FT), F32), lgl=V((2, Z - 1, D // Z, 256), F32), upf=V((D // Z, FT), F32), glf=V((D // Z, 256), F32),
        qr=V((16, M, LT), F32), qi=V((16, M, LT), F32), tab=V((6, M, LT), F32), big=V((64 * M, LT), F32),
        ssrc=V((NR, D), F32), sland=V((8, NR, 128), F32), mine=V((NT, 128), F32), zland=V((Z, NT, 128), F32),
        lsem=DS(3), tsem=DS(2, 2), hsem=DS(4), gss=DS(3, 14), gsr=DS(3, 14), ms=DS(7), mr=DS(7), zs=DS(3, 2, Z - 1), zr=DS(3, 2, Z - 1),
        sa=DS(2, 7), ua=DS(2, 7), sb=DS(2, 7), ga=DS(2, 2, 7), sz=DS(2, Z - 1), free=pltpu.SemaphoreType.REGULAR((2,)))
    names = (*ins, *outs, *scr)
    res = pl.pallas_call(
        functools.partial(layer_kernel, cfg, names),
        out_shape=list(outs.values()), in_specs=list(ins.values()), out_specs=[vm] * len(outs), scratch_shapes=list(scr.values()),
        compiler_params=pltpu.CompilerParams(collective_id=cid, has_side_effects=True, vmem_limit_bytes=67043328),
        name="layer")(*tabs, vecs, upb, rate, freq, cre, cim, prior, x, cot, glu_w, up_w, down_w)
    return dict(zip(outs, res))


def tables(window):
    half = window // 2
    f = np.concatenate([np.arange(half + 1), np.arange(1, half)])[:, None]
    imag = np.arange(window)[:, None] > half
    ph = (f * np.arange(window)[None, :] % window) * (2.0 * np.pi / window)
    fwd = np.where(imag, -np.sin(ph), np.cos(ph))
    wt = np.where((f == 0) | (2 * f == window), 1.0, 2.0) / window
    inv = (wt * fwd).T[half:]
    def parts(a):
        a = np.ascontiguousarray(a).astype(np.float32)
        high = a.astype(ml_dtypes.bfloat16)
        return jnp.asarray(np.stack([high, (a - high.astype(np.float32)).astype(ml_dtypes.bfloat16)]))
    return parts(fwd), parts(inv), parts(inv.T), parts(fwd.T)


def plane_shards(Z, n_seq, inputs, first_gain, first_shift, decay_rate, rotation, out_real, out_imag, skip_gain, glu_weight,
                 glu_bias, second_gain, second_shift, up_weight, up_bias, down_weight, down_bias, prior_state, cotangent):
    T, D = inputs.shape[1:]
    FF, M = up_weight.shape[1], decay_rate.shape[1]
    FT, HB = FF // 8, D // 8 // Z
    cfg = (Z, n_seq, max(1, (n_seq - 1).bit_length()), T, D, FF, M)
    vecs = jnp.stack([first_gain, first_shift, skip_gain, second_gain, second_shift, down_bias, glu_bias[:D], glu_bias[D:]])
    o = layer(cfg, tables(T + KLEN), vecs, up_bias.reshape(8, FT), decay_rate.T, rotation.T, out_real.T, out_imag.T, prior_state,
              inputs[0], cotangent[0], glu_weight, up_weight, down_weight, 0)
    NR = 4 * M + 8
    b = lax.axis_index("batch")
    tot = o["tot"]
    mine = lax.dynamic_slice_in_dim(tot[:NR], b * HB, HB, 1)
    mg = [mine[k * M:(k + 1) * M].T for k in range(4)]
    vg = [mine[4 * M + k] for k in range(6)]
    ub = lax.dynamic_slice_in_dim(tot[NR + 2 * M:NR + 2 * M + FT // 128].reshape(FT), b * (FT // Z), FT // Z, 0)
    gb = lax.dynamic_slice_in_dim(tot[4 * M + 6:NR].reshape(2 * D // 8), b * (2 * HB), 2 * HB, 0)
    state = o["st"].transpose(1, 0, 2).reshape(1, 2, M, D)
    return (o["out"][None], o["ig"][None], state, vg[0], vg[1], mg[0], mg[1], mg[2], mg[3], vg[2], o["glu_out"], gb,
            vg[3], vg[4], o["up_out"], ub, o["down_o"], vg[5])


def solution(mesh):
    in_specs = (
        P("batch", "seq", None),
        P(),
        P(),
        P(),
        P(),
        P(),
        P(),
        P(),
        P(),
        P(),
        P(),
        P(),
        P(),
        P(),
        P(),
        P(),
        P("batch", None, None, None),
        P("batch", "seq", None),
    )
    out_specs = (
        P("batch", "seq", None),
        P("batch", "seq", None),
        P("batch", None, None, None),
        P(("seq", "batch")),
        P(("seq", "batch")),
        P(("seq", "batch"), None),
        P(("seq", "batch"), None),
        P(("seq", "batch"), None),
        P(("seq", "batch"), None),
        P(("seq", "batch")),
        P(("seq", "batch"), None),
        P(("seq", "batch")),
        P(("seq", "batch")),
        P(("seq", "batch")),
        P(("seq", "batch"), None),
        P(("seq", "batch")),
        P(("seq", "batch"), None),
        P(("seq", "batch")),
    )
    body = shards
    if mesh.shape["seq"] == 8:
        body = functools.partial(plane_shards, mesh.shape["batch"], mesh.shape["seq"])
    return jax.shard_map(body, mesh=mesh, in_specs=in_specs, out_specs=out_specs, check_vma=False)
```

```python
import functools
import math

import jax
import jax.numpy as jnp
import ml_dtypes
import numpy as np
from jax import lax
from jax.experimental import pallas as pl
from jax.experimental.pallas import tpu as pltpu
from jax.sharding import PartitionSpec as P

KLEN = 128
LT = 128
MESH = pl.DeviceIdType.MESH
F32, BF16 = jnp.float32, jnp.bfloat16


EPSILON = 1e-05
HIGHEST = lax.Precision.HIGHEST


def from_behind(value, axis, by):
    peers = lax.axis_size(axis)
    pairs = [(i, i + by) for i in range(peers) if 0 <= i + by < peers]
    return lax.ppermute(value, axis, pairs)


def norm_rows(values, gain, shift):
    center = values - jnp.mean(values, axis=-1, keepdims=True)
    spread = jnp.mean(center * center, axis=-1, keepdims=True)
    return center * lax.rsqrt(spread + EPSILON) * gain + shift


def mode_terms(rate_modes, freq_modes, elapsed):
    moment = elapsed[None, :, None]
    damping = jnp.exp(-rate_modes[:, None, :] * moment)
    return (
        damping * jnp.cos(freq_modes[:, None, :] * moment),
        damping * jnp.sin(freq_modes[:, None, :] * moment),
    )


def glu_gate(glu_pre):
    split_at = glu_pre.shape[-1] // 2
    return glu_pre[:, :split_at] * jax.nn.sigmoid(glu_pre[:, split_at:])


def gelu_exact(values):
    return jax.nn.gelu(values, approximate=False)


def shards(
    inputs,
    first_gain,
    first_shift,
    decay_rate,
    rotation,
    out_real,
    out_imag,
    skip_gain,
    glu_weight,
    glu_bias,
    second_gain,
    second_shift,
    up_weight,
    up_bias,
    down_weight,
    down_bias,
    prior_state,
    cotangent,
):
    seg_count, tok_count, feature = inputs.shape
    row_count = seg_count * tok_count
    window = tok_count + KLEN
    half = window // 2 + 1
    offset = lax.axis_index("seq") * tok_count
    freq_index = jnp.arange(half, dtype=jnp.int32)
    time_index = jnp.arange(window, dtype=jnp.int32)
    phase = (freq_index[:, None] * time_index[None, :] % window).astype(jnp.float32) * (
        2.0 * math.pi / window
    )
    cos_half = jnp.cos(phase)
    sin_half = jnp.sin(phase)
    forward_table = jnp.concatenate([cos_half, -sin_half], axis=0)
    weights = jnp.where((freq_index == 0) | (2 * freq_index == window), 1.0, 2.0).astype(
        jnp.float32
    )
    inverse_table = (
        jnp.concatenate(
            [(weights[:, None] * cos_half).T, -(weights[:, None] * sin_half).T], axis=1
        )[KLEN:]
        / window
    )
    local_steps = jnp.arange(tok_count).astype(jnp.float32)
    advance_steps = (offset + 1).astype(jnp.float32)

    def mixing(
        normed, halo_rows, rate_modes, freq_modes, real_modes, imag_modes, skip_local, prior_local
    ):
        table_real, table_imag = mode_terms(rate_modes, freq_modes, local_steps)
        kernel = jnp.einsum("mkh,mh->kh", table_real, real_modes, precision=HIGHEST) - jnp.einsum(
            "mkh,mh->kh", table_imag, imag_modes, precision=HIGHEST
        )
        extended = jnp.concatenate([halo_rows, normed], axis=1)
        spectrum = jnp.einsum("ft,sth->sfh", forward_table, extended, precision=HIGHEST)
        kern_spec = jnp.dot(forward_table[:, :KLEN], kernel, precision=HIGHEST)
        spec_real, spec_imag = (spectrum[:, :half], spectrum[:, half:])
        kern_real, kern_imag = (kern_spec[:half], kern_spec[half:])
        product = jnp.concatenate(
            [
                spec_real * kern_real - spec_imag * kern_imag,
                spec_real * kern_imag + spec_imag * kern_real,
            ],
            axis=1,
        )
        convolved = jnp.einsum("tf,sfh->sth", inverse_table, product, precision=HIGHEST)
        damping = jnp.exp(-rate_modes * advance_steps)
        adv_real = damping * jnp.cos(freq_modes * advance_steps)
        adv_imag = damping * jnp.sin(freq_modes * advance_steps)
        coef_real = real_modes * adv_real - imag_modes * adv_imag
        coef_imag = real_modes * adv_imag + imag_modes * adv_real
        drive_real = coef_real * prior_local[:, 0] - coef_imag * prior_local[:, 1]
        drive_imag = coef_real * prior_local[:, 1] + coef_imag * prior_local[:, 0]
        response = jnp.einsum(
            "mth,smh->sth", table_real, drive_real, precision=HIGHEST
        ) - jnp.einsum("mth,smh->sth", table_imag, drive_imag, precision=HIGHEST)
        return gelu_exact(convolved + skip_local * normed + response)

    source = inputs.astype(jnp.float32)
    normed, first_pull = jax.vjp(norm_rows, source, first_gain, first_shift)
    halo_rows = from_behind(normed, "seq", 1)
    activated, mix_pull = jax.vjp(
        mixing,
        normed,
        halo_rows,
        decay_rate.T,
        rotation.T,
        out_real.T,
        out_imag.T,
        skip_gain,
        prior_state,
    )
    activated_low = activated.reshape(row_count, feature).astype(jnp.bfloat16)
    glu_pre = jnp.dot(activated_low, glu_weight, preferred_element_type=jnp.float32) + glu_bias
    branch, glu_pull = jax.vjp(glu_gate, glu_pre)
    merged = source.reshape(row_count, feature) + branch
    second, second_pull = jax.vjp(norm_rows, merged, second_gain, second_shift)
    second_low = second.astype(jnp.bfloat16)
    up_pre = jnp.dot(second_low, up_weight, preferred_element_type=jnp.float32) + up_bias
    hidden, hidden_pull = jax.vjp(gelu_exact, up_pre)
    hidden_low = hidden.astype(jnp.bfloat16)
    result = (
        merged + jnp.dot(hidden_low, down_weight, preferred_element_type=jnp.float32) + down_bias
    )
    outputs = result.astype(jnp.bfloat16).reshape(seg_count, tok_count, feature)
    grad_out = cotangent.astype(jnp.float32).reshape(row_count, feature)
    down_bias_grad = jnp.sum(grad_out, axis=0)
    grad_low = grad_out.astype(jnp.bfloat16)
    down_grad = jnp.einsum("rf,rh->fh", hidden_low, grad_low, preferred_element_type=jnp.float32)
    grad_hidden = jnp.einsum("rh,fh->rf", grad_low, down_weight, preferred_element_type=jnp.float32)
    (grad_up,) = hidden_pull(grad_hidden)
    up_bias_grad = jnp.sum(grad_up, axis=0)
    up_low = grad_up.astype(jnp.bfloat16)
    up_grad = jnp.einsum("rh,rf->hf", second_low, up_low, preferred_element_type=jnp.float32)
    grad_second = jnp.einsum("rf,hf->rh", up_low, up_weight, preferred_element_type=jnp.float32)
    grad_merged, second_gain_grad, second_shift_grad = second_pull(grad_second)
    grad_merged = grad_merged + grad_out
    (grad_glu,) = glu_pull(grad_merged)
    glu_bias_grad = jnp.sum(grad_glu, axis=0)
    glu_low = grad_glu.astype(jnp.bfloat16)
    glu_grad = jnp.einsum("rh,rg->hg", activated_low, glu_low, preferred_element_type=jnp.float32)
    grad_activated = jnp.einsum(
        "rg,hg->rh", glu_low, glu_weight, preferred_element_type=jnp.float32
    )
    grad_normed, grad_halo, rate_grad, freq_grad, real_grad, imag_grad, skip_grad, prior_grad = (
        mix_pull(grad_activated.reshape(seg_count, tok_count, feature))
    )
    grad_tail = from_behind(grad_halo, "seq", -1)
    grad_normed = jnp.concatenate(
        [grad_normed[:, : tok_count - KLEN], grad_normed + grad_tail], axis=1
    )
    grad_source, first_gain_grad, first_shift_grad = first_pull(grad_normed)
    input_grad = (grad_source + grad_merged.reshape(seg_count, tok_count, feature)).astype(
        jnp.bfloat16
    )
    state_grad = lax.psum(prior_grad, "seq")
    rate_back = rate_grad.T
    freq_back = freq_grad.T
    real_back = real_grad.T
    imag_back = imag_grad.T
    summed = (
        lax.psum_scatter(first_gain_grad, ("seq", "batch"), scatter_dimension=0, tiled=True),
        lax.psum_scatter(first_shift_grad, ("seq", "batch"), scatter_dimension=0, tiled=True),
        lax.psum_scatter(rate_back, ("seq", "batch"), scatter_dimension=0, tiled=True),
        lax.psum_scatter(freq_back, ("seq", "batch"), scatter_dimension=0, tiled=True),
        lax.psum_scatter(real_back, ("seq", "batch"), scatter_dimension=0, tiled=True),
        lax.psum_scatter(imag_back, ("seq", "batch"), scatter_dimension=0, tiled=True),
        lax.psum_scatter(skip_grad, ("seq", "batch"), scatter_dimension=0, tiled=True),
        lax.psum_scatter(glu_grad, ("seq", "batch"), scatter_dimension=0, tiled=True),
        lax.psum_scatter(glu_bias_grad, ("seq", "batch"), scatter_dimension=0, tiled=True),
        lax.psum_scatter(second_gain_grad, ("seq", "batch"), scatter_dimension=0, tiled=True),
        lax.psum_scatter(second_shift_grad, ("seq", "batch"), scatter_dimension=0, tiled=True),
        lax.psum_scatter(up_grad, ("seq", "batch"), scatter_dimension=0, tiled=True),
        lax.psum_scatter(up_bias_grad, ("seq", "batch"), scatter_dimension=0, tiled=True),
        lax.psum_scatter(down_grad, ("seq", "batch"), scatter_dimension=0, tiled=True),
        lax.psum_scatter(down_bias_grad, ("seq", "batch"), scatter_dimension=0, tiled=True),
    )
    return (
        outputs,
        input_grad,
        state_grad,
        summed[0],
        summed[1],
        summed[2],
        summed[3],
        summed[4],
        summed[5],
        summed[6],
        summed[7],
        summed[8],
        summed[9],
        summed[10],
        summed[11],
        summed[12],
        summed[13],
        summed[14],
    )


def plane():
    s = lax.axis_index("seq")
    i = lax.rem(s, 8)
    base = s - i
    c, x, y = lax.rem(i, 2), lax.rem(i // 2, 2), i // 4
    ic, ix, iy = i + 1 - 2 * c, i + 2 - 4 * x, i + 4 - 8 * y
    idg = iy + 2 - 4 * x
    return dict(s=s, i=i, base=base, c=c, x=x, y=y, ic=ic, ix=ix, iy=iy, idg=idg)

def sib_of(p, j):
    return j + 1 - 2 * p["c"]

def remote(src, dst, ss, rs, dev):
    return pltpu.make_async_remote_copy(src_ref=src, dst_ref=dst, send_sem=ss, recv_sem=rs,
                                        device_id=dev, device_id_type=MESH)

def greet(devs):
    bar = pltpu.get_barrier_semaphore()
    for d in devs:
        pl.semaphore_signal(bar, inc=1, device_id=d, device_id_type=MESH)
    pl.semaphore_wait(bar, len(devs))

def peers(p):
    return [lax.rem(p["i"] + k, 8) for k in range(1, 8)]

class Gather:
    def __init__(self, p, own, land, ssem, rsem):
        self.p, self.own, self.land, self.ss, self.rs = p, own, land, ssem, rsem
        self.H = own.shape[0] // 2
        seq = lambda j: {"seq": p["base"] + j}
        self.X, self.Y, self.S = seq(p["ix"]), seq(p["iy"]), seq(p["ic"])

    def cp(self, k, j, h, dev, src=None):
        blk = self.land.at[j, pl.ds(h * self.H, self.H)]
        return remote(blk if src is None else src, blk, self.ss.at[k], self.rs.at[k], dev)

    def plan(self):
        i, ix, iy, idg = self.p["i"], self.p["ix"], self.p["iy"], self.p["idg"]
        return [(0, i, 0, self.X), (2, i, 1, self.Y), (1, i, 1, self.X), (3, i, 0, self.Y), (6, i, 0, self.S), (7, i, 1, self.S),
                (4, ix, 0, self.Y), (8, ix, 0, self.S), (5, iy, 1, self.X), (11, iy, 1, self.S), (9, ix, 1, self.S),
                (10, iy, 0, self.S), (12, idg, 0, self.S), (13, idg, 1, self.S)]

    def _send(self, k, own=False):
        k, j, h, dev = next(e for e in self.plan() if e[0] == k)
        self.cp(k, j, h, dev, self.own.at[pl.ds(h * self.H, self.H)] if own else None).start()

    def _got(self, k, j, h):
        self.cp(k, j, h, self.S).wait_recv()

    def start(self):
        for k in (0, 2, 1, 3, 6, 7):
            self._send(k, True)

    def relay1(self):
        p = self.p
        self._got(0, p["ix"], 0); self._send(4); self._send(8)
        self._got(2, p["iy"], 1); self._send(5); self._send(11)

    def relay2(self):
        p = self.p
        self._got(1, p["ix"], 1); self._send(9)
        self._got(3, p["iy"], 0); self._send(10)

    def relay3(self):
        p = self.p
        self._got(4, p["idg"], 0); self._send(12)
        self._got(5, p["idg"], 1); self._send(13)

    def chip(self, which):
        p = self.p
        k, j = {"own": (6, p["ic"]), "x": (8, sib_of(p, p["ix"])), "y": (10, sib_of(p, p["iy"])), "d": (12, sib_of(p, p["idg"]))}[which]
        self._got(k, j, 0)
        self._got(k + 1, j, 1)
        return (j,) if which == "own" else ({"x": p["ix"], "y": p["iy"], "d": p["idg"]}[which], j)

    def drain(self):
        for k, j, h, dev in self.plan():
            self.cp(k, j, h, dev).wait_send()


def cmul(ar, ai, br, bi):
    return ar * br - ai * bi, ar * bi + ai * br

def lam_of(rate, freq):
    damp = jnp.exp(-rate)
    q = freq * freq
    cosv = 1.0 + q * (-1.0/2 + q * (1.0/24 + q * (-1.0/720 + q * (1.0/40320 + q * (-1.0/3628800)))))
    sinv = freq * (1.0 + q * (-1.0/6 + q * (1.0/120 + q * (-1.0/5040 + q * (1.0/362880)))))
    return damp * cosv, damp * sinv

def power_rows(lr, li, qr, qi, A):
    l2 = cmul(lr, li, lr, li); l4 = cmul(*l2, *l2); l8 = cmul(*l4, *l4)
    cur = (jnp.ones_like(lr), jnp.zeros_like(lr))
    for a in range(A):
        qr[a] = cur[0]; qi[a] = cur[1]
        cur = cmul(*cur, *l8)
    return l2, l4, cur

def offset_power(top, s, nbits):
    res = (jnp.ones_like(top[0]), jnp.zeros_like(top[0]))
    sq = top
    for bit in range(nbits):
        on = lax.rem(lax.div(s, 1 << bit), 2) == 1
        nxt = cmul(*res, *sq)
        res = (jnp.where(on, nxt[0], res[0]), jnp.where(on, nxt[1], res[1]))
        if bit + 1 < nbits: sq = cmul(*sq, *sq)
    return res

def e8_tile(tab, m, b):
    row = lambda k: jnp.broadcast_to(tab[k, pl.ds(m, 1), :], b.shape)
    one, zero = jnp.ones(b.shape, F32), jnp.zeros(b.shape, F32)
    o1, o2, o4 = (b % 2) == 1, ((b // 2) % 2) == 1, b >= 4
    r = jnp.where(o1, row(0), one), jnp.where(o1, row(1), zero)
    r = cmul(*r, jnp.where(o2, row(2), one), jnp.where(o2, row(3), zero))
    return cmul(*r, jnp.where(o4, row(4), one), jnp.where(o4, row(5), zero))

def fwd_tiles(nbits, lo, hi, rate, freq, cre, cim, prior, kern, resp, qr, qi, tab, co):
    M = rate.shape[0]
    A = kern.shape[0] // 8
    s = lax.axis_index("seq")
    b = lax.broadcasted_iota(jnp.int32, (8, LT), 0)
    @pl.loop(lo, hi)
    def _(lt):
        cols = pl.ds(pl.multiple_of(lt * LT, LT), LT)
        lr, li = lam_of(rate[:, cols], freq[:, cols])
        l2, l4, top = power_rows(lr, li, qr, qi, A)
        for k, v in enumerate((lr, li, *l2, *l4)): tab[k] = v
        off = cmul(*offset_power(top, s, nbits), lr, li)
        c = cre[:, cols], cim[:, cols]
        d = cmul(*cmul(*c, *off), prior[0, 0, :, cols], prior[0, 1, :, cols])
        for a in range(A):
            q = qr[a], qi[a]
            for k, v in enumerate((*cmul(*c, *q), *cmul(*d, *q))): co[pl.ds((k * A + a) * M, M), :] = v
        def step(m, accs):
            er, ei = e8_tile(tab, m, b)
            out = []
            for a in range(A):
                row = lambda k: co[pl.ds((k * A + a) * M + m, 1), :]
                out.append(accs[2 * a] + (er * row(0) - ei * row(1)))
                out.append(accs[2 * a + 1] + (er * row(2) - ei * row(3)))
            return tuple(out)
        accs = lax.fori_loop(0, M, step, tuple(jnp.zeros((8, LT), F32) for _ in range(2 * A)))
        for a in range(A):
            kern[pl.ds(8 * a, 8), cols] = accs[2 * a]
            resp[pl.ds(8 * a, 8), cols] = accs[2 * a + 1]


def bwd_tiles(lo, hi, srow, nbits, TOK, rate, freq, cre, cim, prior, kg, gz, out, qr, qi, acc):
    M = rate.shape[0]
    A = kg.shape[0] // 8
    s = lax.axis_index("seq")
    adv = (s * TOK + 1).astype(F32)
    @pl.loop(lo, hi)
    def _(lt):
        cols = pl.ds(pl.multiple_of(lt * LT, LT), LT)
        lr, li = lam_of(rate[:, cols], freq[:, cols])
        l2, l4, top = power_rows(lr, li, qr, qi, A)
        def step(m, carry):
            for j, g in enumerate((kg, gz)):
                z = jnp.zeros((8, LT), F32)
                sr, si, tr, ti = z, z, z, z
                for a in range(A - 1, -1, -1):
                    ga = g[pl.ds(8 * a, 8), cols]
                    sr = sr + ga * qr[a, pl.ds(m, 1), :]
                    si = si + ga * qi[a, pl.ds(m, 1), :]
                    if a > 0:
                        tr = tr + sr
                        ti = ti + si
                for q, v in enumerate((sr, si, tr, ti)):
                    acc[pl.ds(pl.multiple_of(((4 * j + q) * M + m) * 8, 8), 8), :] = v
            return carry
        lax.fori_loop(0, M, step, 0)
        pw = (jnp.ones_like(lr), jnp.zeros_like(lr))
        zero = jnp.zeros_like(lr)
        ar, ai, br, bi = [zero] * 2, [zero] * 2, [zero] * 2, [zero] * 2
        for b in range(8):
            for j in range(2):
                ld = lambda q: acc[pl.ds((4 * j + q) * M * 8 + b, M, stride=8), :]
                S = ld(0), ld(1)
                U = 8.0 * ld(2), 8.0 * ld(3)
                if b: U = U[0] + float(b) * S[0], U[1] + float(b) * S[1]
                w = cmul(*pw, *S)
                ar[j], ai[j] = ar[j] + w[0], ai[j] + w[1]
                w = cmul(*pw, *U)
                br[j], bi[j] = br[j] + w[0], bi[j] + w[1]
            pw = cmul(*pw, lr, li)
        off = cmul(*offset_power(top, s, nbits), lr, li)
        c = cre[:, cols], cim[:, cols]
        ps = cmul(*off, prior[0, 0, :, cols], prior[0, 1, :, cols])
        u = cmul(*ps, ar[1], ai[1])
        v = cmul(*ps, br[1] + adv * ar[1], bi[1] + adv * ai[1])
        v = cmul(*c, v[0] + br[0], v[1] + bi[0])
        w = cmul(*cmul(*c, *off), ar[1], ai[1])
        for k, val in enumerate((-v[0], -v[1], u[0] + ar[0], -(u[1] + ai[0]))): out[k * M:(k + 1) * M, cols] = val
        for k, val in enumerate((w[0], -w[1])): out[srow + k * M:srow + (k + 1) * M, cols] = val


class Bag:
    pass


def dot(a, b, ca=1, cb=0):
    return lax.dot_general(a, b, (((ca,), (cb,)), ((), ())), preferred_element_type=F32)


def split_low(v):
    high = v.astype(BF16)
    return high, (v - high.astype(F32)).astype(BF16)


def table_dot(tab, v, rows=slice(None), cols=slice(None)):
    high, low = split_low(v)
    th, tl = tab[0, rows, cols], tab[1, rows, cols]
    return dot(th, high) + dot(th, low) + dot(tl, high)


def gelu_both(u):
    cdf = 0.5 + 0.5 * lax.erf(u * (0.5 ** 0.5))
    return u * cdf, cdf + u * (jnp.exp(-0.5 * u * u) * ((2.0 * math.pi) ** -0.5))


def tiles(n, step):
    def run(body, init=None):
        if init is None:
            @pl.loop(0, n // step)
            def _(k):
                body(pl.ds(pl.multiple_of(k * step, step), step))
            return None
        return lax.fori_loop(0, n // step, lambda k, c: body(pl.ds(pl.multiple_of(k * step, step), step), c), init)
    return run


def sub(off, q):
    return pl.ds(pl.multiple_of(off + q.start, q.size), q.size)


def row_mean(v):
    return jnp.sum(v, axis=-1, keepdims=True) * (1.0 / v.shape[-1])


def norm_hat(v):
    center = v - row_mean(v)
    inv = lax.rsqrt(row_mean(center * center) + EPSILON)
    return center * inv, inv


def norm_back(gg, hat, inv):
    return inv * (gg - row_mean(gg) - hat * row_mean(gg * hat))


def fold(v):
    return jnp.sum(v, axis=0, keepdims=True)


LC = 256
ROWS = 8
VEC = ("first_gain", "first_shift", "skip_gain", "second_gain", "second_shift", "down_bias", "value_bias", "gate_bias")


def layer_kernel(cfg, names, *refs):
    r = Bag()
    r.__dict__.update(zip(names, refs))
    Z, NSEQ, nbits, T, D, FF, M = cfg
    FT = FF // 8
    HB = D // 8 // Z
    p = plane()
    s, i = p["s"], p["i"]
    z = lax.axis_index("batch")
    vec = {k: (lambda q: (lambda c=slice(None): r.vecs[q:q + 1, c]))(q) for q, k in enumerate(VEC)}
    iblk = pl.ds(pl.multiple_of(i * T, T), T)

    for q, ref in enumerate((r.v0, r.v1, r.v2, r.v3, r.v4, r.v5)): r.vecs[q:q + 1, :] = ref[...].reshape(1, D)
    for q in range(2): r.vecs[6 + q:7 + q, :] = r.v6[q * D:(q + 1) * D].reshape(1, D)
    for q in range(8): r.upb[q:q + 1, :] = r.v7[q * FT:(q + 1) * FT].reshape(1, FT)

    lane = lambda off, n: pl.ds(pl.multiple_of(off, 128), n)
    local = lambda src, dst, sem: pltpu.make_async_copy(src, dst, sem)
    gw_copy = local(r.glu_w, r.gw, r.lsem.at[0])
    gw_copy.start()
    def tile_copy(t, slot):
        return (local(r.up_w.at[:, lane(t * FT, FT)], r.wu.at[slot], r.tsem.at[0, slot]),
                local(r.down_w.at[pl.ds(pl.multiple_of(t * FT, FT), FT)], r.wd.at[slot], r.tsem.at[1, slot]))
    for t in range(2):
        for c in tile_copy(t, t): c.start()
    wgs_copy = [local(r.glu_w.at[:, lane(q * D + i * 128, 128)], r.wgs.at[:, pl.ds(q * 128, 128)], r.lsem.at[1 + q]) for q in range(2)]
    for c in wgs_copy: c.start()

    @tiles(T, 16)
    def _(q):
        r.xs[q, :] = r.x[q, :].astype(F32)
        r.own_cot[q, :] = r.cot[q, :].astype(F32)
    ps = peers(p)
    zu, zd = {"batch": lax.rem(z + 1, Z)}, {"batch": lax.rem(z + Z - 1, Z)}
    zp = [lax.rem(z + k, Z) for k in range(1, Z)]
    greet([{"seq": p["base"] + j} for j in ps] + [{"batch": q} for q in zp])
    nxt, prv = {"seq": lax.rem(s + 1, NSEQ)}, {"seq": lax.rem(s + NSEQ - 1, NSEQ)}
    halo_copy = remote(r.xs, r.halo, r.hsem.at[0], r.hsem.at[1], nxt)
    pl.when(s < NSEQ - 1)(lambda: halo_copy.start())
    gc = Gather(p, r.own_cot, r.land_cot, r.gss.at[0], r.gsr.at[0])
    gs = Gather(p, r.own_sec, r.land_sec, r.gss.at[1], r.gsr.at[1])
    ga = Gather(p, r.own_act, r.land_act, r.gss.at[2], r.gsr.at[2])
    gc.start()

    mode_args = (r.rate, r.freq, r.cre, r.cim, r.prior)
    fwd_tiles(nbits, 0, D // LT, *mode_args, r.kern, r.resp, r.qr, r.qi, r.tab, r.big)
    gc.relay1()

    @tiles(T, ROWS)
    def _(q):
        hat, inv = norm_hat(r.xs[q, :])
        r.xhat[q, :] = hat
        r.xinv[q, :] = jnp.broadcast_to(inv, (ROWS, 128))
        r.ext[sub(T, q), :] = hat * vec["first_gain"]() + vec["first_shift"]()
    @pl.when(s > 0)
    def _():
        halo_copy.wait_recv()
    @pl.when(s == 0)
    def _():
        r.halo[...] = jnp.zeros_like(r.halo)
    keep = jnp.where(s == 0, 0.0, 1.0)
    @tiles(T, ROWS)
    def _(q):
        hat, _ = norm_hat(r.halo[q, :])
        r.ext[q, :] = (hat * vec["first_gain"]() + vec["first_shift"]()) * keep

    inner = lax.broadcasted_iota(jnp.int32, (KLEN, LC), 0) > 0
    @tiles(D, LC)
    def _(c):
        X = table_dot(r.ftab, r.ext[:, c])
        K = table_dot(r.ftab, r.kern[:, c], cols=slice(0, KLEN))
        r.X[:, c] = X
        r.K[:, c] = K
        P_, Q_, KP, KQ = X[:KLEN], X[KLEN:], K[:KLEN], K[KLEN:]
        qq = Q_ * KQ
        po = P_ * KP - jnp.where(inner, qq, 0.0)
        qo = jnp.where(inner, P_ * KQ + Q_ * KP, qq)
        y = table_dot(r.itab, jnp.concatenate([po, qo], 0))
        r.pre[:, c] = y + vec["skip_gain"](c) * r.ext[T:, c] + r.resp[:, c]
    @tiles(T, 16)
    def _(q):
        a = gelu_both(r.pre[q, :])[0].astype(BF16)
        r.own_act[q, :] = a.astype(F32)
        r.act_all[sub(i * T, q), :] = a
    gc.relay2()

    gw_copy.wait()
    act = r.act_all[iblk, :]
    @tiles(D, LC)
    def _(c):
        r.val[:, c] = dot(act, r.gw[:, c])
        r.sg[:, c] = dot(act, r.gw[:, lane(D + c.start, LC)])
    @tiles(T, ROWS)
    def _(q):
        v = r.val[q, :] + vec["value_bias"]()
        g = jax.nn.sigmoid(r.sg[q, :] + vec["gate_bias"]())
        r.val[q, :] = v
        r.sg[q, :] = g
        m = r.xs[q, :] + v * g
        r.merged[q, :] = m
        hat, inv = norm_hat(m)
        r.mhat[q, :] = hat
        r.minv[q, :] = jnp.broadcast_to(inv, (ROWS, 128))
        r.own_sec[q, :] = (hat * vec["second_gain"]() + vec["second_shift"]()).astype(BF16).astype(F32)
    @tiles(T, 16)
    def _(q):
        r.sec_all[sub(i * T, q), :] = r.own_sec[q, :].astype(BF16)
    gs.start()
    gc.relay3()

    r.oacc[...] = jnp.zeros_like(r.oacc)
    r.sacc[...] = jnp.zeros_like(r.sacc)
    sec = r.sec_all[iblk, :]
    @pl.loop(0, 8)
    def _(t):
        slot = lax.rem(t, 2)
        for c in tile_copy(t, slot): c.wait()
        r.u[pl.ds(0, T)] = dot(sec, r.wu[slot])
        r.gh[pl.ds(0, T)] = dot(r.cot[...], r.wd[slot], 1, 1)
        @tiles(T, 16)
        def _(q):
            hid, slope = gelu_both(r.u[q, :] + r.upb[pl.ds(t, 1), :])
            r.hid[q, :] = hid.astype(BF16)
            r.gul[q, :] = (r.gh[q, :] * slope).astype(BF16)
        r.oacc[...] += dot(r.hid[pl.ds(0, T), :], r.wd[slot])
        r.sacc[...] += dot(r.gul[pl.ds(0, T), :], r.wu[slot], 1, 1)
        @pl.when(t < 6)
        def _():
            for c in tile_copy(t + 2, slot): c.start()
        pl.when(t == 4)(gs.relay1)
    for c in tile_copy(i, 0): c.start()
    gs.relay2()
    ga.start()

    zero = jnp.zeros((ROWS, D), F32)
    def rows_a(q, carry):
        r.oacc[q, :] = r.merged[q, :] + r.oacc[q, :] + vec["down_bias"]()
        g, hat, c = r.sacc[q, :], r.mhat[q, :], r.own_cot[q, :]
        gm = c + norm_back(g * vec["second_gain"](), hat, r.minv[q, 0:1])
        r.gm[q, :] = gm
        return carry[0] + g * hat, carry[1] + g, carry[2] + c
    sums = tiles(T, ROWS)(rows_a, (zero,) * 3)
    for k, v in zip((3, 4, 5), sums): r.ssrc[4 * M + k:4 * M + k + 1, :] = fold(v)
    gm_sends = []
    for k, j in enumerate(ps):
        c = remote(r.gm.at[:, lane(j * 128, 128)], r.gm_all.at[i], r.ms.at[k], r.mr.at[k], {"seq": p["base"] + j})
        c.start()
        gm_sends.append(c)
    r.gm_all[i] = r.gm[:, lane(i * 128, 128)]
    @tiles(T, 16)
    def _(q):
        r.out[q, :] = r.oacc[q, :].astype(BF16)
    def rows_b(q, carry):
        gm, g = r.gm[q, :], r.sg[q, :]
        gv, gg = gm * g, gm * r.val[q, :] * g * (1.0 - g)
        r.glow[q, pl.ds(0, D)] = gv.astype(BF16)
        r.glow[q, pl.ds(D, D)] = gg.astype(BF16)
        return carry[0] + jnp.sum(gv.reshape(2, ROWS, D), 0), carry[1] + jnp.sum(gg.reshape(2, ROWS, D), 0)
    gb = tiles(T, 16)(rows_b, (zero,) * 2)
    gb = [fold(v) for v in gb]
    for j in range(8):
        for q in range(2):
            off = (j % 4) * 256 + q * 128
            r.ssrc[4 * M + 6 + q:4 * M + 7 + q, j * 128:(j + 1) * 128] = gb[j // 4][:, off:off + 128]
    glow = r.glow[...]
    @tiles(D, LC)
    def _(c):
        r.gz[:, c] = dot(glow, r.gw[c, :], 1, 1)
    @tiles(T, ROWS)
    def _(q):
        r.gz[q, :] = r.gz[q, :] * gelu_both(r.pre[q, :])[1]

    def settle(g, whole, which):
        for j in g.chip(which):
            @tiles(T, 16)
            def _(q):
                whole[sub(j * T, q), :] = g.land[j, q, :].astype(BF16)
    @tiles(T, 16)
    def _(q):
        r.cot_all[sub(i * T, q), :] = r.cot[q, :]
    chips = (("own", i // 2), ("x", p["ix"] // 2), ("y", p["iy"] // 2), ("d", p["idg"] // 2))
    for which, _ in chips: settle(gc, r.cot_all, which)
    gc.drain()
    pl.when(z < Z - 1)(lambda: pl.semaphore_signal(r.free.at[0], inc=1, device_id=zu, device_id_type=MESH))
    pl.when(z > 0)(lambda: pl.semaphore_signal(r.free.at[1], inc=1, device_id=zd, device_id_type=MESH))

    for c in tile_copy(i, 0): c.wait()
    r.uba[...] = jnp.zeros_like(r.uba)
    @pl.loop(0, 4)
    def _(k):
        for n, (which, _) in enumerate(chips):
            @pl.when(k == n)
            def _():
                if which == "d": gs.relay3()
                settle(gs, r.sec_all, which)
        kx, ky = lax.rem(k, 2), lax.div(k, 2)
        at = (p["y"] + ky * (1 - 2 * p["y"])) * 2 + p["x"] + kx * (1 - 2 * p["x"])
        q = pl.ds(pl.multiple_of(at * 2 * T, 2 * T), 2 * T)
        r.u[...] = dot(r.sec_all[q, :], r.wu[0])
        r.gh[...] = dot(r.cot_all[q, :], r.wd[0], 1, 1)
        def inner_rows(e, acc):
            hid, slope = gelu_both(r.u[e, :] + r.upb[pl.ds(i, 1), :])
            gu = r.gh[e, :] * slope
            r.hid[sub(at * 2 * T, e), :] = hid.astype(BF16)
            r.gul[sub(at * 2 * T, e), :] = gu.astype(BF16)
            return acc + jnp.sum(gu.reshape(2, 8, FT), 0)
        r.uba[...] = tiles(2 * T, 16)(inner_rows, r.uba[...])
    ub = fold(r.uba[...])

    own = (r.upg, r.glg, r.dng)
    LU = (lambda t: r.lup.at[0, t - 1], lambda t: r.lgl.at[0, t - 1], lambda t: r.land_cot.at[t - 1])
    LD = (lambda t: r.lup.at[1, t], lambda t: r.lgl.at[1, t], lambda t: r.land_cot.at[Z - 1 + t])
    def cu(n, t, src=None):
        return remote(LU[n](t) if src is None else src, LU[n](t), r.zs.at[n, 0, t - 1], r.zr.at[n, 0, t - 1], zu)
    def cd(n, t, src=None):
        return remote(LD[n](t) if src is None else src, LD[n](t), r.zs.at[n, 1, t], r.zr.at[n, 1, t], zd)
    def z_start(n):
        @pl.when(z == 0)
        def _():
            for t in range(Z - 1, 0, -1): cu(n, t, own[n].at[t]).start()
        @pl.when(z == Z - 1)
        def _():
            for t in range(Z - 1): cd(n, t, own[n].at[t]).start()
    def add_into(dst, srcs):
        @tiles(dst.shape[0], 16)
        def _(q):
            v = srcs[0][q, :]
            for e in srcs[1:]: v = v + e[q, :]
            dst[q, :] = v
    def z_slot(n, slot):
        for zz in range(1, Z - 1):
            @pl.when(z == zz)
            def _():
                for t in range(Z - 1, zz, -1):
                    if (Z - 1 - t) + zz == slot:
                        c = cu(n, t)
                        c.wait_recv()
                        add_into(LU[n](t), (LU[n](t), own[n].at[t]))
                        c.start()
                for t in range(zz):
                    if t + (Z - 1 - zz) == slot:
                        c = cd(n, t)
                        c.wait_recv()
                        add_into(LD[n](t), (LD[n](t), own[n].at[t]))
                        c.start()
    def z_final(n, dst):
        for zz in range(Z):
            @pl.when(z == zz)
            def _():
                srcs = [own[n].at[zz]]
                if zz > 0:
                    cu(n, zz).wait_recv()
                    srcs.append(LU[n](zz))
                if zz < Z - 1:
                    cd(n, zz).wait_recv()
                    srcs.append(LD[n](zz))
                add_into(dst, srcs)
    def z_drain(n):
        for zz in range(Z):
            @pl.when(z == zz)
            def _():
                for t in range(zz + 1, Z): cu(n, t).wait_send()
                for t in range(zz): cd(n, t).wait_send()

    @tiles(D, 256)
    def _(c):
        g = dot(r.sec_all[:, c], r.gul[...], 0, 0)
        for q in range(256 // HB):
            j = c.start // 128 + q // Z
            r.upg[q % Z, pl.ds(pl.multiple_of(j * HB, HB), HB), :] = g[q * HB:(q + 1) * HB]
    z_start(0)
    for fc in range(FT // 256):
        for nh in range(D // 512):
            g = dot(r.hid[:, fc * 256:(fc + 1) * 256], r.cot_all[:, nh * 512:(nh + 1) * 512], 0, 0)
            n = 256 * Z // FT
            for q in range(n):
                r.dng[fc * n + q, :, nh * 512:(nh + 1) * 512] = g[q * (FT // Z):(q + 1) * (FT // Z)]

    ga.relay1()
    ga.relay2()
    @tiles(D, LC)
    def _(c):
        G = table_dot(r.jtab, r.gz[:, c])
        gp, gq = G[:KLEN], G[KLEN:]
        def pair(ref):
            a, b = ref[pl.ds(0, KLEN), c], ref[pl.ds(KLEN, KLEN), c]
            bq = gq * b
            return jnp.concatenate([gp * a + jnp.where(inner, bq, 0.0), jnp.where(inner, gq * a - gp * b, bq)], 0)
        r.kern[:, c] = table_dot(r.gtab, pair(r.X), rows=slice(0, KLEN))
        r.ext[:, c] = table_dot(r.gtab, pair(r.K))
    tail_copy = remote(r.ext.at[pl.ds(0, T)], r.tail, r.hsem.at[2], r.hsem.at[3], prv)
    pl.when(s > 0)(lambda: tail_copy.start())

    bwd_args = (nbits, T, *mode_args, r.kern, r.gz, r.ssrc, r.qr, r.qi, r.big)
    bwd_tiles(0, 2, 4 * M + 8, *bwd_args)
    z_slot(0, 1)
    bwd_tiles(2, 4, 4 * M + 8, *bwd_args)
    ga.relay3()
    for which, _ in chips: settle(ga, r.act_all, which)
    for k in range(7):
        src = lax.rem(i + 7 - k, 8)
        remote(r.gm_all.at[src], r.gm_all.at[src], r.ms.at[k], r.mr.at[k], nxt).wait_recv()
    for c in wgs_copy: c.wait()
    gbias = jnp.concatenate([r.vecs[6:7, lane(i * 128, 128)], r.vecs[7:8, lane(i * 128, 128)]], 1)
    @tiles(8 * T, 256)
    def _(q):
        r.u[:, pl.ds(0, 256)] = dot(r.act_all[q, :], r.wgs[...]) + gbias
        for h in range(256 // T):
            blk = q.start // T + h
            @tiles(T, 16)
            def _(k):
                row = pl.ds(pl.multiple_of(h * T + k.start, 16), 16)
                v, g = r.u[row, pl.ds(0, 128)], jax.nn.sigmoid(r.u[row, pl.ds(128, 128)])
                gm = r.gm_all[blk, k, :]
                rows = pl.ds(pl.multiple_of(q.start + h * T + k.start, 16), 16)
                r.ggl[rows, :] = jnp.concatenate([gm * g, gm * v * g * (1.0 - g)], 1).astype(BF16)
    @tiles(D, 256)
    def _(c):
        g = dot(r.act_all[:, c], r.ggl[...], 0, 0)
        for q in range(256 // HB):
            j = c.start // 128 + q // Z
            r.glg[q % Z, pl.ds(pl.multiple_of(j * HB, HB), HB), :] = g[q * HB:(q + 1) * HB]
    z_start(1)
    pl.when(z > 0)(lambda: pl.semaphore_wait(r.free.at[0], 1))
    pl.when(z < Z - 1)(lambda: pl.semaphore_wait(r.free.at[1], 1))
    z_start(2)

    bwd_tiles(4, 6, 4 * M + 8, *bwd_args)
    z_slot(0, 2)
    bwd_tiles(6, D // LT, 4 * M + 8, *bwd_args)
    pl.when(s < NSEQ - 1)(lambda: tail_copy.wait_recv())
    @pl.when(s == NSEQ - 1)
    def _():
        r.tail[...] = jnp.zeros_like(r.tail)
    def rows_c(q, carry):
        hat, gz = r.xhat[q, :], r.gz[q, :]
        gn = r.ext[sub(T, q), :] + r.tail[q, :] + vec["skip_gain"]() * gz
        r.oacc[q, :] = r.gm[q, :] + norm_back(gn * vec["first_gain"](), hat, r.xinv[q, 0:1])
        return carry[0] + gn * hat, carry[1] + gn, carry[2] + gz * hat, carry[3] + gz
    sums = [fold(v) for v in tiles(T, ROWS)(rows_c, (zero,) * 4)]
    sums = (sums[0], sums[1], sums[2] * vec["first_gain"]() + sums[3] * vec["first_shift"]())
    for k, v in enumerate(sums): r.ssrc[4 * M + k:4 * M + k + 1, :] = v
    @tiles(T, 16)
    def _(q):
        r.ig[q, :] = r.oacc[q, :].astype(BF16)

    NR, NS = 4 * M + 8 + 2 * M, 2 * M
    sends = []
    def push(src, dst, a, b, dev):
        c = remote(src, dst, a, b, dev)
        c.start()
        sends.append(c)
    for k, j in enumerate(ps):
        push(r.ssrc.at[:, lane(j * 128, 128)], r.sland.at[i], r.sa.at[0, k], r.sa.at[1, k], {"seq": p["base"] + j})
    z_final(0, r.upf)
    for k, j in enumerate(ps):
        push(r.upf.at[pl.ds(pl.multiple_of(j * HB, HB), HB)], r.up_out.at[:, lane(i * FT, FT)], r.ua.at[0, k], r.ua.at[1, k],
             {"seq": p["base"] + j})
    r.up_out[:, lane(i * FT, FT)] = r.upf[pl.ds(pl.multiple_of(i * HB, HB), HB), :]
    z_slot(1, 1)
    tot = r.ssrc[:, lane(i * 128, 128)]
    for k in range(7):
        src = lax.rem(i + 7 - k, 8)
        remote(r.sland.at[src], r.sland.at[src], r.sa.at[0, k], r.sa.at[1, k], nxt).wait_recv()
        tot = tot + r.sland[src]
    r.mine[0:NR, :] = tot
    for q in range(FT // 128): r.mine[NR + q:NR + q + 1, :] = ub[:, q * 128:(q + 1) * 128]
    r.mine[NR + FT // 128:, :] = jnp.zeros((r.mine.shape[0] - NR - FT // 128, 128), F32)
    r.st[i] = tot[NR - NS:NR]
    for k, j in enumerate(ps):
        push(r.mine.at[pl.ds(NR - NS, NS)], r.st.at[i], r.sb.at[0, k], r.sb.at[1, k], {"seq": p["base"] + j})
    for k, q in enumerate(zp):
        push(r.mine, r.zland.at[z], r.sz.at[0, k], r.sz.at[1, k], {"batch": q})
    z_slot(1, 2)
    z_final(1, r.glf)
    for k, j in enumerate(ps):
        for q in range(2):
            push(r.glf.at[pl.ds(pl.multiple_of(j * HB, HB), HB), pl.ds(q * 128, 128)], r.glu_out.at[:, lane(q * D + i * 128, 128)],
                 r.ga.at[0, q, k], r.ga.at[1, q, k], {"seq": p["base"] + j})
    for q in range(2):
        r.glu_out[:, lane(q * D + i * 128, 128)] = r.glf[pl.ds(pl.multiple_of(i * HB, HB), HB), pl.ds(q * 128, 128)]
    z_slot(2, 1)
    acc = r.mine[...]
    for k in range(Z - 1):
        src = lax.rem(z + Z - 1 - k, Z)
        remote(r.mine, r.zland.at[src], r.sz.at[0, k], r.sz.at[1, k], zu).wait_recv()
        acc = acc + r.zland[src]
    r.tot[...] = acc
    z_slot(2, 2)
    for k in range(7):
        src = lax.rem(i + 7 - k, 8)
        blk = r.up_out.at[:, lane(src * FT, FT)]
        remote(blk, blk, r.ua.at[0, k], r.ua.at[1, k], nxt).wait_recv()
        remote(r.st.at[src], r.st.at[src], r.sb.at[0, k], r.sb.at[1, k], nxt).wait_recv()
        for q in range(2):
            blk = r.glu_out.at[:, lane(q * D + src * 128, 128)]
            remote(blk, blk, r.ga.at[0, q, k], r.ga.at[1, q, k], nxt).wait_recv()
    z_final(2, r.down_o)

    pl.when(s < NSEQ - 1)(lambda: halo_copy.wait_send())
    pl.when(s > 0)(lambda: tail_copy.wait_send())
    for c in gm_sends + sends: c.wait_send()
    gs.drain()
    ga.drain()
    for n in range(3): z_drain(n)


def layer(cfg, tabs, vecs, rate, freq, cre, cim, prior, x, cot, glu_w, up_w, down_w, cid):
    Z, NSEQ, nbits, T, D, FF, M = cfg
    FT, HB = FF // 8, D // 8 // Z
    NR = 4 * M + 8 + 2 * M
    NT = -(-(NR + FT // 128) // 8) * 8
    vm, hbm = pl.BlockSpec(memory_space=pltpu.VMEM), pl.BlockSpec(memory_space=pl.ANY)
    S = lambda shape, dt=F32: jax.ShapeDtypeStruct(shape, dt)
    ins = dict(ftab=vm, itab=vm, jtab=vm, gtab=vm, **{f"v{k}": vm for k in range(8)}, rate=vm, freq=vm, cre=vm, cim=vm, prior=vm, x=vm, cot=vm,
               glu_w=hbm, up_w=hbm, down_w=hbm)
    outs = dict(out=S((T, D), BF16), ig=S((T, D), BF16), st=S((8, 2 * M, 128)), tot=S((NT, 128)), down_o=S((FT // Z, D)),
                up_out=S((HB, FF)), glu_out=S((HB, 2 * D)))
    V, DS = pltpu.VMEM, lambda *n: pltpu.SemaphoreType.DMA(n)
    row = lambda: V((T, D), F32)
    scr = dict(
        uba=V((8, FT), F32), vecs=V((8, D), F32), upb=V((8, FT), F32),
        xs=row(), own_cot=row(), own_sec=row(), own_act=row(), halo=row(), tail=row(), xhat=row(), pre=row(), val=row(), sg=row(),
        merged=row(), mhat=row(), gm=row(), gz=row(), oacc=row(), sacc=row(), resp=row(), kern=row(),
        xinv=V((T, 128), F32), minv=V((T, 128), F32), ext=V((2 * T, D), F32), X=V((2 * KLEN, D), F32), K=V((2 * KLEN, D), F32),
        land_cot=V((8, T, D), F32), land_sec=V((8, T, D), F32), land_act=V((8, T, D), F32),
        cot_all=V((8 * T, D), BF16), sec_all=V((8 * T, D), BF16), act_all=V((8 * T, D), BF16),
        gw=V((D, 2 * D), BF16), wu=V((2, D, FT), BF16), wd=V((2, FT, D), BF16), wgs=V((D, 256), BF16),
        u=V((256, FT), F32), gh=V((256, FT), F32), hid=V((8 * T, FT), BF16), gul=V((8 * T, FT), BF16),
        glow=V((T, 2 * D), BF16), gm_all=V((8, T, 128), F32), ggl=V((8 * T, 256), BF16),
        upg=V((Z, D // Z, FT), F32), glg=V((Z, D // Z, 256), F32), dng=V((Z, FT // Z, D), F32),
        lup=V((2, Z - 1, D // Z, FT), F32), lgl=V((2, Z - 1, D // Z, 256), F32), upf=V((D // Z, FT), F32), glf=V((D // Z, 256), F32),
        qr=V((16, M, LT), F32), qi=V((16, M, LT), F32), tab=V((6, M, LT), F32), big=V((64 * M, LT), F32),
        ssrc=V((NR, D), F32), sland=V((8, NR, 128), F32), mine=V((NT, 128), F32), zland=V((Z, NT, 128), F32),
        lsem=DS(3), tsem=DS(2, 2), hsem=DS(4), gss=DS(3, 14), gsr=DS(3, 14), ms=DS(7), mr=DS(7), zs=DS(3, 2, Z - 1), zr=DS(3, 2, Z - 1),
        sa=DS(2, 7), ua=DS(2, 7), sb=DS(2, 7), ga=DS(2, 2, 7), sz=DS(2, Z - 1), free=pltpu.SemaphoreType.REGULAR((2,)))
    names = (*ins, *outs, *scr)
    res = pl.pallas_call(
        functools.partial(layer_kernel, cfg, names),
        out_shape=list(outs.values()), in_specs=list(ins.values()), out_specs=[vm] * len(outs), scratch_shapes=list(scr.values()),
        compiler_params=pltpu.CompilerParams(collective_id=cid, has_side_effects=True, vmem_limit_bytes=67043328),
        name="layer")(*tabs, *vecs, rate, freq, cre, cim, prior, x, cot, glu_w, up_w, down_w)
    return dict(zip(outs, res))


def finish_kernel(cfg, names, *refs):
    r = Bag()
    r.__dict__.update(zip(names, refs))
    Z, NSEQ, nbits, T, D, FF, M = cfg
    HB = D // 8 // Z
    NR = 4 * M + 8 + 2 * M
    b = lax.axis_index("batch")
    for k in ("out", "ig", "glu_out", "up_out", "down_o"): r.__dict__["o_" + k][...] = r.__dict__[k][...]
    for j in range(8): r.o_st[:, j * 128:(j + 1) * 128] = r.st[j]
    r.turned[...] = r.tot[0:4 * M, :].T
    mine = r.turned[pl.ds(pl.multiple_of(b * HB, HB), HB), :]
    for k in range(4): r.__dict__[f"m{k}"][...] = mine[:, k * M:(k + 1) * M]
    v = pltpu.roll(r.tot[4 * M:4 * M + 8, :], lax.rem(128 - b * HB, 128), 1)
    for k in range(6): r.__dict__[f"w{k}"][...] = v[k, 0:HB]
    per = 128 // (2 * HB)
    g = r.tot[pl.ds(4 * M + 6 + b // per, 1), :]
    r.gb[...] = pltpu.roll(jnp.broadcast_to(g, (8, 128)), lax.rem(128 - lax.rem(b, per) * 2 * HB, 128), 1)[0, 0:2 * HB]
    r.ub[...] = r.tot[pl.ds(NR + b, 1), :].reshape(128)


def finish(cfg, o):
    Z, NSEQ, nbits, T, D, FF, M = cfg
    HB = D // 8 // Z
    vm = pl.BlockSpec(memory_space=pltpu.VMEM)
    S = lambda shape, dt=F32: jax.ShapeDtypeStruct(shape, dt)
    outs = {"o_" + k: S(o[k].shape, o[k].dtype) for k in ("out", "ig", "glu_out", "up_out", "down_o")}
    outs["o_st"] = S((2 * M, D))
    outs.update({f"m{k}": S((HB, M)) for k in range(4)})
    outs.update({f"w{k}": S((HB,)) for k in range(6)})
    outs.update(gb=S((2 * HB,)), ub=S((FF // 8 // Z,)))
    names = (*o, *outs, "turned")
    res = pl.pallas_call(functools.partial(finish_kernel, cfg, names), out_shape=list(outs.values()), in_specs=[vm] * len(o),
                         out_specs=[vm] * len(outs), scratch_shapes=[pltpu.VMEM((128, 4 * M), F32)], name="finish")(*o.values())
    return {k.removeprefix("o_"): v for k, v in zip(outs, res)}


def tables(window):
    half = window // 2
    f = np.concatenate([np.arange(half + 1), np.arange(1, half)])[:, None]
    imag = np.arange(window)[:, None] > half
    ph = (f * np.arange(window)[None, :] % window) * (2.0 * np.pi / window)
    fwd = np.where(imag, -np.sin(ph), np.cos(ph))
    wt = np.where((f == 0) | (2 * f == window), 1.0, 2.0) / window
    inv = (wt * fwd).T[half:]
    def parts(a):
        a = np.ascontiguousarray(a).astype(np.float32)
        high = a.astype(ml_dtypes.bfloat16)
        return jnp.asarray(np.stack([high, (a - high.astype(np.float32)).astype(ml_dtypes.bfloat16)]))
    return parts(fwd), parts(inv), parts(inv.T), parts(fwd.T)


def plane_shards(Z, n_seq, inputs, first_gain, first_shift, decay_rate, rotation, out_real, out_imag, skip_gain, glu_weight,
                 glu_bias, second_gain, second_shift, up_weight, up_bias, down_weight, down_bias, prior_state, cotangent):
    T, D = inputs.shape[1:]
    FF, M = up_weight.shape[1], decay_rate.shape[1]
    FT, HB = FF // 8, D // 8 // Z
    cfg = (Z, n_seq, max(1, (n_seq - 1).bit_length()), T, D, FF, M)
    vecs = (first_gain, first_shift, skip_gain, second_gain, second_shift, down_bias, glu_bias, up_bias)
    o = layer(cfg, tables(T + KLEN), vecs, decay_rate.T, rotation.T, out_real.T, out_imag.T, prior_state,
              inputs[0], cotangent[0], glu_weight, up_weight, down_weight, 0)
    f = finish(cfg, o)
    v = [f[f"w{k}"] for k in range(6)]
    m = [f[f"m{k}"] for k in range(4)]
    return (f["out"][None], f["ig"][None], f["st"].reshape(1, 2, M, D), v[0], v[1], *m, v[2], f["glu_out"], f["gb"],
            v[3], v[4], f["up_out"], f["ub"], f["down_o"], v[5])


def solution(mesh):
    in_specs = (
        P("batch", "seq", None),
        P(),
        P(),
        P(),
        P(),
        P(),
        P(),
        P(),
        P(),
        P(),
        P(),
        P(),
        P(),
        P(),
        P(),
        P(),
        P("batch", None, None, None),
        P("batch", "seq", None),
    )
    out_specs = (
        P("batch", "seq", None),
        P("batch", "seq", None),
        P("batch", None, None, None),
        P(("seq", "batch")),
        P(("seq", "batch")),
        P(("seq", "batch"), None),
        P(("seq", "batch"), None),
        P(("seq", "batch"), None),
        P(("seq", "batch"), None),
        P(("seq", "batch")),
        P(("seq", "batch"), None),
        P(("seq", "batch")),
        P(("seq", "batch")),
        P(("seq", "batch")),
        P(("seq", "batch"), None),
        P(("seq", "batch")),
        P(("seq", "batch"), None),
        P(("seq", "batch")),
    )
    body = shards
    if mesh.shape["seq"] == 8:
        body = functools.partial(plane_shards, mesh.shape["batch"], mesh.shape["seq"])
    return jax.shard_map(body, mesh=mesh, in_specs=in_specs, out_specs=out_specs, check_vma=False)
```

```python
import functools
import math

import jax
import jax.numpy as jnp
import ml_dtypes
import numpy as np
from jax import lax
from jax.experimental import pallas as pl
from jax.experimental.pallas import tpu as pltpu
from jax.sharding import PartitionSpec as P

KLEN = 128
LT = 128
MESH = pl.DeviceIdType.MESH
F32, BF16 = jnp.float32, jnp.bfloat16


EPSILON = 1e-05
HIGHEST = lax.Precision.HIGHEST


def from_behind(value, axis, by):
    peers = lax.axis_size(axis)
    pairs = [(i, i + by) for i in range(peers) if 0 <= i + by < peers]
    return lax.ppermute(value, axis, pairs)


def norm_rows(values, gain, shift):
    center = values - jnp.mean(values, axis=-1, keepdims=True)
    spread = jnp.mean(center * center, axis=-1, keepdims=True)
    return center * lax.rsqrt(spread + EPSILON) * gain + shift


def mode_terms(rate_modes, freq_modes, elapsed):
    moment = elapsed[None, :, None]
    damping = jnp.exp(-rate_modes[:, None, :] * moment)
    return (
        damping * jnp.cos(freq_modes[:, None, :] * moment),
        damping * jnp.sin(freq_modes[:, None, :] * moment),
    )


def glu_gate(glu_pre):
    split_at = glu_pre.shape[-1] // 2
    return glu_pre[:, :split_at] * jax.nn.sigmoid(glu_pre[:, split_at:])


def gelu_exact(values):
    return jax.nn.gelu(values, approximate=False)


def shards(
    inputs,
    first_gain,
    first_shift,
    decay_rate,
    rotation,
    out_real,
    out_imag,
    skip_gain,
    glu_weight,
    glu_bias,
    second_gain,
    second_shift,
    up_weight,
    up_bias,
    down_weight,
    down_bias,
    prior_state,
    cotangent,
):
    seg_count, tok_count, feature = inputs.shape
    row_count = seg_count * tok_count
    window = tok_count + KLEN
    half = window // 2 + 1
    offset = lax.axis_index("seq") * tok_count
    freq_index = jnp.arange(half, dtype=jnp.int32)
    time_index = jnp.arange(window, dtype=jnp.int32)
    phase = (freq_index[:, None] * time_index[None, :] % window).astype(jnp.float32) * (
        2.0 * math.pi / window
    )
    cos_half = jnp.cos(phase)
    sin_half = jnp.sin(phase)
    forward_table = jnp.concatenate([cos_half, -sin_half], axis=0)
    weights = jnp.where((freq_index == 0) | (2 * freq_index == window), 1.0, 2.0).astype(
        jnp.float32
    )
    inverse_table = (
        jnp.concatenate(
            [(weights[:, None] * cos_half).T, -(weights[:, None] * sin_half).T], axis=1
        )[KLEN:]
        / window
    )
    local_steps = jnp.arange(tok_count).astype(jnp.float32)
    advance_steps = (offset + 1).astype(jnp.float32)

    def mixing(
        normed, halo_rows, rate_modes, freq_modes, real_modes, imag_modes, skip_local, prior_local
    ):
        table_real, table_imag = mode_terms(rate_modes, freq_modes, local_steps)
        kernel = jnp.einsum("mkh,mh->kh", table_real, real_modes, precision=HIGHEST) - jnp.einsum(
            "mkh,mh->kh", table_imag, imag_modes, precision=HIGHEST
        )
        extended = jnp.concatenate([halo_rows, normed], axis=1)
        spectrum = jnp.einsum("ft,sth->sfh", forward_table, extended, precision=HIGHEST)
        kern_spec = jnp.dot(forward_table[:, :KLEN], kernel, precision=HIGHEST)
        spec_real, spec_imag = (spectrum[:, :half], spectrum[:, half:])
        kern_real, kern_imag = (kern_spec[:half], kern_spec[half:])
        product = jnp.concatenate(
            [
                spec_real * kern_real - spec_imag * kern_imag,
                spec_real * kern_imag + spec_imag * kern_real,
            ],
            axis=1,
        )
        convolved = jnp.einsum("tf,sfh->sth", inverse_table, product, precision=HIGHEST)
        damping = jnp.exp(-rate_modes * advance_steps)
        adv_real = damping * jnp.cos(freq_modes * advance_steps)
        adv_imag = damping * jnp.sin(freq_modes * advance_steps)
        coef_real = real_modes * adv_real - imag_modes * adv_imag
        coef_imag = real_modes * adv_imag + imag_modes * adv_real
        drive_real = coef_real * prior_local[:, 0] - coef_imag * prior_local[:, 1]
        drive_imag = coef_real * prior_local[:, 1] + coef_imag * prior_local[:, 0]
        response = jnp.einsum(
            "mth,smh->sth", table_real, drive_real, precision=HIGHEST
        ) - jnp.einsum("mth,smh->sth", table_imag, drive_imag, precision=HIGHEST)
        return gelu_exact(convolved + skip_local * normed + response)

    source = inputs.astype(jnp.float32)
    normed, first_pull = jax.vjp(norm_rows, source, first_gain, first_shift)
    halo_rows = from_behind(normed, "seq", 1)
    activated, mix_pull = jax.vjp(
        mixing,
        normed,
        halo_rows,
        decay_rate.T,
        rotation.T,
        out_real.T,
        out_imag.T,
        skip_gain,
        prior_state,
    )
    activated_low = activated.reshape(row_count, feature).astype(jnp.bfloat16)
    glu_pre = jnp.dot(activated_low, glu_weight, preferred_element_type=jnp.float32) + glu_bias
    branch, glu_pull = jax.vjp(glu_gate, glu_pre)
    merged = source.reshape(row_count, feature) + branch
    second, second_pull = jax.vjp(norm_rows, merged, second_gain, second_shift)
    second_low = second.astype(jnp.bfloat16)
    up_pre = jnp.dot(second_low, up_weight, preferred_element_type=jnp.float32) + up_bias
    hidden, hidden_pull = jax.vjp(gelu_exact, up_pre)
    hidden_low = hidden.astype(jnp.bfloat16)
    result = (
        merged + jnp.dot(hidden_low, down_weight, preferred_element_type=jnp.float32) + down_bias
    )
    outputs = result.astype(jnp.bfloat16).reshape(seg_count, tok_count, feature)
    grad_out = cotangent.astype(jnp.float32).reshape(row_count, feature)
    down_bias_grad = jnp.sum(grad_out, axis=0)
    grad_low = grad_out.astype(jnp.bfloat16)
    down_grad = jnp.einsum("rf,rh->fh", hidden_low, grad_low, preferred_element_type=jnp.float32)
    grad_hidden = jnp.einsum("rh,fh->rf", grad_low, down_weight, preferred_element_type=jnp.float32)
    (grad_up,) = hidden_pull(grad_hidden)
    up_bias_grad = jnp.sum(grad_up, axis=0)
    up_low = grad_up.astype(jnp.bfloat16)
    up_grad = jnp.einsum("rh,rf->hf", second_low, up_low, preferred_element_type=jnp.float32)
    grad_second = jnp.einsum("rf,hf->rh", up_low, up_weight, preferred_element_type=jnp.float32)
    grad_merged, second_gain_grad, second_shift_grad = second_pull(grad_second)
    grad_merged = grad_merged + grad_out
    (grad_glu,) = glu_pull(grad_merged)
    glu_bias_grad = jnp.sum(grad_glu, axis=0)
    glu_low = grad_glu.astype(jnp.bfloat16)
    glu_grad = jnp.einsum("rh,rg->hg", activated_low, glu_low, preferred_element_type=jnp.float32)
    grad_activated = jnp.einsum(
        "rg,hg->rh", glu_low, glu_weight, preferred_element_type=jnp.float32
    )
    grad_normed, grad_halo, rate_grad, freq_grad, real_grad, imag_grad, skip_grad, prior_grad = (
        mix_pull(grad_activated.reshape(seg_count, tok_count, feature))
    )
    grad_tail = from_behind(grad_halo, "seq", -1)
    grad_normed = jnp.concatenate(
        [grad_normed[:, : tok_count - KLEN], grad_normed + grad_tail], axis=1
    )
    grad_source, first_gain_grad, first_shift_grad = first_pull(grad_normed)
    input_grad = (grad_source + grad_merged.reshape(seg_count, tok_count, feature)).astype(
        jnp.bfloat16
    )
    state_grad = lax.psum(prior_grad, "seq")
    rate_back = rate_grad.T
    freq_back = freq_grad.T
    real_back = real_grad.T
    imag_back = imag_grad.T
    summed = (
        lax.psum_scatter(first_gain_grad, ("seq", "batch"), scatter_dimension=0, tiled=True),
        lax.psum_scatter(first_shift_grad, ("seq", "batch"), scatter_dimension=0, tiled=True),
        lax.psum_scatter(rate_back, ("seq", "batch"), scatter_dimension=0, tiled=True),
        lax.psum_scatter(freq_back, ("seq", "batch"), scatter_dimension=0, tiled=True),
        lax.psum_scatter(real_back, ("seq", "batch"), scatter_dimension=0, tiled=True),
        lax.psum_scatter(imag_back, ("seq", "batch"), scatter_dimension=0, tiled=True),
        lax.psum_scatter(skip_grad, ("seq", "batch"), scatter_dimension=0, tiled=True),
        lax.psum_scatter(glu_grad, ("seq", "batch"), scatter_dimension=0, tiled=True),
        lax.psum_scatter(glu_bias_grad, ("seq", "batch"), scatter_dimension=0, tiled=True),
        lax.psum_scatter(second_gain_grad, ("seq", "batch"), scatter_dimension=0, tiled=True),
        lax.psum_scatter(second_shift_grad, ("seq", "batch"), scatter_dimension=0, tiled=True),
        lax.psum_scatter(up_grad, ("seq", "batch"), scatter_dimension=0, tiled=True),
        lax.psum_scatter(up_bias_grad, ("seq", "batch"), scatter_dimension=0, tiled=True),
        lax.psum_scatter(down_grad, ("seq", "batch"), scatter_dimension=0, tiled=True),
        lax.psum_scatter(down_bias_grad, ("seq", "batch"), scatter_dimension=0, tiled=True),
    )
    return (
        outputs,
        input_grad,
        state_grad,
        summed[0],
        summed[1],
        summed[2],
        summed[3],
        summed[4],
        summed[5],
        summed[6],
        summed[7],
        summed[8],
        summed[9],
        summed[10],
        summed[11],
        summed[12],
        summed[13],
        summed[14],
    )


def plane():
    s = lax.axis_index("seq")
    i = lax.rem(s, 8)
    base = s - i
    c, x, y = lax.rem(i, 2), lax.rem(i // 2, 2), i // 4
    ic, ix, iy = i + 1 - 2 * c, i + 2 - 4 * x, i + 4 - 8 * y
    idg = iy + 2 - 4 * x
    return dict(s=s, i=i, base=base, c=c, x=x, y=y, ic=ic, ix=ix, iy=iy, idg=idg)

def sib_of(p, j):
    return j + 1 - 2 * p["c"]

def remote(src, dst, ss, rs, dev):
    return pltpu.make_async_remote_copy(src_ref=src, dst_ref=dst, send_sem=ss, recv_sem=rs,
                                        device_id=dev, device_id_type=MESH)

def greet(devs):
    bar = pltpu.get_barrier_semaphore()
    for d in devs:
        pl.semaphore_signal(bar, inc=1, device_id=d, device_id_type=MESH)
    pl.semaphore_wait(bar, len(devs))

def peers(p):
    return [lax.rem(p["i"] + k, 8) for k in range(1, 8)]

class Gather:
    def __init__(self, p, own, land, ssem, rsem):
        self.p, self.own, self.land, self.ss, self.rs = p, own, land, ssem, rsem
        self.H = own.shape[0] // 2
        seq = lambda j: {"seq": p["base"] + j}
        self.X, self.Y, self.S = seq(p["ix"]), seq(p["iy"]), seq(p["ic"])

    def cp(self, k, j, h, dev, src=None):
        blk = self.land.at[j, pl.ds(h * self.H, self.H)]
        return remote(blk if src is None else src, blk, self.ss.at[k], self.rs.at[k], dev)

    def plan(self):
        i, ix, iy, idg = self.p["i"], self.p["ix"], self.p["iy"], self.p["idg"]
        return [(0, i, 0, self.X), (2, i, 1, self.Y), (1, i, 1, self.X), (3, i, 0, self.Y), (6, i, 0, self.S), (7, i, 1, self.S),
                (4, ix, 0, self.Y), (8, ix, 0, self.S), (5, iy, 1, self.X), (11, iy, 1, self.S), (9, ix, 1, self.S),
                (10, iy, 0, self.S), (12, idg, 0, self.S), (13, idg, 1, self.S)]

    def _send(self, k, own=False):
        k, j, h, dev = next(e for e in self.plan() if e[0] == k)
        self.cp(k, j, h, dev, self.own.at[pl.ds(h * self.H, self.H)] if own else None).start()

    def _got(self, k, j, h):
        self.cp(k, j, h, self.S).wait_recv()

    def start(self):
        for k in (0, 2, 1, 3, 6, 7):
            self._send(k, True)

    def relay1(self):
        p = self.p
        self._got(0, p["ix"], 0); self._send(4); self._send(8)
        self._got(2, p["iy"], 1); self._send(5); self._send(11)

    def relay2(self):
        p = self.p
        self._got(1, p["ix"], 1); self._send(9)
        self._got(3, p["iy"], 0); self._send(10)

    def relay3(self):
        p = self.p
        self._got(4, p["idg"], 0); self._send(12)
        self._got(5, p["idg"], 1); self._send(13)

    def chip(self, which):
        p = self.p
        k, j = {"own": (6, p["ic"]), "x": (8, sib_of(p, p["ix"])), "y": (10, sib_of(p, p["iy"])), "d": (12, sib_of(p, p["idg"]))}[which]
        self._got(k, j, 0)
        self._got(k + 1, j, 1)
        return (j,) if which == "own" else ({"x": p["ix"], "y": p["iy"], "d": p["idg"]}[which], j)

    def drain(self):
        for k, j, h, dev in self.plan():
            self.cp(k, j, h, dev).wait_send()


class Line:
    def __init__(self, Z, z, p, own, land, ssem, rsem, zu, zd):
        self.Z, self.z, self.c, self.own, self.land, self.ss, self.rs = Z, z, p["c"], own, land, ssem, rsem
        self.H = own.shape[0] // 2
        self.dev = (zu, zd, {"seq": p["base"] + p["ic"]})

    def part(self, chip, core, half):
        return self.land.at[chip * 2 + core, pl.ds(half * self.H, self.H)]

    def cp(self, way, hop, half, chip, core, own=False):
        blk = self.part(chip, core, half)
        src = self.own.at[pl.ds(half * self.H, self.H)] if own else blk
        return remote(src, blk, self.ss.at[way, hop, half], self.rs.at[way, hop, half], self.dev[way])

    def ends(self):
        z, Z = self.z, self.Z
        return ((lambda h: z - h, lambda h: z - h >= 0, z < Z - 1), (lambda h: z + h, lambda h: z + h < Z, z > 0))

    def start(self):
        for half in range(2):
            for way, (chip, there, on) in enumerate(self.ends()):
                pl.when(on)(lambda: self.cp(way, 0, half, self.z, self.c, True).start())
        for half in range(2): self.cp(2, 0, half, self.z, self.c, True).start()

    def _take(self, way, hop, half, chip):
        self.cp(way, hop - 1, half, chip, self.c).wait_recv()
        self.cp(2, hop + way * (self.Z - 1), half, chip, self.c).start()

    def pass_on(self, hop, half):
        for way, (chip, there, on) in enumerate(self.ends()):
            @pl.when(there(hop) & on)
            def _():
                self._take(way, hop, half, chip(hop))
                self.cp(way, hop, half, chip(hop), self.c).start()

    def settle(self, chip_at):
        for way, (chip, there, on) in enumerate(self.ends()):
            for hop in range(1, self.Z):
                @pl.when(chip_at == chip(hop))
                def _():
                    for half in range(2):
                        pl.when(jnp.logical_not(on))(lambda: self._take(way, hop, half, chip(hop)))
                    for half in range(2):
                        self.cp(2, hop + way * (self.Z - 1), half, chip(hop), 1 - self.c).wait_recv()

    def settle_own(self):
        for half in range(2): self.cp(2, 0, half, self.z, 1 - self.c).wait_recv()

    def drain(self):
        for half in range(2):
            self.cp(2, 0, half, self.z, self.c, True).wait_send()
            for way, (chip, there, on) in enumerate(self.ends()):
                for hop in range(self.Z - 1):
                    pl.when(there(hop) & on)(lambda: self.cp(way, hop, half, chip(hop), self.c).wait_send())
                for hop in range(1, self.Z):
                    pl.when(there(hop))(lambda: self.cp(2, hop + way * (self.Z - 1), half, chip(hop), self.c).wait_send())


def cmul(ar, ai, br, bi):
    return ar * br - ai * bi, ar * bi + ai * br

def lam_of(rate, freq):
    damp = jnp.exp(-rate)
    q = freq * freq
    cosv = 1.0 + q * (-1.0/2 + q * (1.0/24 + q * (-1.0/720 + q * (1.0/40320 + q * (-1.0/3628800)))))
    sinv = freq * (1.0 + q * (-1.0/6 + q * (1.0/120 + q * (-1.0/5040 + q * (1.0/362880)))))
    return damp * cosv, damp * sinv

def power_rows(lr, li, qr, qi, A):
    l2 = cmul(lr, li, lr, li); l4 = cmul(*l2, *l2); l8 = cmul(*l4, *l4)
    cur = (jnp.ones_like(lr), jnp.zeros_like(lr))
    for a in range(A):
        qr[a] = cur[0]; qi[a] = cur[1]
        cur = cmul(*cur, *l8)
    return l2, l4, cur

def offset_power(top, s, nbits):
    res = (jnp.ones_like(top[0]), jnp.zeros_like(top[0]))
    sq = top
    for bit in range(nbits):
        on = lax.rem(lax.div(s, 1 << bit), 2) == 1
        nxt = cmul(*res, *sq)
        res = (jnp.where(on, nxt[0], res[0]), jnp.where(on, nxt[1], res[1]))
        if bit + 1 < nbits: sq = cmul(*sq, *sq)
    return res

def fwd_tiles(nbits, lo, hi, rate, freq, cre, cim, prior, kern, resp, co):
    M = rate.shape[0]
    A = kern.shape[0] // 8
    s = lax.axis_index("seq")
    b = lax.broadcasted_iota(jnp.int32, (8, LT), 0)
    o1, o2, o4 = (b % 2) == 1, ((b // 2) % 2) == 1, b >= 4
    one, zero = jnp.ones((8, LT), F32), jnp.zeros((8, LT), F32)
    square = lambda v: cmul(*v, *v)
    @pl.loop(lo, hi)
    def _(lt):
        cols = pl.ds(pl.multiple_of(lt * LT, LT), LT)
        l1 = lam_of(rate[:, cols], freq[:, cols])
        l2 = square(l1)
        l4 = square(l2)
        l8 = square(l4)
        top = l8
        for _ in range((A - 1).bit_length()): top = square(top)
        off = cmul(*offset_power(top, s, nbits), *l1)
        c = cre[:, cols], cim[:, cols]
        d = cmul(*cmul(*c, *off), prior[0, 0, :, cols], prior[0, 1, :, cols])
        rows = (*l1, *l2, *l4, *c, *cmul(*c, *l8), *d, *cmul(*d, *l8), 2.0 * l8[0], -(l8[0] * l8[0] + l8[1] * l8[1]))
        for k, v in enumerate(rows): co[pl.ds(k * M, M), :] = v
        def step(m, accs):
            row = lambda k: jnp.broadcast_to(co[pl.ds(k * M + m, 1), :], (8, LT))
            e = jnp.where(o1, row(0), one), jnp.where(o1, row(1), zero)
            e = cmul(*e, jnp.where(o2, row(2), one), jnp.where(o2, row(3), zero))
            er, ei = cmul(*e, jnp.where(o4, row(4), one), jnp.where(o4, row(5), zero))
            p, q = row(14), row(15)
            k0, k1 = er * row(6) - ei * row(7), er * row(8) - ei * row(9)
            r0, r1 = er * row(10) - ei * row(11), er * row(12) - ei * row(13)
            out = list(accs)
            for a in range(A):
                out[2 * a] = out[2 * a] + k0
                out[2 * a + 1] = out[2 * a + 1] + r0
                if a < A - 1:
                    k0, k1 = k1, p * k1 + q * k0
                    r0, r1 = r1, p * r1 + q * r0
            return tuple(out)
        accs = lax.fori_loop(0, M, step, tuple(jnp.zeros((8, LT), F32) for _ in range(2 * A)), unroll=4)
        for a in range(A):
            kern[pl.ds(8 * a, 8), cols] = accs[2 * a]
            resp[pl.ds(8 * a, 8), cols] = accs[2 * a + 1]


def bwd_tiles(lo, hi, srow, nbits, TOK, rate, freq, cre, cim, prior, kg, gz, out, qr, qi, acc):
    M = rate.shape[0]
    A = kg.shape[0] // 8
    s = lax.axis_index("seq")
    adv = (s * TOK + 1).astype(F32)
    @pl.loop(lo, hi)
    def _(lt):
        cols = pl.ds(pl.multiple_of(lt * LT, LT), LT)
        lr, li = lam_of(rate[:, cols], freq[:, cols])
        l2, l4, top = power_rows(lr, li, qr, qi, A)
        def step(m, carry):
            for j, g in enumerate((kg, gz)):
                z = jnp.zeros((8, LT), F32)
                sr, si, tr, ti = z, z, z, z
                for a in range(A - 1, -1, -1):
                    ga = g[pl.ds(8 * a, 8), cols]
                    sr = sr + ga * qr[a, pl.ds(m, 1), :]
                    si = si + ga * qi[a, pl.ds(m, 1), :]
                    if a > 0:
                        tr = tr + sr
                        ti = ti + si
                for q, v in enumerate((sr, si, tr, ti)):
                    acc[pl.ds(pl.multiple_of(((4 * j + q) * M + m) * 8, 8), 8), :] = v
            return carry
        lax.fori_loop(0, M, step, 0, unroll=4)
        pw = (jnp.ones_like(lr), jnp.zeros_like(lr))
        zero = jnp.zeros_like(lr)
        ar, ai, br, bi = [zero] * 2, [zero] * 2, [zero] * 2, [zero] * 2
        for b in range(8):
            for j in range(2):
                ld = lambda q: acc[pl.ds((4 * j + q) * M * 8 + b, M, stride=8), :]
                S = ld(0), ld(1)
                U = 8.0 * ld(2), 8.0 * ld(3)
                if b: U = U[0] + float(b) * S[0], U[1] + float(b) * S[1]
                w = cmul(*pw, *S)
                ar[j], ai[j] = ar[j] + w[0], ai[j] + w[1]
                w = cmul(*pw, *U)
                br[j], bi[j] = br[j] + w[0], bi[j] + w[1]
            pw = cmul(*pw, lr, li)
        off = cmul(*offset_power(top, s, nbits), lr, li)
        c = cre[:, cols], cim[:, cols]
        ps = cmul(*off, prior[0, 0, :, cols], prior[0, 1, :, cols])
        u = cmul(*ps, ar[1], ai[1])
        v = cmul(*ps, br[1] + adv * ar[1], bi[1] + adv * ai[1])
        v = cmul(*c, v[0] + br[0], v[1] + bi[0])
        w = cmul(*cmul(*c, *off), ar[1], ai[1])
        for k, val in enumerate((-v[0], -v[1], u[0] + ar[0], -(u[1] + ai[0]))): out[k * M:(k + 1) * M, cols] = val
        for k, val in enumerate((w[0], -w[1])): out[srow + k * M:srow + (k + 1) * M, cols] = val


class Bag:
    pass


def dot(a, b, ca=1, cb=0):
    return lax.dot_general(a, b, (((ca,), (cb,)), ((), ())), preferred_element_type=F32)


def split_low(v):
    high = v.astype(BF16)
    return high, (v - high.astype(F32)).astype(BF16)


def table_dot(tab, v, rows=slice(None), cols=slice(None)):
    high, low = split_low(v)
    th, tl = tab[0, rows, cols], tab[1, rows, cols]
    return dot(th, high) + dot(th, low) + dot(tl, high)


def gelu_both(u):
    cdf = 0.5 + 0.5 * lax.erf(u * (0.5 ** 0.5))
    return u * cdf, cdf + u * (jnp.exp(-0.5 * u * u) * ((2.0 * math.pi) ** -0.5))


def tiles(n, step):
    def run(body, init=None):
        if init is None:
            @pl.loop(0, n // step)
            def _(k):
                body(pl.ds(pl.multiple_of(k * step, step), step))
            return None
        return lax.fori_loop(0, n // step, lambda k, c: body(pl.ds(pl.multiple_of(k * step, step), step), c), init)
    return run


def sub(off, q):
    return pl.ds(pl.multiple_of(off + q.start, q.size), q.size)


def row_mean(v):
    return jnp.sum(v, axis=-1, keepdims=True) * (1.0 / v.shape[-1])


def norm_hat(v):
    center = v - row_mean(v)
    inv = lax.rsqrt(row_mean(center * center) + EPSILON)
    return center * inv, inv


def norm_back(gg, hat, inv):
    return inv * (gg - row_mean(gg) - hat * row_mean(gg * hat))


def fold(v):
    return jnp.sum(v, axis=0, keepdims=True)


LC = 256
ROWS = 8
VEC = ("first_gain", "first_shift", "skip_gain", "second_gain", "second_shift", "down_bias", "value_bias", "gate_bias")


def layer_kernel(cfg, names, *refs):
    r = Bag()
    r.__dict__.update(zip(names, refs))
    Z, NSEQ, nbits, T, D, FF, M = cfg
    FT = FF // 8
    HB = D // 8 // Z
    p = plane()
    s, i = p["s"], p["i"]
    z = lax.axis_index("batch")
    vec = {k: (lambda q: (lambda c=slice(None): r.vecs[q:q + 1, c]))(q) for q, k in enumerate(VEC)}
    iblk = pl.ds(pl.multiple_of(i * T, T), T)
    w8, own8 = p["c"] * Z + z, z * 2 + p["c"]
    q0, qx, qy, qd = (v // 2 for v in (i, p["ix"], p["iy"], p["idg"]))
    FB = FF // 32

    for q, ref in enumerate((r.v0, r.v1, r.v2, r.v3, r.v4, r.v5)): r.vecs[q:q + 1, :] = ref[...].reshape(1, D)
    for q in range(2): r.vecs[6 + q:7 + q, :] = r.v6[q * D:(q + 1) * D].reshape(1, D)
    for q in range(8): r.upb[q:q + 1, :] = r.v7[q * FT:(q + 1) * FT].reshape(1, FT)

    lane = lambda off, n: pl.ds(pl.multiple_of(off, 128), n)
    local = lambda src, dst, sem: pltpu.make_async_copy(src, dst, sem)
    gw_copy = local(r.glu_w, r.gw, r.lsem.at[0])
    gw_copy.start()
    def tile_copy(t, slot):
        return (local(r.up_w.at[:, lane(t * FT, FT)], r.wu.at[slot], r.tsem.at[0, slot]),
                local(r.down_w.at[pl.ds(pl.multiple_of(t * FT, FT), FT)], r.wd.at[slot], r.tsem.at[1, slot]))
    for t in range(2):
        for c in tile_copy(t, t): c.start()
    def slice_copy():
        return [c for q in range(4) for c in (
            local(r.up_w.at[:, lane((q * 8 + w8) * FB, FB)], r.wu.at[0, :, pl.ds(q * FB, FB)], r.ssem.at[0, q]),
            local(r.down_w.at[pl.ds(pl.multiple_of((q * 8 + w8) * FB, FB), FB)], r.wd.at[0, pl.ds(q * FB, FB)], r.ssem.at[1, q]))]
    wgs_copy = [local(r.glu_w.at[:, lane(q * D + i * 128, 128)], r.wgs.at[:, pl.ds(q * 128, 128)], r.lsem.at[1 + q]) for q in range(2)]
    for c in wgs_copy: c.start()

    @tiles(T, 16)
    def _(q):
        r.xs[q, :] = r.x[q, :].astype(F32)
        r.own_cot[q, :] = r.cot[q, :].astype(F32)
    ps = peers(p)
    zu, zd = {"batch": lax.rem(z + 1, Z)}, {"batch": lax.rem(z + Z - 1, Z)}
    zp = [lax.rem(z + k, Z) for k in range(1, Z)]
    group = [lax.rem(w8 + k, 8) for k in range(1, 8)]
    seat = lambda w: {"seq": s - p["c"] + w // Z, "batch": lax.rem(w, Z)}
    greet([{"seq": p["base"] + j} for j in ps] + [{"seq": s - p["c"] + e, "batch": q} for q in zp for e in range(2)])
    nxt, prv = {"seq": lax.rem(s + 1, NSEQ)}, {"seq": lax.rem(s + NSEQ - 1, NSEQ)}
    halo_copy = remote(r.xs, r.halo, r.hsem.at[0], r.hsem.at[1], nxt)
    pl.when(s < NSEQ - 1)(lambda: halo_copy.start())
    gc = Line(Z, z, p, r.own_cot, r.land_cot, r.lss.at[0], r.lsr.at[0], zu, zd)
    gs = Line(Z, z, p, r.own_sec, r.land_sec, r.lss.at[1], r.lsr.at[1], zu, zd)
    ga = Gather(p, r.own_act, r.land_act, r.gss, r.gsr)
    gc.start()

    mode_args = (r.rate, r.freq, r.cre, r.cim, r.prior)
    fwd_tiles(nbits, 0, D // LT, *mode_args, r.kern, r.resp, r.big)
    gc.pass_on(1, 0)

    @tiles(T, ROWS)
    def _(q):
        hat, inv = norm_hat(r.xs[q, :])
        r.xhat[q, :] = hat
        r.xinv[q, :] = jnp.broadcast_to(inv, (ROWS, 128))
        r.ext[sub(T, q), :] = hat * vec["first_gain"]() + vec["first_shift"]()
    @pl.when(s > 0)
    def _():
        halo_copy.wait_recv()
    @pl.when(s == 0)
    def _():
        r.halo[...] = jnp.zeros_like(r.halo)
    keep = jnp.where(s == 0, 0.0, 1.0)
    @tiles(T, ROWS)
    def _(q):
        hat, _ = norm_hat(r.halo[q, :])
        r.ext[q, :] = (hat * vec["first_gain"]() + vec["first_shift"]()) * keep

    inner = lax.broadcasted_iota(jnp.int32, (KLEN, LC), 0) > 0
    @tiles(D, LC)
    def _(c):
        X = table_dot(r.ftab, r.ext[:, c])
        K = table_dot(r.ftab, r.kern[:, c], cols=slice(0, KLEN))
        r.X[:, c] = X
        r.K[:, c] = K
        P_, Q_, KP, KQ = X[:KLEN], X[KLEN:], K[:KLEN], K[KLEN:]
        qq = Q_ * KQ
        po = P_ * KP - jnp.where(inner, qq, 0.0)
        qo = jnp.where(inner, P_ * KQ + Q_ * KP, qq)
        y = table_dot(r.itab, jnp.concatenate([po, qo], 0))
        r.pre[:, c] = y + vec["skip_gain"](c) * r.ext[T:, c] + r.resp[:, c]
    @tiles(T, 16)
    def _(q):
        a = gelu_both(r.pre[q, :])[0].astype(BF16)
        r.own_act[q, :] = a.astype(F32)
        r.act_all[sub(i * T, q), :] = a
    gc.pass_on(1, 1)
    ga.start()

    gw_copy.wait()
    act = r.act_all[iblk, :]
    @tiles(D, LC)
    def _(c):
        r.val[:, c] = dot(act, r.gw[:, c])
        r.sg[:, c] = dot(act, r.gw[:, lane(D + c.start, LC)])
    @tiles(T, ROWS)
    def _(q):
        v = r.val[q, :] + vec["value_bias"]()
        g = jax.nn.sigmoid(r.sg[q, :] + vec["gate_bias"]())
        r.val[q, :] = v
        r.sg[q, :] = g
        m = r.xs[q, :] + v * g
        r.merged[q, :] = m
        hat, inv = norm_hat(m)
        r.mhat[q, :] = hat
        r.minv[q, :] = jnp.broadcast_to(inv, (ROWS, 128))
        r.own_sec[q, :] = (hat * vec["second_gain"]() + vec["second_shift"]()).astype(BF16).astype(F32)
    @tiles(T, 16)
    def _(q):
        r.sec_all[sub(own8 * T, q), :] = r.own_sec[q, :].astype(BF16)
    gs.start()
    gc.pass_on(2, 0)

    r.oacc[...] = jnp.zeros_like(r.oacc)
    r.sacc[...] = jnp.zeros_like(r.sacc)
    sec = r.sec_all[pl.ds(pl.multiple_of(own8 * T, T), T), :]
    @pl.loop(0, 8)
    def _(t):
        slot = lax.rem(t, 2)
        for c in tile_copy(t, slot): c.wait()
        r.u[pl.ds(0, T)] = dot(sec, r.wu[slot])
        r.gh[pl.ds(0, T)] = dot(r.cot[...], r.wd[slot], 1, 1)
        def rows_u(q, acc):
            hid, slope = gelu_both(r.u[q, :] + r.upb[pl.ds(t, 1), :])
            gu = r.gh[q, :] * slope
            r.hid[q, :] = hid.astype(BF16)
            r.gul[q, :] = gu.astype(BF16)
            return acc + jnp.sum(gu.reshape(2, 8, FT), 0)
        r.ubg[pl.ds(t, 1), :] = fold(tiles(T, 16)(rows_u, jnp.zeros((8, FT), F32)))
        r.oacc[...] += dot(r.hid[pl.ds(0, T), :], r.wd[slot])
        r.sacc[...] += dot(r.gul[pl.ds(0, T), :], r.wu[slot], 1, 1)
        @pl.when(t < 6)
        def _():
            for c in tile_copy(t + 2, slot): c.start()
        pl.when(t == 1)(lambda: gc.pass_on(2, 1))
        pl.when(t == 2)(ga.relay1)
        @pl.when(t == 5)
        def _():
            gs.pass_on(1, 0)
            ga.relay2()
    for c in slice_copy(): c.start()
    gs.pass_on(1, 1)
    ga.relay3()

    zero = jnp.zeros((ROWS, D), F32)
    def rows_a(q, carry):
        r.oacc[q, :] = r.merged[q, :] + r.oacc[q, :] + vec["down_bias"]()
        g, hat, c = r.sacc[q, :], r.mhat[q, :], r.own_cot[q, :]
        gm = c + norm_back(g * vec["second_gain"](), hat, r.minv[q, 0:1])
        r.gm[q, :] = gm
        return carry[0] + g * hat, carry[1] + g, carry[2] + c
    sums = tiles(T, ROWS)(rows_a, (zero,) * 3)
    for k, v in zip((3, 4, 5), sums): r.ssrc[4 * M + k:4 * M + k + 1, :] = fold(v)
    gm_sends = []
    for k, j in enumerate(ps):
        c = remote(r.gm.at[:, lane(j * 128, 128)], r.gm_all.at[i], r.ms.at[k], r.mr.at[k], {"seq": p["base"] + j})
        c.start()
        gm_sends.append(c)
    r.gm_all[i] = r.gm[:, lane(i * 128, 128)]
    @tiles(T, 16)
    def _(q):
        r.out[q, :] = r.oacc[q, :].astype(BF16)
    def rows_b(q, carry):
        gm, g = r.gm[q, :], r.sg[q, :]
        gv, gg = gm * g, gm * r.val[q, :] * g * (1.0 - g)
        r.glow[q, pl.ds(0, D)] = gv.astype(BF16)
        r.glow[q, pl.ds(D, D)] = gg.astype(BF16)
        return carry[0] + jnp.sum(gv.reshape(2, ROWS, D), 0), carry[1] + jnp.sum(gg.reshape(2, ROWS, D), 0)
    gb = tiles(T, 16)(rows_b, (zero,) * 2)
    gb = [fold(v) for v in gb]
    for j in range(8):
        for q in range(2):
            off = (j % 4) * 256 + q * 128
            r.ssrc[4 * M + 6 + q:4 * M + 7 + q, j * 128:(j + 1) * 128] = gb[j // 4][:, off:off + 128]
    glow = r.glow[...]
    @tiles(D, LC)
    def _(c):
        r.gz[:, c] = dot(glow, r.gw[c, :], 1, 1)
    @tiles(T, ROWS)
    def _(q):
        r.gz[q, :] = r.gz[q, :] * gelu_both(r.pre[q, :])[1]
    gs.pass_on(2, 0)

    @tiles(D, LC)
    def _(c):
        G = table_dot(r.jtab, r.gz[:, c])
        gp, gq = G[:KLEN], G[KLEN:]
        def pair(ref):
            a, b = ref[pl.ds(0, KLEN), c], ref[pl.ds(KLEN, KLEN), c]
            bq = gq * b
            return jnp.concatenate([gp * a + jnp.where(inner, bq, 0.0), jnp.where(inner, gq * a - gp * b, bq)], 0)
        r.kern[:, c] = table_dot(r.gtab, pair(r.X), rows=slice(0, KLEN))
        r.ext[:, c] = table_dot(r.gtab, pair(r.K))
    tail_copy = remote(r.ext.at[pl.ds(0, T)], r.tail, r.hsem.at[2], r.hsem.at[3], prv)
    pl.when(s > 0)(lambda: tail_copy.start())
    gs.pass_on(2, 1)

    for which in ("own", "x", "y", "d"):
        for j in ga.chip(which):
            @tiles(T, 16)
            def _(q):
                r.act_all[sub(j * T, q), :] = ga.land[j, q, :].astype(BF16)
    for k in range(7):
        src = lax.rem(i + 7 - k, 8)
        remote(r.gm_all.at[src], r.gm_all.at[src], r.ms.at[k], r.mr.at[k], nxt).wait_recv()
    for c in wgs_copy: c.wait()
    gbias = jnp.concatenate([r.vecs[6:7, lane(i * 128, 128)], r.vecs[7:8, lane(i * 128, 128)]], 1)
    @tiles(8 * T, 256)
    def _(q):
        r.u[:, pl.ds(0, 256)] = dot(r.act_all[q, :], r.wgs[...]) + gbias
        for h in range(256 // T):
            blk = q.start // T + h
            @tiles(T, 16)
            def _(k):
                row = pl.ds(pl.multiple_of(h * T + k.start, 16), 16)
                v, g = r.u[row, pl.ds(0, 128)], jax.nn.sigmoid(r.u[row, pl.ds(128, 128)])
                gm = r.gm_all[blk, k, :]
                rows = pl.ds(pl.multiple_of(q.start + h * T + k.start, 16), 16)
                r.ggl[rows, :] = jnp.concatenate([gm * g, gm * v * g * (1.0 - g)], 1).astype(BF16)
    @tiles(D, 256)
    def _(c):
        g = dot(r.act_all[:, c], r.ggl[...], 0, 0)
        for q in range(256 // HB):
            j = c.start // 128 + q // Z
            r.glg[q % Z, pl.ds(pl.multiple_of(j * HB, HB), HB), :] = g[q * HB:(q + 1) * HB]

    LU = lambda t: r.lgl.at[0, t - 1]
    LD = lambda t: r.lgl.at[1, t]
    def cu(t, src=None):
        return remote(LU(t) if src is None else src, LU(t), r.zs.at[0, t - 1], r.zr.at[0, t - 1], zu)
    def cd(t, src=None):
        return remote(LD(t) if src is None else src, LD(t), r.zs.at[1, t], r.zr.at[1, t], zd)
    def add_into(dst, srcs):
        @tiles(dst.shape[0], 16)
        def _(q):
            v = srcs[0][q, :]
            for e in srcs[1:]: v = v + e[q, :]
            dst[q, :] = v
    def z_start():
        for h in range(Z - 1, 0, -1):
            pl.when(z == 0)(lambda: cu(h, r.glg.at[h]).start())
            pl.when(z == Z - 1)(lambda: cd(Z - 1 - h, r.glg.at[Z - 1 - h]).start())
    def z_slot(slot):
        for zz in range(1, Z - 1):
            @pl.when(z == zz)
            def _():
                for t in range(Z - 1, zz, -1):
                    if (Z - 1 - t) + zz == slot:
                        cu(t).wait_recv()
                        add_into(LU(t), (LU(t), r.glg.at[t]))
                        cu(t).start()
                for t in range(zz):
                    if t + (Z - 1 - zz) == slot:
                        cd(t).wait_recv()
                        add_into(LD(t), (LD(t), r.glg.at[t]))
                        cd(t).start()
    def z_final(dst):
        for zz in range(Z):
            @pl.when(z == zz)
            def _():
                srcs = [r.glg.at[zz]]
                if zz > 0:
                    cu(zz).wait_recv()
                    srcs.append(LU(zz))
                if zz < Z - 1:
                    cd(zz).wait_recv()
                    srcs.append(LD(zz))
                add_into(dst, srcs)
    def z_drain():
        for zz in range(Z):
            @pl.when(z == zz)
            def _():
                for t in range(zz + 1, Z): cu(t).wait_send()
                for t in range(zz): cd(t).wait_send()
    z_start()

    def low_rows(src, dst, b8):
        @tiles(T, 16)
        def _(q):
            dst[sub(b8 * T, q), :] = src[b8, q, :].astype(BF16)
    @tiles(T, 16)
    def _(q):
        r.cot_all[sub(own8 * T, q), :] = r.cot[q, :]
    gc.settle_own()
    low_rows(r.land_cot, r.cot_all, z * 2 + 1 - p["c"])
    low_half = z < Z // 2
    near_end = jnp.where(low_half, z, Z - 1 - z)
    def chip_at(k):
        at = jnp.where(k <= near_end, near_end - k, k)
        return jnp.where(low_half, at, Z - 1 - at)
    @pl.loop(1, Z)
    def _(k):
        at = chip_at(k)
        gc.settle(at)
        low_rows(r.land_cot, r.cot_all, at * 2)
        low_rows(r.land_cot, r.cot_all, at * 2 + 1)

    bwd_args = (nbits, T, *mode_args, r.kern, r.gz, r.ssrc, r.qr, r.qi, r.big)
    srow = 4 * M + 16
    bwd_tiles(0, 4, srow, *bwd_args)
    z_slot(1)
    bwd_tiles(4, D // LT, srow, *bwd_args)
    z_slot(2)
    pl.when(s < NSEQ - 1)(lambda: tail_copy.wait_recv())
    @pl.when(s == NSEQ - 1)
    def _():
        r.tail[...] = jnp.zeros_like(r.tail)
    def rows_c(q, carry):
        hat, gz = r.xhat[q, :], r.gz[q, :]
        gn = r.ext[sub(T, q), :] + r.tail[q, :] + vec["skip_gain"]() * gz
        r.oacc[q, :] = r.gm[q, :] + norm_back(gn * vec["first_gain"](), hat, r.xinv[q, 0:1])
        return carry[0] + gn * hat, carry[1] + gn, carry[2] + gz * hat, carry[3] + gz
    sums = [fold(v) for v in tiles(T, ROWS)(rows_c, (zero,) * 4)]
    sums = (sums[0], sums[1], sums[2] * vec["first_gain"]() + sums[3] * vec["first_shift"]())
    for k, v in enumerate(sums): r.ssrc[4 * M + k:4 * M + k + 1, :] = v
    @tiles(T, 16)
    def _(q):
        r.ig[q, :] = r.oacc[q, :].astype(BF16)
    r.ssrc[4 * M + 8:4 * M + 16, :] = jnp.zeros((8, D), F32)
    for j in range(8):
        for e in range(FT // 128): r.ssrc[4 * M + 8 + e:4 * M + 9 + e, j * 128:(j + 1) * 128] = r.ubg[j:j + 1, e * 128:(e + 1) * 128]

    NR, NS = 4 * M + 16 + 2 * M, 2 * M
    sends = []
    def push(src, dst, a, b, dev):
        c = remote(src, dst, a, b, dev)
        c.start()
        sends.append(c)
    for k, j in enumerate(ps):
        push(r.ssrc.at[:, lane(j * 128, 128)], r.sland.at[i], r.sa.at[0, k], r.sa.at[1, k], {"seq": p["base"] + j})
    def small_sum():
        tot = r.ssrc[:, lane(i * 128, 128)]
        for k in range(7):
            src = lax.rem(i + 7 - k, 8)
            remote(r.sland.at[src], r.sland.at[src], r.sa.at[0, k], r.sa.at[1, k], nxt).wait_recv()
            tot = tot + r.sland[src]
        r.mine[...] = tot
        r.st[i] = tot[NR - NS:NR]
        for c in small_sends(): c.start()
    def small_sends():
        return ([remote(r.mine.at[pl.ds(NR - NS, NS)], r.st.at[i], r.sb.at[0, k], r.sb.at[1, k], {"seq": p["base"] + j}) for k, j in enumerate(ps)]
                + [remote(r.mine, r.zland.at[z], r.sz.at[0, k], r.sz.at[1, k], {"batch": q}) for k, q in enumerate(zp)])

    for c in slice_copy(): c.wait()
    for zz in range(Z):
        @pl.when(z == zz)
        def _():
            for q in range(4): r.upbs[0:1, q * FB:(q + 1) * FB] = r.upb[pl.ds(q * 2 + p["c"], 1), :][:, zz * FB:(zz + 1) * FB]
    @pl.loop(0, Z)
    def _(k):
        at = chip_at(k)
        @pl.when(k == 0)
        def _():
            gs.settle_own()
            low_rows(r.land_sec, r.sec_all, z * 2 + 1 - p["c"])
        pl.when(k == Z - 1)(small_sum)
        @pl.when(k > 0)
        def _():
            gs.settle(at)
            low_rows(r.land_sec, r.sec_all, at * 2)
            low_rows(r.land_sec, r.sec_all, at * 2 + 1)
        q = pl.ds(pl.multiple_of(at * 2 * T, 2 * T), 2 * T)
        r.u[...] = dot(r.sec_all[q, :], r.wu[0])
        r.gh[...] = dot(r.cot_all[q, :], r.wd[0], 1, 1)
        @tiles(2 * T, 16)
        def _(e):
            hid, slope = gelu_both(r.u[e, :] + r.upbs[0:1, :])
            r.hid[sub(at * 2 * T, e), :] = hid.astype(BF16)
            r.gul[sub(at * 2 * T, e), :] = (r.gh[e, :] * slope).astype(BF16)

    own, land = (r.upg, r.dng), (r.lup, r.ldn)
    X, Y = {"seq": p["base"] + p["ix"]}, {"seq": p["base"] + p["iy"]}
    def piece(n, q, h):
        half = own[n].shape[1] // 2
        return own[n].at[q, pl.ds(h * half, half)]
    def hop(n, k, dev, src=None):
        return remote(land[n].at[k] if src is None else src, land[n].at[k], r.rs.at[0, n, k], r.rs.at[1, n, k], dev)
    def plane_start(n):
        for k, dev, q, h in ((0, X, qd, 0), (2, Y, qd, 1), (1, X, qx, 0), (3, Y, qy, 1)): hop(n, k, dev, piece(n, q, h)).start()
    def plane_middle(n):
        for k, q, h, k2, dev in ((0, qy, 0, 4, Y), (2, qx, 1, 5, X)):
            hop(n, k, X).wait_recv()
            add_into(land[n].at[k], (land[n].at[k], piece(n, q, h)))
            hop(n, k2, dev, land[n].at[k]).start()
    def plane_end(n, dst):
        half = own[n].shape[1] // 2
        for h, near, second in ((0, 1, 4), (1, 3, 5)):
            hop(n, near, X).wait_recv()
            hop(n, second, X).wait_recv()
            add_into(dst.at[pl.ds(h * half, half)], (piece(n, q0, h), land[n].at[near], land[n].at[second]))
    @tiles(D, 256)
    def _(c):
        r.upg[c.start // 256] = dot(r.sec_all[:, c], r.gul[...], 0, 0)
    plane_start(0)
    for fc in range(FT // 256):
        for nh in range(D // 512):
            g = dot(r.hid[:, fc * 256:(fc + 1) * 256], r.cot_all[:, nh * 512:(nh + 1) * 512], 0, 0)
            n = 256 // FB
            for q in range(n): r.dng[fc * n + q, :, nh * 512:(nh + 1) * 512] = g[q * FB:(q + 1) * FB]
    plane_middle(0)
    plane_start(1)
    z_final(r.glf)
    for k, j in enumerate(ps):
        for q in range(2):
            push(r.glf.at[pl.ds(pl.multiple_of(j * HB, HB), HB), pl.ds(q * 128, 128)], r.glu_out.at[:, lane(q * D + i * 128, 128)],
                 r.ga.at[0, q, k], r.ga.at[1, q, k], {"seq": p["base"] + j})
    for q in range(2):
        r.glu_out[:, lane(q * D + i * 128, 128)] = r.glf[pl.ds(pl.multiple_of(i * HB, HB), HB), pl.ds(q * 128, 128)]
    plane_end(0, r.upf)
    for k, w in enumerate(group):
        push(r.upf.at[pl.ds(pl.multiple_of(w * HB, HB), HB)], r.uland.at[w8], r.ua.at[0, k], r.ua.at[1, k], seat(w))
    r.uland[w8] = r.upf[pl.ds(pl.multiple_of(w8 * HB, HB), HB), :]
    acc = r.mine[...]
    for k in range(Z - 1):
        src = lax.rem(z + Z - 1 - k, Z)
        remote(r.mine, r.zland.at[src], r.sz.at[0, k], r.sz.at[1, k], zu).wait_recv()
        acc = acc + r.zland[src]
    r.tot[...] = acc
    plane_middle(1)
    for k in range(7):
        src = lax.rem(i + 7 - k, 8)
        remote(r.st.at[src], r.st.at[src], r.sb.at[0, k], r.sb.at[1, k], nxt).wait_recv()
        for q in range(2):
            blk = r.glu_out.at[:, lane(q * D + src * 128, 128)]
            remote(blk, blk, r.ga.at[0, q, k], r.ga.at[1, q, k], nxt).wait_recv()
    for k in range(7):
        src = lax.rem(w8 + 7 - k, 8)
        remote(r.uland.at[src], r.uland.at[src], r.ua.at[0, k], r.ua.at[1, k], nxt).wait_recv()
    for w in range(8):
        for q in range(4): r.up_out[:, (q * 8 + w) * FB:(q * 8 + w + 1) * FB] = r.uland[w, :, q * FB:(q + 1) * FB]
    plane_end(1, r.down_o)

    pl.when(s < NSEQ - 1)(lambda: halo_copy.wait_send())
    pl.when(s > 0)(lambda: tail_copy.wait_send())
    for c in gm_sends + sends + small_sends(): c.wait_send()
    gc.drain()
    gs.drain()
    ga.drain()
    z_drain()
    for n in range(2):
        for k in range(6): hop(n, k, X).wait_send()


def layer(cfg, tabs, vecs, rate, freq, cre, cim, prior, x, cot, glu_w, up_w, down_w, cid):
    Z, NSEQ, nbits, T, D, FF, M = cfg
    FT, HB = FF // 8, D // 8 // Z
    NR = 4 * M + 16 + 2 * M
    NT = NR
    vm, hbm = pl.BlockSpec(memory_space=pltpu.VMEM), pl.BlockSpec(memory_space=pl.ANY)
    S = lambda shape, dt=F32: jax.ShapeDtypeStruct(shape, dt)
    ins = dict(ftab=vm, itab=vm, jtab=vm, gtab=vm, **{f"v{k}": vm for k in range(8)}, rate=vm, freq=vm, cre=vm, cim=vm, prior=vm, x=vm, cot=vm,
               glu_w=hbm, up_w=hbm, down_w=hbm)
    outs = dict(out=S((T, D), BF16), ig=S((T, D), BF16), st=S((8, 2 * M, 128)), tot=S((NT, 128)), down_o=S((FT // Z, D)),
                up_out=S((HB, FF)), glu_out=S((HB, 2 * D)))
    V, DS = pltpu.VMEM, lambda *n: pltpu.SemaphoreType.DMA(n)
    row = lambda: V((T, D), F32)
    scr = dict(
        vecs=V((8, D), F32), upb=V((8, FT), F32),
        xs=row(), own_cot=row(), own_sec=row(), own_act=row(), halo=row(), tail=row(), xhat=row(), pre=row(), val=row(), sg=row(),
        merged=row(), mhat=row(), gm=row(), gz=row(), oacc=row(), sacc=row(), resp=row(), kern=row(),
        xinv=V((T, 128), F32), minv=V((T, 128), F32), ext=V((2 * T, D), F32), X=V((2 * KLEN, D), F32), K=V((2 * KLEN, D), F32),
        land_cot=V((8, T, D), F32), land_sec=V((8, T, D), F32), land_act=V((8, T, D), F32),
        cot_all=V((8 * T, D), BF16), sec_all=V((8 * T, D), BF16), act_all=V((8 * T, D), BF16),
        gw=V((D, 2 * D), BF16), wu=V((2, D, FT), BF16), wd=V((2, FT, D), BF16), wgs=V((D, 256), BF16),
        u=V((256, FT), F32), gh=V((256, FT), F32), hid=V((8 * T, FT), BF16), gul=V((8 * T, FT), BF16),
        glow=V((T, 2 * D), BF16), gm_all=V((8, T, 128), F32), ggl=V((8 * T, 256), BF16),
        upg=V((Z, D // Z, FT), F32), glg=V((Z, D // Z, 256), F32), dng=V((Z, FT // Z, D), F32),
        lup=V((6, D // 8, FT), F32), ldn=V((6, FF // 64, D), F32), uland=V((8, HB, FT), F32), ubg=V((8, FT), F32), upbs=V((8, FT), F32),
        lgl=V((2, Z - 1, D // Z, 256), F32), upf=V((D // Z, FT), F32), glf=V((D // Z, 256), F32),
        qr=V((16, M, LT), F32), qi=V((16, M, LT), F32), big=V((64 * M, LT), F32),
        ssrc=V((NR, D), F32), sland=V((8, NR, 128), F32), mine=V((NT, 128), F32), zland=V((Z, NT, 128), F32),
        lsem=DS(3), tsem=DS(2, 2), hsem=DS(4), gss=DS(14), gsr=DS(14), ms=DS(7), mr=DS(7), zs=DS(2, Z - 1), zr=DS(2, Z - 1),
        lss=DS(2, 3, 2 * Z - 1, 2), lsr=DS(2, 3, 2 * Z - 1, 2), rs=DS(2, 2, 6), ssem=DS(2, 4),
        sa=DS(2, 7), ua=DS(2, 7), sb=DS(2, 7), ga=DS(2, 2, 7), sz=DS(2, Z - 1))
    names = (*ins, *outs, *scr)
    res = pl.pallas_call(
        functools.partial(layer_kernel, cfg, names),
        out_shape=list(outs.values()), in_specs=list(ins.values()), out_specs=[vm] * len(outs), scratch_shapes=list(scr.values()),
        compiler_params=pltpu.CompilerParams(collective_id=cid, has_side_effects=True, vmem_limit_bytes=67043328),
        name="layer")(*tabs, *vecs, rate, freq, cre, cim, prior, x, cot, glu_w, up_w, down_w)
    return dict(zip(outs, res))


def finish_kernel(cfg, names, *refs):
    r = Bag()
    r.__dict__.update(zip(names, refs))
    Z, NSEQ, nbits, T, D, FF, M = cfg
    HB = D // 8 // Z
    b = lax.axis_index("batch")
    for k in ("out", "ig", "glu_out", "up_out", "down_o"): r.__dict__["o_" + k][...] = r.__dict__[k][...]
    for j in range(8): r.o_st[:, j * 128:(j + 1) * 128] = r.st[j]
    r.turned[...] = r.tot[0:4 * M, :].T
    mine = r.turned[pl.ds(pl.multiple_of(b * HB, HB), HB), :]
    for k in range(4): r.__dict__[f"m{k}"][...] = mine[:, k * M:(k + 1) * M]
    v = pltpu.roll(r.tot[4 * M:4 * M + 8, :], lax.rem(128 - b * HB, 128), 1)
    for k in range(6): r.__dict__[f"w{k}"][...] = v[k, 0:HB]
    per = 128 // (2 * HB)
    g = r.tot[pl.ds(4 * M + 6 + b // per, 1), :]
    r.gb[...] = pltpu.roll(jnp.broadcast_to(g, (8, 128)), lax.rem(128 - lax.rem(b, per) * 2 * HB, 128), 1)[0, 0:2 * HB]
    r.ub[...] = r.tot[pl.ds(4 * M + 8 + b, 1), :].reshape(128)


def finish(cfg, o):
    Z, NSEQ, nbits, T, D, FF, M = cfg
    HB = D // 8 // Z
    vm = pl.BlockSpec(memory_space=pltpu.VMEM)
    S = lambda shape, dt=F32: jax.ShapeDtypeStruct(shape, dt)
    outs = {"o_" + k: S(o[k].shape, o[k].dtype) for k in ("out", "ig", "glu_out", "up_out", "down_o")}
    outs["o_st"] = S((2 * M, D))
    outs.update({f"m{k}": S((HB, M)) for k in range(4)})
    outs.update({f"w{k}": S((HB,)) for k in range(6)})
    outs.update(gb=S((2 * HB,)), ub=S((FF // 8 // Z,)))
    names = (*o, *outs, "turned")
    res = pl.pallas_call(functools.partial(finish_kernel, cfg, names), out_shape=list(outs.values()), in_specs=[vm] * len(o),
                         out_specs=[vm] * len(outs), scratch_shapes=[pltpu.VMEM((128, 4 * M), F32)], name="finish")(*o.values())
    return {k.removeprefix("o_"): v for k, v in zip(outs, res)}


def tables(window):
    half = window // 2
    f = np.concatenate([np.arange(half + 1), np.arange(1, half)])[:, None]
    imag = np.arange(window)[:, None] > half
    ph = (f * np.arange(window)[None, :] % window) * (2.0 * np.pi / window)
    fwd = np.where(imag, -np.sin(ph), np.cos(ph))
    wt = np.where((f == 0) | (2 * f == window), 1.0, 2.0) / window
    inv = (wt * fwd).T[half:]
    def parts(a):
        a = np.ascontiguousarray(a).astype(np.float32)
        high = a.astype(ml_dtypes.bfloat16)
        return jnp.asarray(np.stack([high, (a - high.astype(np.float32)).astype(ml_dtypes.bfloat16)]))
    return parts(fwd), parts(inv), parts(inv.T), parts(fwd.T)


def plane_shards(Z, n_seq, inputs, first_gain, first_shift, decay_rate, rotation, out_real, out_imag, skip_gain, glu_weight,
                 glu_bias, second_gain, second_shift, up_weight, up_bias, down_weight, down_bias, prior_state, cotangent):
    T, D = inputs.shape[1:]
    FF, M = up_weight.shape[1], decay_rate.shape[1]
    FT, HB = FF // 8, D // 8 // Z
    cfg = (Z, n_seq, max(1, (n_seq - 1).bit_length()), T, D, FF, M)
    vecs = (first_gain, first_shift, skip_gain, second_gain, second_shift, down_bias, glu_bias, up_bias)
    o = layer(cfg, tables(T + KLEN), vecs, decay_rate.T, rotation.T, out_real.T, out_imag.T, prior_state,
              inputs[0], cotangent[0], glu_weight, up_weight, down_weight, 0)
    f = finish(cfg, o)
    v = [f[f"w{k}"] for k in range(6)]
    m = [f[f"m{k}"] for k in range(4)]
    return (f["out"][None], f["ig"][None], f["st"].reshape(1, 2, M, D), v[0], v[1], *m, v[2], f["glu_out"], f["gb"],
            v[3], v[4], f["up_out"], f["ub"], f["down_o"], v[5])


def solution(mesh):
    in_specs = (
        P("batch", "seq", None),
        P(),
        P(),
        P(),
        P(),
        P(),
        P(),
        P(),
        P(),
        P(),
        P(),
        P(),
        P(),
        P(),
        P(),
        P(),
        P("batch", None, None, None),
        P("batch", "seq", None),
    )
    out_specs = (
        P("batch", "seq", None),
        P("batch", "seq", None),
        P("batch", None, None, None),
        P(("seq", "batch")),
        P(("seq", "batch")),
        P(("seq", "batch"), None),
        P(("seq", "batch"), None),
        P(("seq", "batch"), None),
        P(("seq", "batch"), None),
        P(("seq", "batch")),
        P(("seq", "batch"), None),
        P(("seq", "batch")),
        P(("seq", "batch")),
        P(("seq", "batch")),
        P(("seq", "batch"), None),
        P(("seq", "batch")),
        P(("seq", "batch"), None),
        P(("seq", "batch")),
    )
    body = shards
    if mesh.shape["seq"] == 8:
        body = functools.partial(plane_shards, mesh.shape["batch"], mesh.shape["seq"])
    return jax.shard_map(body, mesh=mesh, in_specs=in_specs, out_specs=out_specs, check_vma=False)
```

```python
import functools
import math

import jax
import jax.numpy as jnp
import ml_dtypes
import numpy as np
from jax import lax
from jax.experimental import pallas as pl
from jax.experimental.pallas import tpu as pltpu
from jax.sharding import PartitionSpec as P

KLEN = 128
LT = 128
MESH = pl.DeviceIdType.MESH
F32, BF16 = jnp.float32, jnp.bfloat16


EPSILON = 1e-05
HIGHEST = lax.Precision.HIGHEST


def from_behind(value, axis, by):
    peers = lax.axis_size(axis)
    pairs = [(i, i + by) for i in range(peers) if 0 <= i + by < peers]
    return lax.ppermute(value, axis, pairs)


def norm_rows(values, gain, shift):
    center = values - jnp.mean(values, axis=-1, keepdims=True)
    spread = jnp.mean(center * center, axis=-1, keepdims=True)
    return center * lax.rsqrt(spread + EPSILON) * gain + shift


def mode_terms(rate_modes, freq_modes, elapsed):
    moment = elapsed[None, :, None]
    damping = jnp.exp(-rate_modes[:, None, :] * moment)
    return (
        damping * jnp.cos(freq_modes[:, None, :] * moment),
        damping * jnp.sin(freq_modes[:, None, :] * moment),
    )


def glu_gate(glu_pre):
    split_at = glu_pre.shape[-1] // 2
    return glu_pre[:, :split_at] * jax.nn.sigmoid(glu_pre[:, split_at:])


def gelu_exact(values):
    return jax.nn.gelu(values, approximate=False)


def shards(
    inputs,
    first_gain,
    first_shift,
    decay_rate,
    rotation,
    out_real,
    out_imag,
    skip_gain,
    glu_weight,
    glu_bias,
    second_gain,
    second_shift,
    up_weight,
    up_bias,
    down_weight,
    down_bias,
    prior_state,
    cotangent,
):
    seg_count, tok_count, feature = inputs.shape
    row_count = seg_count * tok_count
    window = tok_count + KLEN
    half = window // 2 + 1
    offset = lax.axis_index("seq") * tok_count
    freq_index = jnp.arange(half, dtype=jnp.int32)
    time_index = jnp.arange(window, dtype=jnp.int32)
    phase = (freq_index[:, None] * time_index[None, :] % window).astype(jnp.float32) * (
        2.0 * math.pi / window
    )
    cos_half = jnp.cos(phase)
    sin_half = jnp.sin(phase)
    forward_table = jnp.concatenate([cos_half, -sin_half], axis=0)
    weights = jnp.where((freq_index == 0) | (2 * freq_index == window), 1.0, 2.0).astype(
        jnp.float32
    )
    inverse_table = (
        jnp.concatenate(
            [(weights[:, None] * cos_half).T, -(weights[:, None] * sin_half).T], axis=1
        )[KLEN:]
        / window
    )
    local_steps = jnp.arange(tok_count).astype(jnp.float32)
    advance_steps = (offset + 1).astype(jnp.float32)

    def mixing(
        normed, halo_rows, rate_modes, freq_modes, real_modes, imag_modes, skip_local, prior_local
    ):
        table_real, table_imag = mode_terms(rate_modes, freq_modes, local_steps)
        kernel = jnp.einsum("mkh,mh->kh", table_real, real_modes, precision=HIGHEST) - jnp.einsum(
            "mkh,mh->kh", table_imag, imag_modes, precision=HIGHEST
        )
        extended = jnp.concatenate([halo_rows, normed], axis=1)
        spectrum = jnp.einsum("ft,sth->sfh", forward_table, extended, precision=HIGHEST)
        kern_spec = jnp.dot(forward_table[:, :KLEN], kernel, precision=HIGHEST)
        spec_real, spec_imag = (spectrum[:, :half], spectrum[:, half:])
        kern_real, kern_imag = (kern_spec[:half], kern_spec[half:])
        product = jnp.concatenate(
            [
                spec_real * kern_real - spec_imag * kern_imag,
                spec_real * kern_imag + spec_imag * kern_real,
            ],
            axis=1,
        )
        convolved = jnp.einsum("tf,sfh->sth", inverse_table, product, precision=HIGHEST)
        damping = jnp.exp(-rate_modes * advance_steps)
        adv_real = damping * jnp.cos(freq_modes * advance_steps)
        adv_imag = damping * jnp.sin(freq_modes * advance_steps)
        coef_real = real_modes * adv_real - imag_modes * adv_imag
        coef_imag = real_modes * adv_imag + imag_modes * adv_real
        drive_real = coef_real * prior_local[:, 0] - coef_imag * prior_local[:, 1]
        drive_imag = coef_real * prior_local[:, 1] + coef_imag * prior_local[:, 0]
        response = jnp.einsum(
            "mth,smh->sth", table_real, drive_real, precision=HIGHEST
        ) - jnp.einsum("mth,smh->sth", table_imag, drive_imag, precision=HIGHEST)
        return gelu_exact(convolved + skip_local * normed + response)

    source = inputs.astype(jnp.float32)
    normed, first_pull = jax.vjp(norm_rows, source, first_gain, first_shift)
    halo_rows = from_behind(normed, "seq", 1)
    activated, mix_pull = jax.vjp(
        mixing,
        normed,
        halo_rows,
        decay_rate.T,
        rotation.T,
        out_real.T,
        out_imag.T,
        skip_gain,
        prior_state,
    )
    activated_low = activated.reshape(row_count, feature).astype(jnp.bfloat16)
    glu_pre = jnp.dot(activated_low, glu_weight, preferred_element_type=jnp.float32) + glu_bias
    branch, glu_pull = jax.vjp(glu_gate, glu_pre)
    merged = source.reshape(row_count, feature) + branch
    second, second_pull = jax.vjp(norm_rows, merged, second_gain, second_shift)
    second_low = second.astype(jnp.bfloat16)
    up_pre = jnp.dot(second_low, up_weight, preferred_element_type=jnp.float32) + up_bias
    hidden, hidden_pull = jax.vjp(gelu_exact, up_pre)
    hidden_low = hidden.astype(jnp.bfloat16)
    result = (
        merged + jnp.dot(hidden_low, down_weight, preferred_element_type=jnp.float32) + down_bias
    )
    outputs = result.astype(jnp.bfloat16).reshape(seg_count, tok_count, feature)
    grad_out = cotangent.astype(jnp.float32).reshape(row_count, feature)
    down_bias_grad = jnp.sum(grad_out, axis=0)
    grad_low = grad_out.astype(jnp.bfloat16)
    down_grad = jnp.einsum("rf,rh->fh", hidden_low, grad_low, preferred_element_type=jnp.float32)
    grad_hidden = jnp.einsum("rh,fh->rf", grad_low, down_weight, preferred_element_type=jnp.float32)
    (grad_up,) = hidden_pull(grad_hidden)
    up_bias_grad = jnp.sum(grad_up, axis=0)
    up_low = grad_up.astype(jnp.bfloat16)
    up_grad = jnp.einsum("rh,rf->hf", second_low, up_low, preferred_element_type=jnp.float32)
    grad_second = jnp.einsum("rf,hf->rh", up_low, up_weight, preferred_element_type=jnp.float32)
    grad_merged, second_gain_grad, second_shift_grad = second_pull(grad_second)
    grad_merged = grad_merged + grad_out
    (grad_glu,) = glu_pull(grad_merged)
    glu_bias_grad = jnp.sum(grad_glu, axis=0)
    glu_low = grad_glu.astype(jnp.bfloat16)
    glu_grad = jnp.einsum("rh,rg->hg", activated_low, glu_low, preferred_element_type=jnp.float32)
    grad_activated = jnp.einsum(
        "rg,hg->rh", glu_low, glu_weight, preferred_element_type=jnp.float32
    )
    grad_normed, grad_halo, rate_grad, freq_grad, real_grad, imag_grad, skip_grad, prior_grad = (
        mix_pull(grad_activated.reshape(seg_count, tok_count, feature))
    )
    grad_tail = from_behind(grad_halo, "seq", -1)
    grad_normed = jnp.concatenate(
        [grad_normed[:, : tok_count - KLEN], grad_normed + grad_tail], axis=1
    )
    grad_source, first_gain_grad, first_shift_grad = first_pull(grad_normed)
    input_grad = (grad_source + grad_merged.reshape(seg_count, tok_count, feature)).astype(
        jnp.bfloat16
    )
    state_grad = lax.psum(prior_grad, "seq")
    rate_back = rate_grad.T
    freq_back = freq_grad.T
    real_back = real_grad.T
    imag_back = imag_grad.T
    summed = (
        lax.psum_scatter(first_gain_grad, ("seq", "batch"), scatter_dimension=0, tiled=True),
        lax.psum_scatter(first_shift_grad, ("seq", "batch"), scatter_dimension=0, tiled=True),
        lax.psum_scatter(rate_back, ("seq", "batch"), scatter_dimension=0, tiled=True),
        lax.psum_scatter(freq_back, ("seq", "batch"), scatter_dimension=0, tiled=True),
        lax.psum_scatter(real_back, ("seq", "batch"), scatter_dimension=0, tiled=True),
        lax.psum_scatter(imag_back, ("seq", "batch"), scatter_dimension=0, tiled=True),
        lax.psum_scatter(skip_grad, ("seq", "batch"), scatter_dimension=0, tiled=True),
        lax.psum_scatter(glu_grad, ("seq", "batch"), scatter_dimension=0, tiled=True),
        lax.psum_scatter(glu_bias_grad, ("seq", "batch"), scatter_dimension=0, tiled=True),
        lax.psum_scatter(second_gain_grad, ("seq", "batch"), scatter_dimension=0, tiled=True),
        lax.psum_scatter(second_shift_grad, ("seq", "batch"), scatter_dimension=0, tiled=True),
        lax.psum_scatter(up_grad, ("seq", "batch"), scatter_dimension=0, tiled=True),
        lax.psum_scatter(up_bias_grad, ("seq", "batch"), scatter_dimension=0, tiled=True),
        lax.psum_scatter(down_grad, ("seq", "batch"), scatter_dimension=0, tiled=True),
        lax.psum_scatter(down_bias_grad, ("seq", "batch"), scatter_dimension=0, tiled=True),
    )
    return (
        outputs,
        input_grad,
        state_grad,
        summed[0],
        summed[1],
        summed[2],
        summed[3],
        summed[4],
        summed[5],
        summed[6],
        summed[7],
        summed[8],
        summed[9],
        summed[10],
        summed[11],
        summed[12],
        summed[13],
        summed[14],
    )


def plane():
    s = lax.axis_index("seq")
    i = lax.rem(s, 8)
    base = s - i
    c, x, y = lax.rem(i, 2), lax.rem(i // 2, 2), i // 4
    ic, ix, iy = i + 1 - 2 * c, i + 2 - 4 * x, i + 4 - 8 * y
    idg = iy + 2 - 4 * x
    return dict(s=s, i=i, base=base, c=c, x=x, y=y, ic=ic, ix=ix, iy=iy, idg=idg)

def sib_of(p, j):
    return j + 1 - 2 * p["c"]

def remote(src, dst, ss, rs, dev):
    return pltpu.make_async_remote_copy(src_ref=src, dst_ref=dst, send_sem=ss, recv_sem=rs,
                                        device_id=dev, device_id_type=MESH)

def greet(devs):
    bar = pltpu.get_barrier_semaphore()
    for d in devs:
        pl.semaphore_signal(bar, inc=1, device_id=d, device_id_type=MESH)
    pl.semaphore_wait(bar, len(devs))

def peers(p):
    return [lax.rem(p["i"] + k, 8) for k in range(1, 8)]

class Gather:
    def __init__(self, p, own, land, ssem, rsem):
        self.p, self.own, self.land, self.ss, self.rs = p, own, land, ssem, rsem
        self.H = own.shape[0] // 2
        seq = lambda j: {"seq": p["base"] + j}
        self.X, self.Y, self.S = seq(p["ix"]), seq(p["iy"]), seq(p["ic"])

    def cp(self, k, j, h, dev, src=None):
        blk = self.land.at[j, pl.ds(h * self.H, self.H)]
        return remote(blk if src is None else src, blk, self.ss.at[k], self.rs.at[k], dev)

    def plan(self):
        i, ix, iy, idg = self.p["i"], self.p["ix"], self.p["iy"], self.p["idg"]
        return [(0, i, 0, self.X), (2, i, 1, self.Y), (1, i, 1, self.X), (3, i, 0, self.Y), (6, i, 0, self.S), (7, i, 1, self.S),
                (4, ix, 0, self.Y), (8, ix, 0, self.S), (5, iy, 1, self.X), (11, iy, 1, self.S), (9, ix, 1, self.S),
                (10, iy, 0, self.S), (12, idg, 0, self.S), (13, idg, 1, self.S)]

    def _send(self, k, own=False):
        k, j, h, dev = next(e for e in self.plan() if e[0] == k)
        self.cp(k, j, h, dev, self.own.at[pl.ds(h * self.H, self.H)] if own else None).start()

    def _got(self, k, j, h):
        self.cp(k, j, h, self.S).wait_recv()

    def start(self):
        for k in (0, 2, 1, 3, 6, 7):
            self._send(k, True)

    def relay1(self):
        p = self.p
        self._got(0, p["ix"], 0); self._send(4); self._send(8)
        self._got(2, p["iy"], 1); self._send(5); self._send(11)

    def relay2(self):
        p = self.p
        self._got(1, p["ix"], 1); self._send(9)
        self._got(3, p["iy"], 0); self._send(10)

    def relay3(self):
        p = self.p
        self._got(4, p["idg"], 0); self._send(12)
        self._got(5, p["idg"], 1); self._send(13)

    def chip(self, which):
        p = self.p
        k, j = {"own": (6, p["ic"]), "x": (8, sib_of(p, p["ix"])), "y": (10, sib_of(p, p["iy"])), "d": (12, sib_of(p, p["idg"]))}[which]
        self._got(k, j, 0)
        self._got(k + 1, j, 1)
        return (j,) if which == "own" else ({"x": p["ix"], "y": p["iy"], "d": p["idg"]}[which], j)

    def drain(self):
        for k, j, h, dev in self.plan():
            self.cp(k, j, h, dev).wait_send()


class Line:
    def __init__(self, Z, z, p, own, land, ssem, rsem, zu, zd):
        self.Z, self.z, self.c, self.own, self.land, self.ss, self.rs = Z, z, p["c"], own, land, ssem, rsem
        self.H = own.shape[0] // 2
        self.dev = (zu, zd, {"seq": p["base"] + p["ic"]})

    def part(self, chip, core, half):
        return self.land.at[chip * 2 + core, pl.ds(half * self.H, self.H)]

    def cp(self, way, hop, half, chip, core, own=False):
        blk = self.part(chip, core, half)
        src = self.own.at[pl.ds(half * self.H, self.H)] if own else blk
        return remote(src, blk, self.ss.at[way, hop, half], self.rs.at[way, hop, half], self.dev[way])

    def ends(self):
        z, Z = self.z, self.Z
        return ((lambda h: z - h, lambda h: z - h >= 0, z < Z - 1), (lambda h: z + h, lambda h: z + h < Z, z > 0))

    def start(self):
        for half in range(2):
            for way, (chip, there, on) in enumerate(self.ends()):
                pl.when(on)(lambda: self.cp(way, 0, half, self.z, self.c, True).start())
        for half in range(2): self.cp(2, 0, half, self.z, self.c, True).start()

    def _take(self, way, hop, half, chip):
        self.cp(way, hop - 1, half, chip, self.c).wait_recv()
        self.cp(2, hop + way * (self.Z - 1), half, chip, self.c).start()

    def pass_on(self, hop, half):
        for way, (chip, there, on) in enumerate(self.ends()):
            @pl.when(there(hop) & on)
            def _():
                self._take(way, hop, half, chip(hop))
                self.cp(way, hop, half, chip(hop), self.c).start()

    def settle(self, chip_at):
        for way, (chip, there, on) in enumerate(self.ends()):
            for hop in range(1, self.Z):
                @pl.when(chip_at == chip(hop))
                def _():
                    for half in range(2):
                        pl.when(jnp.logical_not(on))(lambda: self._take(way, hop, half, chip(hop)))
                    for half in range(2):
                        self.cp(2, hop + way * (self.Z - 1), half, chip(hop), 1 - self.c).wait_recv()

    def settle_own(self):
        for half in range(2): self.cp(2, 0, half, self.z, 1 - self.c).wait_recv()

    def drain(self):
        for half in range(2):
            self.cp(2, 0, half, self.z, self.c, True).wait_send()
            for way, (chip, there, on) in enumerate(self.ends()):
                for hop in range(self.Z - 1):
                    pl.when(there(hop) & on)(lambda: self.cp(way, hop, half, chip(hop), self.c).wait_send())
                for hop in range(1, self.Z):
                    pl.when(there(hop))(lambda: self.cp(2, hop + way * (self.Z - 1), half, chip(hop), self.c).wait_send())


def cmul(ar, ai, br, bi):
    return ar * br - ai * bi, ar * bi + ai * br

def lam_of(rate, freq):
    damp = jnp.exp(-rate)
    q = freq * freq
    cosv = 1.0 + q * (-1.0/2 + q * (1.0/24 + q * (-1.0/720 + q * (1.0/40320 + q * (-1.0/3628800)))))
    sinv = freq * (1.0 + q * (-1.0/6 + q * (1.0/120 + q * (-1.0/5040 + q * (1.0/362880)))))
    return damp * cosv, damp * sinv

def power_rows(lr, li, qr, qi, A):
    l2 = cmul(lr, li, lr, li); l4 = cmul(*l2, *l2); l8 = cmul(*l4, *l4)
    cur = (jnp.ones_like(lr), jnp.zeros_like(lr))
    for a in range(A):
        qr[a] = cur[0]; qi[a] = cur[1]
        cur = cmul(*cur, *l8)
    return l2, l4, cur

def offset_power(top, s, nbits):
    res = (jnp.ones_like(top[0]), jnp.zeros_like(top[0]))
    sq = top
    for bit in range(nbits):
        on = lax.rem(lax.div(s, 1 << bit), 2) == 1
        nxt = cmul(*res, *sq)
        res = (jnp.where(on, nxt[0], res[0]), jnp.where(on, nxt[1], res[1]))
        if bit + 1 < nbits: sq = cmul(*sq, *sq)
    return res

def fwd_tiles(nbits, lo, hi, rate, freq, cre, cim, prior, kern, resp, co):
    M = rate.shape[0]
    A = kern.shape[0] // 8
    s = lax.axis_index("seq")
    b = lax.broadcasted_iota(jnp.int32, (8, LT), 0)
    o1, o2, o4 = (b % 2) == 1, ((b // 2) % 2) == 1, b >= 4
    one, zero = jnp.ones((8, LT), F32), jnp.zeros((8, LT), F32)
    square = lambda v: cmul(*v, *v)
    @pl.loop(lo, hi)
    def _(lt):
        cols = pl.ds(pl.multiple_of(lt * LT, LT), LT)
        l1 = lam_of(rate[:, cols], freq[:, cols])
        l2 = square(l1)
        l4 = square(l2)
        l8 = square(l4)
        top = l8
        for _ in range((A - 1).bit_length()): top = square(top)
        off = cmul(*offset_power(top, s, nbits), *l1)
        c = cre[:, cols], cim[:, cols]
        d = cmul(*cmul(*c, *off), prior[0, 0, :, cols], prior[0, 1, :, cols])
        rows = (*l1, *l2, *l4, *c, *cmul(*c, *l8), *d, *cmul(*d, *l8), 2.0 * l8[0], -(l8[0] * l8[0] + l8[1] * l8[1]))
        for k, v in enumerate(rows): co[pl.ds(k * M, M), :] = v
        def step(m, accs):
            row = lambda k: jnp.broadcast_to(co[pl.ds(k * M + m, 1), :], (8, LT))
            e = jnp.where(o1, row(0), one), jnp.where(o1, row(1), zero)
            e = cmul(*e, jnp.where(o2, row(2), one), jnp.where(o2, row(3), zero))
            er, ei = cmul(*e, jnp.where(o4, row(4), one), jnp.where(o4, row(5), zero))
            p, q = row(14), row(15)
            k0, k1 = er * row(6) - ei * row(7), er * row(8) - ei * row(9)
            r0, r1 = er * row(10) - ei * row(11), er * row(12) - ei * row(13)
            out = list(accs)
            for a in range(A):
                out[2 * a] = out[2 * a] + k0
                out[2 * a + 1] = out[2 * a + 1] + r0
                if a < A - 1:
                    k0, k1 = k1, p * k1 + q * k0
                    r0, r1 = r1, p * r1 + q * r0
            return tuple(out)
        accs = lax.fori_loop(0, M, step, tuple(jnp.zeros((8, LT), F32) for _ in range(2 * A)), unroll=4)
        for a in range(A):
            kern[pl.ds(8 * a, 8), cols] = accs[2 * a]
            resp[pl.ds(8 * a, 8), cols] = accs[2 * a + 1]


def bwd_tiles(lo, hi, srow, nbits, TOK, rate, freq, cre, cim, prior, kg, gz, out, qr, qi, acc):
    M = rate.shape[0]
    A = kg.shape[0] // 8
    s = lax.axis_index("seq")
    adv = (s * TOK + 1).astype(F32)
    @pl.loop(lo, hi)
    def _(lt):
        cols = pl.ds(pl.multiple_of(lt * LT, LT), LT)
        lr, li = lam_of(rate[:, cols], freq[:, cols])
        l2, l4, top = power_rows(lr, li, qr, qi, A)
        def step(m, carry):
            for j, g in enumerate((kg, gz)):
                z = jnp.zeros((8, LT), F32)
                sr, si, tr, ti = z, z, z, z
                for a in range(A - 1, -1, -1):
                    ga = g[pl.ds(8 * a, 8), cols]
                    sr = sr + ga * qr[a, pl.ds(m, 1), :]
                    si = si + ga * qi[a, pl.ds(m, 1), :]
                    if a > 0:
                        tr = tr + sr
                        ti = ti + si
                for q, v in enumerate((sr, si, tr, ti)):
                    acc[pl.ds(pl.multiple_of(((4 * j + q) * M + m) * 8, 8), 8), :] = v
            return carry
        lax.fori_loop(0, M, step, 0, unroll=4)
        pw = (jnp.ones_like(lr), jnp.zeros_like(lr))
        zero = jnp.zeros_like(lr)
        ar, ai, br, bi = [zero] * 2, [zero] * 2, [zero] * 2, [zero] * 2
        for b in range(8):
            for j in range(2):
                ld = lambda q: acc[pl.ds((4 * j + q) * M * 8 + b, M, stride=8), :]
                S = ld(0), ld(1)
                U = 8.0 * ld(2), 8.0 * ld(3)
                if b: U = U[0] + float(b) * S[0], U[1] + float(b) * S[1]
                w = cmul(*pw, *S)
                ar[j], ai[j] = ar[j] + w[0], ai[j] + w[1]
                w = cmul(*pw, *U)
                br[j], bi[j] = br[j] + w[0], bi[j] + w[1]
            pw = cmul(*pw, lr, li)
        off = cmul(*offset_power(top, s, nbits), lr, li)
        c = cre[:, cols], cim[:, cols]
        ps = cmul(*off, prior[0, 0, :, cols], prior[0, 1, :, cols])
        u = cmul(*ps, ar[1], ai[1])
        v = cmul(*ps, br[1] + adv * ar[1], bi[1] + adv * ai[1])
        v = cmul(*c, v[0] + br[0], v[1] + bi[0])
        w = cmul(*cmul(*c, *off), ar[1], ai[1])
        for k, val in enumerate((-v[0], -v[1], u[0] + ar[0], -(u[1] + ai[0]))): out[k * M:(k + 1) * M, cols] = val
        for k, val in enumerate((w[0], -w[1])): out[srow + k * M:srow + (k + 1) * M, cols] = val


class Bag:
    pass


def dot(a, b, ca=1, cb=0):
    return lax.dot_general(a, b, (((ca,), (cb,)), ((), ())), preferred_element_type=F32)


def split_low(v):
    high = v.astype(BF16)
    return high, (v - high.astype(F32)).astype(BF16)


def table_dot(tab, v, rows=slice(None), cols=slice(None)):
    high, low = split_low(v)
    th, tl = tab[0, rows, cols], tab[1, rows, cols]
    return dot(th, high) + dot(th, low) + dot(tl, high)


def gelu_both(u):
    cdf = 0.5 + 0.5 * lax.erf(u * (0.5 ** 0.5))
    return u * cdf, cdf + u * (jnp.exp(-0.5 * u * u) * ((2.0 * math.pi) ** -0.5))


def tiles(n, step):
    def run(body, init=None):
        if init is None:
            @pl.loop(0, n // step)
            def _(k):
                body(pl.ds(pl.multiple_of(k * step, step), step))
            return None
        return lax.fori_loop(0, n // step, lambda k, c: body(pl.ds(pl.multiple_of(k * step, step), step), c), init)
    return run


def sub(off, q):
    return pl.ds(pl.multiple_of(off + q.start, q.size), q.size)


def row_mean(v):
    return jnp.sum(v, axis=-1, keepdims=True) * (1.0 / v.shape[-1])


def norm_hat(v):
    center = v - row_mean(v)
    inv = lax.rsqrt(row_mean(center * center) + EPSILON)
    return center * inv, inv


def norm_back(gg, hat, inv):
    return inv * (gg - row_mean(gg) - hat * row_mean(gg * hat))


def fold(v):
    return jnp.sum(v, axis=0, keepdims=True)


LC = 256
ROWS = 8
VEC = ("first_gain", "first_shift", "skip_gain", "second_gain", "second_shift", "down_bias", "value_bias", "gate_bias")


def layer_kernel(cfg, names, *refs):
    r = Bag()
    r.__dict__.update(zip(names, refs))
    Z, NSEQ, nbits, T, D, FF, M = cfg
    FT = FF // 8
    HB = D // 8 // Z
    p = plane()
    s, i = p["s"], p["i"]
    z = lax.axis_index("batch")
    vec = {k: (lambda q: (lambda c=slice(None): r.vecs[q:q + 1, c]))(q) for q, k in enumerate(VEC)}
    iblk = pl.ds(pl.multiple_of(i * T, T), T)
    w8, own8 = p["c"] * Z + z, z * 2 + p["c"]
    q0, qx, qy, qd = (v // 2 for v in (i, p["ix"], p["iy"], p["idg"]))
    FB = FF // 32

    for q, ref in enumerate((r.v0, r.v1, r.v2, r.v3, r.v4, r.v5)): r.vecs[q:q + 1, :] = ref[...].reshape(1, D)
    for q in range(2): r.vecs[6 + q:7 + q, :] = r.v6[q * D:(q + 1) * D].reshape(1, D)
    for q in range(8): r.upb[q:q + 1, :] = r.v7[q * FT:(q + 1) * FT].reshape(1, FT)

    lane = lambda off, n: pl.ds(pl.multiple_of(off, 128), n)
    local = lambda src, dst, sem: pltpu.make_async_copy(src, dst, sem)
    gw_copy = local(r.glu_w, r.gw, r.lsem.at[0])
    gw_copy.start()
    def tile_copy(t, slot):
        return (local(r.up_w.at[:, lane(t * FT, FT)], r.wu.at[slot], r.tsem.at[0, slot]),
                local(r.down_w.at[pl.ds(pl.multiple_of(t * FT, FT), FT)], r.wd.at[slot], r.tsem.at[1, slot]))
    for t in range(2):
        for c in tile_copy(t, t): c.start()
    def slice_copy():
        return [c for q in range(4) for c in (
            local(r.up_w.at[:, lane((q * 8 + w8) * FB, FB)], r.wu.at[0, :, pl.ds(q * FB, FB)], r.ssem.at[0, q]),
            local(r.down_w.at[pl.ds(pl.multiple_of((q * 8 + w8) * FB, FB), FB)], r.wd.at[0, pl.ds(q * FB, FB)], r.ssem.at[1, q]))]
    wgs_copy = [local(r.glu_w.at[:, lane(q * D + i * 128, 128)], r.wgs.at[:, pl.ds(q * 128, 128)], r.lsem.at[1 + q]) for q in range(2)]
    for c in wgs_copy: c.start()

    @tiles(T, 16)
    def _(q):
        r.xs[q, :] = r.x[q, :].astype(F32)
        r.own_cot[q, :] = r.cot[q, :].astype(F32)
    ps = peers(p)
    zu, zd = {"batch": lax.rem(z + 1, Z)}, {"batch": lax.rem(z + Z - 1, Z)}
    zp = [lax.rem(z + k, Z) for k in range(1, Z)]
    group = [lax.rem(w8 + k, 8) for k in range(1, 8)]
    seat = lambda w: {"seq": s - p["c"] + w // Z, "batch": lax.rem(w, Z)}
    greet([{"seq": p["base"] + j} for j in ps] + [{"seq": s - p["c"] + e, "batch": q} for q in zp for e in range(2)])
    nxt, prv = {"seq": lax.rem(s + 1, NSEQ)}, {"seq": lax.rem(s + NSEQ - 1, NSEQ)}
    halo_copy = remote(r.xs, r.halo, r.hsem.at[0], r.hsem.at[1], nxt)
    pl.when(s < NSEQ - 1)(lambda: halo_copy.start())
    gc = Line(Z, z, p, r.own_cot, r.land_cot, r.lss.at[0], r.lsr.at[0], zu, zd)
    gs = Line(Z, z, p, r.own_sec, r.land_sec, r.lss.at[1], r.lsr.at[1], zu, zd)
    ga = Gather(p, r.own_act, r.land_act, r.gss, r.gsr)
    gc.start()

    mode_args = (r.rate, r.freq, r.cre, r.cim, r.prior)
    fwd_tiles(nbits, 0, D // LT, *mode_args, r.kern, r.resp, r.big)
    gc.pass_on(1, 0)

    @tiles(T, ROWS)
    def _(q):
        hat, inv = norm_hat(r.xs[q, :])
        r.xhat[q, :] = hat
        r.xinv[q, :] = jnp.broadcast_to(inv, (ROWS, 128))
        r.ext[sub(T, q), :] = hat * vec["first_gain"]() + vec["first_shift"]()
    @pl.when(s > 0)
    def _():
        halo_copy.wait_recv()
    @pl.when(s == 0)
    def _():
        r.halo[...] = jnp.zeros_like(r.halo)
    keep = jnp.where(s == 0, 0.0, 1.0)
    @tiles(T, ROWS)
    def _(q):
        hat, _ = norm_hat(r.halo[q, :])
        r.ext[q, :] = (hat * vec["first_gain"]() + vec["first_shift"]()) * keep

    inner = lax.broadcasted_iota(jnp.int32, (KLEN, LC), 0) > 0
    @tiles(D, LC)
    def _(c):
        X = table_dot(r.ftab, r.ext[:, c])
        K = table_dot(r.ftab, r.kern[:, c], cols=slice(0, KLEN))
        r.X[:, c] = X
        r.K[:, c] = K
        P_, Q_, KP, KQ = X[:KLEN], X[KLEN:], K[:KLEN], K[KLEN:]
        qq = Q_ * KQ
        po = P_ * KP - jnp.where(inner, qq, 0.0)
        qo = jnp.where(inner, P_ * KQ + Q_ * KP, qq)
        y = table_dot(r.itab, jnp.concatenate([po, qo], 0))
        r.pre[:, c] = y + vec["skip_gain"](c) * r.ext[T:, c] + r.resp[:, c]
    @tiles(T, 16)
    def _(q):
        a = gelu_both(r.pre[q, :])[0].astype(BF16)
        r.own_act[q, :] = a.astype(F32)
        r.act_all[sub(i * T, q), :] = a
    gc.pass_on(1, 1)
    ga.start()

    gw_copy.wait()
    act = r.act_all[iblk, :]
    @tiles(D, LC)
    def _(c):
        r.val[:, c] = dot(act, r.gw[:, c])
        r.sg[:, c] = dot(act, r.gw[:, lane(D + c.start, LC)])
    @tiles(T, ROWS)
    def _(q):
        v = r.val[q, :] + vec["value_bias"]()
        g = jax.nn.sigmoid(r.sg[q, :] + vec["gate_bias"]())
        r.val[q, :] = v
        r.sg[q, :] = g
        m = r.xs[q, :] + v * g
        r.merged[q, :] = m
        hat, inv = norm_hat(m)
        r.mhat[q, :] = hat
        r.minv[q, :] = jnp.broadcast_to(inv, (ROWS, 128))
        r.own_sec[q, :] = (hat * vec["second_gain"]() + vec["second_shift"]()).astype(BF16).astype(F32)
    @tiles(T, 16)
    def _(q):
        r.sec_all[sub(own8 * T, q), :] = r.own_sec[q, :].astype(BF16)
    gs.start()
    gc.pass_on(2, 0)

    r.oacc[...] = jnp.zeros_like(r.oacc)
    r.sacc[...] = jnp.zeros_like(r.sacc)
    sec = r.sec_all[pl.ds(pl.multiple_of(own8 * T, T), T), :]
    @pl.loop(0, 8)
    def _(t):
        slot = lax.rem(t, 2)
        for c in tile_copy(t, slot): c.wait()
        r.u[pl.ds(0, T)] = dot(sec, r.wu[slot])
        r.gh[pl.ds(0, T)] = dot(r.cot[...], r.wd[slot], 1, 1)
        def rows_u(q, acc):
            hid, slope = gelu_both(r.u[q, :] + r.upb[pl.ds(t, 1), :])
            gu = r.gh[q, :] * slope
            r.hid[q, :] = hid.astype(BF16)
            r.gul[q, :] = gu.astype(BF16)
            return acc + jnp.sum(gu.reshape(2, 8, FT), 0)
        r.ubg[pl.ds(t, 1), :] = fold(tiles(T, 16)(rows_u, jnp.zeros((8, FT), F32)))
        r.oacc[...] += dot(r.hid[pl.ds(0, T), :], r.wd[slot])
        r.sacc[...] += dot(r.gul[pl.ds(0, T), :], r.wu[slot], 1, 1)
        @pl.when(t < 6)
        def _():
            for c in tile_copy(t + 2, slot): c.start()
        pl.when(t == 1)(lambda: gc.pass_on(2, 1))
        pl.when(t == 2)(ga.relay1)
        @pl.when(t == 5)
        def _():
            gs.pass_on(1, 0)
            ga.relay2()
    for c in slice_copy(): c.start()
    gs.pass_on(1, 1)
    ga.relay3()

    zero = jnp.zeros((ROWS, D), F32)
    def rows_a(q, carry):
        r.oacc[q, :] = r.merged[q, :] + r.oacc[q, :] + vec["down_bias"]()
        g, hat, c = r.sacc[q, :], r.mhat[q, :], r.own_cot[q, :]
        gm = c + norm_back(g * vec["second_gain"](), hat, r.minv[q, 0:1])
        r.gm[q, :] = gm
        return carry[0] + g * hat, carry[1] + g, carry[2] + c
    sums = tiles(T, ROWS)(rows_a, (zero,) * 3)
    for k, v in zip((3, 4, 5), sums): r.ssrc[4 * M + k:4 * M + k + 1, :] = fold(v)
    gm_sends = []
    for k, j in enumerate(ps):
        c = remote(r.gm.at[:, lane(j * 128, 128)], r.gm_all.at[i], r.ms.at[k], r.mr.at[k], {"seq": p["base"] + j})
        c.start()
        gm_sends.append(c)
    r.gm_all[i] = r.gm[:, lane(i * 128, 128)]
    @tiles(T, 16)
    def _(q):
        r.out[q, :] = r.oacc[q, :].astype(BF16)
    def rows_b(q, carry):
        gm, g = r.gm[q, :], r.sg[q, :]
        gv, gg = gm * g, gm * r.val[q, :] * g * (1.0 - g)
        r.glow[q, pl.ds(0, D)] = gv.astype(BF16)
        r.glow[q, pl.ds(D, D)] = gg.astype(BF16)
        return carry[0] + jnp.sum(gv.reshape(2, ROWS, D), 0), carry[1] + jnp.sum(gg.reshape(2, ROWS, D), 0)
    gb = tiles(T, 16)(rows_b, (zero,) * 2)
    gb = [fold(v) for v in gb]
    for j in range(8):
        for q in range(2):
            off = (j % 4) * 256 + q * 128
            r.ssrc[4 * M + 6 + q:4 * M + 7 + q, j * 128:(j + 1) * 128] = gb[j // 4][:, off:off + 128]
    glow = r.glow[...]
    @tiles(D, LC)
    def _(c):
        r.gz[:, c] = dot(glow, r.gw[c, :], 1, 1)
    @tiles(T, ROWS)
    def _(q):
        r.gz[q, :] = r.gz[q, :] * gelu_both(r.pre[q, :])[1]
    @tiles(D, LC)
    def _(c):
        G = table_dot(r.jtab, r.gz[:, c])
        gp, gq = G[:KLEN], G[KLEN:]
        def pair(ref):
            a, b = ref[pl.ds(0, KLEN), c], ref[pl.ds(KLEN, KLEN), c]
            bq = gq * b
            return jnp.concatenate([gp * a + jnp.where(inner, bq, 0.0), jnp.where(inner, gq * a - gp * b, bq)], 0)
        r.kern[:, c] = table_dot(r.gtab, pair(r.X), rows=slice(0, KLEN))
        r.ext[:, c] = table_dot(r.gtab, pair(r.K))
    tail_copy = remote(r.ext.at[pl.ds(0, T)], r.tail, r.hsem.at[2], r.hsem.at[3], prv)
    pl.when(s > 0)(lambda: tail_copy.start())
    bwd_args = (nbits, T, *mode_args, r.kern, r.gz, r.ssrc, r.qr, r.qi, r.big)
    srow = 4 * M + 16
    gs.pass_on(2, 0)
    bwd_tiles(0, 4, srow, *bwd_args)
    gs.pass_on(2, 1)
    bwd_tiles(4, D // LT, srow, *bwd_args)
    pl.when(s < NSEQ - 1)(lambda: tail_copy.wait_recv())
    @pl.when(s == NSEQ - 1)
    def _():
        r.tail[...] = jnp.zeros_like(r.tail)
    def rows_c(q, carry):
        hat, gz = r.xhat[q, :], r.gz[q, :]
        gn = r.ext[sub(T, q), :] + r.tail[q, :] + vec["skip_gain"]() * gz
        r.oacc[q, :] = r.gm[q, :] + norm_back(gn * vec["first_gain"](), hat, r.xinv[q, 0:1])
        return carry[0] + gn * hat, carry[1] + gn, carry[2] + gz * hat, carry[3] + gz
    sums = [fold(v) for v in tiles(T, ROWS)(rows_c, (zero,) * 4)]
    sums = (sums[0], sums[1], sums[2] * vec["first_gain"]() + sums[3] * vec["first_shift"]())
    for k, v in enumerate(sums): r.ssrc[4 * M + k:4 * M + k + 1, :] = v
    @tiles(T, 16)
    def _(q):
        r.ig[q, :] = r.oacc[q, :].astype(BF16)
    r.ssrc[4 * M + 8:4 * M + 16, :] = jnp.zeros((8, D), F32)
    for j in range(8):
        for e in range(FT // 128): r.ssrc[4 * M + 8 + e:4 * M + 9 + e, j * 128:(j + 1) * 128] = r.ubg[j:j + 1, e * 128:(e + 1) * 128]

    NR, NS = 4 * M + 16 + 2 * M, 2 * M
    sends = []
    def push(src, dst, a, b, dev):
        c = remote(src, dst, a, b, dev)
        c.start()
        sends.append(c)
    for k, j in enumerate(ps):
        push(r.ssrc.at[:, lane(j * 128, 128)], r.sland.at[i], r.sa.at[0, k], r.sa.at[1, k], {"seq": p["base"] + j})
    def small_sum():
        tot = r.ssrc[:, lane(i * 128, 128)]
        for k in range(7):
            src = lax.rem(i + 7 - k, 8)
            remote(r.sland.at[src], r.sland.at[src], r.sa.at[0, k], r.sa.at[1, k], nxt).wait_recv()
            tot = tot + r.sland[src]
        r.mine[...] = tot
        r.st[i] = tot[NR - NS:NR]
        for c in small_sends(): c.start()
    def small_sends():
        return ([remote(r.mine.at[pl.ds(NR - NS, NS)], r.st.at[i], r.sb.at[0, k], r.sb.at[1, k], {"seq": p["base"] + j}) for k, j in enumerate(ps)]
                + [remote(r.mine, r.zland.at[z], r.sz.at[0, k], r.sz.at[1, k], {"batch": q}) for k, q in enumerate(zp)])

    for which in ("own", "x", "y", "d"):
        for j in ga.chip(which):
            @tiles(T, 16)
            def _(q):
                r.act_all[sub(j * T, q), :] = ga.land[j, q, :].astype(BF16)
    for k in range(7):
        src = lax.rem(i + 7 - k, 8)
        remote(r.gm_all.at[src], r.gm_all.at[src], r.ms.at[k], r.mr.at[k], nxt).wait_recv()
    for c in wgs_copy: c.wait()
    gbias = jnp.concatenate([r.vecs[6:7, lane(i * 128, 128)], r.vecs[7:8, lane(i * 128, 128)]], 1)
    @tiles(8 * T, 256)
    def _(q):
        r.u[:, pl.ds(0, 256)] = dot(r.act_all[q, :], r.wgs[...]) + gbias
        for h in range(256 // T):
            blk = q.start // T + h
            @tiles(T, 16)
            def _(k):
                row = pl.ds(pl.multiple_of(h * T + k.start, 16), 16)
                v, g = r.u[row, pl.ds(0, 128)], jax.nn.sigmoid(r.u[row, pl.ds(128, 128)])
                gm = r.gm_all[blk, k, :]
                rows = pl.ds(pl.multiple_of(q.start + h * T + k.start, 16), 16)
                r.ggl[rows, :] = jnp.concatenate([gm * g, gm * v * g * (1.0 - g)], 1).astype(BF16)
    @tiles(D, 256)
    def _(c):
        g = dot(r.act_all[:, c], r.ggl[...], 0, 0)
        for q in range(256 // HB):
            j = c.start // 128 + q // Z
            r.glg[q % Z, pl.ds(pl.multiple_of(j * HB, HB), HB), :] = g[q * HB:(q + 1) * HB]

    LU = lambda t: r.lgl.at[0, t - 1]
    LD = lambda t: r.lgl.at[1, t]
    def cu(t, src=None):
        return remote(LU(t) if src is None else src, LU(t), r.zs.at[0, t - 1], r.zr.at[0, t - 1], zu)
    def cd(t, src=None):
        return remote(LD(t) if src is None else src, LD(t), r.zs.at[1, t], r.zr.at[1, t], zd)
    def add_into(dst, srcs):
        @tiles(dst.shape[0], 16)
        def _(q):
            v = srcs[0][q, :]
            for e in srcs[1:]: v = v + e[q, :]
            dst[q, :] = v
    def z_start():
        for h in range(Z - 1, 0, -1):
            pl.when(z == 0)(lambda: cu(h, r.glg.at[h]).start())
            pl.when(z == Z - 1)(lambda: cd(Z - 1 - h, r.glg.at[Z - 1 - h]).start())
    def z_slot(slot):
        for zz in range(1, Z - 1):
            @pl.when(z == zz)
            def _():
                for t in range(Z - 1, zz, -1):
                    if (Z - 1 - t) + zz == slot:
                        cu(t).wait_recv()
                        add_into(LU(t), (LU(t), r.glg.at[t]))
                        cu(t).start()
                for t in range(zz):
                    if t + (Z - 1 - zz) == slot:
                        cd(t).wait_recv()
                        add_into(LD(t), (LD(t), r.glg.at[t]))
                        cd(t).start()
    def z_final(dst):
        for zz in range(Z):
            @pl.when(z == zz)
            def _():
                srcs = [r.glg.at[zz]]
                if zz > 0:
                    cu(zz).wait_recv()
                    srcs.append(LU(zz))
                if zz < Z - 1:
                    cd(zz).wait_recv()
                    srcs.append(LD(zz))
                add_into(dst, srcs)
    def z_drain():
        for zz in range(Z):
            @pl.when(z == zz)
            def _():
                for t in range(zz + 1, Z): cu(t).wait_send()
                for t in range(zz): cd(t).wait_send()
    z_start()

    def low_rows(src, dst, b8):
        @tiles(T, 16)
        def _(q):
            dst[sub(b8 * T, q), :] = src[b8, q, :].astype(BF16)
    @tiles(T, 16)
    def _(q):
        r.cot_all[sub(own8 * T, q), :] = r.cot[q, :]
    gc.settle_own()
    low_rows(r.land_cot, r.cot_all, z * 2 + 1 - p["c"])
    low_half = z < Z // 2
    near_end = jnp.where(low_half, z, Z - 1 - z)
    def chip_at(k):
        at = jnp.where(k <= near_end, near_end - k, k)
        return jnp.where(low_half, at, Z - 1 - at)
    @pl.loop(1, Z)
    def _(k):
        at = chip_at(k)
        gc.settle(at)
        low_rows(r.land_cot, r.cot_all, at * 2)
        low_rows(r.land_cot, r.cot_all, at * 2 + 1)


    for c in slice_copy(): c.wait()
    for zz in range(Z):
        @pl.when(z == zz)
        def _():
            for q in range(4): r.upbs[0:1, q * FB:(q + 1) * FB] = r.upb[pl.ds(q * 2 + p["c"], 1), :][:, zz * FB:(zz + 1) * FB]
    def slice_chunk(k):
        at = chip_at(k)
        @pl.when(k == 0)
        def _():
            gs.settle_own()
            low_rows(r.land_sec, r.sec_all, z * 2 + 1 - p["c"])
        @pl.when(k > 0)
        def _():
            gs.settle(at)
            low_rows(r.land_sec, r.sec_all, at * 2)
            low_rows(r.land_sec, r.sec_all, at * 2 + 1)
        q = pl.ds(pl.multiple_of(at * 2 * T, 2 * T), 2 * T)
        r.u[...] = dot(r.sec_all[q, :], r.wu[0])
        r.gh[...] = dot(r.cot_all[q, :], r.wd[0], 1, 1)
        @tiles(2 * T, 16)
        def _(e):
            hid, slope = gelu_both(r.u[e, :] + r.upbs[0:1, :])
            r.hid[sub(at * 2 * T, e), :] = hid.astype(BF16)
            r.gul[sub(at * 2 * T, e), :] = (r.gh[e, :] * slope).astype(BF16)
    pl.loop(0, 2)(slice_chunk)
    small_sum()
    pl.loop(2, Z - 1)(slice_chunk)
    pl.loop(Z - 1, Z)(slice_chunk)

    own, land = (r.upg, r.dng), (r.lup, r.ldn)
    X, Y = {"seq": p["base"] + p["ix"]}, {"seq": p["base"] + p["iy"]}
    def piece(n, q, h):
        half = own[n].shape[1] // 2
        return own[n].at[q, pl.ds(h * half, half)]
    def hop(n, k, dev, src=None):
        return remote(land[n].at[k] if src is None else src, land[n].at[k], r.rs.at[0, n, k], r.rs.at[1, n, k], dev)
    def plane_start(n):
        for k, dev, q, h in ((0, X, qd, 0), (2, Y, qd, 1), (1, X, qx, 0), (3, Y, qy, 1)): hop(n, k, dev, piece(n, q, h)).start()
    def plane_middle(n):
        for k, q, h, k2, dev in ((0, qy, 0, 4, Y), (2, qx, 1, 5, X)):
            hop(n, k, X).wait_recv()
            add_into(land[n].at[k], (land[n].at[k], piece(n, q, h)))
            hop(n, k2, dev, land[n].at[k]).start()
    def plane_end(n, dst):
        half = own[n].shape[1] // 2
        for h, near, second in ((0, 1, 4), (1, 3, 5)):
            hop(n, near, X).wait_recv()
            hop(n, second, X).wait_recv()
            add_into(dst.at[pl.ds(h * half, half)], (piece(n, q0, h), land[n].at[near], land[n].at[second]))
    @tiles(D, 256)
    def _(c):
        r.upg[c.start // 256] = dot(r.sec_all[:, c], r.gul[...], 0, 0)
    plane_start(0)
    for fc in range(FT // 256):
        for nh in range(D // 512):
            g = dot(r.hid[:, fc * 256:(fc + 1) * 256], r.cot_all[:, nh * 512:(nh + 1) * 512], 0, 0)
            n = 256 // FB
            for q in range(n): r.dng[fc * n + q, :, nh * 512:(nh + 1) * 512] = g[q * FB:(q + 1) * FB]
    z_slot(1)
    plane_middle(0)
    plane_start(1)
    z_slot(2)
    plane_end(0, r.upf)
    for k, w in enumerate(group):
        push(r.upf.at[pl.ds(pl.multiple_of(w * HB, HB), HB)], r.uland.at[w8], r.ua.at[0, k], r.ua.at[1, k], seat(w))
    r.uland[w8] = r.upf[pl.ds(pl.multiple_of(w8 * HB, HB), HB), :]
    acc = r.mine[...]
    for k in range(Z - 1):
        src = lax.rem(z + Z - 1 - k, Z)
        remote(r.mine, r.zland.at[src], r.sz.at[0, k], r.sz.at[1, k], zu).wait_recv()
        acc = acc + r.zland[src]
    r.tot[...] = acc
    plane_middle(1)
    z_final(r.glf)
    for k, j in enumerate(ps):
        for q in range(2):
            push(r.glf.at[pl.ds(pl.multiple_of(j * HB, HB), HB), pl.ds(q * 128, 128)], r.glu_out.at[:, lane(q * D + i * 128, 128)],
                 r.ga.at[0, q, k], r.ga.at[1, q, k], {"seq": p["base"] + j})
    for q in range(2):
        r.glu_out[:, lane(q * D + i * 128, 128)] = r.glf[pl.ds(pl.multiple_of(i * HB, HB), HB), pl.ds(q * 128, 128)]
    for k in range(7):
        src = lax.rem(i + 7 - k, 8)
        remote(r.st.at[src], r.st.at[src], r.sb.at[0, k], r.sb.at[1, k], nxt).wait_recv()
        for q in range(2):
            blk = r.glu_out.at[:, lane(q * D + src * 128, 128)]
            remote(blk, blk, r.ga.at[0, q, k], r.ga.at[1, q, k], nxt).wait_recv()
    for k in range(7):
        src = lax.rem(w8 + 7 - k, 8)
        remote(r.uland.at[src], r.uland.at[src], r.ua.at[0, k], r.ua.at[1, k], nxt).wait_recv()
    for w in range(8):
        for q in range(4): r.up_out[:, (q * 8 + w) * FB:(q * 8 + w + 1) * FB] = r.uland[w, :, q * FB:(q + 1) * FB]
    plane_end(1, r.down_o)

    pl.when(s < NSEQ - 1)(lambda: halo_copy.wait_send())
    pl.when(s > 0)(lambda: tail_copy.wait_send())
    for c in gm_sends + sends + small_sends(): c.wait_send()
    gc.drain()
    gs.drain()
    ga.drain()
    z_drain()
    for n in range(2):
        for k in range(6): hop(n, k, X).wait_send()


def layer(cfg, tabs, vecs, rate, freq, cre, cim, prior, x, cot, glu_w, up_w, down_w, cid):
    Z, NSEQ, nbits, T, D, FF, M = cfg
    FT, HB = FF // 8, D // 8 // Z
    NR = 4 * M + 16 + 2 * M
    NT = NR
    vm, hbm = pl.BlockSpec(memory_space=pltpu.VMEM), pl.BlockSpec(memory_space=pl.ANY)
    S = lambda shape, dt=F32: jax.ShapeDtypeStruct(shape, dt)
    ins = dict(ftab=vm, itab=vm, jtab=vm, gtab=vm, **{f"v{k}": vm for k in range(8)}, rate=vm, freq=vm, cre=vm, cim=vm, prior=vm, x=vm, cot=vm,
               glu_w=hbm, up_w=hbm, down_w=hbm)
    outs = dict(out=S((T, D), BF16), ig=S((T, D), BF16), st=S((8, 2 * M, 128)), tot=S((NT, 128)), down_o=S((FT // Z, D)),
                up_out=S((HB, FF)), glu_out=S((HB, 2 * D)))
    V, DS = pltpu.VMEM, lambda *n: pltpu.SemaphoreType.DMA(n)
    row = lambda: V((T, D), F32)
    scr = dict(
        vecs=V((8, D), F32), upb=V((8, FT), F32),
        xs=row(), own_cot=row(), own_sec=row(), own_act=row(), halo=row(), tail=row(), xhat=row(), pre=row(), val=row(), sg=row(),
        merged=row(), mhat=row(), gm=row(), gz=row(), oacc=row(), sacc=row(), resp=row(), kern=row(),
        xinv=V((T, 128), F32), minv=V((T, 128), F32), ext=V((2 * T, D), F32), X=V((2 * KLEN, D), F32), K=V((2 * KLEN, D), F32),
        land_cot=V((8, T, D), F32), land_sec=V((8, T, D), F32), land_act=V((8, T, D), F32),
        cot_all=V((8 * T, D), BF16), sec_all=V((8 * T, D), BF16), act_all=V((8 * T, D), BF16),
        gw=V((D, 2 * D), BF16), wu=V((2, D, FT), BF16), wd=V((2, FT, D), BF16), wgs=V((D, 256), BF16),
        u=V((256, FT), F32), gh=V((256, FT), F32), hid=V((8 * T, FT), BF16), gul=V((8 * T, FT), BF16),
        glow=V((T, 2 * D), BF16), gm_all=V((8, T, 128), F32), ggl=V((8 * T, 256), BF16),
        upg=V((Z, D // Z, FT), F32), glg=V((Z, D // Z, 256), F32), dng=V((Z, FT // Z, D), F32),
        lup=V((6, D // 8, FT), F32), ldn=V((6, FF // 64, D), F32), uland=V((8, HB, FT), F32), ubg=V((8, FT), F32), upbs=V((8, FT), F32),
        lgl=V((2, Z - 1, D // Z, 256), F32), upf=V((D // Z, FT), F32), glf=V((D // Z, 256), F32),
        qr=V((16, M, LT), F32), qi=V((16, M, LT), F32), big=V((64 * M, LT), F32),
        ssrc=V((NR, D), F32), sland=V((8, NR, 128), F32), mine=V((NT, 128), F32), zland=V((Z, NT, 128), F32),
        lsem=DS(3), tsem=DS(2, 2), hsem=DS(4), gss=DS(14), gsr=DS(14), ms=DS(7), mr=DS(7), zs=DS(2, Z - 1), zr=DS(2, Z - 1),
        lss=DS(2, 3, 2 * Z - 1, 2), lsr=DS(2, 3, 2 * Z - 1, 2), rs=DS(2, 2, 6), ssem=DS(2, 4),
        sa=DS(2, 7), ua=DS(2, 7), sb=DS(2, 7), ga=DS(2, 2, 7), sz=DS(2, Z - 1))
    names = (*ins, *outs, *scr)
    res = pl.pallas_call(
        functools.partial(layer_kernel, cfg, names),
        out_shape=list(outs.values()), in_specs=list(ins.values()), out_specs=[vm] * len(outs), scratch_shapes=list(scr.values()),
        compiler_params=pltpu.CompilerParams(collective_id=cid, has_side_effects=True, vmem_limit_bytes=67043328),
        name="layer")(*tabs, *vecs, rate, freq, cre, cim, prior, x, cot, glu_w, up_w, down_w)
    return dict(zip(outs, res))


def finish_kernel(cfg, names, *refs):
    r = Bag()
    r.__dict__.update(zip(names, refs))
    Z, NSEQ, nbits, T, D, FF, M = cfg
    HB = D // 8 // Z
    b = lax.axis_index("batch")
    for k in ("out", "ig", "glu_out", "up_out", "down_o"): r.__dict__["o_" + k][...] = r.__dict__[k][...]
    for j in range(8): r.o_st[:, j * 128:(j + 1) * 128] = r.st[j]
    r.turned[...] = r.tot[0:4 * M, :].T
    mine = r.turned[pl.ds(pl.multiple_of(b * HB, HB), HB), :]
    for k in range(4): r.__dict__[f"m{k}"][...] = mine[:, k * M:(k + 1) * M]
    v = pltpu.roll(r.tot[4 * M:4 * M + 8, :], lax.rem(128 - b * HB, 128), 1)
    for k in range(6): r.__dict__[f"w{k}"][...] = v[k, 0:HB]
    per = 128 // (2 * HB)
    g = r.tot[pl.ds(4 * M + 6 + b // per, 1), :]
    r.gb[...] = pltpu.roll(jnp.broadcast_to(g, (8, 128)), lax.rem(128 - lax.rem(b, per) * 2 * HB, 128), 1)[0, 0:2 * HB]
    r.ub[...] = r.tot[pl.ds(4 * M + 8 + b, 1), :].reshape(128)


def finish(cfg, o):
    Z, NSEQ, nbits, T, D, FF, M = cfg
    HB = D // 8 // Z
    vm = pl.BlockSpec(memory_space=pltpu.VMEM)
    S = lambda shape, dt=F32: jax.ShapeDtypeStruct(shape, dt)
    outs = {"o_" + k: S(o[k].shape, o[k].dtype) for k in ("out", "ig", "glu_out", "up_out", "down_o")}
    outs["o_st"] = S((2 * M, D))
    outs.update({f"m{k}": S((HB, M)) for k in range(4)})
    outs.update({f"w{k}": S((HB,)) for k in range(6)})
    outs.update(gb=S((2 * HB,)), ub=S((FF // 8 // Z,)))
    names = (*o, *outs, "turned")
    res = pl.pallas_call(functools.partial(finish_kernel, cfg, names), out_shape=list(outs.values()), in_specs=[vm] * len(o),
                         out_specs=[vm] * len(outs), scratch_shapes=[pltpu.VMEM((128, 4 * M), F32)], name="finish")(*o.values())
    return {k.removeprefix("o_"): v for k, v in zip(outs, res)}


def tables(window):
    half = window // 2
    f = np.concatenate([np.arange(half + 1), np.arange(1, half)])[:, None]
    imag = np.arange(window)[:, None] > half
    ph = (f * np.arange(window)[None, :] % window) * (2.0 * np.pi / window)
    fwd = np.where(imag, -np.sin(ph), np.cos(ph))
    wt = np.where((f == 0) | (2 * f == window), 1.0, 2.0) / window
    inv = (wt * fwd).T[half:]
    def parts(a):
        a = np.ascontiguousarray(a).astype(np.float32)
        high = a.astype(ml_dtypes.bfloat16)
        return jnp.asarray(np.stack([high, (a - high.astype(np.float32)).astype(ml_dtypes.bfloat16)]))
    return parts(fwd), parts(inv), parts(inv.T), parts(fwd.T)


def plane_shards(Z, n_seq, inputs, first_gain, first_shift, decay_rate, rotation, out_real, out_imag, skip_gain, glu_weight,
                 glu_bias, second_gain, second_shift, up_weight, up_bias, down_weight, down_bias, prior_state, cotangent):
    T, D = inputs.shape[1:]
    FF, M = up_weight.shape[1], decay_rate.shape[1]
    FT, HB = FF // 8, D // 8 // Z
    cfg = (Z, n_seq, max(1, (n_seq - 1).bit_length()), T, D, FF, M)
    vecs = (first_gain, first_shift, skip_gain, second_gain, second_shift, down_bias, glu_bias, up_bias)
    o = layer(cfg, tables(T + KLEN), vecs, decay_rate.T, rotation.T, out_real.T, out_imag.T, prior_state,
              inputs[0], cotangent[0], glu_weight, up_weight, down_weight, 0)
    f = finish(cfg, o)
    v = [f[f"w{k}"] for k in range(6)]
    m = [f[f"m{k}"] for k in range(4)]
    return (f["out"][None], f["ig"][None], f["st"].reshape(1, 2, M, D), v[0], v[1], *m, v[2], f["glu_out"], f["gb"],
            v[3], v[4], f["up_out"], f["ub"], f["down_o"], v[5])


def solution(mesh):
    in_specs = (
        P("batch", "seq", None),
        P(),
        P(),
        P(),
        P(),
        P(),
        P(),
        P(),
        P(),
        P(),
        P(),
        P(),
        P(),
        P(),
        P(),
        P(),
        P("batch", None, None, None),
        P("batch", "seq", None),
    )
    out_specs = (
        P("batch", "seq", None),
        P("batch", "seq", None),
        P("batch", None, None, None),
        P(("seq", "batch")),
        P(("seq", "batch")),
        P(("seq", "batch"), None),
        P(("seq", "batch"), None),
        P(("seq", "batch"), None),
        P(("seq", "batch"), None),
        P(("seq", "batch")),
        P(("seq", "batch"), None),
        P(("seq", "batch")),
        P(("seq", "batch")),
        P(("seq", "batch")),
        P(("seq", "batch"), None),
        P(("seq", "batch")),
        P(("seq", "batch"), None),
        P(("seq", "batch")),
    )
    body = shards
    if mesh.shape["seq"] == 8:
        body = functools.partial(plane_shards, mesh.shape["batch"], mesh.shape["seq"])
    return jax.shard_map(body, mesh=mesh, in_specs=in_specs, out_specs=out_specs, check_vma=False)
```

```python
import functools
import math

import jax
import jax.numpy as jnp
import ml_dtypes
import numpy as np
from jax import lax
from jax.experimental import pallas as pl
from jax.experimental.pallas import tpu as pltpu
from jax.sharding import PartitionSpec as P

KLEN = 128
LT = 128
MESH = pl.DeviceIdType.MESH
F32, BF16 = jnp.float32, jnp.bfloat16


EPSILON = 1e-05
HIGHEST = lax.Precision.HIGHEST


def from_behind(value, axis, by):
    peers = lax.axis_size(axis)
    pairs = [(i, i + by) for i in range(peers) if 0 <= i + by < peers]
    return lax.ppermute(value, axis, pairs)


def norm_rows(values, gain, shift):
    center = values - jnp.mean(values, axis=-1, keepdims=True)
    spread = jnp.mean(center * center, axis=-1, keepdims=True)
    return center * lax.rsqrt(spread + EPSILON) * gain + shift


def mode_terms(rate_modes, freq_modes, elapsed):
    moment = elapsed[None, :, None]
    damping = jnp.exp(-rate_modes[:, None, :] * moment)
    return (
        damping * jnp.cos(freq_modes[:, None, :] * moment),
        damping * jnp.sin(freq_modes[:, None, :] * moment),
    )


def glu_gate(glu_pre):
    split_at = glu_pre.shape[-1] // 2
    return glu_pre[:, :split_at] * jax.nn.sigmoid(glu_pre[:, split_at:])


def gelu_exact(values):
    return jax.nn.gelu(values, approximate=False)


def shards(
    inputs,
    first_gain,
    first_shift,
    decay_rate,
    rotation,
    out_real,
    out_imag,
    skip_gain,
    glu_weight,
    glu_bias,
    second_gain,
    second_shift,
    up_weight,
    up_bias,
    down_weight,
    down_bias,
    prior_state,
    cotangent,
):
    seg_count, tok_count, feature = inputs.shape
    row_count = seg_count * tok_count
    window = tok_count + KLEN
    half = window // 2 + 1
    offset = lax.axis_index("seq") * tok_count
    freq_index = jnp.arange(half, dtype=jnp.int32)
    time_index = jnp.arange(window, dtype=jnp.int32)
    phase = (freq_index[:, None] * time_index[None, :] % window).astype(jnp.float32) * (
        2.0 * math.pi / window
    )
    cos_half = jnp.cos(phase)
    sin_half = jnp.sin(phase)
    forward_table = jnp.concatenate([cos_half, -sin_half], axis=0)
    weights = jnp.where((freq_index == 0) | (2 * freq_index == window), 1.0, 2.0).astype(
        jnp.float32
    )
    inverse_table = (
        jnp.concatenate(
            [(weights[:, None] * cos_half).T, -(weights[:, None] * sin_half).T], axis=1
        )[KLEN:]
        / window
    )
    local_steps = jnp.arange(tok_count).astype(jnp.float32)
    advance_steps = (offset + 1).astype(jnp.float32)

    def mixing(
        normed, halo_rows, rate_modes, freq_modes, real_modes, imag_modes, skip_local, prior_local
    ):
        table_real, table_imag = mode_terms(rate_modes, freq_modes, local_steps)
        kernel = jnp.einsum("mkh,mh->kh", table_real, real_modes, precision=HIGHEST) - jnp.einsum(
            "mkh,mh->kh", table_imag, imag_modes, precision=HIGHEST
        )
        extended = jnp.concatenate([halo_rows, normed], axis=1)
        spectrum = jnp.einsum("ft,sth->sfh", forward_table, extended, precision=HIGHEST)
        kern_spec = jnp.dot(forward_table[:, :KLEN], kernel, precision=HIGHEST)
        spec_real, spec_imag = (spectrum[:, :half], spectrum[:, half:])
        kern_real, kern_imag = (kern_spec[:half], kern_spec[half:])
        product = jnp.concatenate(
            [
                spec_real * kern_real - spec_imag * kern_imag,
                spec_real * kern_imag + spec_imag * kern_real,
            ],
            axis=1,
        )
        convolved = jnp.einsum("tf,sfh->sth", inverse_table, product, precision=HIGHEST)
        damping = jnp.exp(-rate_modes * advance_steps)
        adv_real = damping * jnp.cos(freq_modes * advance_steps)
        adv_imag = damping * jnp.sin(freq_modes * advance_steps)
        coef_real = real_modes * adv_real - imag_modes * adv_imag
        coef_imag = real_modes * adv_imag + imag_modes * adv_real
        drive_real = coef_real * prior_local[:, 0] - coef_imag * prior_local[:, 1]
        drive_imag = coef_real * prior_local[:, 1] + coef_imag * prior_local[:, 0]
        response = jnp.einsum(
            "mth,smh->sth", table_real, drive_real, precision=HIGHEST
        ) - jnp.einsum("mth,smh->sth", table_imag, drive_imag, precision=HIGHEST)
        return gelu_exact(convolved + skip_local * normed + response)

    source = inputs.astype(jnp.float32)
    normed, first_pull = jax.vjp(norm_rows, source, first_gain, first_shift)
    halo_rows = from_behind(normed, "seq", 1)
    activated, mix_pull = jax.vjp(
        mixing,
        normed,
        halo_rows,
        decay_rate.T,
        rotation.T,
        out_real.T,
        out_imag.T,
        skip_gain,
        prior_state,
    )
    activated_low = activated.reshape(row_count, feature).astype(jnp.bfloat16)
    glu_pre = jnp.dot(activated_low, glu_weight, preferred_element_type=jnp.float32) + glu_bias
    branch, glu_pull = jax.vjp(glu_gate, glu_pre)
    merged = source.reshape(row_count, feature) + branch
    second, second_pull = jax.vjp(norm_rows, merged, second_gain, second_shift)
    second_low = second.astype(jnp.bfloat16)
    up_pre = jnp.dot(second_low, up_weight, preferred_element_type=jnp.float32) + up_bias
    hidden, hidden_pull = jax.vjp(gelu_exact, up_pre)
    hidden_low = hidden.astype(jnp.bfloat16)
    result = (
        merged + jnp.dot(hidden_low, down_weight, preferred_element_type=jnp.float32) + down_bias
    )
    outputs = result.astype(jnp.bfloat16).reshape(seg_count, tok_count, feature)
    grad_out = cotangent.astype(jnp.float32).reshape(row_count, feature)
    down_bias_grad = jnp.sum(grad_out, axis=0)
    grad_low = grad_out.astype(jnp.bfloat16)
    down_grad = jnp.einsum("rf,rh->fh", hidden_low, grad_low, preferred_element_type=jnp.float32)
    grad_hidden = jnp.einsum("rh,fh->rf", grad_low, down_weight, preferred_element_type=jnp.float32)
    (grad_up,) = hidden_pull(grad_hidden)
    up_bias_grad = jnp.sum(grad_up, axis=0)
    up_low = grad_up.astype(jnp.bfloat16)
    up_grad = jnp.einsum("rh,rf->hf", second_low, up_low, preferred_element_type=jnp.float32)
    grad_second = jnp.einsum("rf,hf->rh", up_low, up_weight, preferred_element_type=jnp.float32)
    grad_merged, second_gain_grad, second_shift_grad = second_pull(grad_second)
    grad_merged = grad_merged + grad_out
    (grad_glu,) = glu_pull(grad_merged)
    glu_bias_grad = jnp.sum(grad_glu, axis=0)
    glu_low = grad_glu.astype(jnp.bfloat16)
    glu_grad = jnp.einsum("rh,rg->hg", activated_low, glu_low, preferred_element_type=jnp.float32)
    grad_activated = jnp.einsum(
        "rg,hg->rh", glu_low, glu_weight, preferred_element_type=jnp.float32
    )
    grad_normed, grad_halo, rate_grad, freq_grad, real_grad, imag_grad, skip_grad, prior_grad = (
        mix_pull(grad_activated.reshape(seg_count, tok_count, feature))
    )
    grad_tail = from_behind(grad_halo, "seq", -1)
    grad_normed = jnp.concatenate(
        [grad_normed[:, : tok_count - KLEN], grad_normed + grad_tail], axis=1
    )
    grad_source, first_gain_grad, first_shift_grad = first_pull(grad_normed)
    input_grad = (grad_source + grad_merged.reshape(seg_count, tok_count, feature)).astype(
        jnp.bfloat16
    )
    state_grad = lax.psum(prior_grad, "seq")
    rate_back = rate_grad.T
    freq_back = freq_grad.T
    real_back = real_grad.T
    imag_back = imag_grad.T
    summed = (
        lax.psum_scatter(first_gain_grad, ("seq", "batch"), scatter_dimension=0, tiled=True),
        lax.psum_scatter(first_shift_grad, ("seq", "batch"), scatter_dimension=0, tiled=True),
        lax.psum_scatter(rate_back, ("seq", "batch"), scatter_dimension=0, tiled=True),
        lax.psum_scatter(freq_back, ("seq", "batch"), scatter_dimension=0, tiled=True),
        lax.psum_scatter(real_back, ("seq", "batch"), scatter_dimension=0, tiled=True),
        lax.psum_scatter(imag_back, ("seq", "batch"), scatter_dimension=0, tiled=True),
        lax.psum_scatter(skip_grad, ("seq", "batch"), scatter_dimension=0, tiled=True),
        lax.psum_scatter(glu_grad, ("seq", "batch"), scatter_dimension=0, tiled=True),
        lax.psum_scatter(glu_bias_grad, ("seq", "batch"), scatter_dimension=0, tiled=True),
        lax.psum_scatter(second_gain_grad, ("seq", "batch"), scatter_dimension=0, tiled=True),
        lax.psum_scatter(second_shift_grad, ("seq", "batch"), scatter_dimension=0, tiled=True),
        lax.psum_scatter(up_grad, ("seq", "batch"), scatter_dimension=0, tiled=True),
        lax.psum_scatter(up_bias_grad, ("seq", "batch"), scatter_dimension=0, tiled=True),
        lax.psum_scatter(down_grad, ("seq", "batch"), scatter_dimension=0, tiled=True),
        lax.psum_scatter(down_bias_grad, ("seq", "batch"), scatter_dimension=0, tiled=True),
    )
    return (
        outputs,
        input_grad,
        state_grad,
        summed[0],
        summed[1],
        summed[2],
        summed[3],
        summed[4],
        summed[5],
        summed[6],
        summed[7],
        summed[8],
        summed[9],
        summed[10],
        summed[11],
        summed[12],
        summed[13],
        summed[14],
    )


def plane():
    s = lax.axis_index("seq")
    i = lax.rem(s, 8)
    base = s - i
    c, x, y = lax.rem(i, 2), lax.rem(i // 2, 2), i // 4
    ic, ix, iy = i + 1 - 2 * c, i + 2 - 4 * x, i + 4 - 8 * y
    idg = iy + 2 - 4 * x
    return dict(s=s, i=i, base=base, c=c, x=x, y=y, ic=ic, ix=ix, iy=iy, idg=idg)

def sib_of(p, j):
    return j + 1 - 2 * p["c"]

def remote(src, dst, ss, rs, dev):
    return pltpu.make_async_remote_copy(src_ref=src, dst_ref=dst, send_sem=ss, recv_sem=rs,
                                        device_id=dev, device_id_type=MESH)

def greet(devs):
    bar = pltpu.get_barrier_semaphore()
    for d in devs:
        pl.semaphore_signal(bar, inc=1, device_id=d, device_id_type=MESH)
    return lambda: pl.semaphore_wait(bar, len(devs))

def peers(p):
    return [lax.rem(p["i"] + k, 8) for k in range(1, 8)]

class Gather:
    def __init__(self, p, own, land, ssem, rsem):
        self.p, self.own, self.land, self.ss, self.rs = p, own, land, ssem, rsem
        self.H = own.shape[0] // 2
        seq = lambda j: {"seq": p["base"] + j}
        self.X, self.Y, self.S = seq(p["ix"]), seq(p["iy"]), seq(p["ic"])

    def cp(self, k, j, h, dev, src=None):
        blk = self.land.at[j, pl.ds(h * self.H, self.H)]
        return remote(blk if src is None else src, blk, self.ss.at[k], self.rs.at[k], dev)

    def plan(self):
        i, ix, iy, idg = self.p["i"], self.p["ix"], self.p["iy"], self.p["idg"]
        return [(0, i, 0, self.X), (2, i, 1, self.Y), (1, i, 1, self.X), (3, i, 0, self.Y), (6, i, 0, self.S), (7, i, 1, self.S),
                (4, ix, 0, self.Y), (8, ix, 0, self.S), (5, iy, 1, self.X), (11, iy, 1, self.S), (9, ix, 1, self.S),
                (10, iy, 0, self.S), (12, idg, 0, self.S), (13, idg, 1, self.S)]

    def _send(self, k, own=False):
        k, j, h, dev = next(e for e in self.plan() if e[0] == k)
        self.cp(k, j, h, dev, self.own.at[pl.ds(h * self.H, self.H)] if own else None).start()

    def _got(self, k, j, h):
        self.cp(k, j, h, self.S).wait_recv()

    def start(self):
        for k in (0, 2, 1, 3, 6, 7):
            self._send(k, True)

    def relay1(self):
        p = self.p
        self._got(0, p["ix"], 0); self._send(4); self._send(8)
        self._got(2, p["iy"], 1); self._send(5); self._send(11)

    def relay2(self):
        p = self.p
        self._got(1, p["ix"], 1); self._send(9)
        self._got(3, p["iy"], 0); self._send(10)

    def relay3(self):
        p = self.p
        self._got(4, p["idg"], 0); self._send(12)
        self._got(5, p["idg"], 1); self._send(13)

    def chip(self, which):
        p = self.p
        k, j = {"own": (6, p["ic"]), "x": (8, sib_of(p, p["ix"])), "y": (10, sib_of(p, p["iy"])), "d": (12, sib_of(p, p["idg"]))}[which]
        self._got(k, j, 0)
        self._got(k + 1, j, 1)
        return (j,) if which == "own" else ({"x": p["ix"], "y": p["iy"], "d": p["idg"]}[which], j)

    def drain(self):
        for k, j, h, dev in self.plan():
            self.cp(k, j, h, dev).wait_send()


class Line:
    def __init__(self, Z, z, p, own, land, ssem, rsem, zu, zd):
        self.Z, self.z, self.c, self.own, self.land, self.ss, self.rs = Z, z, p["c"], own, land, ssem, rsem
        self.H = own.shape[0] // 2
        self.dev = (zu, zd, {"seq": p["base"] + p["ic"]})

    def part(self, chip, core, half):
        return self.land.at[chip * 2 + core, pl.ds(half * self.H, self.H)]

    def cp(self, way, hop, half, chip, core, own=False):
        blk = self.part(chip, core, half)
        src = self.own.at[pl.ds(half * self.H, self.H)] if own else blk
        return remote(src, blk, self.ss.at[way, hop, half], self.rs.at[way, hop, half], self.dev[way])

    def ends(self):
        z, Z = self.z, self.Z
        return ((lambda h: z - h, lambda h: z - h >= 0, z < Z - 1), (lambda h: z + h, lambda h: z + h < Z, z > 0))

    def start(self):
        for half in range(2):
            for way, (chip, there, on) in enumerate(self.ends()):
                pl.when(on)(lambda: self.cp(way, 0, half, self.z, self.c, True).start())
        for half in range(2): self.cp(2, 0, half, self.z, self.c, True).start()

    def _take(self, way, hop, half, chip):
        self.cp(way, hop - 1, half, chip, self.c).wait_recv()
        self.cp(2, hop + way * (self.Z - 1), half, chip, self.c).start()

    def pass_on(self, hop, half):
        for way, (chip, there, on) in enumerate(self.ends()):
            @pl.when(there(hop) & on)
            def _():
                self._take(way, hop, half, chip(hop))
                self.cp(way, hop, half, chip(hop), self.c).start()

    def settle(self, chip_at):
        for way, (chip, there, on) in enumerate(self.ends()):
            for hop in range(1, self.Z):
                @pl.when(chip_at == chip(hop))
                def _():
                    for half in range(2):
                        pl.when(jnp.logical_not(on))(lambda: self._take(way, hop, half, chip(hop)))
                    for half in range(2):
                        self.cp(2, hop + way * (self.Z - 1), half, chip(hop), 1 - self.c).wait_recv()

    def settle_own(self):
        for half in range(2): self.cp(2, 0, half, self.z, 1 - self.c).wait_recv()

    def drain(self):
        for half in range(2):
            self.cp(2, 0, half, self.z, self.c, True).wait_send()
            for way, (chip, there, on) in enumerate(self.ends()):
                for hop in range(self.Z - 1):
                    pl.when(there(hop) & on)(lambda: self.cp(way, hop, half, chip(hop), self.c).wait_send())
                for hop in range(1, self.Z):
                    pl.when(there(hop))(lambda: self.cp(2, hop + way * (self.Z - 1), half, chip(hop), self.c).wait_send())


def cmul(ar, ai, br, bi):
    return ar * br - ai * bi, ar * bi + ai * br

def lam_of(rate, freq):
    damp = jnp.exp(-rate)
    q = freq * freq
    cosv = 1.0 + q * (-1.0/2 + q * (1.0/24 + q * (-1.0/720 + q * (1.0/40320 + q * (-1.0/3628800)))))
    sinv = freq * (1.0 + q * (-1.0/6 + q * (1.0/120 + q * (-1.0/5040 + q * (1.0/362880)))))
    return damp * cosv, damp * sinv

def power_rows(lr, li, qr, qi, A):
    l2 = cmul(lr, li, lr, li); l4 = cmul(*l2, *l2); l8 = cmul(*l4, *l4)
    cur = (jnp.ones_like(lr), jnp.zeros_like(lr))
    for a in range(A):
        qr[a] = cur[0]; qi[a] = cur[1]
        cur = cmul(*cur, *l8)
    return l2, l4, cur

def offset_power(top, s, nbits):
    res = (jnp.ones_like(top[0]), jnp.zeros_like(top[0]))
    sq = top
    for bit in range(nbits):
        on = lax.rem(lax.div(s, 1 << bit), 2) == 1
        nxt = cmul(*res, *sq)
        res = (jnp.where(on, nxt[0], res[0]), jnp.where(on, nxt[1], res[1]))
        if bit + 1 < nbits: sq = cmul(*sq, *sq)
    return res

def fwd_tiles(nbits, lo, hi, rate, freq, cre, cim, prior, kern, resp, co):
    M = rate.shape[0]
    A = kern.shape[0] // 8
    s = lax.axis_index("seq")
    b = lax.broadcasted_iota(jnp.int32, (8, LT), 0)
    o1, o2, o4 = (b % 2) == 1, ((b // 2) % 2) == 1, b >= 4
    one, zero = jnp.ones((8, LT), F32), jnp.zeros((8, LT), F32)
    square = lambda v: cmul(*v, *v)
    @pl.loop(lo, hi)
    def _(lt):
        cols = pl.ds(pl.multiple_of(lt * LT, LT), LT)
        l1 = lam_of(rate[:, cols], freq[:, cols])
        l2 = square(l1)
        l4 = square(l2)
        l8 = square(l4)
        top = l8
        for _ in range((A - 1).bit_length()): top = square(top)
        off = cmul(*offset_power(top, s, nbits), *l1)
        c = cre[:, cols], cim[:, cols]
        d = cmul(*cmul(*c, *off), prior[0, 0, :, cols], prior[0, 1, :, cols])
        rows = (*l1, *l2, *l4, *c, *cmul(*c, *l8), *d, *cmul(*d, *l8), 2.0 * l8[0], -(l8[0] * l8[0] + l8[1] * l8[1]))
        for k, v in enumerate(rows): co[pl.ds(k * M, M), :] = v
        def step(m, accs):
            row = lambda k: jnp.broadcast_to(co[pl.ds(k * M + m, 1), :], (8, LT))
            e = jnp.where(o1, row(0), one), jnp.where(o1, row(1), zero)
            e = cmul(*e, jnp.where(o2, row(2), one), jnp.where(o2, row(3), zero))
            er, ei = cmul(*e, jnp.where(o4, row(4), one), jnp.where(o4, row(5), zero))
            p, q = row(14), row(15)
            k0, k1 = er * row(6) - ei * row(7), er * row(8) - ei * row(9)
            r0, r1 = er * row(10) - ei * row(11), er * row(12) - ei * row(13)
            out = list(accs)
            for a in range(A):
                out[2 * a] = out[2 * a] + k0
                out[2 * a + 1] = out[2 * a + 1] + r0
                if a < A - 1:
                    k0, k1 = k1, p * k1 + q * k0
                    r0, r1 = r1, p * r1 + q * r0
            return tuple(out)
        accs = lax.fori_loop(0, M, step, tuple(jnp.zeros((8, LT), F32) for _ in range(2 * A)), unroll=4)
        for a in range(A):
            kern[pl.ds(8 * a, 8), cols] = accs[2 * a]
            resp[pl.ds(8 * a, 8), cols] = accs[2 * a + 1]


def bwd_tiles(lo, hi, srow, nbits, TOK, rate, freq, cre, cim, prior, kg, gz, out, qr, qi, acc):
    M = rate.shape[0]
    A = kg.shape[0] // 8
    s = lax.axis_index("seq")
    adv = (s * TOK + 1).astype(F32)
    @pl.loop(lo, hi)
    def _(lt):
        cols = pl.ds(pl.multiple_of(lt * LT, LT), LT)
        lr, li = lam_of(rate[:, cols], freq[:, cols])
        l2, l4, top = power_rows(lr, li, qr, qi, A)
        def step(m, carry):
            for j, g in enumerate((kg, gz)):
                z = jnp.zeros((8, LT), F32)
                sr, si, tr, ti = z, z, z, z
                for a in range(A - 1, -1, -1):
                    ga = g[pl.ds(8 * a, 8), cols]
                    sr = sr + ga * qr[a, pl.ds(m, 1), :]
                    si = si + ga * qi[a, pl.ds(m, 1), :]
                    if a > 0:
                        tr = tr + sr
                        ti = ti + si
                for q, v in enumerate((sr, si, tr, ti)):
                    acc[pl.ds(pl.multiple_of(((4 * j + q) * M + m) * 8, 8), 8), :] = v
            return carry
        lax.fori_loop(0, M, step, 0, unroll=8)
        pw = (jnp.ones_like(lr), jnp.zeros_like(lr))
        zero = jnp.zeros_like(lr)
        ar, ai, br, bi = [zero] * 2, [zero] * 2, [zero] * 2, [zero] * 2
        for b in range(8):
            for j in range(2):
                ld = lambda q: acc[pl.ds((4 * j + q) * M * 8 + b, M, stride=8), :]
                S = ld(0), ld(1)
                U = 8.0 * ld(2), 8.0 * ld(3)
                if b: U = U[0] + float(b) * S[0], U[1] + float(b) * S[1]
                w = cmul(*pw, *S)
                ar[j], ai[j] = ar[j] + w[0], ai[j] + w[1]
                w = cmul(*pw, *U)
                br[j], bi[j] = br[j] + w[0], bi[j] + w[1]
            pw = cmul(*pw, lr, li)
        off = cmul(*offset_power(top, s, nbits), lr, li)
        c = cre[:, cols], cim[:, cols]
        ps = cmul(*off, prior[0, 0, :, cols], prior[0, 1, :, cols])
        u = cmul(*ps, ar[1], ai[1])
        v = cmul(*ps, br[1] + adv * ar[1], bi[1] + adv * ai[1])
        v = cmul(*c, v[0] + br[0], v[1] + bi[0])
        w = cmul(*cmul(*c, *off), ar[1], ai[1])
        for k, val in enumerate((-v[0], -v[1], u[0] + ar[0], -(u[1] + ai[0]))): out[k * M:(k + 1) * M, cols] = val
        for k, val in enumerate((w[0], -w[1])): out[srow + k * M:srow + (k + 1) * M, cols] = val


class Bag:
    pass


def dot(a, b, ca=1, cb=0):
    return lax.dot_general(a, b, (((ca,), (cb,)), ((), ())), preferred_element_type=F32)


def split_low(v):
    high = v.astype(BF16)
    return high, (v - high.astype(F32)).astype(BF16)


def table_dot(tab, v, rows=slice(None), cols=slice(None)):
    high, low = split_low(v)
    th, tl = tab[0, rows, cols], tab[1, rows, cols]
    return dot(th, high) + dot(th, low) + dot(tl, high)


def gelu_both(u):
    cdf = 0.5 + 0.5 * lax.erf(u * (0.5 ** 0.5))
    return u * cdf, cdf + u * (jnp.exp(-0.5 * u * u) * ((2.0 * math.pi) ** -0.5))


def tiles(n, step):
    def run(body, init=None):
        if init is None:
            @pl.loop(0, n // step)
            def _(k):
                body(pl.ds(pl.multiple_of(k * step, step), step))
            return None
        return lax.fori_loop(0, n // step, lambda k, c: body(pl.ds(pl.multiple_of(k * step, step), step), c), init)
    return run


def sub(off, q):
    return pl.ds(pl.multiple_of(off + q.start, q.size), q.size)


def row_mean(v):
    return jnp.sum(v, axis=-1, keepdims=True) * (1.0 / v.shape[-1])


def norm_hat(v):
    center = v - row_mean(v)
    inv = lax.rsqrt(row_mean(center * center) + EPSILON)
    return center * inv, inv


def norm_back(gg, hat, inv):
    return inv * (gg - row_mean(gg) - hat * row_mean(gg * hat))


def fold(v):
    return jnp.sum(v, axis=0, keepdims=True)


LC = 256
ROWS = 8
FETCH = ("rate", "freq", "cre", "cim", "prior", "ftab", "itab", "jtab", "gtab")
VEC = ("first_gain", "first_shift", "skip_gain", "second_gain", "second_shift", "down_bias", "value_bias", "gate_bias")


def layer_kernel(cfg, names, *refs):
    r = Bag()
    r.__dict__.update(zip(names, refs))
    Z, NSEQ, nbits, T, D, FF, M = cfg
    FT = FF // 8
    HB = D // 8 // Z
    p = plane()
    s, i = p["s"], p["i"]
    z = lax.axis_index("batch")
    vec = {k: (lambda q: (lambda c=slice(None): r.vecs[q:q + 1, c]))(q) for q, k in enumerate(VEC)}
    iblk = pl.ds(pl.multiple_of(i * T, T), T)
    w8, own8 = p["c"] * Z + z, z * 2 + p["c"]
    q0, qx, qy, qd = (v // 2 for v in (i, p["ix"], p["iy"], p["idg"]))
    FB = FF // 32

    ps = peers(p)
    zu, zd = {"batch": lax.rem(z + 1, Z)}, {"batch": lax.rem(z + Z - 1, Z)}
    zp = [lax.rem(z + k, Z) for k in range(1, Z)]
    group = [lax.rem(w8 + k, 8) for k in range(1, 8)]
    seat = lambda w: {"seq": s - p["c"] + w // Z, "batch": lax.rem(w, Z)}
    all_here = greet([{"seq": p["base"] + j} for j in ps] + [{"seq": s - p["c"] + e, "batch": q} for q in zp for e in range(2)])

    local = lambda src, dst, sem: pltpu.make_async_copy(src, dst, sem)
    fetched = {k: local(r.__dict__["h_" + k], r.__dict__[k], r.isem.at[n]) for n, k in enumerate(FETCH)}
    for c in fetched.values(): c.start()

    for q, ref in enumerate((r.v0, r.v1, r.v2, r.v3, r.v4, r.v5)): r.vecs[q:q + 1, :] = ref[...].reshape(1, D)
    for q in range(2): r.vecs[6 + q:7 + q, :] = r.v6[q * D:(q + 1) * D].reshape(1, D)
    for q in range(8): r.upb[q:q + 1, :] = r.v7[q * FT:(q + 1) * FT].reshape(1, FT)

    lane = lambda off, n: pl.ds(pl.multiple_of(off, 128), n)
    local = lambda src, dst, sem: pltpu.make_async_copy(src, dst, sem)
    gw_copy = local(r.glu_w, r.gw, r.lsem.at[0])
    gw_copy.start()
    def tile_copy(t, slot):
        return (local(r.up_w.at[:, lane(t * FT, FT)], r.wu.at[slot], r.tsem.at[0, slot]),
                local(r.down_w.at[pl.ds(pl.multiple_of(t * FT, FT), FT)], r.wd.at[slot], r.tsem.at[1, slot]))
    for t in range(2):
        for c in tile_copy(t, t): c.start()
    def slice_copy():
        return [c for q in range(4) for c in (
            local(r.up_w.at[:, lane((q * 8 + w8) * FB, FB)], r.wu.at[0, :, pl.ds(q * FB, FB)], r.ssem.at[0, q]),
            local(r.down_w.at[pl.ds(pl.multiple_of((q * 8 + w8) * FB, FB), FB)], r.wd.at[0, pl.ds(q * FB, FB)], r.ssem.at[1, q]))]
    wgs_copy = [local(r.glu_w.at[:, lane(q * D + i * 128, 128)], r.wgs.at[:, pl.ds(q * 128, 128)], r.lsem.at[1 + q]) for q in range(2)]
    for c in wgs_copy: c.start()

    @tiles(T, 16)
    def _(q):
        r.xs[q, :] = r.x[q, :].astype(F32)
        r.own_cot[q, :] = r.cot[q, :].astype(F32)
    all_here()
    nxt, prv = {"seq": lax.rem(s + 1, NSEQ)}, {"seq": lax.rem(s + NSEQ - 1, NSEQ)}
    halo_copy = remote(r.xs, r.halo, r.hsem.at[0], r.hsem.at[1], nxt)
    pl.when(s < NSEQ - 1)(lambda: halo_copy.start())
    gc = Line(Z, z, p, r.own_cot, r.land_cot, r.lss.at[0], r.lsr.at[0], zu, zd)
    gs = Line(Z, z, p, r.own_sec, r.land_sec, r.lss.at[1], r.lsr.at[1], zu, zd)
    ga = Gather(p, r.own_act, r.land_act, r.gss, r.gsr)
    gc.start()

    for k in ("rate", "freq", "cre", "cim", "prior"): fetched[k].wait()
    mode_args = (r.rate, r.freq, r.cre, r.cim, r.prior)
    fwd_tiles(nbits, 0, D // LT, *mode_args, r.kern, r.resp, r.big)
    gc.pass_on(1, 0)

    @tiles(T, ROWS)
    def _(q):
        hat, inv = norm_hat(r.xs[q, :])
        r.xhat[q, :] = hat
        r.xinv[q, :] = jnp.broadcast_to(inv, (ROWS, 128))
        r.ext[sub(T, q), :] = hat * vec["first_gain"]() + vec["first_shift"]()
    @pl.when(s > 0)
    def _():
        halo_copy.wait_recv()
    @pl.when(s == 0)
    def _():
        r.halo[...] = jnp.zeros_like(r.halo)
    keep = jnp.where(s == 0, 0.0, 1.0)
    @tiles(T, ROWS)
    def _(q):
        hat, _ = norm_hat(r.halo[q, :])
        r.ext[q, :] = (hat * vec["first_gain"]() + vec["first_shift"]()) * keep

    for k in ("ftab", "itab", "jtab", "gtab"): fetched[k].wait()
    inner = lax.broadcasted_iota(jnp.int32, (KLEN, LC), 0) > 0
    @tiles(D, LC)
    def _(c):
        X = table_dot(r.ftab, r.ext[:, c])
        K = table_dot(r.ftab, r.kern[:, c], cols=slice(0, KLEN))
        r.X[:, c] = X
        r.K[:, c] = K
        P_, Q_, KP, KQ = X[:KLEN], X[KLEN:], K[:KLEN], K[KLEN:]
        qq = Q_ * KQ
        po = P_ * KP - jnp.where(inner, qq, 0.0)
        qo = jnp.where(inner, P_ * KQ + Q_ * KP, qq)
        y = table_dot(r.itab, jnp.concatenate([po, qo], 0))
        r.pre[:, c] = y + vec["skip_gain"](c) * r.ext[T:, c] + r.resp[:, c]
    @tiles(T, 16)
    def _(q):
        a = gelu_both(r.pre[q, :])[0].astype(BF16)
        r.own_act[q, :] = a.astype(F32)
        r.act_all[sub(i * T, q), :] = a
    gc.pass_on(1, 1)
    ga.start()

    gw_copy.wait()
    act = r.act_all[iblk, :]
    @tiles(D, LC)
    def _(c):
        r.val[:, c] = dot(act, r.gw[:, c])
        r.sg[:, c] = dot(act, r.gw[:, lane(D + c.start, LC)])
    @tiles(T, ROWS)
    def _(q):
        v = r.val[q, :] + vec["value_bias"]()
        g = jax.nn.sigmoid(r.sg[q, :] + vec["gate_bias"]())
        r.val[q, :] = v
        r.sg[q, :] = g
        m = r.xs[q, :] + v * g
        r.merged[q, :] = m
        hat, inv = norm_hat(m)
        r.mhat[q, :] = hat
        r.minv[q, :] = jnp.broadcast_to(inv, (ROWS, 128))
        r.own_sec[q, :] = (hat * vec["second_gain"]() + vec["second_shift"]()).astype(BF16).astype(F32)
    @tiles(T, 16)
    def _(q):
        r.sec_all[sub(own8 * T, q), :] = r.own_sec[q, :].astype(BF16)
    gs.start()
    gc.pass_on(2, 0)

    r.oacc[...] = jnp.zeros_like(r.oacc)
    r.sacc[...] = jnp.zeros_like(r.sacc)
    sec = r.sec_all[pl.ds(pl.multiple_of(own8 * T, T), T), :]
    @pl.loop(0, 8)
    def _(t):
        slot = lax.rem(t, 2)
        for c in tile_copy(t, slot): c.wait()
        r.u[pl.ds(0, T)] = dot(sec, r.wu[slot])
        r.gh[pl.ds(0, T)] = dot(r.cot[...], r.wd[slot], 1, 1)
        def rows_u(q, acc):
            hid, slope = gelu_both(r.u[q, :] + r.upb[pl.ds(t, 1), :])
            gu = r.gh[q, :] * slope
            r.hid[q, :] = hid.astype(BF16)
            r.gul[q, :] = gu.astype(BF16)
            return acc + jnp.sum(gu.reshape(8, 8, FT), 0)
        r.ubg[pl.ds(t, 1), :] = fold(tiles(T, 64)(rows_u, jnp.zeros((8, FT), F32)))
        r.oacc[...] += dot(r.hid[pl.ds(0, T), :], r.wd[slot])
        r.sacc[...] += dot(r.gul[pl.ds(0, T), :], r.wu[slot], 1, 1)
        @pl.when(t < 6)
        def _():
            for c in tile_copy(t + 2, slot): c.start()
        pl.when(t == 1)(lambda: gc.pass_on(2, 1))
        pl.when(t == 2)(ga.relay1)
        @pl.when(t == 5)
        def _():
            gs.pass_on(1, 0)
            ga.relay2()
    for c in slice_copy(): c.start()
    gs.pass_on(1, 1)
    ga.relay3()

    zero = jnp.zeros((ROWS, D), F32)
    def rows_a(q, carry):
        r.oacc[q, :] = r.merged[q, :] + r.oacc[q, :] + vec["down_bias"]()
        g, hat, c = r.sacc[q, :], r.mhat[q, :], r.own_cot[q, :]
        gm = c + norm_back(g * vec["second_gain"](), hat, r.minv[q, 0:1])
        r.gm[q, :] = gm
        return carry[0] + g * hat, carry[1] + g, carry[2] + c
    sums = tiles(T, ROWS)(rows_a, (zero,) * 3)
    for k, v in zip((3, 4, 5), sums): r.ssrc[4 * M + k:4 * M + k + 1, :] = fold(v)
    gm_sends = []
    for k, j in enumerate(ps):
        c = remote(r.gm.at[:, lane(j * 128, 128)], r.gm_all.at[i], r.ms.at[k], r.mr.at[k], {"seq": p["base"] + j})
        c.start()
        gm_sends.append(c)
    r.gm_all[i] = r.gm[:, lane(i * 128, 128)]
    @tiles(T, 16)
    def _(q):
        r.out_v[q, :] = r.oacc[q, :].astype(BF16)
    def rows_b(q, carry):
        gm, g = r.gm[q, :], r.sg[q, :]
        gv, gg = gm * g, gm * r.val[q, :] * g * (1.0 - g)
        r.glow[q, pl.ds(0, D)] = gv.astype(BF16)
        r.glow[q, pl.ds(D, D)] = gg.astype(BF16)
        return carry[0] + jnp.sum(gv.reshape(2, ROWS, D), 0), carry[1] + jnp.sum(gg.reshape(2, ROWS, D), 0)
    gb = tiles(T, 16)(rows_b, (zero,) * 2)
    gb = [fold(v) for v in gb]
    for j in range(8):
        for q in range(2):
            off = (j % 4) * 256 + q * 128
            r.ssrc[4 * M + 6 + q:4 * M + 7 + q, j * 128:(j + 1) * 128] = gb[j // 4][:, off:off + 128]
    glow = r.glow[...]
    @tiles(D, LC)
    def _(c):
        r.gz[:, c] = dot(glow, r.gw[c, :], 1, 1)
    @tiles(T, ROWS)
    def _(q):
        r.gz[q, :] = r.gz[q, :] * gelu_both(r.pre[q, :])[1]
    @tiles(D, LC)
    def _(c):
        G = table_dot(r.jtab, r.gz[:, c])
        gp, gq = G[:KLEN], G[KLEN:]
        def pair(ref):
            a, b = ref[pl.ds(0, KLEN), c], ref[pl.ds(KLEN, KLEN), c]
            bq = gq * b
            return jnp.concatenate([gp * a + jnp.where(inner, bq, 0.0), jnp.where(inner, gq * a - gp * b, bq)], 0)
        r.kern[:, c] = table_dot(r.gtab, pair(r.X), rows=slice(0, KLEN))
        r.ext[:, c] = table_dot(r.gtab, pair(r.K))
    tail_copy = remote(r.ext.at[pl.ds(0, T)], r.tail, r.hsem.at[2], r.hsem.at[3], prv)
    pl.when(s > 0)(lambda: tail_copy.start())
    gs.pass_on(2, 0)

    for which in ("own", "x", "y", "d"):
        for j in ga.chip(which):
            @tiles(T, 16)
            def _(q):
                r.act_all[sub(j * T, q), :] = ga.land[j, q, :].astype(BF16)
    for k in range(7):
        src = lax.rem(i + 7 - k, 8)
        remote(r.gm_all.at[src], r.gm_all.at[src], r.ms.at[k], r.mr.at[k], nxt).wait_recv()
    for c in wgs_copy: c.wait()
    gbias = jnp.concatenate([r.vecs[6:7, lane(i * 128, 128)], r.vecs[7:8, lane(i * 128, 128)]], 1)
    @tiles(8 * T, 256)
    def _(q):
        r.u[:, pl.ds(0, 256)] = dot(r.act_all[q, :], r.wgs[...]) + gbias
        for h in range(256 // T):
            blk = q.start // T + h
            @tiles(T, 32)
            def _(k):
                row = pl.ds(pl.multiple_of(h * T + k.start, 32), 32)
                v, g = r.u[row, pl.ds(0, 128)], jax.nn.sigmoid(r.u[row, pl.ds(128, 128)])
                gm = r.gm_all[blk, k, :]
                rows = pl.ds(pl.multiple_of(q.start + h * T + k.start, 32), 32)
                r.ggl[rows, :] = jnp.concatenate([gm * g, gm * v * g * (1.0 - g)], 1).astype(BF16)
    @tiles(D, 256)
    def _(c):
        g = dot(r.act_all[:, c], r.ggl[...], 0, 0)
        for q in range(256 // HB):
            j = c.start // 128 + q // Z
            r.glg[q % Z, pl.ds(pl.multiple_of(j * HB, HB), HB), :] = g[q * HB:(q + 1) * HB]

    LU = lambda t: r.lgl.at[0, t - 1]
    LD = lambda t: r.lgl.at[1, t]
    def cu(t, src=None):
        return remote(LU(t) if src is None else src, LU(t), r.zs.at[0, t - 1], r.zr.at[0, t - 1], zu)
    def cd(t, src=None):
        return remote(LD(t) if src is None else src, LD(t), r.zs.at[1, t], r.zr.at[1, t], zd)
    def add_into(dst, srcs):
        @tiles(dst.shape[0], 16)
        def _(q):
            v = srcs[0][q, :]
            for e in srcs[1:]: v = v + e[q, :]
            dst[q, :] = v
    def z_start():
        for h in range(Z - 1, 0, -1):
            pl.when(z == 0)(lambda: cu(h, r.glg.at[h]).start())
            pl.when(z == Z - 1)(lambda: cd(Z - 1 - h, r.glg.at[Z - 1 - h]).start())
    def z_slot(slot):
        for zz in range(1, Z - 1):
            @pl.when(z == zz)
            def _():
                for t in range(Z - 1, zz, -1):
                    if (Z - 1 - t) + zz == slot:
                        cu(t).wait_recv()
                        add_into(LU(t), (LU(t), r.glg.at[t]))
                        cu(t).start()
                for t in range(zz):
                    if t + (Z - 1 - zz) == slot:
                        cd(t).wait_recv()
                        add_into(LD(t), (LD(t), r.glg.at[t]))
                        cd(t).start()
    def z_final(dst):
        for zz in range(Z):
            @pl.when(z == zz)
            def _():
                srcs = [r.glg.at[zz]]
                if zz > 0:
                    cu(zz).wait_recv()
                    srcs.append(LU(zz))
                if zz < Z - 1:
                    cd(zz).wait_recv()
                    srcs.append(LD(zz))
                add_into(dst, srcs)
    def z_drain():
        for zz in range(Z):
            @pl.when(z == zz)
            def _():
                for t in range(zz + 1, Z): cu(t).wait_send()
                for t in range(zz): cd(t).wait_send()
    z_start()

    gs.pass_on(2, 1)

    bwd_args = (nbits, T, *mode_args, r.kern, r.gz, r.ssrc, r.qr, r.qi, r.big)
    srow = 4 * M + 16
    bwd_tiles(0, 4, srow, *bwd_args)
    bwd_tiles(4, D // LT, srow, *bwd_args)
    pl.when(s < NSEQ - 1)(lambda: tail_copy.wait_recv())
    @pl.when(s == NSEQ - 1)
    def _():
        r.tail[...] = jnp.zeros_like(r.tail)
    def rows_c(q, carry):
        hat, gz = r.xhat[q, :], r.gz[q, :]
        gn = r.ext[sub(T, q), :] + r.tail[q, :] + vec["skip_gain"]() * gz
        r.oacc[q, :] = r.gm[q, :] + norm_back(gn * vec["first_gain"](), hat, r.xinv[q, 0:1])
        return carry[0] + gn * hat, carry[1] + gn, carry[2] + gz * hat, carry[3] + gz
    sums = [fold(v) for v in tiles(T, ROWS)(rows_c, (zero,) * 4)]
    sums = (sums[0], sums[1], sums[2] * vec["first_gain"]() + sums[3] * vec["first_shift"]())
    for k, v in enumerate(sums): r.ssrc[4 * M + k:4 * M + k + 1, :] = v
    @tiles(T, 16)
    def _(q):
        r.ig_v[q, :] = r.oacc[q, :].astype(BF16)
    early = [local(r.out_v, r.out, r.osem.at[0]), local(r.ig_v, r.ig, r.osem.at[1])]
    for c in early: c.start()
    r.ssrc[4 * M + 8:4 * M + 16, :] = jnp.zeros((8, D), F32)
    for j in range(8):
        for e in range(FT // 128): r.ssrc[4 * M + 8 + e:4 * M + 9 + e, j * 128:(j + 1) * 128] = r.ubg[j:j + 1, e * 128:(e + 1) * 128]

    NR, NS = 4 * M + 16 + 2 * M, 2 * M
    sends = []
    def push(src, dst, a, b, dev):
        c = remote(src, dst, a, b, dev)
        c.start()
        sends.append(c)
    for k, j in enumerate(ps):
        push(r.ssrc.at[:, lane(j * 128, 128)], r.sland.at[i], r.sa.at[0, k], r.sa.at[1, k], {"seq": p["base"] + j})
    def small_sum():
        tot = r.ssrc[:, lane(i * 128, 128)]
        for k in range(7):
            src = lax.rem(i + 7 - k, 8)
            remote(r.sland.at[src], r.sland.at[src], r.sa.at[0, k], r.sa.at[1, k], nxt).wait_recv()
            tot = tot + r.sland[src]
        r.mine[...] = tot
        r.st[i] = tot[NR - NS:NR]
        for c in small_sends()[:7]: c.start()
    def small_sends():
        return ([remote(r.mine.at[pl.ds(NR - NS, NS)], r.st.at[i], r.sb.at[0, k], r.sb.at[1, k], {"seq": p["base"] + j}) for k, j in enumerate(ps)]
                + [remote(r.mine, r.zland.at[z], r.sz.at[0, k], r.sz.at[1, k], {"batch": q}) for k, q in enumerate(zp)])

    z_slot(1)

    def low_rows(src, dst, b8):
        @tiles(T, 32)
        def _(q):
            dst[sub(b8 * T, q), :] = src[b8, q, :].astype(BF16)
    @tiles(T, 16)
    def _(q):
        r.cot_all[sub(own8 * T, q), :] = r.cot[q, :]
    gc.settle_own()
    low_rows(r.land_cot, r.cot_all, z * 2 + 1 - p["c"])
    low_half = z < Z // 2
    near_end = jnp.where(low_half, z, Z - 1 - z)
    def chip_at(k):
        at = jnp.where(k <= near_end, near_end - k, k)
        return jnp.where(low_half, at, Z - 1 - at)
    @pl.loop(1, Z)
    def _(k):
        at = chip_at(k)
        gc.settle(at)
        low_rows(r.land_cot, r.cot_all, at * 2)
        low_rows(r.land_cot, r.cot_all, at * 2 + 1)


    for c in slice_copy(): c.wait()
    for zz in range(Z):
        @pl.when(z == zz)
        def _():
            for q in range(4): r.upbs[0:1, q * FB:(q + 1) * FB] = r.upb[pl.ds(q * 2 + p["c"], 1), :][:, zz * FB:(zz + 1) * FB]
    def slice_chunk(k):
        at = chip_at(k)
        @pl.when(k == 0)
        def _():
            gs.settle_own()
            low_rows(r.land_sec, r.sec_all, z * 2 + 1 - p["c"])
        @pl.when(k > 0)
        def _():
            gs.settle(at)
            low_rows(r.land_sec, r.sec_all, at * 2)
            low_rows(r.land_sec, r.sec_all, at * 2 + 1)
        q = pl.ds(pl.multiple_of(at * 2 * T, 2 * T), 2 * T)
        r.u[...] = dot(r.sec_all[q, :], r.wu[0])
        r.gh[...] = dot(r.cot_all[q, :], r.wd[0], 1, 1)
        @tiles(2 * T, 64)
        def _(e):
            hid, slope = gelu_both(r.u[e, :] + r.upbs[0:1, :])
            r.hid[sub(at * 2 * T, e), :] = hid.astype(BF16)
            r.gul[sub(at * 2 * T, e), :] = (r.gh[e, :] * slope).astype(BF16)
    pl.loop(0, 2)(slice_chunk)
    z_slot(2)
    small_sum()
    pl.loop(2, Z - 1)(slice_chunk)
    pl.loop(Z - 1, Z)(slice_chunk)
    z_final(r.glf)
    for k, j in enumerate(ps):
        for q in range(2):
            push(r.glf.at[pl.ds(pl.multiple_of(j * HB, HB), HB), pl.ds(q * 128, 128)], r.glu_out.at[:, lane(q * D + i * 128, 128)],
                 r.ga.at[0, q, k], r.ga.at[1, q, k], {"seq": p["base"] + j})

    own, land = (r.upg, r.dng), (r.lup, r.ldn)
    X, Y = {"seq": p["base"] + p["ix"]}, {"seq": p["base"] + p["iy"]}
    def piece(n, q, h):
        half = own[n].shape[1] // 2
        return own[n].at[q, pl.ds(h * half, half)]
    def hop(n, k, dev, src=None):
        return remote(land[n].at[k] if src is None else src, land[n].at[k], r.rs.at[0, n, k], r.rs.at[1, n, k], dev)
    def plane_start(n):
        for k, dev, q, h in ((0, X, qd, 0), (2, Y, qd, 1), (1, X, qx, 0), (3, Y, qy, 1)): hop(n, k, dev, piece(n, q, h)).start()
    def plane_middle(n):
        for k, q, h, k2, dev in ((0, qy, 0, 4, Y), (2, qx, 1, 5, X)):
            hop(n, k, X).wait_recv()
            add_into(land[n].at[k], (land[n].at[k], piece(n, q, h)))
            hop(n, k2, dev, land[n].at[k]).start()
    def plane_end(n, dst):
        half = own[n].shape[1] // 2
        for h, near, second in ((0, 1, 4), (1, 3, 5)):
            hop(n, near, X).wait_recv()
            hop(n, second, X).wait_recv()
            add_into(dst.at[pl.ds(h * half, half)], (piece(n, q0, h), land[n].at[near], land[n].at[second]))
    @tiles(D, 256)
    def _(c):
        r.upg[c.start // 256] = dot(r.sec_all[:, c], r.gul[...], 0, 0)
    plane_start(0)
    for c in small_sends()[7:]: c.start()
    for fc in range(FT // 256):
        for nh in range(D // 512):
            g = dot(r.hid[:, fc * 256:(fc + 1) * 256], r.cot_all[:, nh * 512:(nh + 1) * 512], 0, 0)
            n = 256 // FB
            for q in range(n): r.dng[fc * n + q, :, nh * 512:(nh + 1) * 512] = g[q * FB:(q + 1) * FB]
    plane_middle(0)
    plane_start(1)
    plane_end(0, r.upf)
    for k, w in enumerate(group):
        push(r.upf.at[pl.ds(pl.multiple_of(w * HB, HB), HB)], r.uland.at[w8], r.ua.at[0, k], r.ua.at[1, k], seat(w))
    r.uland[w8] = r.upf[pl.ds(pl.multiple_of(w8 * HB, HB), HB), :]
    acc = r.mine[...]
    for k in range(Z - 1):
        src = lax.rem(z + Z - 1 - k, Z)
        remote(r.mine, r.zland.at[src], r.sz.at[0, k], r.sz.at[1, k], zu).wait_recv()
        acc = acc + r.zland[src]
    r.tot[...] = acc
    plane_middle(1)
    for q in range(2):
        r.glu_out[:, lane(q * D + i * 128, 128)] = r.glf[pl.ds(pl.multiple_of(i * HB, HB), HB), pl.ds(q * 128, 128)]
    for k in range(7):
        src = lax.rem(i + 7 - k, 8)
        remote(r.st.at[src], r.st.at[src], r.sb.at[0, k], r.sb.at[1, k], nxt).wait_recv()
        for q in range(2):
            blk = r.glu_out.at[:, lane(q * D + src * 128, 128)]
            remote(blk, blk, r.ga.at[0, q, k], r.ga.at[1, q, k], nxt).wait_recv()
    for k in range(7):
        src = lax.rem(w8 + 7 - k, 8)
        remote(r.uland.at[src], r.uland.at[src], r.ua.at[0, k], r.ua.at[1, k], nxt).wait_recv()
    for w in range(8):
        for q in range(4): r.up_out[:, (q * 8 + w) * FB:(q * 8 + w + 1) * FB] = r.uland[w, :, q * FB:(q + 1) * FB]
    plane_end(1, r.down_o)

    for c in early: c.wait()
    pl.when(s < NSEQ - 1)(lambda: halo_copy.wait_send())
    pl.when(s > 0)(lambda: tail_copy.wait_send())
    for c in gm_sends + sends + small_sends(): c.wait_send()
    gc.drain()
    gs.drain()
    ga.drain()
    z_drain()
    for n in range(2):
        for k in range(6): hop(n, k, X).wait_send()


def layer(cfg, tabs, vecs, rate, freq, cre, cim, prior, x, cot, glu_w, up_w, down_w, cid):
    Z, NSEQ, nbits, T, D, FF, M = cfg
    FT, HB = FF // 8, D // 8 // Z
    NR = 4 * M + 16 + 2 * M
    NT = NR
    vm, hbm = pl.BlockSpec(memory_space=pltpu.VMEM), pl.BlockSpec(memory_space=pl.ANY)
    S = lambda shape, dt=F32: jax.ShapeDtypeStruct(shape, dt)
    given = dict(zip(("ftab", "itab", "jtab", "gtab"), tabs), rate=rate, freq=freq, cre=cre, cim=cim, prior=prior)
    ins = dict(h_ftab=hbm, h_itab=hbm, h_jtab=hbm, h_gtab=hbm, **{f"v{k}": vm for k in range(8)}, h_rate=hbm, h_freq=hbm, h_cre=hbm, h_cim=hbm, h_prior=hbm, x=vm, cot=vm,
               glu_w=hbm, up_w=hbm, down_w=hbm)
    outs = dict(out=S((T, D), BF16), ig=S((T, D), BF16), st=S((8, 2 * M, 128)), tot=S((NT, 128)), down_o=S((FT // Z, D)),
                up_out=S((HB, FF)), glu_out=S((HB, 2 * D)))
    V, DS = pltpu.VMEM, lambda *n: pltpu.SemaphoreType.DMA(n)
    row = lambda: V((T, D), F32)
    scr = dict(
        **{k: V(given[k].shape, given[k].dtype) for k in FETCH}, isem=DS(len(FETCH)), osem=DS(2),
        out_v=V((T, D), BF16), ig_v=V((T, D), BF16),
        vecs=V((8, D), F32), upb=V((8, FT), F32),
        xs=row(), own_cot=row(), own_sec=row(), own_act=row(), halo=row(), tail=row(), xhat=row(), pre=row(), val=row(), sg=row(),
        merged=row(), mhat=row(), gm=row(), gz=row(), oacc=row(), sacc=row(), resp=row(), kern=row(),
        xinv=V((T, 128), F32), minv=V((T, 128), F32), ext=V((2 * T, D), F32), X=V((2 * KLEN, D), F32), K=V((2 * KLEN, D), F32),
        land_cot=V((8, T, D), F32), land_sec=V((8, T, D), F32), land_act=V((8, T, D), F32),
        cot_all=V((8 * T, D), BF16), sec_all=V((8 * T, D), BF16), act_all=V((8 * T, D), BF16),
        gw=V((D, 2 * D), BF16), wu=V((2, D, FT), BF16), wd=V((2, FT, D), BF16), wgs=V((D, 256), BF16),
        u=V((256, FT), F32), gh=V((256, FT), F32), hid=V((8 * T, FT), BF16), gul=V((8 * T, FT), BF16),
        glow=V((T, 2 * D), BF16), gm_all=V((8, T, 128), F32), ggl=V((8 * T, 256), BF16),
        upg=V((Z, D // Z, FT), F32), glg=V((Z, D // Z, 256), F32), dng=V((Z, FT // Z, D), F32),
        lup=V((6, D // 8, FT), F32), ldn=V((6, FF // 64, D), F32), uland=V((8, HB, FT), F32), ubg=V((8, FT), F32), upbs=V((8, FT), F32),
        lgl=V((2, Z - 1, D // Z, 256), F32), upf=V((D // Z, FT), F32), glf=V((D // Z, 256), F32),
        qr=V((16, M, LT), F32), qi=V((16, M, LT), F32), big=V((64 * M, LT), F32),
        ssrc=V((NR, D), F32), sland=V((8, NR, 128), F32), mine=V((NT, 128), F32), zland=V((Z, NT, 128), F32),
        lsem=DS(3), tsem=DS(2, 2), hsem=DS(4), gss=DS(14), gsr=DS(14), ms=DS(7), mr=DS(7), zs=DS(2, Z - 1), zr=DS(2, Z - 1),
        lss=DS(2, 3, 2 * Z - 1, 2), lsr=DS(2, 3, 2 * Z - 1, 2), rs=DS(2, 2, 6), ssem=DS(2, 4),
        sa=DS(2, 7), ua=DS(2, 7), sb=DS(2, 7), ga=DS(2, 2, 7), sz=DS(2, Z - 1))
    names = (*ins, *outs, *scr)
    res = pl.pallas_call(
        functools.partial(layer_kernel, cfg, names),
        out_shape=list(outs.values()), in_specs=list(ins.values()), out_specs=[pl.BlockSpec(memory_space=pltpu.HBM)] * 2 + [vm] * (len(outs) - 2), scratch_shapes=list(scr.values()),
        compiler_params=pltpu.CompilerParams(collective_id=cid, has_side_effects=True, vmem_limit_bytes=67043328),
        name="layer")(*tabs, *vecs, rate, freq, cre, cim, prior, x, cot, glu_w, up_w, down_w)
    return dict(zip(outs, res))


def finish_kernel(cfg, names, *refs):
    r = Bag()
    r.__dict__.update(zip(names, refs))
    Z, NSEQ, nbits, T, D, FF, M = cfg
    HB = D // 8 // Z
    b = lax.axis_index("batch")
    for k in ("out", "ig", "glu_out", "up_out", "down_o"): r.__dict__["o_" + k][...] = r.__dict__[k][...]
    for j in range(8): r.o_st[:, j * 128:(j + 1) * 128] = r.st[j]
    r.turned[...] = r.tot[0:4 * M, :].T
    mine = r.turned[pl.ds(pl.multiple_of(b * HB, HB), HB), :]
    for k in range(4): r.__dict__[f"m{k}"][...] = mine[:, k * M:(k + 1) * M]
    v = pltpu.roll(r.tot[4 * M:4 * M + 8, :], lax.rem(128 - b * HB, 128), 1)
    for k in range(6): r.__dict__[f"w{k}"][...] = v[k, 0:HB]
    per = 128 // (2 * HB)
    g = r.tot[pl.ds(4 * M + 6 + b // per, 1), :]
    r.gb[...] = pltpu.roll(jnp.broadcast_to(g, (8, 128)), lax.rem(128 - lax.rem(b, per) * 2 * HB, 128), 1)[0, 0:2 * HB]
    r.ub[...] = r.tot[pl.ds(4 * M + 8 + b, 1), :].reshape(128)


def finish(cfg, o):
    Z, NSEQ, nbits, T, D, FF, M = cfg
    HB = D // 8 // Z
    vm = pl.BlockSpec(memory_space=pltpu.VMEM)
    S = lambda shape, dt=F32: jax.ShapeDtypeStruct(shape, dt)
    outs = {"o_" + k: S(o[k].shape, o[k].dtype) for k in ("out", "ig", "glu_out", "up_out", "down_o")}
    outs["o_st"] = S((2 * M, D))
    outs.update({f"m{k}": S((HB, M)) for k in range(4)})
    outs.update({f"w{k}": S((HB,)) for k in range(6)})
    outs.update(gb=S((2 * HB,)), ub=S((FF // 8 // Z,)))
    names = (*o, *outs, "turned")
    res = pl.pallas_call(functools.partial(finish_kernel, cfg, names), out_shape=list(outs.values()), in_specs=[vm] * len(o),
                         out_specs=[vm] * len(outs), scratch_shapes=[pltpu.VMEM((128, 4 * M), F32)], name="finish")(*o.values())
    return {k.removeprefix("o_"): v for k, v in zip(outs, res)}


def tables(window):
    half = window // 2
    f = np.concatenate([np.arange(half + 1), np.arange(1, half)])[:, None]
    imag = np.arange(window)[:, None] > half
    ph = (f * np.arange(window)[None, :] % window) * (2.0 * np.pi / window)
    fwd = np.where(imag, -np.sin(ph), np.cos(ph))
    wt = np.where((f == 0) | (2 * f == window), 1.0, 2.0) / window
    inv = (wt * fwd).T[half:]
    def parts(a):
        a = np.ascontiguousarray(a).astype(np.float32)
        high = a.astype(ml_dtypes.bfloat16)
        return jnp.asarray(np.stack([high, (a - high.astype(np.float32)).astype(ml_dtypes.bfloat16)]))
    return parts(fwd), parts(inv), parts(inv.T), parts(fwd.T)


def plane_shards(Z, n_seq, inputs, first_gain, first_shift, decay_rate, rotation, out_real, out_imag, skip_gain, glu_weight,
                 glu_bias, second_gain, second_shift, up_weight, up_bias, down_weight, down_bias, prior_state, cotangent):
    T, D = inputs.shape[1:]
    FF, M = up_weight.shape[1], decay_rate.shape[1]
    FT, HB = FF // 8, D // 8 // Z
    cfg = (Z, n_seq, max(1, (n_seq - 1).bit_length()), T, D, FF, M)
    vecs = (first_gain, first_shift, skip_gain, second_gain, second_shift, down_bias, glu_bias, up_bias)
    o = layer(cfg, tables(T + KLEN), vecs, decay_rate.T, rotation.T, out_real.T, out_imag.T, prior_state,
              inputs[0], cotangent[0], glu_weight, up_weight, down_weight, 0)
    f = finish(cfg, o)
    v = [f[f"w{k}"] for k in range(6)]
    m = [f[f"m{k}"] for k in range(4)]
    return (f["out"][None], f["ig"][None], f["st"].reshape(1, 2, M, D), v[0], v[1], *m, v[2], f["glu_out"], f["gb"],
            v[3], v[4], f["up_out"], f["ub"], f["down_o"], v[5])


def solution(mesh):
    in_specs = (
        P("batch", "seq", None),
        P(),
        P(),
        P(),
        P(),
        P(),
        P(),
        P(),
        P(),
        P(),
        P(),
        P(),
        P(),
        P(),
        P(),
        P(),
        P("batch", None, None, None),
        P("batch", "seq", None),
    )
    out_specs = (
        P("batch", "seq", None),
        P("batch", "seq", None),
        P("batch", None, None, None),
        P(("seq", "batch")),
        P(("seq", "batch")),
        P(("seq", "batch"), None),
        P(("seq", "batch"), None),
        P(("seq", "batch"), None),
        P(("seq", "batch"), None),
        P(("seq", "batch")),
        P(("seq", "batch"), None),
        P(("seq", "batch")),
        P(("seq", "batch")),
        P(("seq", "batch")),
        P(("seq", "batch"), None),
        P(("seq", "batch")),
        P(("seq", "batch"), None),
        P(("seq", "batch")),
    )
    body = shards
    if mesh.shape["seq"] == 8:
        body = functools.partial(plane_shards, mesh.shape["batch"], mesh.shape["seq"])
    return jax.shard_map(body, mesh=mesh, in_specs=in_specs, out_specs=out_specs, check_vma=False)
```

```python
import functools
import math

import jax
import jax.numpy as jnp
import ml_dtypes
import numpy as np
from jax import lax
from jax.experimental import pallas as pl
from jax.experimental.pallas import tpu as pltpu
from jax.sharding import PartitionSpec as P

KLEN = 128
BOTH = ("seq", "batch")
LT = 128
MESH = pl.DeviceIdType.MESH
F32, BF16 = jnp.float32, jnp.bfloat16


EPSILON = 1e-05
HIGHEST = lax.Precision.HIGHEST


def from_behind(value, axis, by):
    peers = lax.axis_size(axis)
    pairs = [(i, i + by) for i in range(peers) if 0 <= i + by < peers]
    return lax.ppermute(value, axis, pairs)


def norm_rows(values, gain, shift):
    center = values - jnp.mean(values, axis=-1, keepdims=True)
    spread = jnp.mean(center * center, axis=-1, keepdims=True)
    return center * lax.rsqrt(spread + EPSILON) * gain + shift


def mode_terms(rate_modes, freq_modes, elapsed):
    moment = elapsed[None, :, None]
    damping = jnp.exp(-rate_modes[:, None, :] * moment)
    return (
        damping * jnp.cos(freq_modes[:, None, :] * moment),
        damping * jnp.sin(freq_modes[:, None, :] * moment),
    )


def glu_gate(glu_pre):
    split_at = glu_pre.shape[-1] // 2
    return glu_pre[:, :split_at] * jax.nn.sigmoid(glu_pre[:, split_at:])


def gelu_exact(values):
    return jax.nn.gelu(values, approximate=False)


def shards(
    inputs,
    first_gain,
    first_shift,
    decay_rate,
    rotation,
    out_real,
    out_imag,
    skip_gain,
    glu_weight,
    glu_bias,
    second_gain,
    second_shift,
    up_weight,
    up_bias,
    down_weight,
    down_bias,
    prior_state,
    cotangent,
):
    seg_count, tok_count, feature = inputs.shape
    row_count = seg_count * tok_count
    window = tok_count + KLEN
    half = window // 2 + 1
    offset = lax.axis_index("seq") * tok_count
    freq_index = jnp.arange(half, dtype=jnp.int32)
    time_index = jnp.arange(window, dtype=jnp.int32)
    phase = (freq_index[:, None] * time_index[None, :] % window).astype(jnp.float32) * (
        2.0 * math.pi / window
    )
    cos_half = jnp.cos(phase)
    sin_half = jnp.sin(phase)
    forward_table = jnp.concatenate([cos_half, -sin_half], axis=0)
    weights = jnp.where((freq_index == 0) | (2 * freq_index == window), 1.0, 2.0).astype(
        jnp.float32
    )
    inverse_table = (
        jnp.concatenate(
            [(weights[:, None] * cos_half).T, -(weights[:, None] * sin_half).T], axis=1
        )[KLEN:]
        / window
    )
    local_steps = jnp.arange(tok_count).astype(jnp.float32)
    advance_steps = (offset + 1).astype(jnp.float32)

    def mixing(
        normed, halo_rows, rate_modes, freq_modes, real_modes, imag_modes, skip_local, prior_local
    ):
        table_real, table_imag = mode_terms(rate_modes, freq_modes, local_steps)
        kernel = jnp.einsum("mkh,mh->kh", table_real, real_modes, precision=HIGHEST) - jnp.einsum(
            "mkh,mh->kh", table_imag, imag_modes, precision=HIGHEST
        )
        extended = jnp.concatenate([halo_rows, normed], axis=1)
        spectrum = jnp.einsum("ft,sth->sfh", forward_table, extended, precision=HIGHEST)
        kern_spec = jnp.dot(forward_table[:, :KLEN], kernel, precision=HIGHEST)
        spec_real, spec_imag = (spectrum[:, :half], spectrum[:, half:])
        kern_real, kern_imag = (kern_spec[:half], kern_spec[half:])
        product = jnp.concatenate(
            [
                spec_real * kern_real - spec_imag * kern_imag,
                spec_real * kern_imag + spec_imag * kern_real,
            ],
            axis=1,
        )
        convolved = jnp.einsum("tf,sfh->sth", inverse_table, product, precision=HIGHEST)
        damping = jnp.exp(-rate_modes * advance_steps)
        adv_real = damping * jnp.cos(freq_modes * advance_steps)
        adv_imag = damping * jnp.sin(freq_modes * advance_steps)
        coef_real = real_modes * adv_real - imag_modes * adv_imag
        coef_imag = real_modes * adv_imag + imag_modes * adv_real
        drive_real = coef_real * prior_local[:, 0] - coef_imag * prior_local[:, 1]
        drive_imag = coef_real * prior_local[:, 1] + coef_imag * prior_local[:, 0]
        response = jnp.einsum(
            "mth,smh->sth", table_real, drive_real, precision=HIGHEST
        ) - jnp.einsum("mth,smh->sth", table_imag, drive_imag, precision=HIGHEST)
        return gelu_exact(convolved + skip_local * normed + response)

    source = inputs.astype(jnp.float32)
    normed, first_pull = jax.vjp(norm_rows, source, first_gain, first_shift)
    halo_rows = from_behind(normed, "seq", 1)
    activated, mix_pull = jax.vjp(
        mixing,
        normed,
        halo_rows,
        decay_rate.T,
        rotation.T,
        out_real.T,
        out_imag.T,
        skip_gain,
        prior_state,
    )
    activated_low = activated.reshape(row_count, feature).astype(jnp.bfloat16)
    glu_pre = jnp.dot(activated_low, glu_weight, preferred_element_type=jnp.float32) + glu_bias
    branch, glu_pull = jax.vjp(glu_gate, glu_pre)
    merged = source.reshape(row_count, feature) + branch
    second, second_pull = jax.vjp(norm_rows, merged, second_gain, second_shift)
    second_low = second.astype(jnp.bfloat16)
    up_pre = jnp.dot(second_low, up_weight, preferred_element_type=jnp.float32) + up_bias
    hidden, hidden_pull = jax.vjp(gelu_exact, up_pre)
    hidden_low = hidden.astype(jnp.bfloat16)
    result = (
        merged + jnp.dot(hidden_low, down_weight, preferred_element_type=jnp.float32) + down_bias
    )
    outputs = result.astype(jnp.bfloat16).reshape(seg_count, tok_count, feature)
    grad_out = cotangent.astype(jnp.float32).reshape(row_count, feature)
    down_bias_grad = jnp.sum(grad_out, axis=0)
    grad_low = grad_out.astype(jnp.bfloat16)
    down_grad = jnp.einsum("rf,rh->fh", hidden_low, grad_low, preferred_element_type=jnp.float32)
    grad_hidden = jnp.einsum("rh,fh->rf", grad_low, down_weight, preferred_element_type=jnp.float32)
    (grad_up,) = hidden_pull(grad_hidden)
    up_bias_grad = jnp.sum(grad_up, axis=0)
    up_low = grad_up.astype(jnp.bfloat16)
    up_grad = jnp.einsum("rh,rf->hf", second_low, up_low, preferred_element_type=jnp.float32)
    grad_second = jnp.einsum("rf,hf->rh", up_low, up_weight, preferred_element_type=jnp.float32)
    grad_merged, second_gain_grad, second_shift_grad = second_pull(grad_second)
    grad_merged = grad_merged + grad_out
    (grad_glu,) = glu_pull(grad_merged)
    glu_bias_grad = jnp.sum(grad_glu, axis=0)
    glu_low = grad_glu.astype(jnp.bfloat16)
    glu_grad = jnp.einsum("rh,rg->hg", activated_low, glu_low, preferred_element_type=jnp.float32)
    grad_activated = jnp.einsum(
        "rg,hg->rh", glu_low, glu_weight, preferred_element_type=jnp.float32
    )
    grad_normed, grad_halo, rate_grad, freq_grad, real_grad, imag_grad, skip_grad, prior_grad = (
        mix_pull(grad_activated.reshape(seg_count, tok_count, feature))
    )
    grad_tail = from_behind(grad_halo, "seq", -1)
    grad_normed = jnp.concatenate(
        [grad_normed[:, : tok_count - KLEN], grad_normed + grad_tail], axis=1
    )
    grad_source, first_gain_grad, first_shift_grad = first_pull(grad_normed)
    input_grad = (grad_source + grad_merged.reshape(seg_count, tok_count, feature)).astype(
        jnp.bfloat16
    )
    state_grad = lax.psum(prior_grad, "seq")
    rate_back = rate_grad.T
    freq_back = freq_grad.T
    real_back = real_grad.T
    imag_back = imag_grad.T
    summed = (
        lax.psum_scatter(first_gain_grad, BOTH, scatter_dimension=0, tiled=True),
        lax.psum_scatter(first_shift_grad, BOTH, scatter_dimension=0, tiled=True),
        lax.psum_scatter(rate_back, BOTH, scatter_dimension=0, tiled=True),
        lax.psum_scatter(freq_back, BOTH, scatter_dimension=0, tiled=True),
        lax.psum_scatter(real_back, BOTH, scatter_dimension=0, tiled=True),
        lax.psum_scatter(imag_back, BOTH, scatter_dimension=0, tiled=True),
        lax.psum_scatter(skip_grad, BOTH, scatter_dimension=0, tiled=True),
        lax.psum_scatter(glu_grad, BOTH, scatter_dimension=0, tiled=True),
        lax.psum_scatter(glu_bias_grad, BOTH, scatter_dimension=0, tiled=True),
        lax.psum_scatter(second_gain_grad, BOTH, scatter_dimension=0, tiled=True),
        lax.psum_scatter(second_shift_grad, BOTH, scatter_dimension=0, tiled=True),
        lax.psum_scatter(up_grad, BOTH, scatter_dimension=0, tiled=True),
        lax.psum_scatter(up_bias_grad, BOTH, scatter_dimension=0, tiled=True),
        lax.psum_scatter(down_grad, BOTH, scatter_dimension=0, tiled=True),
        lax.psum_scatter(down_bias_grad, BOTH, scatter_dimension=0, tiled=True),
    )
    return (
        outputs,
        input_grad,
        state_grad,
        summed[0],
        summed[1],
        summed[2],
        summed[3],
        summed[4],
        summed[5],
        summed[6],
        summed[7],
        summed[8],
        summed[9],
        summed[10],
        summed[11],
        summed[12],
        summed[13],
        summed[14],
    )


def plane():
    s = lax.axis_index("seq")
    i = lax.rem(s, 8)
    base = s - i
    c, x, y = lax.rem(i, 2), lax.rem(i // 2, 2), i // 4
    ic, ix, iy = i + 1 - 2 * c, i + 2 - 4 * x, i + 4 - 8 * y
    idg = iy + 2 - 4 * x
    return dict(s=s, i=i, base=base, c=c, x=x, y=y, ic=ic, ix=ix, iy=iy, idg=idg)

def sib_of(p, j):
    return j + 1 - 2 * p["c"]

def remote(src, dst, ss, rs, dev):
    return pltpu.make_async_remote_copy(src_ref=src, dst_ref=dst, send_sem=ss, recv_sem=rs,
                                        device_id=dev, device_id_type=MESH)

def greet(devs):
    bar = pltpu.get_barrier_semaphore()
    for d in devs:
        pl.semaphore_signal(bar, inc=1, device_id=d, device_id_type=MESH)
    return lambda: pl.semaphore_wait(bar, len(devs))

def peers(p):
    return [lax.rem(p["i"] + k, 8) for k in range(1, 8)]

class Gather:
    def __init__(self, p, own, land, ssem, rsem):
        self.p, self.own, self.land, self.ss, self.rs = p, own, land, ssem, rsem
        self.H = own.shape[0] // 2
        seq = lambda j: {"seq": p["base"] + j}
        self.X, self.Y, self.S = seq(p["ix"]), seq(p["iy"]), seq(p["ic"])

    def cp(self, k, j, h, dev, src=None):
        blk = self.land.at[j, pl.ds(h * self.H, self.H)]
        return remote(blk if src is None else src, blk, self.ss.at[k], self.rs.at[k], dev)

    def plan(self):
        i, ix, iy, idg = self.p["i"], self.p["ix"], self.p["iy"], self.p["idg"]
        return [(0, i, 0, self.X), (2, i, 1, self.Y), (1, i, 1, self.X), (3, i, 0, self.Y), (6, i, 0, self.S), (7, i, 1, self.S),
                (4, ix, 0, self.Y), (8, ix, 0, self.S), (5, iy, 1, self.X), (11, iy, 1, self.S), (9, ix, 1, self.S),
                (10, iy, 0, self.S), (12, idg, 0, self.S), (13, idg, 1, self.S)]

    def _send(self, k, own=False):
        k, j, h, dev = next(e for e in self.plan() if e[0] == k)
        self.cp(k, j, h, dev, self.own.at[pl.ds(h * self.H, self.H)] if own else None).start()

    def _got(self, k, j, h):
        self.cp(k, j, h, self.S).wait_recv()

    def start(self):
        for k in (0, 2, 1, 3, 6, 7):
            self._send(k, True)

    def relay1(self):
        p = self.p
        self._got(0, p["ix"], 0); self._send(4); self._send(8)
        self._got(2, p["iy"], 1); self._send(5); self._send(11)

    def relay2(self):
        p = self.p
        self._got(1, p["ix"], 1); self._send(9)
        self._got(3, p["iy"], 0); self._send(10)

    def relay3(self):
        p = self.p
        self._got(4, p["idg"], 0); self._send(12)
        self._got(5, p["idg"], 1); self._send(13)

    def chip(self, which):
        p = self.p
        k, j = {"own": (6, p["ic"]), "x": (8, sib_of(p, p["ix"])), "y": (10, sib_of(p, p["iy"])), "d": (12, sib_of(p, p["idg"]))}[which]
        self._got(k, j, 0)
        self._got(k + 1, j, 1)
        return (j,) if which == "own" else ({"x": p["ix"], "y": p["iy"], "d": p["idg"]}[which], j)

    def drain(self):
        for k, j, h, dev in self.plan():
            self.cp(k, j, h, dev).wait_send()


class Line:
    def __init__(self, Z, z, p, own, land, ssem, rsem, zu, zd):
        self.Z, self.z, self.c, self.own, self.land, self.ss, self.rs = Z, z, p["c"], own, land, ssem, rsem
        self.H = own.shape[0] // 2
        self.dev = (zu, zd, {"seq": p["base"] + p["ic"]})

    def part(self, chip, core, half):
        return self.land.at[chip * 2 + core, pl.ds(half * self.H, self.H)]

    def cp(self, way, hop, half, chip, core, own=False):
        blk = self.part(chip, core, half)
        src = self.own.at[pl.ds(half * self.H, self.H)] if own else blk
        return remote(src, blk, self.ss.at[way, hop, half], self.rs.at[way, hop, half], self.dev[way])

    def ends(self):
        z, Z = self.z, self.Z
        return ((lambda h: z - h, lambda h: z - h >= 0, z < Z - 1), (lambda h: z + h, lambda h: z + h < Z, z > 0))

    def start(self):
        for half in range(2):
            for way, (chip, there, on) in enumerate(self.ends()):
                pl.when(on)(lambda: self.cp(way, 0, half, self.z, self.c, True).start())
        for half in range(2): self.cp(2, 0, half, self.z, self.c, True).start()

    def _take(self, way, hop, half, chip):
        self.cp(way, hop - 1, half, chip, self.c).wait_recv()
        self.cp(2, hop + way * (self.Z - 1), half, chip, self.c).start()

    def pass_on(self, hop, half):
        for way, (chip, there, on) in enumerate(self.ends()):
            @pl.when(there(hop) & on)
            def _():
                self._take(way, hop, half, chip(hop))
                self.cp(way, hop, half, chip(hop), self.c).start()

    def settle(self, chip_at):
        for way, (chip, there, on) in enumerate(self.ends()):
            for hop in range(1, self.Z):
                @pl.when(chip_at == chip(hop))
                def _():
                    for half in range(2):
                        pl.when(jnp.logical_not(on))(lambda: self._take(way, hop, half, chip(hop)))
                    for half in range(2):
                        self.cp(2, hop + way * (self.Z - 1), half, chip(hop), 1 - self.c).wait_recv()

    def settle_own(self):
        for half in range(2): self.cp(2, 0, half, self.z, 1 - self.c).wait_recv()

    def drain(self):
        for half in range(2):
            self.cp(2, 0, half, self.z, self.c, True).wait_send()
            for way, (chip, there, on) in enumerate(self.ends()):
                for hop in range(self.Z - 1):
                    pl.when(there(hop) & on)(lambda: self.cp(way, hop, half, chip(hop), self.c).wait_send())
                for hop in range(1, self.Z):
                    pl.when(there(hop))(lambda: self.cp(2, hop + way * (self.Z - 1), half, chip(hop), self.c).wait_send())


def cmul(ar, ai, br, bi):
    return ar * br - ai * bi, ar * bi + ai * br

def lam_of(rate, freq):
    damp = jnp.exp(-rate)
    q = freq * freq
    cosv = 1.0 + q * (-1.0/2 + q * (1.0/24 + q * (-1.0/720 + q * (1.0/40320 + q * (-1.0/3628800)))))
    sinv = freq * (1.0 + q * (-1.0/6 + q * (1.0/120 + q * (-1.0/5040 + q * (1.0/362880)))))
    return damp * cosv, damp * sinv

def power_rows(lr, li, qr, qi, A):
    l2 = cmul(lr, li, lr, li); l4 = cmul(*l2, *l2); l8 = cmul(*l4, *l4)
    cur = (jnp.ones_like(lr), jnp.zeros_like(lr))
    for a in range(A):
        qr[a] = cur[0]; qi[a] = cur[1]
        cur = cmul(*cur, *l8)
    return l2, l4, cur

def offset_power(top, s, nbits):
    res = (jnp.ones_like(top[0]), jnp.zeros_like(top[0]))
    sq = top
    for bit in range(nbits):
        on = lax.rem(lax.div(s, 1 << bit), 2) == 1
        nxt = cmul(*res, *sq)
        res = (jnp.where(on, nxt[0], res[0]), jnp.where(on, nxt[1], res[1]))
        if bit + 1 < nbits: sq = cmul(*sq, *sq)
    return res

def fwd_tiles(nbits, lo, hi, rate, freq, cre, cim, prior, kern, resp, co):
    M = rate.shape[0]
    A = kern.shape[0] // 8
    s = lax.axis_index("seq")
    b = lax.broadcasted_iota(jnp.int32, (8, LT), 0)
    o1, o2, o4 = (b % 2) == 1, ((b // 2) % 2) == 1, b >= 4
    one, zero = jnp.ones((8, LT), F32), jnp.zeros((8, LT), F32)
    square = lambda v: cmul(*v, *v)
    @pl.loop(lo, hi)
    def _(lt):
        cols = pl.ds(pl.multiple_of(lt * LT, LT), LT)
        l1 = lam_of(rate[:, cols], freq[:, cols])
        l2 = square(l1)
        l4 = square(l2)
        l8 = square(l4)
        top = l8
        for _ in range((A - 1).bit_length()): top = square(top)
        off = cmul(*offset_power(top, s, nbits), *l1)
        c = cre[:, cols], cim[:, cols]
        d = cmul(*cmul(*c, *off), prior[0, 0, :, cols], prior[0, 1, :, cols])
        rows = (*l1, *l2, *l4, *c, *cmul(*c, *l8), *d, *cmul(*d, *l8), 2.0 * l8[0], -(l8[0] * l8[0] + l8[1] * l8[1]))
        for k, v in enumerate(rows): co[pl.ds(k * M, M), :] = v
        def step(m, accs):
            row = lambda k: jnp.broadcast_to(co[pl.ds(k * M + m, 1), :], (8, LT))
            e = jnp.where(o1, row(0), one), jnp.where(o1, row(1), zero)
            e = cmul(*e, jnp.where(o2, row(2), one), jnp.where(o2, row(3), zero))
            er, ei = cmul(*e, jnp.where(o4, row(4), one), jnp.where(o4, row(5), zero))
            p, q = row(14), row(15)
            k0, k1 = er * row(6) - ei * row(7), er * row(8) - ei * row(9)
            r0, r1 = er * row(10) - ei * row(11), er * row(12) - ei * row(13)
            out = list(accs)
            for a in range(A):
                out[2 * a] = out[2 * a] + k0
                out[2 * a + 1] = out[2 * a + 1] + r0
                if a < A - 1:
                    k0, k1 = k1, p * k1 + q * k0
                    r0, r1 = r1, p * r1 + q * r0
            return tuple(out)
        accs = lax.fori_loop(0, M, step, tuple(jnp.zeros((8, LT), F32) for _ in range(2 * A)), unroll=4)
        for a in range(A):
            kern[pl.ds(8 * a, 8), cols] = accs[2 * a]
            resp[pl.ds(8 * a, 8), cols] = accs[2 * a + 1]


def bwd_tiles(lo, hi, srow, nbits, TOK, rate, freq, cre, cim, prior, kg, gz, out, qr, qi, acc):
    M = rate.shape[0]
    A = kg.shape[0] // 8
    s = lax.axis_index("seq")
    adv = (s * TOK + 1).astype(F32)
    @pl.loop(lo, hi)
    def _(lt):
        cols = pl.ds(pl.multiple_of(lt * LT, LT), LT)
        lr, li = lam_of(rate[:, cols], freq[:, cols])
        l2, l4, top = power_rows(lr, li, qr, qi, A)
        def step(m, carry):
            for j, g in enumerate((kg, gz)):
                z = jnp.zeros((8, LT), F32)
                sr, si, tr, ti = z, z, z, z
                for a in range(A - 1, -1, -1):
                    ga = g[pl.ds(8 * a, 8), cols]
                    sr = sr + ga * qr[a, pl.ds(m, 1), :]
                    si = si + ga * qi[a, pl.ds(m, 1), :]
                    if a > 0:
                        tr = tr + sr
                        ti = ti + si
                for q, v in enumerate((sr, si, tr, ti)):
                    acc[pl.ds(pl.multiple_of(((4 * j + q) * M + m) * 8, 8), 8), :] = v
            return carry
        lax.fori_loop(0, M, step, 0, unroll=8)
        pw = (jnp.ones_like(lr), jnp.zeros_like(lr))
        zero = jnp.zeros_like(lr)
        ar, ai, br, bi = [zero] * 2, [zero] * 2, [zero] * 2, [zero] * 2
        for b in range(8):
            for j in range(2):
                ld = lambda q: acc[pl.ds((4 * j + q) * M * 8 + b, M, stride=8), :]
                S = ld(0), ld(1)
                U = 8.0 * ld(2), 8.0 * ld(3)
                if b: U = U[0] + float(b) * S[0], U[1] + float(b) * S[1]
                w = cmul(*pw, *S)
                ar[j], ai[j] = ar[j] + w[0], ai[j] + w[1]
                w = cmul(*pw, *U)
                br[j], bi[j] = br[j] + w[0], bi[j] + w[1]
            pw = cmul(*pw, lr, li)
        off = cmul(*offset_power(top, s, nbits), lr, li)
        c = cre[:, cols], cim[:, cols]
        ps = cmul(*off, prior[0, 0, :, cols], prior[0, 1, :, cols])
        u = cmul(*ps, ar[1], ai[1])
        v = cmul(*ps, br[1] + adv * ar[1], bi[1] + adv * ai[1])
        v = cmul(*c, v[0] + br[0], v[1] + bi[0])
        w = cmul(*cmul(*c, *off), ar[1], ai[1])
        for k, val in enumerate((-v[0], -v[1], u[0] + ar[0], -(u[1] + ai[0]))): out[k * M:(k + 1) * M, cols] = val
        for k, val in enumerate((w[0], -w[1])): out[srow + k * M:srow + (k + 1) * M, cols] = val


class Bag:
    pass


def dot(a, b, ca=1, cb=0):
    return lax.dot_general(a, b, (((ca,), (cb,)), ((), ())), preferred_element_type=F32)


def split_low(v):
    high = v.astype(BF16)
    return high, (v - high.astype(F32)).astype(BF16)


def table_dot(tab, v, rows=slice(None), cols=slice(None)):
    high, low = split_low(v)
    th, tl = tab[0, rows, cols], tab[1, rows, cols]
    return dot(th, high) + dot(th, low) + dot(tl, high)


def gelu_both(u):
    cdf = 0.5 + 0.5 * lax.erf(u * (0.5 ** 0.5))
    return u * cdf, cdf + u * (jnp.exp(-0.5 * u * u) * ((2.0 * math.pi) ** -0.5))


def tiles(n, step):
    def run(body, init=None):
        if init is None:
            @pl.loop(0, n // step)
            def _(k):
                body(pl.ds(pl.multiple_of(k * step, step), step))
            return None
        return lax.fori_loop(0, n // step, lambda k, c: body(pl.ds(pl.multiple_of(k * step, step), step), c), init)
    return run


def sub(off, q):
    return pl.ds(pl.multiple_of(off + q.start, q.size), q.size)


def row_mean(v):
    return jnp.sum(v, axis=-1, keepdims=True) * (1.0 / v.shape[-1])


def norm_hat(v):
    center = v - row_mean(v)
    inv = lax.rsqrt(row_mean(center * center) + EPSILON)
    return center * inv, inv


def norm_back(gg, hat, inv):
    return inv * (gg - row_mean(gg) - hat * row_mean(gg * hat))


def fold(v):
    return jnp.sum(v, axis=0, keepdims=True)


LC = 256
ROWS = 8
FETCH = ("rate", "freq", "cre", "cim", "prior", "ftab", "itab", "jtab", "gtab")
VEC = ("first_gain", "first_shift", "skip_gain", "second_gain", "second_shift", "down_bias", "value_bias", "gate_bias")


def layer_kernel(cfg, names, *refs):
    r = Bag()
    r.__dict__.update(zip(names, refs))
    Z, NSEQ, nbits, T, D, FF, M = cfg
    FT = FF // 8
    HB = D // 8 // Z
    p = plane()
    s, i = p["s"], p["i"]
    z = lax.axis_index("batch")
    vec = {k: (lambda q: (lambda c=slice(None): r.vecs[q:q + 1, c]))(q) for q, k in enumerate(VEC)}
    iblk = pl.ds(pl.multiple_of(i * T, T), T)
    w8, own8 = p["c"] * Z + z, z * 2 + p["c"]
    q0, qx, qy, qd = (v // 2 for v in (i, p["ix"], p["iy"], p["idg"]))
    FB = FF // 32

    ps = peers(p)
    zu, zd = {"batch": lax.rem(z + 1, Z)}, {"batch": lax.rem(z + Z - 1, Z)}
    zp = [lax.rem(z + k, Z) for k in range(1, Z)]
    group = [lax.rem(w8 + k, 8) for k in range(1, 8)]
    seat = lambda w: {"seq": s - p["c"] + w // Z, "batch": lax.rem(w, Z)}
    all_here = greet([{"seq": p["base"] + j} for j in ps] + [{"seq": s - p["c"] + e, "batch": q} for q in zp for e in range(2)])

    local = lambda src, dst, sem: pltpu.make_async_copy(src, dst, sem)
    fetched = {k: local(r.__dict__["h_" + k], r.__dict__[k], r.isem.at[n]) for n, k in enumerate(FETCH)}
    for c in fetched.values(): c.start()

    for q, ref in enumerate((r.v0, r.v1, r.v2, r.v3, r.v4, r.v5)): r.vecs[q:q + 1, :] = ref[...].reshape(1, D)
    for q in range(2): r.vecs[6 + q:7 + q, :] = r.v6[q * D:(q + 1) * D].reshape(1, D)
    for q in range(8): r.upb[q:q + 1, :] = r.v7[q * FT:(q + 1) * FT].reshape(1, FT)

    lane = lambda off, n: pl.ds(pl.multiple_of(off, 128), n)
    local = lambda src, dst, sem: pltpu.make_async_copy(src, dst, sem)
    gw_copy = local(r.glu_w, r.gw, r.lsem.at[0])
    gw_copy.start()
    def tile_copy(t, slot):
        return (local(r.up_w.at[:, lane(t * FT, FT)], r.wu.at[slot], r.tsem.at[0, slot]),
                local(r.down_w.at[pl.ds(pl.multiple_of(t * FT, FT), FT)], r.wd.at[slot], r.tsem.at[1, slot]))
    for t in range(2):
        for c in tile_copy(t, t): c.start()
    def slice_copy():
        return [c for q in range(4) for c in (
            local(r.up_w.at[:, lane((q * 8 + w8) * FB, FB)], r.wu.at[0, :, pl.ds(q * FB, FB)], r.ssem.at[0, q]),
            local(r.down_w.at[pl.ds(pl.multiple_of((q * 8 + w8) * FB, FB), FB)], r.wd.at[0, pl.ds(q * FB, FB)], r.ssem.at[1, q]))]
    wgs_copy = [local(r.glu_w.at[:, lane(q * D + i * 128, 128)], r.wgs.at[:, pl.ds(q * 128, 128)], r.lsem.at[1 + q]) for q in range(2)]
    for c in wgs_copy: c.start()

    @tiles(T, 16)
    def _(q):
        r.xs[q, :] = r.x[q, :].astype(F32)
        r.own_cot[q, :] = r.cot[q, :].astype(F32)
    all_here()
    nxt, prv = {"seq": lax.rem(s + 1, NSEQ)}, {"seq": lax.rem(s + NSEQ - 1, NSEQ)}
    halo_copy = remote(r.xs, r.halo, r.hsem.at[0], r.hsem.at[1], nxt)
    pl.when(s < NSEQ - 1)(lambda: halo_copy.start())
    gc = Line(Z, z, p, r.own_cot, r.land_cot, r.lss.at[0], r.lsr.at[0], zu, zd)
    gs = Line(Z, z, p, r.own_sec, r.land_sec, r.lss.at[1], r.lsr.at[1], zu, zd)
    ga = Gather(p, r.own_act, r.land_act, r.gss, r.gsr)
    gc.start()

    for k in FETCH[:5]: fetched[k].wait()
    mode_args = (r.rate, r.freq, r.cre, r.cim, r.prior)
    fwd_tiles(nbits, 0, D // LT, *mode_args, r.kern, r.resp, r.big)
    gc.pass_on(1, 0)

    @tiles(T, ROWS)
    def _(q):
        hat, inv = norm_hat(r.xs[q, :])
        r.xhat[q, :] = hat
        r.xinv[q, :] = jnp.broadcast_to(inv, (ROWS, 128))
        r.ext[sub(T, q), :] = hat * vec["first_gain"]() + vec["first_shift"]()
    @pl.when(s > 0)
    def _():
        halo_copy.wait_recv()
    @pl.when(s == 0)
    def _():
        r.halo[...] = jnp.zeros_like(r.halo)
    keep = jnp.where(s == 0, 0.0, 1.0)
    @tiles(T, ROWS)
    def _(q):
        hat, _ = norm_hat(r.halo[q, :])
        r.ext[q, :] = (hat * vec["first_gain"]() + vec["first_shift"]()) * keep

    for k in FETCH[5:]: fetched[k].wait()
    inner = lax.broadcasted_iota(jnp.int32, (KLEN, LC), 0) > 0
    @tiles(D, LC)
    def _(c):
        X = table_dot(r.ftab, r.ext[:, c])
        K = table_dot(r.ftab, r.kern[:, c], cols=slice(0, KLEN))
        r.X[:, c] = X
        r.K[:, c] = K
        P_, Q_, KP, KQ = X[:KLEN], X[KLEN:], K[:KLEN], K[KLEN:]
        qq = Q_ * KQ
        po = P_ * KP - jnp.where(inner, qq, 0.0)
        qo = jnp.where(inner, P_ * KQ + Q_ * KP, qq)
        y = table_dot(r.itab, jnp.concatenate([po, qo], 0))
        r.pre[:, c] = y + vec["skip_gain"](c) * r.ext[T:, c] + r.resp[:, c]
    @tiles(T, 16)
    def _(q):
        a = gelu_both(r.pre[q, :])[0].astype(BF16)
        r.own_act[q, :] = a.astype(F32)
        r.act_all[sub(i * T, q), :] = a
    gc.pass_on(1, 1)
    ga.start()

    gw_copy.wait()
    act = r.act_all[iblk, :]
    @tiles(D, LC)
    def _(c):
        r.val[:, c] = dot(act, r.gw[:, c])
        r.sg[:, c] = dot(act, r.gw[:, lane(D + c.start, LC)])
    @tiles(T, ROWS)
    def _(q):
        v = r.val[q, :] + vec["value_bias"]()
        g = jax.nn.sigmoid(r.sg[q, :] + vec["gate_bias"]())
        r.val[q, :] = v
        r.sg[q, :] = g
        m = r.xs[q, :] + v * g
        r.merged[q, :] = m
        hat, inv = norm_hat(m)
        r.mhat[q, :] = hat
        r.minv[q, :] = jnp.broadcast_to(inv, (ROWS, 128))
        r.own_sec[q, :] = (hat * vec["second_gain"]() + vec["second_shift"]()).astype(BF16).astype(F32)
    @tiles(T, 16)
    def _(q):
        r.sec_all[sub(own8 * T, q), :] = r.own_sec[q, :].astype(BF16)
    gs.start()
    gc.pass_on(2, 0)

    r.oacc[...] = jnp.zeros_like(r.oacc)
    r.sacc[...] = jnp.zeros_like(r.sacc)
    sec = r.sec_all[pl.ds(pl.multiple_of(own8 * T, T), T), :]
    @pl.loop(0, 8)
    def _(t):
        slot = lax.rem(t, 2)
        for c in tile_copy(t, slot): c.wait()
        r.u[pl.ds(0, T)] = dot(sec, r.wu[slot])
        r.gh[pl.ds(0, T)] = dot(r.cot[...], r.wd[slot], 1, 1)
        def rows_u(q, acc):
            hid, slope = gelu_both(r.u[q, :] + r.upb[pl.ds(t, 1), :])
            gu = r.gh[q, :] * slope
            r.hid[q, :] = hid.astype(BF16)
            r.gul[q, :] = gu.astype(BF16)
            return acc + jnp.sum(gu.reshape(8, 8, FT), 0)
        r.ubg[pl.ds(t, 1), :] = fold(tiles(T, 64)(rows_u, jnp.zeros((8, FT), F32)))
        r.oacc[...] += dot(r.hid[pl.ds(0, T), :], r.wd[slot])
        r.sacc[...] += dot(r.gul[pl.ds(0, T), :], r.wu[slot], 1, 1)
        @pl.when(t < 6)
        def _():
            for c in tile_copy(t + 2, slot): c.start()
        pl.when(t == 1)(lambda: gc.pass_on(2, 1))
        pl.when(t == 2)(ga.relay1)
        @pl.when(t == 5)
        def _():
            gs.pass_on(1, 0)
            ga.relay2()
    for c in slice_copy(): c.start()
    gs.pass_on(1, 1)
    ga.relay3()

    zero = jnp.zeros((ROWS, D), F32)
    def rows_a(q, carry):
        r.oacc[q, :] = r.merged[q, :] + r.oacc[q, :] + vec["down_bias"]()
        g, hat, c = r.sacc[q, :], r.mhat[q, :], r.own_cot[q, :]
        gm = c + norm_back(g * vec["second_gain"](), hat, r.minv[q, 0:1])
        r.gm[q, :] = gm
        return carry[0] + g * hat, carry[1] + g, carry[2] + c
    sums = tiles(T, ROWS)(rows_a, (zero,) * 3)
    for k, v in zip((3, 4, 5), sums): r.ssrc[4 * M + k:4 * M + k + 1, :] = fold(v)
    gm_sends = []
    for k, j in enumerate(ps):
        c = remote(r.gm.at[:, lane(j * 128, 128)], r.gm_all.at[i], r.ms.at[k], r.mr.at[k], {"seq": p["base"] + j})
        c.start()
        gm_sends.append(c)
    r.gm_all[i] = r.gm[:, lane(i * 128, 128)]
    @tiles(T, 16)
    def _(q):
        r.out_v[q, :] = r.oacc[q, :].astype(BF16)
    def rows_b(q, carry):
        gm, g = r.gm[q, :], r.sg[q, :]
        gv, gg = gm * g, gm * r.val[q, :] * g * (1.0 - g)
        r.glow[q, pl.ds(0, D)] = gv.astype(BF16)
        r.glow[q, pl.ds(D, D)] = gg.astype(BF16)
        return carry[0] + jnp.sum(gv.reshape(2, ROWS, D), 0), carry[1] + jnp.sum(gg.reshape(2, ROWS, D), 0)
    gb = tiles(T, 16)(rows_b, (zero,) * 2)
    gb = [fold(v) for v in gb]
    for j in range(8):
        for q in range(2):
            off = (j % 4) * 256 + q * 128
            r.ssrc[4 * M + 6 + q:4 * M + 7 + q, j * 128:(j + 1) * 128] = gb[j // 4][:, off:off + 128]
    glow = r.glow[...]
    @tiles(D, LC)
    def _(c):
        r.gz[:, c] = dot(glow, r.gw[c, :], 1, 1)
    @tiles(T, ROWS)
    def _(q):
        r.gz[q, :] = r.gz[q, :] * gelu_both(r.pre[q, :])[1]
    @tiles(D, LC)
    def _(c):
        G = table_dot(r.jtab, r.gz[:, c])
        gp, gq = G[:KLEN], G[KLEN:]
        def pair(ref):
            a, b = ref[pl.ds(0, KLEN), c], ref[pl.ds(KLEN, KLEN), c]
            bq = gq * b
            return jnp.concatenate([gp * a + jnp.where(inner, bq, 0.0), jnp.where(inner, gq * a - gp * b, bq)], 0)
        r.kern[:, c] = table_dot(r.gtab, pair(r.X), rows=slice(0, KLEN))
        r.ext[:, c] = table_dot(r.gtab, pair(r.K))
    tail_copy = remote(r.ext.at[pl.ds(0, T)], r.tail, r.hsem.at[2], r.hsem.at[3], prv)
    pl.when(s > 0)(lambda: tail_copy.start())
    gs.pass_on(2, 0)

    for which in ("own", "x", "y", "d"):
        for j in ga.chip(which):
            @tiles(T, 16)
            def _(q):
                r.act_all[sub(j * T, q), :] = ga.land[j, q, :].astype(BF16)
    for k in range(7):
        src = lax.rem(i + 7 - k, 8)
        remote(r.gm_all.at[src], r.gm_all.at[src], r.ms.at[k], r.mr.at[k], nxt).wait_recv()
    for c in wgs_copy: c.wait()
    gbias = jnp.concatenate([r.vecs[6:7, lane(i * 128, 128)], r.vecs[7:8, lane(i * 128, 128)]], 1)
    @tiles(8 * T, 256)
    def _(q):
        r.u[:, pl.ds(0, 256)] = dot(r.act_all[q, :], r.wgs[...]) + gbias
        for h in range(256 // T):
            blk = q.start // T + h
            @tiles(T, 32)
            def _(k):
                row = pl.ds(pl.multiple_of(h * T + k.start, 32), 32)
                v, g = r.u[row, pl.ds(0, 128)], jax.nn.sigmoid(r.u[row, pl.ds(128, 128)])
                gm = r.gm_all[blk, k, :]
                rows = pl.ds(pl.multiple_of(q.start + h * T + k.start, 32), 32)
                r.ggl[rows, :] = jnp.concatenate([gm * g, gm * v * g * (1.0 - g)], 1).astype(BF16)
    @tiles(D, 256)
    def _(c):
        g = dot(r.act_all[:, c], r.ggl[...], 0, 0)
        for q in range(256 // HB):
            j = c.start // 128 + q // Z
            r.glg[q % Z, pl.ds(pl.multiple_of(j * HB, HB), HB), :] = g[q * HB:(q + 1) * HB]

    LU = lambda t: r.lgl.at[0, t - 1]
    LD = lambda t: r.lgl.at[1, t]
    def cu(t, src=None):
        return remote(LU(t) if src is None else src, LU(t), r.zs.at[0, t - 1], r.zr.at[0, t - 1], zu)
    def cd(t, src=None):
        return remote(LD(t) if src is None else src, LD(t), r.zs.at[1, t], r.zr.at[1, t], zd)
    def add_into(dst, srcs):
        @tiles(dst.shape[0], 16)
        def _(q):
            v = srcs[0][q, :]
            for e in srcs[1:]: v = v + e[q, :]
            dst[q, :] = v
    def z_start():
        for h in range(Z - 1, 0, -1):
            pl.when(z == 0)(lambda: cu(h, r.glg.at[h]).start())
            pl.when(z == Z - 1)(lambda: cd(Z - 1 - h, r.glg.at[Z - 1 - h]).start())
    def z_slot(slot):
        for zz in range(1, Z - 1):
            @pl.when(z == zz)
            def _():
                for t in range(Z - 1, zz, -1):
                    if (Z - 1 - t) + zz == slot:
                        cu(t).wait_recv()
                        add_into(LU(t), (LU(t), r.glg.at[t]))
                        cu(t).start()
                for t in range(zz):
                    if t + (Z - 1 - zz) == slot:
                        cd(t).wait_recv()
                        add_into(LD(t), (LD(t), r.glg.at[t]))
                        cd(t).start()
    def z_final(dst):
        for zz in range(Z):
            @pl.when(z == zz)
            def _():
                srcs = [r.glg.at[zz]]
                if zz > 0:
                    cu(zz).wait_recv()
                    srcs.append(LU(zz))
                if zz < Z - 1:
                    cd(zz).wait_recv()
                    srcs.append(LD(zz))
                add_into(dst, srcs)
    def z_drain():
        for zz in range(Z):
            @pl.when(z == zz)
            def _():
                for t in range(zz + 1, Z): cu(t).wait_send()
                for t in range(zz): cd(t).wait_send()
    z_start()

    gs.pass_on(2, 1)

    bwd_args = (nbits, T, *mode_args, r.kern, r.gz, r.ssrc, r.qr, r.qi, r.big)
    srow = 4 * M + 16
    bwd_tiles(0, 4, srow, *bwd_args)
    bwd_tiles(4, D // LT, srow, *bwd_args)
    pl.when(s < NSEQ - 1)(lambda: tail_copy.wait_recv())
    @pl.when(s == NSEQ - 1)
    def _():
        r.tail[...] = jnp.zeros_like(r.tail)
    def rows_c(q, carry):
        hat, gz = r.xhat[q, :], r.gz[q, :]
        gn = r.ext[sub(T, q), :] + r.tail[q, :] + vec["skip_gain"]() * gz
        r.oacc[q, :] = r.gm[q, :] + norm_back(gn * vec["first_gain"](), hat, r.xinv[q, 0:1])
        return carry[0] + gn * hat, carry[1] + gn, carry[2] + gz * hat, carry[3] + gz
    sums = [fold(v) for v in tiles(T, ROWS)(rows_c, (zero,) * 4)]
    sums = (sums[0], sums[1], sums[2] * vec["first_gain"]() + sums[3] * vec["first_shift"]())
    for k, v in enumerate(sums): r.ssrc[4 * M + k:4 * M + k + 1, :] = v
    @tiles(T, 16)
    def _(q):
        r.ig_v[q, :] = r.oacc[q, :].astype(BF16)
    early = [local(r.out_v, r.out, r.osem.at[0]), local(r.ig_v, r.ig, r.osem.at[1])]
    for c in early: c.start()
    r.ssrc[4 * M + 8:4 * M + 16, :] = jnp.zeros((8, D), F32)
    for j in range(8):
        for e in range(FT // 128): r.ssrc[4 * M + 8 + e:4 * M + 9 + e, j * 128:(j + 1) * 128] = r.ubg[j:j + 1, e * 128:(e + 1) * 128]

    NR, NS = 4 * M + 16 + 2 * M, 2 * M
    sends = []
    def push(src, dst, a, b, dev):
        c = remote(src, dst, a, b, dev)
        c.start()
        sends.append(c)
    for k, j in enumerate(ps):
        push(r.ssrc.at[:, lane(j * 128, 128)], r.sland.at[i], r.sa.at[0, k], r.sa.at[1, k], {"seq": p["base"] + j})
    def small_sum():
        tot = r.ssrc[:, lane(i * 128, 128)]
        for k in range(7):
            src = lax.rem(i + 7 - k, 8)
            remote(r.sland.at[src], r.sland.at[src], r.sa.at[0, k], r.sa.at[1, k], nxt).wait_recv()
            tot = tot + r.sland[src]
        r.mine[...] = tot
        r.st[i] = tot[NR - NS:NR]
        for c in small_sends()[:7]: c.start()
    def small_sends():
        return ([remote(r.mine.at[pl.ds(NR - NS, NS)], r.st.at[i], r.sb.at[0, k], r.sb.at[1, k], {"seq": p["base"] + j}) for k, j in enumerate(ps)]
                + [remote(r.mine, r.zland.at[z], r.sz.at[0, k], r.sz.at[1, k], {"batch": q}) for k, q in enumerate(zp)])

    z_slot(1)

    def low_rows(src, dst, b8):
        @tiles(T, 32)
        def _(q):
            dst[sub(b8 * T, q), :] = src[b8, q, :].astype(BF16)
    @tiles(T, 16)
    def _(q):
        r.cot_all[sub(own8 * T, q), :] = r.cot[q, :]
    gc.settle_own()
    low_rows(r.land_cot, r.cot_all, z * 2 + 1 - p["c"])
    low_half = z < Z // 2
    near_end = jnp.where(low_half, z, Z - 1 - z)
    def chip_at(k):
        at = jnp.where(k <= near_end, near_end - k, k)
        return jnp.where(low_half, at, Z - 1 - at)
    @pl.loop(1, Z)
    def _(k):
        at = chip_at(k)
        gc.settle(at)
        low_rows(r.land_cot, r.cot_all, at * 2)
        low_rows(r.land_cot, r.cot_all, at * 2 + 1)


    for c in slice_copy(): c.wait()
    for zz in range(Z):
        @pl.when(z == zz)
        def _():
            for q in range(4): r.upbs[0:1, q * FB:(q + 1) * FB] = r.upb[pl.ds(q * 2 + p["c"], 1), :][:, zz * FB:(zz + 1) * FB]
    def slice_chunk(k):
        at = chip_at(k)
        @pl.when(k == 0)
        def _():
            gs.settle_own()
            low_rows(r.land_sec, r.sec_all, z * 2 + 1 - p["c"])
        @pl.when(k > 0)
        def _():
            gs.settle(at)
            low_rows(r.land_sec, r.sec_all, at * 2)
            low_rows(r.land_sec, r.sec_all, at * 2 + 1)
        q = pl.ds(pl.multiple_of(at * 2 * T, 2 * T), 2 * T)
        r.u[...] = dot(r.sec_all[q, :], r.wu[0])
        r.gh[...] = dot(r.cot_all[q, :], r.wd[0], 1, 1)
        @tiles(2 * T, 64)
        def _(e):
            hid, slope = gelu_both(r.u[e, :] + r.upbs[0:1, :])
            r.hid[sub(at * 2 * T, e), :] = hid.astype(BF16)
            r.gul[sub(at * 2 * T, e), :] = (r.gh[e, :] * slope).astype(BF16)
    pl.loop(0, 2)(slice_chunk)
    z_slot(2)
    small_sum()
    pl.loop(2, Z - 1)(slice_chunk)
    pl.loop(Z - 1, Z)(slice_chunk)
    z_final(r.glf)
    for k, j in enumerate(ps):
        for q in range(2):
            push(r.glf.at[pl.ds(pl.multiple_of(j * HB, HB), HB), pl.ds(q * 128, 128)], r.glu_out.at[:, lane(q * D + i * 128, 128)],
                 r.ga.at[0, q, k], r.ga.at[1, q, k], {"seq": p["base"] + j})

    own, land = (r.upg, r.dng), (r.lup, r.ldn)
    X, Y = {"seq": p["base"] + p["ix"]}, {"seq": p["base"] + p["iy"]}
    def piece(n, q, h):
        half = own[n].shape[1] // 2
        return own[n].at[q, pl.ds(h * half, half)]
    def hop(n, k, dev, src=None):
        return remote(land[n].at[k] if src is None else src, land[n].at[k], r.rs.at[0, n, k], r.rs.at[1, n, k], dev)
    def plane_start(n):
        for k, dev, q, h in ((0, X, qd, 0), (2, Y, qd, 1), (1, X, qx, 0), (3, Y, qy, 1)): hop(n, k, dev, piece(n, q, h)).start()
    def plane_middle(n):
        for k, q, h, k2, dev in ((0, qy, 0, 4, Y), (2, qx, 1, 5, X)):
            hop(n, k, X).wait_recv()
            add_into(land[n].at[k], (land[n].at[k], piece(n, q, h)))
            hop(n, k2, dev, land[n].at[k]).start()
    def plane_end(n, dst):
        half = own[n].shape[1] // 2
        for h, near, second in ((0, 1, 4), (1, 3, 5)):
            hop(n, near, X).wait_recv()
            hop(n, second, X).wait_recv()
            add_into(dst.at[pl.ds(h * half, half)], (piece(n, q0, h), land[n].at[near], land[n].at[second]))
    @tiles(D, 256)
    def _(c):
        r.upg[c.start // 256] = dot(r.sec_all[:, c], r.gul[...], 0, 0)
    plane_start(0)
    for c in small_sends()[7:]: c.start()
    for fc in range(FT // 256):
        for nh in range(D // 512):
            g = dot(r.hid[:, fc * 256:(fc + 1) * 256], r.cot_all[:, nh * 512:(nh + 1) * 512], 0, 0)
            n = 256 // FB
            for q in range(n): r.dng[fc * n + q, :, nh * 512:(nh + 1) * 512] = g[q * FB:(q + 1) * FB]
    plane_middle(0)
    plane_start(1)
    plane_end(0, r.upf)
    for k, w in enumerate(group):
        push(r.upf.at[pl.ds(pl.multiple_of(w * HB, HB), HB)], r.uland.at[w8], r.ua.at[0, k], r.ua.at[1, k], seat(w))
    r.uland[w8] = r.upf[pl.ds(pl.multiple_of(w8 * HB, HB), HB), :]
    acc = r.mine[...]
    for k in range(Z - 1):
        src = lax.rem(z + Z - 1 - k, Z)
        remote(r.mine, r.zland.at[src], r.sz.at[0, k], r.sz.at[1, k], zu).wait_recv()
        acc = acc + r.zland[src]
    r.tot[...] = acc
    plane_middle(1)
    for q in range(2):
        r.glu_out[:, lane(q * D + i * 128, 128)] = r.glf[pl.ds(pl.multiple_of(i * HB, HB), HB), pl.ds(q * 128, 128)]
    for k in range(7):
        src = lax.rem(i + 7 - k, 8)
        remote(r.st.at[src], r.st.at[src], r.sb.at[0, k], r.sb.at[1, k], nxt).wait_recv()
        for q in range(2):
            blk = r.glu_out.at[:, lane(q * D + src * 128, 128)]
            remote(blk, blk, r.ga.at[0, q, k], r.ga.at[1, q, k], nxt).wait_recv()
    for k in range(7):
        src = lax.rem(w8 + 7 - k, 8)
        remote(r.uland.at[src], r.uland.at[src], r.ua.at[0, k], r.ua.at[1, k], nxt).wait_recv()
    for w in range(8):
        for q in range(4): r.up_out[:, (q * 8 + w) * FB:(q * 8 + w + 1) * FB] = r.uland[w, :, q * FB:(q + 1) * FB]
    plane_end(1, r.down_o)

    for c in early: c.wait()
    pl.when(s < NSEQ - 1)(lambda: halo_copy.wait_send())
    pl.when(s > 0)(lambda: tail_copy.wait_send())
    for c in gm_sends + sends + small_sends(): c.wait_send()
    gc.drain()
    gs.drain()
    ga.drain()
    z_drain()
    for n in range(2):
        for k in range(6): hop(n, k, X).wait_send()


def layer(cfg, tabs, vecs, rate, freq, cre, cim, prior, x, cot, glu_w, up_w, down_w, cid):
    Z, NSEQ, nbits, T, D, FF, M = cfg
    FT, HB = FF // 8, D // 8 // Z
    NR = 4 * M + 16 + 2 * M
    NT = NR
    vm, hbm = pl.BlockSpec(memory_space=pltpu.VMEM), pl.BlockSpec(memory_space=pl.ANY)
    S = lambda shape, dt=F32: jax.ShapeDtypeStruct(shape, dt)
    given = dict(zip(FETCH[5:], tabs), rate=rate, freq=freq, cre=cre, cim=cim, prior=prior)
    ins = dict(h_ftab=hbm, h_itab=hbm, h_jtab=hbm, h_gtab=hbm, **{f"v{k}": vm for k in range(8)}, h_rate=hbm, h_freq=hbm, h_cre=hbm, h_cim=hbm, h_prior=hbm, x=vm, cot=vm,
               glu_w=hbm, up_w=hbm, down_w=hbm)
    outs = dict(out=S((T, D), BF16), ig=S((T, D), BF16), st=S((8, 2 * M, 128)), tot=S((NT, 128)), down_o=S((FT // Z, D)),
                up_out=S((HB, FF)), glu_out=S((HB, 2 * D)))
    V, DS = pltpu.VMEM, lambda *n: pltpu.SemaphoreType.DMA(n)
    row = lambda: V((T, D), F32)
    scr = dict(
        **{k: V(given[k].shape, given[k].dtype) for k in FETCH}, isem=DS(len(FETCH)), osem=DS(2),
        out_v=V((T, D), BF16), ig_v=V((T, D), BF16),
        vecs=V((8, D), F32), upb=V((8, FT), F32),
        xs=row(), own_cot=row(), own_sec=row(), own_act=row(), halo=row(), tail=row(), xhat=row(), pre=row(), val=row(), sg=row(),
        merged=row(), mhat=row(), gm=row(), gz=row(), oacc=row(), sacc=row(), resp=row(), kern=row(),
        xinv=V((T, 128), F32), minv=V((T, 128), F32), ext=V((2 * T, D), F32), X=V((2 * KLEN, D), F32), K=V((2 * KLEN, D), F32),
        land_cot=V((8, T, D), F32), land_sec=V((8, T, D), F32), land_act=V((8, T, D), F32),
        cot_all=V((8 * T, D), BF16), sec_all=V((8 * T, D), BF16), act_all=V((8 * T, D), BF16),
        gw=V((D, 2 * D), BF16), wu=V((2, D, FT), BF16), wd=V((2, FT, D), BF16), wgs=V((D, 256), BF16),
        u=V((256, FT), F32), gh=V((256, FT), F32), hid=V((8 * T, FT), BF16), gul=V((8 * T, FT), BF16),
        glow=V((T, 2 * D), BF16), gm_all=V((8, T, 128), F32), ggl=V((8 * T, 256), BF16),
        upg=V((Z, D // Z, FT), F32), glg=V((Z, D // Z, 256), F32), dng=V((Z, FT // Z, D), F32),
        lup=V((6, D // 8, FT), F32), ldn=V((6, FF // 64, D), F32), uland=V((8, HB, FT), F32), ubg=V((8, FT), F32), upbs=V((8, FT), F32),
        lgl=V((2, Z - 1, D // Z, 256), F32), upf=V((D // Z, FT), F32), glf=V((D // Z, 256), F32),
        qr=V((16, M, LT), F32), qi=V((16, M, LT), F32), big=V((64 * M, LT), F32),
        ssrc=V((NR, D), F32), sland=V((8, NR, 128), F32), mine=V((NT, 128), F32), zland=V((Z, NT, 128), F32),
        lsem=DS(3), tsem=DS(2, 2), hsem=DS(4), gss=DS(14), gsr=DS(14), ms=DS(7), mr=DS(7), zs=DS(2, Z - 1), zr=DS(2, Z - 1),
        lss=DS(2, 3, 2 * Z - 1, 2), lsr=DS(2, 3, 2 * Z - 1, 2), rs=DS(2, 2, 6), ssem=DS(2, 4),
        sa=DS(2, 7), ua=DS(2, 7), sb=DS(2, 7), ga=DS(2, 2, 7), sz=DS(2, Z - 1))
    names = (*ins, *outs, *scr)
    res = pl.pallas_call(
        functools.partial(layer_kernel, cfg, names),
        out_shape=list(outs.values()), in_specs=list(ins.values()), out_specs=[pl.BlockSpec(memory_space=pltpu.HBM)] * 2 + [vm] * (len(outs) - 2), scratch_shapes=list(scr.values()),
        compiler_params=pltpu.CompilerParams(collective_id=cid, has_side_effects=True, vmem_limit_bytes=67043328),
        name="layer")(*tabs, *vecs, rate, freq, cre, cim, prior, x, cot, glu_w, up_w, down_w)
    return dict(zip(outs, res))


def finish_kernel(cfg, names, *refs):
    r = Bag()
    r.__dict__.update(zip(names, refs))
    Z, NSEQ, nbits, T, D, FF, M = cfg
    HB = D // 8 // Z
    b = lax.axis_index("batch")
    for k in ("out", "ig", "glu_out", "up_out", "down_o"): r.__dict__["o_" + k][...] = r.__dict__[k][...]
    for j in range(8): r.o_st[:, j * 128:(j + 1) * 128] = r.st[j]
    r.turned[...] = r.tot[0:4 * M, :].T
    mine = r.turned[pl.ds(pl.multiple_of(b * HB, HB), HB), :]
    for k in range(4): r.__dict__[f"m{k}"][...] = mine[:, k * M:(k + 1) * M]
    v = pltpu.roll(r.tot[4 * M:4 * M + 8, :], lax.rem(128 - b * HB, 128), 1)
    for k in range(6): r.__dict__[f"w{k}"][...] = v[k, 0:HB]
    per = 128 // (2 * HB)
    g = r.tot[pl.ds(4 * M + 6 + b // per, 1), :]
    r.gb[...] = pltpu.roll(jnp.broadcast_to(g, (8, 128)), lax.rem(128 - lax.rem(b, per) * 2 * HB, 128), 1)[0, 0:2 * HB]
    r.ub[...] = r.tot[pl.ds(4 * M + 8 + b, 1), :].reshape(128)


def finish(cfg, o):
    Z, NSEQ, nbits, T, D, FF, M = cfg
    HB = D // 8 // Z
    vm = pl.BlockSpec(memory_space=pltpu.VMEM)
    S = lambda shape, dt=F32: jax.ShapeDtypeStruct(shape, dt)
    outs = {"o_" + k: S(o[k].shape, o[k].dtype) for k in ("out", "ig", "glu_out", "up_out", "down_o")}
    outs["o_st"] = S((2 * M, D))
    outs.update({f"m{k}": S((HB, M)) for k in range(4)})
    outs.update({f"w{k}": S((HB,)) for k in range(6)})
    outs.update(gb=S((2 * HB,)), ub=S((FF // 8 // Z,)))
    names = (*o, *outs, "turned")
    res = pl.pallas_call(functools.partial(finish_kernel, cfg, names), out_shape=list(outs.values()), in_specs=[vm] * len(o),
                         out_specs=[vm] * len(outs), scratch_shapes=[pltpu.VMEM((128, 4 * M), F32)], name="finish")(*o.values())
    return {k.removeprefix("o_"): v for k, v in zip(outs, res)}


def tables(window):
    half = window // 2
    f = np.concatenate([np.arange(half + 1), np.arange(1, half)])[:, None]
    imag = np.arange(window)[:, None] > half
    ph = (f * np.arange(window)[None, :] % window) * (2.0 * np.pi / window)
    fwd = np.where(imag, -np.sin(ph), np.cos(ph))
    wt = np.where((f == 0) | (2 * f == window), 1.0, 2.0) / window
    inv = (wt * fwd).T[half:]
    def parts(a):
        a = np.ascontiguousarray(a).astype(np.float32)
        high = a.astype(ml_dtypes.bfloat16)
        return jnp.asarray(np.stack([high, (a - high.astype(np.float32)).astype(ml_dtypes.bfloat16)]))
    return parts(fwd), parts(inv), parts(inv.T), parts(fwd.T)


def plane_shards(Z, n_seq, inputs, first_gain, first_shift, decay_rate, rotation, out_real, out_imag, skip_gain, glu_weight,
                 glu_bias, second_gain, second_shift, up_weight, up_bias, down_weight, down_bias, prior_state, cotangent):
    T, D = inputs.shape[1:]
    FF, M = up_weight.shape[1], decay_rate.shape[1]
    FT, HB = FF // 8, D // 8 // Z
    cfg = (Z, n_seq, max(1, (n_seq - 1).bit_length()), T, D, FF, M)
    vecs = (first_gain, first_shift, skip_gain, second_gain, second_shift, down_bias, glu_bias, up_bias)
    o = layer(cfg, tables(T + KLEN), vecs, decay_rate.T, rotation.T, out_real.T, out_imag.T, prior_state,
              inputs[0], cotangent[0], glu_weight, up_weight, down_weight, 0)
    f = finish(cfg, o)
    v = [f[f"w{k}"] for k in range(6)]
    m = [f[f"m{k}"] for k in range(4)]
    return (f["out"][None], f["ig"][None], f["st"].reshape(1, 2, M, D), v[0], v[1], *m, v[2], f["glu_out"], f["gb"],
            v[3], v[4], f["up_out"], f["ub"], f["down_o"], v[5])


def solution(mesh):
    in_specs = (
        P("batch", "seq", None),
        P(),
        P(),
        P(),
        P(),
        P(),
        P(),
        P(),
        P(),
        P(),
        P(),
        P(),
        P(),
        P(),
        P(),
        P(),
        P("batch", None, None, None),
        P("batch", "seq", None),
    )
    out_specs = (
        P("batch", "seq", None),
        P("batch", "seq", None),
        P("batch", None, None, None),
        P(BOTH),
        P(BOTH),
        P(BOTH, None),
        P(BOTH, None),
        P(BOTH, None),
        P(BOTH, None),
        P(BOTH),
        P(BOTH, None),
        P(BOTH),
        P(BOTH),
        P(BOTH),
        P(BOTH, None),
        P(BOTH),
        P(BOTH, None),
        P(BOTH),
    )
    body = shards
    if mesh.shape["seq"] == 8:
        body = functools.partial(plane_shards, mesh.shape["batch"], mesh.shape["seq"])
    return jax.shard_map(body, mesh=mesh, in_specs=in_specs, out_specs=out_specs, check_vma=False)
```

```python
import functools
import math

import jax
import jax.numpy as jnp
import ml_dtypes
import numpy as np
from jax import lax
from jax.experimental import pallas as pl
from jax.experimental.pallas import tpu as pltpu
from jax.sharding import PartitionSpec as P

KLEN = 128
BOTH = ("seq", "batch")
LT = 128
MESH = pl.DeviceIdType.MESH
F32, BF16 = jnp.float32, jnp.bfloat16


EPSILON = 1e-05
HIGHEST = lax.Precision.HIGHEST


def from_behind(value, axis, by):
    peers = lax.axis_size(axis)
    pairs = [(i, i + by) for i in range(peers) if 0 <= i + by < peers]
    return lax.ppermute(value, axis, pairs)


def norm_rows(values, gain, shift):
    center = values - jnp.mean(values, axis=-1, keepdims=True)
    spread = jnp.mean(center * center, axis=-1, keepdims=True)
    return center * lax.rsqrt(spread + EPSILON) * gain + shift


def mode_terms(rate_modes, freq_modes, elapsed):
    moment = elapsed[None, :, None]
    damping = jnp.exp(-rate_modes[:, None, :] * moment)
    return (
        damping * jnp.cos(freq_modes[:, None, :] * moment),
        damping * jnp.sin(freq_modes[:, None, :] * moment),
    )


def glu_gate(glu_pre):
    split_at = glu_pre.shape[-1] // 2
    return glu_pre[:, :split_at] * jax.nn.sigmoid(glu_pre[:, split_at:])


def gelu_exact(values):
    return jax.nn.gelu(values, approximate=False)


def shards(
    inputs,
    first_gain,
    first_shift,
    decay_rate,
    rotation,
    out_real,
    out_imag,
    skip_gain,
    glu_weight,
    glu_bias,
    second_gain,
    second_shift,
    up_weight,
    up_bias,
    down_weight,
    down_bias,
    prior_state,
    cotangent,
):
    seg_count, tok_count, feature = inputs.shape
    row_count = seg_count * tok_count
    window = tok_count + KLEN
    half = window // 2 + 1
    offset = lax.axis_index("seq") * tok_count
    freq_index = jnp.arange(half, dtype=jnp.int32)
    time_index = jnp.arange(window, dtype=jnp.int32)
    phase = (freq_index[:, None] * time_index[None, :] % window).astype(jnp.float32) * (
        2.0 * math.pi / window
    )
    cos_half = jnp.cos(phase)
    sin_half = jnp.sin(phase)
    forward_table = jnp.concatenate([cos_half, -sin_half], axis=0)
    weights = jnp.where((freq_index == 0) | (2 * freq_index == window), 1.0, 2.0).astype(
        jnp.float32
    )
    inverse_table = (
        jnp.concatenate(
            [(weights[:, None] * cos_half).T, -(weights[:, None] * sin_half).T], axis=1
        )[KLEN:]
        / window
    )
    local_steps = jnp.arange(tok_count).astype(jnp.float32)
    advance_steps = (offset + 1).astype(jnp.float32)

    def mixing(
        normed, halo_rows, rate_modes, freq_modes, real_modes, imag_modes, skip_local, prior_local
    ):
        table_real, table_imag = mode_terms(rate_modes, freq_modes, local_steps)
        kernel = jnp.einsum("mkh,mh->kh", table_real, real_modes, precision=HIGHEST) - jnp.einsum(
            "mkh,mh->kh", table_imag, imag_modes, precision=HIGHEST
        )
        extended = jnp.concatenate([halo_rows, normed], axis=1)
        spectrum = jnp.einsum("ft,sth->sfh", forward_table, extended, precision=HIGHEST)
        kern_spec = jnp.dot(forward_table[:, :KLEN], kernel, precision=HIGHEST)
        spec_real, spec_imag = (spectrum[:, :half], spectrum[:, half:])
        kern_real, kern_imag = (kern_spec[:half], kern_spec[half:])
        product = jnp.concatenate(
            [
                spec_real * kern_real - spec_imag * kern_imag,
                spec_real * kern_imag + spec_imag * kern_real,
            ],
            axis=1,
        )
        convolved = jnp.einsum("tf,sfh->sth", inverse_table, product, precision=HIGHEST)
        damping = jnp.exp(-rate_modes * advance_steps)
        adv_real = damping * jnp.cos(freq_modes * advance_steps)
        adv_imag = damping * jnp.sin(freq_modes * advance_steps)
        coef_real = real_modes * adv_real - imag_modes * adv_imag
        coef_imag = real_modes * adv_imag + imag_modes * adv_real
        drive_real = coef_real * prior_local[:, 0] - coef_imag * prior_local[:, 1]
        drive_imag = coef_real * prior_local[:, 1] + coef_imag * prior_local[:, 0]
        response = jnp.einsum(
            "mth,smh->sth", table_real, drive_real, precision=HIGHEST
        ) - jnp.einsum("mth,smh->sth", table_imag, drive_imag, precision=HIGHEST)
        return gelu_exact(convolved + skip_local * normed + response)

    source = inputs.astype(jnp.float32)
    normed, first_pull = jax.vjp(norm_rows, source, first_gain, first_shift)
    halo_rows = from_behind(normed, "seq", 1)
    activated, mix_pull = jax.vjp(
        mixing,
        normed,
        halo_rows,
        decay_rate.T,
        rotation.T,
        out_real.T,
        out_imag.T,
        skip_gain,
        prior_state,
    )
    activated_low = activated.reshape(row_count, feature).astype(jnp.bfloat16)
    glu_pre = jnp.dot(activated_low, glu_weight, preferred_element_type=jnp.float32) + glu_bias
    branch, glu_pull = jax.vjp(glu_gate, glu_pre)
    merged = source.reshape(row_count, feature) + branch
    second, second_pull = jax.vjp(norm_rows, merged, second_gain, second_shift)
    second_low = second.astype(jnp.bfloat16)
    up_pre = jnp.dot(second_low, up_weight, preferred_element_type=jnp.float32) + up_bias
    hidden, hidden_pull = jax.vjp(gelu_exact, up_pre)
    hidden_low = hidden.astype(jnp.bfloat16)
    result = (
        merged + jnp.dot(hidden_low, down_weight, preferred_element_type=jnp.float32) + down_bias
    )
    outputs = result.astype(jnp.bfloat16).reshape(seg_count, tok_count, feature)
    grad_out = cotangent.astype(jnp.float32).reshape(row_count, feature)
    down_bias_grad = jnp.sum(grad_out, axis=0)
    grad_low = grad_out.astype(jnp.bfloat16)
    down_grad = jnp.einsum("rf,rh->fh", hidden_low, grad_low, preferred_element_type=jnp.float32)
    grad_hidden = jnp.einsum("rh,fh->rf", grad_low, down_weight, preferred_element_type=jnp.float32)
    (grad_up,) = hidden_pull(grad_hidden)
    up_bias_grad = jnp.sum(grad_up, axis=0)
    up_low = grad_up.astype(jnp.bfloat16)
    up_grad = jnp.einsum("rh,rf->hf", second_low, up_low, preferred_element_type=jnp.float32)
    grad_second = jnp.einsum("rf,hf->rh", up_low, up_weight, preferred_element_type=jnp.float32)
    grad_merged, second_gain_grad, second_shift_grad = second_pull(grad_second)
    grad_merged = grad_merged + grad_out
    (grad_glu,) = glu_pull(grad_merged)
    glu_bias_grad = jnp.sum(grad_glu, axis=0)
    glu_low = grad_glu.astype(jnp.bfloat16)
    glu_grad = jnp.einsum("rh,rg->hg", activated_low, glu_low, preferred_element_type=jnp.float32)
    grad_activated = jnp.einsum(
        "rg,hg->rh", glu_low, glu_weight, preferred_element_type=jnp.float32
    )
    grad_normed, grad_halo, rate_grad, freq_grad, real_grad, imag_grad, skip_grad, prior_grad = (
        mix_pull(grad_activated.reshape(seg_count, tok_count, feature))
    )
    grad_tail = from_behind(grad_halo, "seq", -1)
    grad_normed = jnp.concatenate(
        [grad_normed[:, : tok_count - KLEN], grad_normed + grad_tail], axis=1
    )
    grad_source, first_gain_grad, first_shift_grad = first_pull(grad_normed)
    input_grad = (grad_source + grad_merged.reshape(seg_count, tok_count, feature)).astype(
        jnp.bfloat16
    )
    state_grad = lax.psum(prior_grad, "seq")
    rate_back = rate_grad.T
    freq_back = freq_grad.T
    real_back = real_grad.T
    imag_back = imag_grad.T
    summed = (
        lax.psum_scatter(first_gain_grad, BOTH, scatter_dimension=0, tiled=True),
        lax.psum_scatter(first_shift_grad, BOTH, scatter_dimension=0, tiled=True),
        lax.psum_scatter(rate_back, BOTH, scatter_dimension=0, tiled=True),
        lax.psum_scatter(freq_back, BOTH, scatter_dimension=0, tiled=True),
        lax.psum_scatter(real_back, BOTH, scatter_dimension=0, tiled=True),
        lax.psum_scatter(imag_back, BOTH, scatter_dimension=0, tiled=True),
        lax.psum_scatter(skip_grad, BOTH, scatter_dimension=0, tiled=True),
        lax.psum_scatter(glu_grad, BOTH, scatter_dimension=0, tiled=True),
        lax.psum_scatter(glu_bias_grad, BOTH, scatter_dimension=0, tiled=True),
        lax.psum_scatter(second_gain_grad, BOTH, scatter_dimension=0, tiled=True),
        lax.psum_scatter(second_shift_grad, BOTH, scatter_dimension=0, tiled=True),
        lax.psum_scatter(up_grad, BOTH, scatter_dimension=0, tiled=True),
        lax.psum_scatter(up_bias_grad, BOTH, scatter_dimension=0, tiled=True),
        lax.psum_scatter(down_grad, BOTH, scatter_dimension=0, tiled=True),
        lax.psum_scatter(down_bias_grad, BOTH, scatter_dimension=0, tiled=True),
    )
    return (
        outputs,
        input_grad,
        state_grad,
        summed[0],
        summed[1],
        summed[2],
        summed[3],
        summed[4],
        summed[5],
        summed[6],
        summed[7],
        summed[8],
        summed[9],
        summed[10],
        summed[11],
        summed[12],
        summed[13],
        summed[14],
    )


def plane():
    s = lax.axis_index("seq")
    i = lax.rem(s, 8)
    base = s - i
    c, x, y = lax.rem(i, 2), lax.rem(i // 2, 2), i // 4
    ic, ix, iy = i + 1 - 2 * c, i + 2 - 4 * x, i + 4 - 8 * y
    idg = iy + 2 - 4 * x
    return dict(s=s, i=i, base=base, c=c, x=x, y=y, ic=ic, ix=ix, iy=iy, idg=idg)

def sib_of(p, j):
    return j + 1 - 2 * p["c"]

def remote(src, dst, ss, rs, dev):
    return pltpu.make_async_remote_copy(src_ref=src, dst_ref=dst, send_sem=ss, recv_sem=rs,
                                        device_id=dev, device_id_type=MESH)

def greet(devs):
    bar = pltpu.get_barrier_semaphore()
    for d in devs:
        pl.semaphore_signal(bar, inc=1, device_id=d, device_id_type=MESH)
    return lambda: pl.semaphore_wait(bar, len(devs))

def peers(p):
    return [lax.rem(p["i"] + k, 8) for k in range(1, 8)]

class Gather:
    def __init__(self, p, own, land, ssem, rsem):
        self.p, self.own, self.land, self.ss, self.rs = p, own, land, ssem, rsem
        self.H = own.shape[0] // 2
        seq = lambda j: {"seq": p["base"] + j}
        self.X, self.Y, self.S = seq(p["ix"]), seq(p["iy"]), seq(p["ic"])

    def cp(self, k, j, h, dev, src=None):
        blk = self.land.at[j, pl.ds(h * self.H, self.H)]
        return remote(blk if src is None else src, blk, self.ss.at[k], self.rs.at[k], dev)

    def plan(self):
        i, ix, iy, idg = self.p["i"], self.p["ix"], self.p["iy"], self.p["idg"]
        return [(0, i, 0, self.X), (2, i, 1, self.Y), (1, i, 1, self.X), (3, i, 0, self.Y), (6, i, 0, self.S), (7, i, 1, self.S),
                (4, ix, 0, self.Y), (8, ix, 0, self.S), (5, iy, 1, self.X), (11, iy, 1, self.S), (9, ix, 1, self.S),
                (10, iy, 0, self.S), (12, idg, 0, self.S), (13, idg, 1, self.S)]

    def _send(self, k, own=False):
        k, j, h, dev = next(e for e in self.plan() if e[0] == k)
        self.cp(k, j, h, dev, self.own.at[pl.ds(h * self.H, self.H)] if own else None).start()

    def _got(self, k, j, h):
        self.cp(k, j, h, self.S).wait_recv()

    def start(self):
        for k in (0, 2, 1, 3, 6, 7):
            self._send(k, True)

    def relay1(self):
        p = self.p
        self._got(0, p["ix"], 0); self._send(4); self._send(8)
        self._got(2, p["iy"], 1); self._send(5); self._send(11)

    def relay2(self):
        p = self.p
        self._got(1, p["ix"], 1); self._send(9)
        self._got(3, p["iy"], 0); self._send(10)

    def relay3(self):
        p = self.p
        self._got(4, p["idg"], 0); self._send(12)
        self._got(5, p["idg"], 1); self._send(13)

    def chip(self, which):
        p = self.p
        k, j = {"own": (6, p["ic"]), "x": (8, sib_of(p, p["ix"])), "y": (10, sib_of(p, p["iy"])), "d": (12, sib_of(p, p["idg"]))}[which]
        self._got(k, j, 0)
        self._got(k + 1, j, 1)
        return (j,) if which == "own" else ({"x": p["ix"], "y": p["iy"], "d": p["idg"]}[which], j)

    def drain(self):
        for k, j, h, dev in self.plan():
            self.cp(k, j, h, dev).wait_send()


class Line:
    def __init__(self, Z, z, p, own, land, ssem, rsem, zu, zd):
        self.Z, self.z, self.c, self.own, self.land, self.ss, self.rs = Z, z, p["c"], own, land, ssem, rsem
        self.H = own.shape[0] // 2
        self.dev = (zu, zd, {"seq": p["base"] + p["ic"]})

    def part(self, chip, core, half):
        return self.land.at[chip * 2 + core, pl.ds(half * self.H, self.H)]

    def cp(self, way, hop, half, chip, core, own=False):
        blk = self.part(chip, core, half)
        src = self.own.at[pl.ds(half * self.H, self.H)] if own else blk
        return remote(src, blk, self.ss.at[way, hop, half], self.rs.at[way, hop, half], self.dev[way])

    def ends(self):
        z, Z = self.z, self.Z
        return ((lambda h: z - h, lambda h: z - h >= 0, z < Z - 1), (lambda h: z + h, lambda h: z + h < Z, z > 0))

    def start(self):
        for half in range(2):
            for way, (chip, there, on) in enumerate(self.ends()):
                pl.when(on)(lambda: self.cp(way, 0, half, self.z, self.c, True).start())
        for half in range(2): self.cp(2, 0, half, self.z, self.c, True).start()

    def _take(self, way, hop, half, chip):
        self.cp(way, hop - 1, half, chip, self.c).wait_recv()
        self.cp(2, hop + way * (self.Z - 1), half, chip, self.c).start()

    def pass_on(self, hop, half):
        for way, (chip, there, on) in enumerate(self.ends()):
            @pl.when(there(hop) & on)
            def _():
                self._take(way, hop, half, chip(hop))
                self.cp(way, hop, half, chip(hop), self.c).start()

    def settle(self, chip_at):
        for way, (chip, there, on) in enumerate(self.ends()):
            for hop in range(1, self.Z):
                @pl.when(chip_at == chip(hop))
                def _():
                    for half in range(2):
                        pl.when(jnp.logical_not(on))(lambda: self._take(way, hop, half, chip(hop)))
                    for half in range(2):
                        self.cp(2, hop + way * (self.Z - 1), half, chip(hop), 1 - self.c).wait_recv()

    def settle_own(self):
        for half in range(2): self.cp(2, 0, half, self.z, 1 - self.c).wait_recv()

    def drain(self):
        for half in range(2):
            self.cp(2, 0, half, self.z, self.c, True).wait_send()
            for way, (chip, there, on) in enumerate(self.ends()):
                for hop in range(self.Z - 1):
                    pl.when(there(hop) & on)(lambda: self.cp(way, hop, half, chip(hop), self.c).wait_send())
                for hop in range(1, self.Z):
                    pl.when(there(hop))(lambda: self.cp(2, hop + way * (self.Z - 1), half, chip(hop), self.c).wait_send())


def cmul(ar, ai, br, bi):
    return ar * br - ai * bi, ar * bi + ai * br

def lam_of(rate, freq):
    damp = jnp.exp(-rate)
    q = freq * freq
    cosv = 1.0 + q * (-1.0/2 + q * (1.0/24 + q * (-1.0/720 + q * (1.0/40320 + q * (-1.0/3628800)))))
    sinv = freq * (1.0 + q * (-1.0/6 + q * (1.0/120 + q * (-1.0/5040 + q * (1.0/362880)))))
    return damp * cosv, damp * sinv

def power_rows(lr, li, qr, qi, A):
    l2 = cmul(lr, li, lr, li); l4 = cmul(*l2, *l2); l8 = cmul(*l4, *l4)
    cur = (jnp.ones_like(lr), jnp.zeros_like(lr))
    for a in range(A):
        qr[a] = cur[0]; qi[a] = cur[1]
        cur = cmul(*cur, *l8)
    return l2, l4, cur

def offset_power(top, s, nbits):
    res = (jnp.ones_like(top[0]), jnp.zeros_like(top[0]))
    sq = top
    for bit in range(nbits):
        on = lax.rem(lax.div(s, 1 << bit), 2) == 1
        nxt = cmul(*res, *sq)
        res = (jnp.where(on, nxt[0], res[0]), jnp.where(on, nxt[1], res[1]))
        if bit + 1 < nbits: sq = cmul(*sq, *sq)
    return res

def fwd_tiles(nbits, lo, hi, rate, freq, cre, cim, prior, kern, resp, co):
    M = rate.shape[0]
    A = kern.shape[0] // 8
    s = lax.axis_index("seq")
    b = lax.broadcasted_iota(jnp.int32, (8, LT), 0)
    o1, o2, o4 = (b % 2) == 1, ((b // 2) % 2) == 1, b >= 4
    one, zero = jnp.ones((8, LT), F32), jnp.zeros((8, LT), F32)
    square = lambda v: cmul(*v, *v)
    @pl.loop(lo, hi)
    def _(lt):
        cols = pl.ds(pl.multiple_of(lt * LT, LT), LT)
        l1 = lam_of(rate[:, cols], freq[:, cols])
        l2 = square(l1)
        l4 = square(l2)
        l8 = square(l4)
        top = l8
        for _ in range((A - 1).bit_length()): top = square(top)
        off = cmul(*offset_power(top, s, nbits), *l1)
        c = cre[:, cols], cim[:, cols]
        d = cmul(*cmul(*c, *off), prior[0, 0, :, cols], prior[0, 1, :, cols])
        rows = (*l1, *l2, *l4, *c, *cmul(*c, *l8), *d, *cmul(*d, *l8), 2.0 * l8[0], -(l8[0] * l8[0] + l8[1] * l8[1]))
        for k, v in enumerate(rows): co[pl.ds(k * M, M), :] = v
        def step(m, accs):
            row = lambda k: jnp.broadcast_to(co[pl.ds(k * M + m, 1), :], (8, LT))
            e = jnp.where(o1, row(0), one), jnp.where(o1, row(1), zero)
            e = cmul(*e, jnp.where(o2, row(2), one), jnp.where(o2, row(3), zero))
            er, ei = cmul(*e, jnp.where(o4, row(4), one), jnp.where(o4, row(5), zero))
            p, q = row(14), row(15)
            k0, k1 = er * row(6) - ei * row(7), er * row(8) - ei * row(9)
            r0, r1 = er * row(10) - ei * row(11), er * row(12) - ei * row(13)
            out = list(accs)
            for a in range(A):
                out[2 * a] = out[2 * a] + k0
                out[2 * a + 1] = out[2 * a + 1] + r0
                if a < A - 1:
                    k0, k1 = k1, p * k1 + q * k0
                    r0, r1 = r1, p * r1 + q * r0
            return tuple(out)
        accs = lax.fori_loop(0, M, step, tuple(jnp.zeros((8, LT), F32) for _ in range(2 * A)), unroll=4)
        for a in range(A):
            kern[pl.ds(8 * a, 8), cols] = accs[2 * a]
            resp[pl.ds(8 * a, 8), cols] = accs[2 * a + 1]


def bwd_tiles(lo, hi, srow, nbits, TOK, rate, freq, cre, cim, prior, kg, gz, out, qr, qi, acc):
    M = rate.shape[0]
    A = kg.shape[0] // 8
    s = lax.axis_index("seq")
    adv = (s * TOK + 1).astype(F32)
    @pl.loop(lo, hi)
    def _(lt):
        cols = pl.ds(pl.multiple_of(lt * LT, LT), LT)
        lr, li = lam_of(rate[:, cols], freq[:, cols])
        l2, l4, top = power_rows(lr, li, qr, qi, A)
        def step(m, carry):
            for j, g in enumerate((kg, gz)):
                z = jnp.zeros((8, LT), F32)
                sr, si, tr, ti = z, z, z, z
                for a in range(A - 1, -1, -1):
                    ga = g[pl.ds(8 * a, 8), cols]
                    sr = sr + ga * qr[a, pl.ds(m, 1), :]
                    si = si + ga * qi[a, pl.ds(m, 1), :]
                    if a > 0:
                        tr = tr + sr
                        ti = ti + si
                for q, v in enumerate((sr, si, tr, ti)):
                    acc[pl.ds(pl.multiple_of(((4 * j + q) * M + m) * 8, 8), 8), :] = v
            return carry
        lax.fori_loop(0, M, step, 0, unroll=8)
        pw = (jnp.ones_like(lr), jnp.zeros_like(lr))
        zero = jnp.zeros_like(lr)
        ar, ai, br, bi = [zero] * 2, [zero] * 2, [zero] * 2, [zero] * 2
        for b in range(8):
            for j in range(2):
                ld = lambda q: acc[pl.ds((4 * j + q) * M * 8 + b, M, stride=8), :]
                S = ld(0), ld(1)
                U = 8.0 * ld(2), 8.0 * ld(3)
                if b: U = U[0] + float(b) * S[0], U[1] + float(b) * S[1]
                w = cmul(*pw, *S)
                ar[j], ai[j] = ar[j] + w[0], ai[j] + w[1]
                w = cmul(*pw, *U)
                br[j], bi[j] = br[j] + w[0], bi[j] + w[1]
            pw = cmul(*pw, lr, li)
        off = cmul(*offset_power(top, s, nbits), lr, li)
        c = cre[:, cols], cim[:, cols]
        ps = cmul(*off, prior[0, 0, :, cols], prior[0, 1, :, cols])
        u = cmul(*ps, ar[1], ai[1])
        v = cmul(*ps, br[1] + adv * ar[1], bi[1] + adv * ai[1])
        v = cmul(*c, v[0] + br[0], v[1] + bi[0])
        w = cmul(*cmul(*c, *off), ar[1], ai[1])
        for k, val in enumerate((-v[0], -v[1], u[0] + ar[0], -(u[1] + ai[0]))): out[k * M:(k + 1) * M, cols] = val
        for k, val in enumerate((w[0], -w[1])): out[srow + k * M:srow + (k + 1) * M, cols] = val


class Bag:
    pass


def dot(a, b, ca=1, cb=0):
    return lax.dot_general(a, b, (((ca,), (cb,)), ((), ())), preferred_element_type=F32)


def split_low(v):
    high = v.astype(BF16)
    return high, (v - high.astype(F32)).astype(BF16)


def table_dot(tab, v, rows=slice(None), cols=slice(None)):
    high, low = split_low(v)
    th, tl = tab[0, rows, cols], tab[1, rows, cols]
    return dot(th, high) + dot(th, low) + dot(tl, high)


def gelu_both(u):
    cdf = 0.5 + 0.5 * lax.erf(u * (0.5 ** 0.5))
    return u * cdf, cdf + u * (jnp.exp(-0.5 * u * u) * ((2.0 * math.pi) ** -0.5))


def tiles(n, step):
    def run(body, init=None):
        if init is None:
            @pl.loop(0, n // step)
            def _(k):
                body(pl.ds(pl.multiple_of(k * step, step), step))
            return None
        return lax.fori_loop(0, n // step, lambda k, c: body(pl.ds(pl.multiple_of(k * step, step), step), c), init)
    return run


def sub(off, q):
    return pl.ds(pl.multiple_of(off + q.start, q.size), q.size)


def row_mean(v):
    return jnp.sum(v, axis=-1, keepdims=True) * (1.0 / v.shape[-1])


def norm_hat(v):
    center = v - row_mean(v)
    inv = lax.rsqrt(row_mean(center * center) + EPSILON)
    return center * inv, inv


def norm_back(gg, hat, inv):
    return inv * (gg - row_mean(gg) - hat * row_mean(gg * hat))


def fold(v):
    return jnp.sum(v, axis=0, keepdims=True)


LC = 256
ROWS = 8
FETCH = ("rate", "freq", "cre", "cim", "prior", "ftab", "itab", "jtab", "gtab")
VEC = ("first_gain", "first_shift", "skip_gain", "second_gain", "second_shift", "down_bias", "value_bias", "gate_bias")


def layer_kernel(cfg, names, *refs):
    r = Bag()
    r.__dict__.update(zip(names, refs))
    Z, NSEQ, nbits, T, D, FF, M = cfg
    FT = FF // 8
    HB = D // 8 // Z
    p = plane()
    s, i = p["s"], p["i"]
    z = lax.axis_index("batch")
    vec = {k: (lambda q: (lambda c=slice(None): r.vecs[q:q + 1, c]))(q) for q, k in enumerate(VEC)}
    iblk = pl.ds(pl.multiple_of(i * T, T), T)
    w8, own8 = p["c"] * Z + z, z * 2 + p["c"]
    q0, qx, qy, qd = (v // 2 for v in (i, p["ix"], p["iy"], p["idg"]))
    FB = FF // 32

    ps = peers(p)
    zu, zd = {"batch": lax.rem(z + 1, Z)}, {"batch": lax.rem(z + Z - 1, Z)}
    zp = [lax.rem(z + k, Z) for k in range(1, Z)]
    group = [lax.rem(w8 + k, 8) for k in range(1, 8)]
    seat = lambda w: {"seq": s - p["c"] + w // Z, "batch": lax.rem(w, Z)}
    all_here = greet([{"seq": p["base"] + j} for j in ps] + [{"seq": s - p["c"] + e, "batch": q} for q in zp for e in range(2)])

    local = lambda src, dst, sem: pltpu.make_async_copy(src, dst, sem)
    fetched = {k: local(r.__dict__["h_" + k], r.__dict__[k], r.isem.at[n]) for n, k in enumerate(FETCH)}
    for c in fetched.values(): c.start()

    for q, ref in enumerate((r.v0, r.v1, r.v2, r.v3, r.v4, r.v5)): r.vecs[q:q + 1, :] = ref[...].reshape(1, D)
    for q in range(2): r.vecs[6 + q:7 + q, :] = r.v6[q * D:(q + 1) * D].reshape(1, D)
    for q in range(8): r.upb[q:q + 1, :] = r.v7[q * FT:(q + 1) * FT].reshape(1, FT)

    lane = lambda off, n: pl.ds(pl.multiple_of(off, 128), n)
    local = lambda src, dst, sem: pltpu.make_async_copy(src, dst, sem)
    gw_copy = local(r.glu_w, r.gw, r.lsem.at[0])
    gw_copy.start()
    def tile_copy(t, slot):
        return (local(r.up_w.at[:, lane(t * FT, FT)], r.wu.at[slot], r.tsem.at[0, slot]),
                local(r.down_w.at[pl.ds(pl.multiple_of(t * FT, FT), FT)], r.wd.at[slot], r.tsem.at[1, slot]))
    for t in range(2):
        for c in tile_copy(t, t): c.start()
    def slice_copy():
        return [c for q in range(4) for c in (
            local(r.up_w.at[:, lane((q * 8 + w8) * FB, FB)], r.wu.at[0, :, pl.ds(q * FB, FB)], r.ssem.at[0, q]),
            local(r.down_w.at[pl.ds(pl.multiple_of((q * 8 + w8) * FB, FB), FB)], r.wd.at[0, pl.ds(q * FB, FB)], r.ssem.at[1, q]))]
    wgs_copy = [local(r.glu_w.at[:, lane(q * D + i * 128, 128)], r.wgs.at[:, pl.ds(q * 128, 128)], r.lsem.at[1 + q]) for q in range(2)]
    for c in wgs_copy: c.start()

    @tiles(T, 16)
    def _(q):
        r.xs[q, :] = r.x[q, :].astype(F32)
        r.own_cot[q, :] = r.cot[q, :].astype(F32)
    all_here()
    nxt, prv = {"seq": lax.rem(s + 1, NSEQ)}, {"seq": lax.rem(s + NSEQ - 1, NSEQ)}
    halo_copy = remote(r.xs, r.halo, r.hsem.at[0], r.hsem.at[1], nxt)
    pl.when(s < NSEQ - 1)(lambda: halo_copy.start())
    gc = Line(Z, z, p, r.own_cot, r.land_cot, r.lss.at[0], r.lsr.at[0], zu, zd)
    gs = Line(Z, z, p, r.own_sec, r.land_sec, r.lss.at[1], r.lsr.at[1], zu, zd)
    ga = Gather(p, r.own_act, r.land_act, r.gss, r.gsr)
    gc.start()

    for k in FETCH[:5]: fetched[k].wait()
    mode_args = (r.rate, r.freq, r.cre, r.cim, r.prior)
    fwd_tiles(nbits, 0, D // LT, *mode_args, r.kern, r.resp, r.big)
    gc.pass_on(1, 0)

    @tiles(T, ROWS)
    def _(q):
        hat, inv = norm_hat(r.xs[q, :])
        r.xhat[q, :] = hat
        r.xinv[q, :] = jnp.broadcast_to(inv, (ROWS, 128))
        r.ext[sub(T, q), :] = hat * vec["first_gain"]() + vec["first_shift"]()
    @pl.when(s > 0)
    def _():
        halo_copy.wait_recv()
    @pl.when(s == 0)
    def _():
        r.halo[...] = jnp.zeros_like(r.halo)
    keep = jnp.where(s == 0, 0.0, 1.0)
    @tiles(T, ROWS)
    def _(q):
        hat, _ = norm_hat(r.halo[q, :])
        r.ext[q, :] = (hat * vec["first_gain"]() + vec["first_shift"]()) * keep

    for k in FETCH[5:]: fetched[k].wait()
    inner = lax.broadcasted_iota(jnp.int32, (KLEN, LC), 0) > 0
    @tiles(D, LC)
    def _(c):
        X = table_dot(r.ftab, r.ext[:, c])
        K = table_dot(r.ftab, r.kern[:, c], cols=slice(0, KLEN))
        r.X[:, c] = X
        r.K[:, c] = K
        P_, Q_, KP, KQ = X[:KLEN], X[KLEN:], K[:KLEN], K[KLEN:]
        qq = Q_ * KQ
        po = P_ * KP - jnp.where(inner, qq, 0.0)
        qo = jnp.where(inner, P_ * KQ + Q_ * KP, qq)
        y = table_dot(r.itab, jnp.concatenate([po, qo], 0))
        r.pre[:, c] = y + vec["skip_gain"](c) * r.ext[T:, c] + r.resp[:, c]
    @tiles(T, 16)
    def _(q):
        a = gelu_both(r.pre[q, :])[0].astype(BF16)
        r.own_act[q, :] = a.astype(F32)
        r.act_all[sub(i * T, q), :] = a
    gc.pass_on(1, 1)
    ga.start()

    gw_copy.wait()
    act = r.act_all[iblk, :]
    @tiles(D, LC)
    def _(c):
        r.val[:, c] = dot(act, r.gw[:, c])
        r.sg[:, c] = dot(act, r.gw[:, lane(D + c.start, LC)])
    @tiles(T, ROWS)
    def _(q):
        v = r.val[q, :] + vec["value_bias"]()
        g = jax.nn.sigmoid(r.sg[q, :] + vec["gate_bias"]())
        r.val[q, :] = v
        r.sg[q, :] = g
        m = r.xs[q, :] + v * g
        r.merged[q, :] = m
        hat, inv = norm_hat(m)
        r.mhat[q, :] = hat
        r.minv[q, :] = jnp.broadcast_to(inv, (ROWS, 128))
        r.own_sec[q, :] = (hat * vec["second_gain"]() + vec["second_shift"]()).astype(BF16).astype(F32)
    @tiles(T, 16)
    def _(q):
        r.sec_all[sub(own8 * T, q), :] = r.own_sec[q, :].astype(BF16)
    gs.start()
    gc.pass_on(2, 0)

    r.oacc[...] = jnp.zeros_like(r.oacc)
    r.sacc[...] = jnp.zeros_like(r.sacc)
    sec = r.sec_all[pl.ds(pl.multiple_of(own8 * T, T), T), :]
    @pl.loop(0, 8)
    def _(t):
        slot = lax.rem(t, 2)
        for c in tile_copy(t, slot): c.wait()
        r.u[pl.ds(0, T)] = dot(sec, r.wu[slot])
        r.gh[pl.ds(0, T)] = dot(r.cot[...], r.wd[slot], 1, 1)
        def rows_u(q, acc):
            hid, slope = gelu_both(r.u[q, :] + r.upb[pl.ds(t, 1), :])
            gu = r.gh[q, :] * slope
            r.hid[q, :] = hid.astype(BF16)
            r.gul[q, :] = gu.astype(BF16)
            return acc + jnp.sum(gu.reshape(8, 8, FT), 0)
        r.ubg[pl.ds(t, 1), :] = fold(tiles(T, 64)(rows_u, jnp.zeros((8, FT), F32)))
        r.oacc[...] += dot(r.hid[pl.ds(0, T), :], r.wd[slot])
        r.sacc[...] += dot(r.gul[pl.ds(0, T), :], r.wu[slot], 1, 1)
        @pl.when(t < 6)
        def _():
            for c in tile_copy(t + 2, slot): c.start()
        pl.when(t == 1)(lambda: gc.pass_on(2, 1))
        pl.when(t == 2)(ga.relay1)
        @pl.when(t == 5)
        def _():
            gs.pass_on(1, 0)
            ga.relay2()
    for c in slice_copy(): c.start()
    gs.pass_on(1, 1)
    ga.relay3()

    zero = jnp.zeros((ROWS, D), F32)
    def rows_a(q, carry):
        r.oacc[q, :] = r.merged[q, :] + r.oacc[q, :] + vec["down_bias"]()
        g, hat, c = r.sacc[q, :], r.mhat[q, :], r.own_cot[q, :]
        gm = c + norm_back(g * vec["second_gain"](), hat, r.minv[q, 0:1])
        r.gm[q, :] = gm
        return carry[0] + g * hat, carry[1] + g, carry[2] + c
    sums = tiles(T, ROWS)(rows_a, (zero,) * 3)
    for k, v in zip((3, 4, 5), sums): r.ssrc[4 * M + k:4 * M + k + 1, :] = fold(v)
    gm_sends = []
    for k, j in enumerate(ps):
        c = remote(r.gm.at[:, lane(j * 128, 128)], r.gm_all.at[i], r.ms.at[k], r.mr.at[k], {"seq": p["base"] + j})
        c.start()
        gm_sends.append(c)
    r.gm_all[i] = r.gm[:, lane(i * 128, 128)]
    @tiles(T, 16)
    def _(q):
        r.out_v[q, :] = r.oacc[q, :].astype(BF16)
    def rows_b(q, carry):
        gm, g = r.gm[q, :], r.sg[q, :]
        gv, gg = gm * g, gm * r.val[q, :] * g * (1.0 - g)
        r.glow[q, pl.ds(0, D)] = gv.astype(BF16)
        r.glow[q, pl.ds(D, D)] = gg.astype(BF16)
        return carry[0] + jnp.sum(gv.reshape(2, ROWS, D), 0), carry[1] + jnp.sum(gg.reshape(2, ROWS, D), 0)
    gb = tiles(T, 16)(rows_b, (zero,) * 2)
    gb = [fold(v) for v in gb]
    for j in range(8):
        for q in range(2):
            off = (j % 4) * 256 + q * 128
            r.ssrc[4 * M + 6 + q:4 * M + 7 + q, j * 128:(j + 1) * 128] = gb[j // 4][:, off:off + 128]
    glow = r.glow[...]
    @tiles(D, LC)
    def _(c):
        r.gz[:, c] = dot(glow, r.gw[c, :], 1, 1)
    @tiles(T, ROWS)
    def _(q):
        r.gz[q, :] = r.gz[q, :] * gelu_both(r.pre[q, :])[1]
    @tiles(D, LC)
    def _(c):
        G = table_dot(r.jtab, r.gz[:, c])
        gp, gq = G[:KLEN], G[KLEN:]
        def pair(ref):
            a, b = ref[pl.ds(0, KLEN), c], ref[pl.ds(KLEN, KLEN), c]
            bq = gq * b
            return jnp.concatenate([gp * a + jnp.where(inner, bq, 0.0), jnp.where(inner, gq * a - gp * b, bq)], 0)
        r.kern[:, c] = table_dot(r.gtab, pair(r.X), rows=slice(0, KLEN))
        r.ext[:, c] = table_dot(r.gtab, pair(r.K))
    tail_copy = remote(r.ext.at[pl.ds(0, T)], r.tail, r.hsem.at[2], r.hsem.at[3], prv)
    pl.when(s > 0)(lambda: tail_copy.start())
    gs.pass_on(2, 0)

    for which in ("own", "x", "y", "d"):
        for j in ga.chip(which):
            @tiles(T, 32)
            def _(q):
                r.act_all[sub(j * T, q), :] = ga.land[j, q, :].astype(BF16)
    for k in range(7):
        src = lax.rem(i + 7 - k, 8)
        remote(r.gm_all.at[src], r.gm_all.at[src], r.ms.at[k], r.mr.at[k], nxt).wait_recv()
    for c in wgs_copy: c.wait()
    gbias = jnp.concatenate([r.vecs[6:7, lane(i * 128, 128)], r.vecs[7:8, lane(i * 128, 128)]], 1)
    @tiles(8 * T, 256)
    def _(q):
        r.u[:, pl.ds(0, 256)] = dot(r.act_all[q, :], r.wgs[...]) + gbias
        for h in range(256 // T):
            blk = q.start // T + h
            @tiles(T, 32)
            def _(k):
                row = pl.ds(pl.multiple_of(h * T + k.start, 32), 32)
                v, g = r.u[row, pl.ds(0, 128)], jax.nn.sigmoid(r.u[row, pl.ds(128, 128)])
                gm = r.gm_all[blk, k, :]
                rows = pl.ds(pl.multiple_of(q.start + h * T + k.start, 32), 32)
                r.ggl[rows, :] = jnp.concatenate([gm * g, gm * v * g * (1.0 - g)], 1).astype(BF16)
    @tiles(D, 256)
    def _(c):
        g = dot(r.act_all[:, c], r.ggl[...], 0, 0)
        for q in range(256 // HB):
            j = c.start // 128 + q // Z
            r.glg[q % Z, pl.ds(pl.multiple_of(j * HB, HB), HB), :] = g[q * HB:(q + 1) * HB]

    LU = lambda t: r.lgl.at[0, t - 1]
    LD = lambda t: r.lgl.at[1, t]
    def cu(t, src=None):
        return remote(LU(t) if src is None else src, LU(t), r.zs.at[0, t - 1], r.zr.at[0, t - 1], zu)
    def cd(t, src=None):
        return remote(LD(t) if src is None else src, LD(t), r.zs.at[1, t], r.zr.at[1, t], zd)
    def add_into(dst, srcs):
        @tiles(dst.shape[0], 32)
        def _(q):
            v = srcs[0][q, :]
            for e in srcs[1:]: v = v + e[q, :]
            dst[q, :] = v
    def z_start():
        for h in range(Z - 1, 0, -1):
            pl.when(z == 0)(lambda: cu(h, r.glg.at[h]).start())
            pl.when(z == Z - 1)(lambda: cd(Z - 1 - h, r.glg.at[Z - 1 - h]).start())
    def z_slot(slot):
        for zz in range(1, Z - 1):
            @pl.when(z == zz)
            def _():
                for t in range(Z - 1, zz, -1):
                    if (Z - 1 - t) + zz == slot:
                        cu(t).wait_recv()
                        add_into(LU(t), (LU(t), r.glg.at[t]))
                        cu(t).start()
                for t in range(zz):
                    if t + (Z - 1 - zz) == slot:
                        cd(t).wait_recv()
                        add_into(LD(t), (LD(t), r.glg.at[t]))
                        cd(t).start()
    def z_final(dst):
        for zz in range(Z):
            @pl.when(z == zz)
            def _():
                srcs = [r.glg.at[zz]]
                if zz > 0:
                    cu(zz).wait_recv()
                    srcs.append(LU(zz))
                if zz < Z - 1:
                    cd(zz).wait_recv()
                    srcs.append(LD(zz))
                add_into(dst, srcs)
    def z_drain():
        for zz in range(Z):
            @pl.when(z == zz)
            def _():
                for t in range(zz + 1, Z): cu(t).wait_send()
                for t in range(zz): cd(t).wait_send()
    z_start()

    gs.pass_on(2, 1)

    bwd_args = (nbits, T, *mode_args, r.kern, r.gz, r.ssrc, r.qr, r.qi, r.big)
    srow = 4 * M + 16
    bwd_tiles(0, 4, srow, *bwd_args)
    bwd_tiles(4, D // LT, srow, *bwd_args)
    pl.when(s < NSEQ - 1)(lambda: tail_copy.wait_recv())
    @pl.when(s == NSEQ - 1)
    def _():
        r.tail[...] = jnp.zeros_like(r.tail)
    def rows_c(q, carry):
        hat, gz = r.xhat[q, :], r.gz[q, :]
        gn = r.ext[sub(T, q), :] + r.tail[q, :] + vec["skip_gain"]() * gz
        r.oacc[q, :] = r.gm[q, :] + norm_back(gn * vec["first_gain"](), hat, r.xinv[q, 0:1])
        return carry[0] + gn * hat, carry[1] + gn, carry[2] + gz * hat, carry[3] + gz
    sums = [fold(v) for v in tiles(T, ROWS)(rows_c, (zero,) * 4)]
    sums = (sums[0], sums[1], sums[2] * vec["first_gain"]() + sums[3] * vec["first_shift"]())
    for k, v in enumerate(sums): r.ssrc[4 * M + k:4 * M + k + 1, :] = v
    @tiles(T, 16)
    def _(q):
        r.ig_v[q, :] = r.oacc[q, :].astype(BF16)
    early = [local(r.out_v, r.out, r.osem.at[0]), local(r.ig_v, r.ig, r.osem.at[1])]
    for c in early: c.start()
    r.ssrc[4 * M + 8:4 * M + 16, :] = jnp.zeros((8, D), F32)
    for j in range(8):
        for e in range(FT // 128): r.ssrc[4 * M + 8 + e:4 * M + 9 + e, j * 128:(j + 1) * 128] = r.ubg[j:j + 1, e * 128:(e + 1) * 128]

    NR, NS = 4 * M + 16 + 2 * M, 2 * M
    sends = []
    def push(src, dst, a, b, dev):
        c = remote(src, dst, a, b, dev)
        c.start()
        sends.append(c)
    for k, j in enumerate(ps):
        push(r.ssrc.at[:, lane(j * 128, 128)], r.sland.at[i], r.sa.at[0, k], r.sa.at[1, k], {"seq": p["base"] + j})
    def small_sum():
        tot = r.ssrc[:, lane(i * 128, 128)]
        for k in range(7):
            src = lax.rem(i + 7 - k, 8)
            remote(r.sland.at[src], r.sland.at[src], r.sa.at[0, k], r.sa.at[1, k], nxt).wait_recv()
            tot = tot + r.sland[src]
        r.mine[...] = tot
        r.st[i] = tot[NR - NS:NR]
        for c in small_sends()[:7]: c.start()
    def small_sends():
        return ([remote(r.mine.at[pl.ds(NR - NS, NS)], r.st.at[i], r.sb.at[0, k], r.sb.at[1, k], {"seq": p["base"] + j}) for k, j in enumerate(ps)]
                + [remote(r.mine, r.zland.at[z], r.sz.at[0, k], r.sz.at[1, k], {"batch": q}) for k, q in enumerate(zp)])

    z_slot(1)

    def low_rows(src, dst, b8):
        @tiles(T, 32)
        def _(q):
            dst[sub(b8 * T, q), :] = src[b8, q, :].astype(BF16)
    @tiles(T, 16)
    def _(q):
        r.cot_all[sub(own8 * T, q), :] = r.cot[q, :]
    gc.settle_own()
    low_rows(r.land_cot, r.cot_all, z * 2 + 1 - p["c"])
    low_half = z < Z // 2
    near_end = jnp.where(low_half, z, Z - 1 - z)
    def chip_at(k):
        at = jnp.where(k <= near_end, near_end - k, k)
        return jnp.where(low_half, at, Z - 1 - at)
    @pl.loop(1, Z)
    def _(k):
        at = chip_at(k)
        gc.settle(at)
        low_rows(r.land_cot, r.cot_all, at * 2)
        low_rows(r.land_cot, r.cot_all, at * 2 + 1)


    for c in slice_copy(): c.wait()
    for zz in range(Z):
        @pl.when(z == zz)
        def _():
            for q in range(4): r.upbs[0:1, q * FB:(q + 1) * FB] = r.upb[pl.ds(q * 2 + p["c"], 1), :][:, zz * FB:(zz + 1) * FB]
    def slice_chunk(k):
        at = chip_at(k)
        @pl.when(k == 0)
        def _():
            gs.settle_own()
            low_rows(r.land_sec, r.sec_all, z * 2 + 1 - p["c"])
        @pl.when(k > 0)
        def _():
            gs.settle(at)
            low_rows(r.land_sec, r.sec_all, at * 2)
            low_rows(r.land_sec, r.sec_all, at * 2 + 1)
        q = pl.ds(pl.multiple_of(at * 2 * T, 2 * T), 2 * T)
        r.u[...] = dot(r.sec_all[q, :], r.wu[0])
        r.gh[...] = dot(r.cot_all[q, :], r.wd[0], 1, 1)
        @tiles(2 * T, 64)
        def _(e):
            hid, slope = gelu_both(r.u[e, :] + r.upbs[0:1, :])
            r.hid[sub(at * 2 * T, e), :] = hid.astype(BF16)
            r.gul[sub(at * 2 * T, e), :] = (r.gh[e, :] * slope).astype(BF16)
    pl.loop(0, 2)(slice_chunk)
    z_slot(2)
    small_sum()
    pl.loop(2, Z - 1)(slice_chunk)
    pl.loop(Z - 1, Z)(slice_chunk)
    z_final(r.glf)
    for k, j in enumerate(ps):
        for q in range(2):
            push(r.glf.at[pl.ds(pl.multiple_of(j * HB, HB), HB), pl.ds(q * 128, 128)], r.glu_out.at[:, lane(q * D + i * 128, 128)],
                 r.ga.at[0, q, k], r.ga.at[1, q, k], {"seq": p["base"] + j})

    own, land = (r.upg, r.dng), (r.lup, r.ldn)
    X, Y = {"seq": p["base"] + p["ix"]}, {"seq": p["base"] + p["iy"]}
    def piece(n, q, h):
        half = own[n].shape[1] // 2
        return own[n].at[q, pl.ds(h * half, half)]
    def hop(n, k, dev, src=None):
        return remote(land[n].at[k] if src is None else src, land[n].at[k], r.rs.at[0, n, k], r.rs.at[1, n, k], dev)
    def plane_start(n):
        for k, dev, q, h in ((0, X, qd, 0), (2, Y, qd, 1), (1, X, qx, 0), (3, Y, qy, 1)): hop(n, k, dev, piece(n, q, h)).start()
    def plane_middle(n):
        for k, q, h, k2, dev in ((0, qy, 0, 4, Y), (2, qx, 1, 5, X)):
            hop(n, k, X).wait_recv()
            add_into(land[n].at[k], (land[n].at[k], piece(n, q, h)))
            hop(n, k2, dev, land[n].at[k]).start()
    def plane_end(n, dst):
        half = own[n].shape[1] // 2
        for h, near, second in ((0, 1, 4), (1, 3, 5)):
            hop(n, near, X).wait_recv()
            hop(n, second, X).wait_recv()
            add_into(dst.at[pl.ds(h * half, half)], (piece(n, q0, h), land[n].at[near], land[n].at[second]))
    @tiles(D, 256)
    def _(c):
        r.upg[c.start // 256] = dot(r.sec_all[:, c], r.gul[...], 0, 0)
    plane_start(0)
    for c in small_sends()[7:]: c.start()
    for fc in range(FT // 256):
        for nh in range(D // 512):
            g = dot(r.hid[:, fc * 256:(fc + 1) * 256], r.cot_all[:, nh * 512:(nh + 1) * 512], 0, 0)
            n = 256 // FB
            for q in range(n): r.dng[fc * n + q, :, nh * 512:(nh + 1) * 512] = g[q * FB:(q + 1) * FB]
    plane_middle(0)
    plane_start(1)
    plane_end(0, r.upf)
    for k, w in enumerate(group):
        push(r.upf.at[pl.ds(pl.multiple_of(w * HB, HB), HB)], r.uland.at[w8], r.ua.at[0, k], r.ua.at[1, k], seat(w))
    r.uland[w8] = r.upf[pl.ds(pl.multiple_of(w8 * HB, HB), HB), :]
    acc = r.mine[...]
    for k in range(Z - 1):
        src = lax.rem(z + Z - 1 - k, Z)
        remote(r.mine, r.zland.at[src], r.sz.at[0, k], r.sz.at[1, k], zu).wait_recv()
        acc = acc + r.zland[src]
    r.tot[...] = acc
    plane_middle(1)
    for q in range(2):
        r.glu_out[:, lane(q * D + i * 128, 128)] = r.glf[pl.ds(pl.multiple_of(i * HB, HB), HB), pl.ds(q * 128, 128)]
    for k in range(7):
        src = lax.rem(i + 7 - k, 8)
        remote(r.st.at[src], r.st.at[src], r.sb.at[0, k], r.sb.at[1, k], nxt).wait_recv()
        for q in range(2):
            blk = r.glu_out.at[:, lane(q * D + src * 128, 128)]
            remote(blk, blk, r.ga.at[0, q, k], r.ga.at[1, q, k], nxt).wait_recv()
    for k in range(7):
        src = lax.rem(w8 + 7 - k, 8)
        remote(r.uland.at[src], r.uland.at[src], r.ua.at[0, k], r.ua.at[1, k], nxt).wait_recv()
    for w in range(8):
        for q in range(4): r.up_out[:, (q * 8 + w) * FB:(q * 8 + w + 1) * FB] = r.uland[w, :, q * FB:(q + 1) * FB]
    plane_end(1, r.down_o)

    for c in early: c.wait()
    pl.when(s < NSEQ - 1)(lambda: halo_copy.wait_send())
    pl.when(s > 0)(lambda: tail_copy.wait_send())
    for c in gm_sends + sends + small_sends(): c.wait_send()
    gc.drain()
    gs.drain()
    ga.drain()
    z_drain()
    for n in range(2):
        for k in range(6): hop(n, k, X).wait_send()


def layer(cfg, tabs, vecs, rate, freq, cre, cim, prior, x, cot, glu_w, up_w, down_w, cid):
    Z, NSEQ, nbits, T, D, FF, M = cfg
    FT, HB = FF // 8, D // 8 // Z
    NR = 4 * M + 16 + 2 * M
    NT = NR
    vm, hbm = pl.BlockSpec(memory_space=pltpu.VMEM), pl.BlockSpec(memory_space=pl.ANY)
    S = lambda shape, dt=F32: jax.ShapeDtypeStruct(shape, dt)
    given = dict(zip(FETCH[5:], tabs), rate=rate, freq=freq, cre=cre, cim=cim, prior=prior)
    ins = dict(h_ftab=hbm, h_itab=hbm, h_jtab=hbm, h_gtab=hbm, **{f"v{k}": vm for k in range(8)}, h_rate=hbm, h_freq=hbm, h_cre=hbm, h_cim=hbm, h_prior=hbm, x=vm, cot=vm,
               glu_w=hbm, up_w=hbm, down_w=hbm)
    outs = dict(out=S((T, D), BF16), ig=S((T, D), BF16), st=S((8, 2 * M, 128)), tot=S((NT, 128)), down_o=S((FT // Z, D)),
                up_out=S((HB, FF)), glu_out=S((HB, 2 * D)))
    V, DS = pltpu.VMEM, lambda *n: pltpu.SemaphoreType.DMA(n)
    row = lambda: V((T, D), F32)
    scr = dict(
        **{k: V(given[k].shape, given[k].dtype) for k in FETCH}, isem=DS(len(FETCH)), osem=DS(2),
        out_v=V((T, D), BF16), ig_v=V((T, D), BF16),
        vecs=V((8, D), F32), upb=V((8, FT), F32),
        xs=row(), own_cot=row(), own_sec=row(), own_act=row(), halo=row(), tail=row(), xhat=row(), pre=row(), val=row(), sg=row(),
        merged=row(), mhat=row(), gm=row(), gz=row(), oacc=row(), sacc=row(), resp=row(), kern=row(),
        xinv=V((T, 128), F32), minv=V((T, 128), F32), ext=V((2 * T, D), F32), X=V((2 * KLEN, D), F32), K=V((2 * KLEN, D), F32),
        land_cot=V((8, T, D), F32), land_sec=V((8, T, D), F32), land_act=V((8, T, D), F32),
        cot_all=V((8 * T, D), BF16), sec_all=V((8 * T, D), BF16), act_all=V((8 * T, D), BF16),
        gw=V((D, 2 * D), BF16), wu=V((2, D, FT), BF16), wd=V((2, FT, D), BF16), wgs=V((D, 256), BF16),
        u=V((256, FT), F32), gh=V((256, FT), F32), hid=V((8 * T, FT), BF16), gul=V((8 * T, FT), BF16),
        glow=V((T, 2 * D), BF16), gm_all=V((8, T, 128), F32), ggl=V((8 * T, 256), BF16),
        upg=V((Z, D // Z, FT), F32), glg=V((Z, D // Z, 256), F32), dng=V((Z, FT // Z, D), F32),
        lup=V((6, D // 8, FT), F32), ldn=V((6, FF // 64, D), F32), uland=V((8, HB, FT), F32), ubg=V((8, FT), F32), upbs=V((8, FT), F32),
        lgl=V((2, Z - 1, D // Z, 256), F32), upf=V((D // Z, FT), F32), glf=V((D // Z, 256), F32),
        qr=V((16, M, LT), F32), qi=V((16, M, LT), F32), big=V((64 * M, LT), F32),
        ssrc=V((NR, D), F32), sland=V((8, NR, 128), F32), mine=V((NT, 128), F32), zland=V((Z, NT, 128), F32),
        lsem=DS(3), tsem=DS(2, 2), hsem=DS(4), gss=DS(14), gsr=DS(14), ms=DS(7), mr=DS(7), zs=DS(2, Z - 1), zr=DS(2, Z - 1),
        lss=DS(2, 3, 2 * Z - 1, 2), lsr=DS(2, 3, 2 * Z - 1, 2), rs=DS(2, 2, 6), ssem=DS(2, 4),
        sa=DS(2, 7), ua=DS(2, 7), sb=DS(2, 7), ga=DS(2, 2, 7), sz=DS(2, Z - 1))
    names = (*ins, *outs, *scr)
    res = pl.pallas_call(
        functools.partial(layer_kernel, cfg, names),
        out_shape=list(outs.values()), in_specs=list(ins.values()), out_specs=[pl.BlockSpec(memory_space=pltpu.HBM)] * 2 + [vm] * (len(outs) - 2), scratch_shapes=list(scr.values()),
        compiler_params=pltpu.CompilerParams(collective_id=cid, has_side_effects=True, vmem_limit_bytes=67043328),
        name="layer")(*tabs, *vecs, rate, freq, cre, cim, prior, x, cot, glu_w, up_w, down_w)
    return dict(zip(outs, res))


def finish_kernel(cfg, names, *refs):
    r = Bag()
    r.__dict__.update(zip(names, refs))
    Z, NSEQ, nbits, T, D, FF, M = cfg
    HB = D // 8 // Z
    b = lax.axis_index("batch")
    for k in ("out", "ig", "glu_out", "up_out", "down_o"): r.__dict__["o_" + k][...] = r.__dict__[k][...]
    for j in range(8): r.o_st[:, j * 128:(j + 1) * 128] = r.st[j]
    r.turned[...] = r.tot[0:4 * M, :].T
    mine = r.turned[pl.ds(pl.multiple_of(b * HB, HB), HB), :]
    for k in range(4): r.__dict__[f"m{k}"][...] = mine[:, k * M:(k + 1) * M]
    v = pltpu.roll(r.tot[4 * M:4 * M + 8, :], lax.rem(128 - b * HB, 128), 1)
    for k in range(6): r.__dict__[f"w{k}"][...] = v[k, 0:HB]
    per = 128 // (2 * HB)
    g = r.tot[pl.ds(4 * M + 6 + b // per, 1), :]
    r.gb[...] = pltpu.roll(jnp.broadcast_to(g, (8, 128)), lax.rem(128 - lax.rem(b, per) * 2 * HB, 128), 1)[0, 0:2 * HB]
    r.ub[...] = r.tot[pl.ds(4 * M + 8 + b, 1), :].reshape(128)


def finish(cfg, o):
    Z, NSEQ, nbits, T, D, FF, M = cfg
    HB = D // 8 // Z
    vm = pl.BlockSpec(memory_space=pltpu.VMEM)
    S = lambda shape, dt=F32: jax.ShapeDtypeStruct(shape, dt)
    outs = {"o_" + k: S(o[k].shape, o[k].dtype) for k in ("out", "ig", "glu_out", "up_out", "down_o")}
    outs["o_st"] = S((2 * M, D))
    outs.update({f"m{k}": S((HB, M)) for k in range(4)})
    outs.update({f"w{k}": S((HB,)) for k in range(6)})
    outs.update(gb=S((2 * HB,)), ub=S((FF // 8 // Z,)))
    names = (*o, *outs, "turned")
    res = pl.pallas_call(functools.partial(finish_kernel, cfg, names), out_shape=list(outs.values()), in_specs=[vm] * len(o),
                         out_specs=[vm] * len(outs), scratch_shapes=[pltpu.VMEM((128, 4 * M), F32)], name="finish")(*o.values())
    return {k.removeprefix("o_"): v for k, v in zip(outs, res)}


def tables(window):
    half = window // 2
    f = np.concatenate([np.arange(half + 1), np.arange(1, half)])[:, None]
    imag = np.arange(window)[:, None] > half
    ph = (f * np.arange(window)[None, :] % window) * (2.0 * np.pi / window)
    fwd = np.where(imag, -np.sin(ph), np.cos(ph))
    wt = np.where((f == 0) | (2 * f == window), 1.0, 2.0) / window
    inv = (wt * fwd).T[half:]
    def parts(a):
        a = np.ascontiguousarray(a).astype(np.float32)
        high = a.astype(ml_dtypes.bfloat16)
        return jnp.asarray(np.stack([high, (a - high.astype(np.float32)).astype(ml_dtypes.bfloat16)]))
    return parts(fwd), parts(inv), parts(inv.T), parts(fwd.T)


def plane_shards(Z, n_seq, inputs, first_gain, first_shift, decay_rate, rotation, out_real, out_imag, skip_gain, glu_weight,
                 glu_bias, second_gain, second_shift, up_weight, up_bias, down_weight, down_bias, prior_state, cotangent):
    T, D = inputs.shape[1:]
    FF, M = up_weight.shape[1], decay_rate.shape[1]
    FT, HB = FF // 8, D // 8 // Z
    cfg = (Z, n_seq, max(1, (n_seq - 1).bit_length()), T, D, FF, M)
    vecs = (first_gain, first_shift, skip_gain, second_gain, second_shift, down_bias, glu_bias, up_bias)
    o = layer(cfg, tables(T + KLEN), vecs, decay_rate.T, rotation.T, out_real.T, out_imag.T, prior_state,
              inputs[0], cotangent[0], glu_weight, up_weight, down_weight, 0)
    f = finish(cfg, o)
    v = [f[f"w{k}"] for k in range(6)]
    m = [f[f"m{k}"] for k in range(4)]
    return (f["out"][None], f["ig"][None], f["st"].reshape(1, 2, M, D), v[0], v[1], *m, v[2], f["glu_out"], f["gb"],
            v[3], v[4], f["up_out"], f["ub"], f["down_o"], v[5])


def solution(mesh):
    in_specs = (
        P("batch", "seq", None),
        P(),
        P(),
        P(),
        P(),
        P(),
        P(),
        P(),
        P(),
        P(),
        P(),
        P(),
        P(),
        P(),
        P(),
        P(),
        P("batch", None, None, None),
        P("batch", "seq", None),
    )
    out_specs = (
        P("batch", "seq", None),
        P("batch", "seq", None),
        P("batch", None, None, None),
        P(BOTH),
        P(BOTH),
        P(BOTH, None),
        P(BOTH, None),
        P(BOTH, None),
        P(BOTH, None),
        P(BOTH),
        P(BOTH, None),
        P(BOTH),
        P(BOTH),
        P(BOTH),
        P(BOTH, None),
        P(BOTH),
        P(BOTH, None),
        P(BOTH),
    )
    body = shards
    if mesh.shape["seq"] == 8:
        body = functools.partial(plane_shards, mesh.shape["batch"], mesh.shape["seq"])
    return jax.shard_map(body, mesh=mesh, in_specs=in_specs, out_specs=out_specs, check_vma=False)
```
